32 devices in a mesh: head: 2 (over y), blk: 16 (over z, x, core).
Axes of the slice: x: 2, y: 2, z: 4, core: 2. Of those that a mesh axis runs over, the one named last changes fastest.
Arguments:
- tokens: bfloat16 [2, 2048, 768], P(None, ('blk', 'head')), may hold values from -6 to 6
- doc_ids: int32 [2, 2048], P(None, ('blk', 'head')), may hold values from 0 to 3, never falling along the last dimension, each value on 1 to 1536 neighbouring positions
- cotangent: bfloat16 [2, 2048, 768], P(None, ('blk', 'head')), may hold values from -6 to 6
- attn_weight: float32 [4, 768, 768], P(None, ('blk', 'head'))
- ffn_weight: float32 [3, 768, 2048], P(None, ('blk', 'head'))
- attn_moment: float32 [4, 768, 768], P(None, ('blk', 'head'))
- ffn_moment: float32 [3, 768, 2048], P(None, ('blk', 'head'))
Outputs:
- output: bfloat16 [2, 2048, 768], P(None, ('blk', 'head'))
- input_grad: float32 [2, 2048, 768], P(None, ('blk', 'head'))
- attn_grad: float32 [4, 768, 768], P(None, ('blk', 'head'))
- ffn_grad: float32 [3, 768, 2048], P(None, ('blk', 'head'))
- attn_master: float32 [4, 768, 768], P(None, ('blk', 'head'))
- ffn_master: float32 [3, 768, 2048], P(None, ('blk', 'head'))
- attn_moment_new: float32 [4, 768, 768], P(None, ('blk', 'head'))
- ffn_moment_new: float32 [3, 768, 2048], P(None, ('blk', 'head'))
- attn_copy: bfloat16 [4, 768, 768], P(None, ('blk', 'head'))
- ffn_copy: bfloat16 [3, 768, 2048], P(None, ('blk', 'head'))
The draws below stay inside these ranges and needn't reach their ends.
Inputs may be any that keep to these rules, and one draw needn't show every extreme that they name: `doc_ids`: in each micro-batch the document numbers never fall along the sequence; every document has 1 to 1536 positions and one has exactly 1536.
All inputs are finite; a program needn't handle non-finite values.
Results may differ from the reference program's by a relative error of at most 0.04.
Values may be sent and summed in bfloat16 or wider, within the bound.
A program may use at most 320 MiB of HBM per device.

```python
import math
import jax
import jax.numpy as jnp
import numpy as np
from jax import lax

D = 768
HEADS = 12
HEAD_DIM = 64
FF = 2048
MB = 2
DOCS = 4
NS_STEPS = 5
LEN = 2048
MOST = 1536


def scaled_draw(key, shape, scales):
    base = jax.random.normal(key, shape, jnp.float32)
    return base * jnp.asarray(scales, jnp.float32)[:, None, None]


def draw_attn_weight(key, part):
    inverse = D ** (-0.5)
    return scaled_draw(jax.random.fold_in(key, 11), (4, D, D), [inverse, inverse, inverse, 0.5])


def draw_ffn_weight(key, part):
    return scaled_draw(jax.random.fold_in(key, 23), (3, D, FF), [D ** (-0.5), D ** (-0.5), FF ** (-0.5)])


def draw_attn_moment(key, part):
    return scaled_draw(jax.random.fold_in(key, 37), (4, D, D), [10.0, 10.0, 10.0, 10.0])


def draw_ffn_moment(key, part):
    return scaled_draw(jax.random.fold_in(key, 41), (3, D, FF), [50.0, 50.0, 50.0])


def steps_of(rng, extent, split, least, high):
    def one(dim, parts):
        heights = jax.random.uniform(jax.random.fold_in(jax.random.fold_in(rng, 6), dim), (parts,), jnp.float32, least / len(split), high / len(split))
        return jnp.repeat(jnp.exp(heights), extent[dim] // parts).reshape((-1,) + (1,) * (len(extent) - dim - 1))

    factor_of = one(*split[0])
    for cut in split[1:]:
        factor_of = factor_of * one(*cut)
    return factor_of


def profile(count, total, limit, skew):
    portions = [(1 << 20) // math.isqrt(standing ** skew) + 1 for standing in range(2, count + 1)]
    surplus, holding = total - limit - (count - 1), [1] * (count - 1)
    while surplus > 0:
        candidates = [i for i in range(count - 1) if holding[i] < limit]
        pool, remaining = sum([portions[i] for i in candidates]), surplus
        for i in candidates:
            extra = min(limit - holding[i], max(1, remaining * portions[i] // pool), surplus)
            holding[i] = holding[i] + extra
            surplus = surplus - extra
    return np.array([limit] + holding)


def ragged(rng, number_of, total, bound, lean):
    if number_of == 2:
        one = jax.random.randint(rng, (), max(1, total - bound), min(bound, total - 1) + 1)
        return jnp.stack([one, total - one])
    lengths = jnp.asarray(profile(number_of, total, bound, lean), jnp.int32)
    pairs = (number_of - 1) // 2
    source_of, sink = lengths[1:1 + 2 * pairs:2], lengths[2:2 + 2 * pairs:2]
    slack = jnp.minimum(source_of - 1, bound - sink)
    passed = jax.random.randint(jax.random.fold_in(rng, 1), (pairs,), 0, 1 << 20) % (slack + 1)
    lengths = lengths.at[1:1 + 2 * pairs:2].set(source_of - passed).at[2:2 + 2 * pairs:2].set(sink + passed)
    return lengths[jax.random.permutation(jax.random.fold_in(rng, 2), number_of)]


def bell_draw(rng, extent, scale, most, cuts=(), kind=jnp.bfloat16):
    result = scale * jax.random.normal(rng, extent, jnp.float32)
    if cuts:
        result = result * steps_of(rng, extent, cuts, -0.22, 0.18)
    return jnp.clip(result, -most, most).astype(kind)


def setup_inputs(seed: int = 0) -> dict:
    arg_keys = jax.random.split(jax.random.key(seed), 8)
    return {
        "tokens": bell_draw(arg_keys[0], (MB, LEN, D), 1.0, 6.0, ((1, 32),)),
        "doc_ids": jax.vmap(lambda own: jnp.searchsorted(jnp.cumsum(ragged(own, DOCS, LEN, MOST, 2)), jnp.arange(LEN), side="right"))(jax.random.split(arg_keys[1], MB)).reshape((MB, LEN)).astype(jnp.int32),
        "cotangent": bell_draw(arg_keys[2], (MB, LEN, D), 1.0, 6.0, ((1, 32),)),
        "attn_weight": draw_attn_weight(jax.random.fold_in(arg_keys[7], 71), 0),
        "ffn_weight": draw_ffn_weight(jax.random.fold_in(arg_keys[7], 71), 0),
        "attn_moment": draw_attn_moment(jax.random.fold_in(arg_keys[7], 71), 0),
        "ffn_moment": draw_ffn_moment(jax.random.fold_in(arg_keys[7], 71), 0),
    }


HIGHEST = lax.Precision.HIGHEST
EPSILON = 1e-05
NEGATIVE = -1e+30
RATES = (0.5, 0.5, 0.5, 7.0, 1.0, 1.0, 0.5)
COEFF_A = 3.4445
COEFF_B = -4.775
COEFF_C = 2.0315

@jax.custom_vjp
def low(v):
    return lax.optimization_barrier(v.astype(jnp.bfloat16)).astype(jnp.float32)

@jax.custom_vjp
def low_back(v):
    return v

def low_keep(v):
    return (low(v), None)

def low_pass(kept, grad):
    return (grad,)

def back_keep(v):
    return (v, None)

def back_low(kept, grad):
    return (low(grad),)
low.defvjp(low_keep, low_pass)
low_back.defvjp(back_keep, back_low)

def matmul(left, right):
    return jnp.dot(left, right, precision=HIGHEST)

def layer_norm(values):
    center = values - lax.optimization_barrier(jnp.mean(values, axis=-1, keepdims=True))
    spread = lax.optimization_barrier(jnp.mean(center * center, axis=-1, keepdims=True))
    return center * lax.rsqrt(spread + EPSILON)

def rotate(values, cosine_table, sine_table):
    shaped = values.reshape(values.shape[0], -1, 2, HEAD_DIM // 2)
    first_half = shaped[:, :, 0, :]
    second_half = shaped[:, :, 1, :]
    cosine_part = cosine_table[:, None, :]
    sine_part = sine_table[:, None, :]
    turned = jnp.stack([first_half * cosine_part - second_half * sine_part, second_half * cosine_part + first_half * sine_part], axis=2)
    return turned.reshape(values.shape)

def frequency_tables(position):
    inverse = 10000.0 ** (-(jnp.arange(HEAD_DIM // 2, dtype=jnp.float32) * 2.0) / HEAD_DIM)
    angles = position[:, None] * inverse[None, :]
    return (jnp.cos(angles), jnp.sin(angles))

def doc_starts(counts, row_index):
    starts = jnp.cumsum(counts) - counts
    chosen = jnp.where(starts[None, :] <= row_index[:, None], starts[None, :], 0.0)
    return lax.optimization_barrier(jnp.max(chosen, axis=1))

def attend_block(query_block, key_part, value_part, index_block, start_block):
    key_count = key_part.shape[0]
    query_heads = query_block.reshape(query_block.shape[0], HEADS, HEAD_DIM)
    key_heads = key_part.reshape(key_count, HEADS, HEAD_DIM)
    value_heads = value_part.reshape(key_count, HEADS, HEAD_DIM)
    key_index = jnp.arange(key_count).astype(jnp.float32)
    scores = jnp.einsum('qhd,khd->hqk', query_heads, key_heads, precision=HIGHEST)
    scores = low_back(scores) * HEAD_DIM ** (-0.5)
    allowed = (key_index[None, :] <= index_block[:, None]) & (key_index[None, :] >= start_block[:, None])
    scores = jnp.where(allowed[None], scores, NEGATIVE)
    row_top = lax.optimization_barrier(jnp.max(scores, axis=-1, keepdims=True))
    weights = jnp.where(allowed[None], jnp.exp(scores - row_top), 0.0)
    probabilities = weights / lax.optimization_barrier(jnp.sum(weights, axis=-1, keepdims=True))
    mixed_rows = jnp.einsum('hqk,khd->qhd', low(probabilities), value_heads, precision=HIGHEST)
    return mixed_rows.reshape(query_block.shape[0], HEADS * HEAD_DIM)

def attention(queries, key_rows, value_rows, row_index, row_start):
    key_total = queries.shape[0]
    block_rows = math.gcd(key_total, 512)
    pieces = []
    for block_index in range(key_total // block_rows):
        block_end = (block_index + 1) * block_rows
        block_begin = block_end - block_rows
        pieces.append(jax.checkpoint(attend_block)(queries[block_begin:block_end], key_rows[:block_end], value_rows[:block_end], row_index[block_begin:block_end], row_start[block_begin:block_end]))
    return jnp.concatenate(pieces, axis=0)

def forward(inputs, attn_master, ffn_master, tables):
    attn_low = low(attn_master)
    ffn_low = low(ffn_master)
    results = []
    for micro_index in range(MB):
        cosine_table, sine_table, row_index, row_start = tables[micro_index]
        hidden = inputs[micro_index]
        normed = low(layer_norm(hidden))
        queries = low(rotate(low_back(matmul(normed, attn_low[0])), cosine_table, sine_table))
        key_rows = low(rotate(low_back(matmul(normed, attn_low[1])), cosine_table, sine_table))
        value_rows = low(low_back(matmul(normed, attn_low[2])))
        mixed_rows = low(low_back(attention(queries, key_rows, value_rows, row_index, row_start)))
        middle = hidden + low_back(matmul(mixed_rows, attn_low[3]))
        second = low(layer_norm(middle))
        gate_values = low_back(matmul(second, ffn_low[0]))
        upward = low_back(matmul(second, ffn_low[1]))
        product = low(jax.nn.silu(gate_values) * upward)
        results.append(middle + matmul(product, ffn_low[2].T))
    return jnp.stack(results)

def orthogonal(update):
    rounded = low(update)
    frobenius = jnp.sqrt(jnp.sum(rounded * rounded))
    current = low(rounded / (frobenius + 1e-07))
    for step_index in range(NS_STEPS):
        gram_matrix = low(jnp.dot(current, current.T, precision=HIGHEST))
        polynomial = low(COEFF_B * gram_matrix + COEFF_C * jnp.dot(gram_matrix, gram_matrix, precision=HIGHEST))
        current = low(COEFF_A * current + jnp.dot(polynomial, current, precision=HIGHEST))
    return current

def reference(tokens, doc_ids, cotangent, attn_weight, ffn_weight, attn_moment, ffn_moment):
    key_total = tokens.shape[1]
    row_index = jnp.arange(key_total).astype(jnp.float32)
    tables = []
    for micro_index in range(MB):
        counts = lax.optimization_barrier(jnp.sum((doc_ids[micro_index][:, None] == jnp.arange(DOCS)[None, :]).astype(jnp.float32), axis=0))
        row_start = doc_starts(counts, row_index)
        cosine_table, sine_table = frequency_tables(row_index - row_start)
        tables.append((cosine_table, sine_table, row_index, row_start))
    inputs = tokens.astype(jnp.float32)

    def closed(layer_input, attn_master, ffn_master):
        return forward(layer_input, attn_master, ffn_master, tables)
    outputs, pullback = jax.vjp(closed, inputs, attn_weight, ffn_weight)
    input_grad, attn_grad, ffn_grad = pullback(cotangent.astype(jnp.float32))
    attn_moment_new = 0.5 * attn_moment + 0.5 * attn_grad
    ffn_moment_new = 0.5 * ffn_moment + 0.5 * ffn_grad
    attn_update = 0.5 * attn_grad + 0.5 * attn_moment_new
    ffn_update = 0.5 * ffn_grad + 0.5 * ffn_moment_new
    attn_master = attn_weight - jnp.stack([RATES[matrix_index] * orthogonal(attn_update[matrix_index]) for matrix_index in range(4)])
    ffn_master = ffn_weight - jnp.stack([RATES[4 + matrix_index] * orthogonal(ffn_update[matrix_index]) for matrix_index in range(3)])
    return (outputs.astype(jnp.bfloat16), input_grad, attn_grad, ffn_grad, attn_master, ffn_master, attn_moment_new, ffn_moment_new, attn_master.astype(jnp.bfloat16), ffn_master.astype(jnp.bfloat16))
```

```python
import functools
import math

import jax
import jax.numpy as jnp
from jax import lax
from jax.experimental import pallas as pl
from jax.experimental.pallas import tpu as pltpu
from jax.sharding import PartitionSpec as P

D = 768
HEADS = 12
HEAD_DIM = 64
HALF = 32
FF = 2048
DOCS = 4
NS_STEPS = 5
GROUP = 8
SPARE = 2
BLOCK = 256

EPSILON = 1e-05
NEGATIVE = -1e30
RATES = (0.5, 0.5, 0.5, 7.0, 1.0, 1.0, 0.5)
COEFF_A = 3.4445
COEFF_B = -4.775
COEFF_C = 2.0315
OWNERS = (0, 9, 28, 21, 16, 17, 20)
MESH = pl.DeviceIdType.MESH
ANY = pl.BlockSpec(memory_space=pl.ANY)
VMEM = pl.BlockSpec(memory_space=pltpu.VMEM)
SMEM = pl.BlockSpec(memory_space=pltpu.SMEM)
SCALE = HEAD_DIM ** (-0.5)


def nt(a, b):
    return lax.dot_general(a, b, (((1,), (1,)), ((), ())), preferred_element_type=jnp.float32)


def nn(a, b):
    return jnp.dot(a, b, preferred_element_type=jnp.float32)


def attends(device):
    plane = device // GROUP
    return jnp.logical_and(plane < 4, plane != SPARE)


def combo_of(device):
    plane = device // GROUP
    place = device % GROUP
    return (place // 4) * HEADS + 4 * (plane - plane // 3) + place % 4


def device_of(combo):
    group = (combo % HEADS) // 4
    return GROUP * (group + group // 2) + 4 * (combo // HEADS) + combo % 4


class Net:
    def __init__(self, mesh):
        self.inner = mesh.shape["head"]
        self.count = mesh.shape["head"] * mesh.shape["blk"]

    def me(self):
        return lax.axis_index("blk") * self.inner + lax.axis_index("head")

    def at(self, device):
        return {"blk": device // self.inner, "head": device % self.inner}

    def meet(self, me):
        barrier = pltpu.get_barrier_semaphore()

        def greet(k, carry):
            other = (me + k) % self.count
            pl.semaphore_signal(barrier, inc=1, device_id=self.at(other), device_id_type=MESH)
            return carry

        lax.fori_loop(1, self.count, greet, 0)
        pl.semaphore_wait(barrier, self.count - 1)


def exchange_kernel(net, flows, sources, *refs):
    inputs = refs[:sources]
    outputs = refs[sources:-3]
    send, receive, local = refs[-3:]
    count = net.count
    me = net.me()
    net.meet(me)

    def remote(flow, number, i, j, k):
        source, target, goes, take, put = flow
        return pltpu.make_async_remote_copy(
            inputs[source].at[take(i, j)],
            outputs[target].at[put(i, j)],
            send.at[number, k],
            receive.at[number, k],
            device_id=net.at(j),
            device_id_type=MESH,
        )

    for number, flow in enumerate(flows):
        source, target, goes, take, put = flow

        def start(k, carry, flow=flow, number=number, goes=goes):
            other = (me + k) % count

            @pl.when(goes(me, other))
            def _():
                remote(flow, number, me, other, k).start()

            return carry

        lax.fori_loop(1, count, start, 0)

        @pl.when(goes(me, me))
        def _(source=source, target=target, take=take, put=put, number=number):
            pltpu.make_async_copy(
                inputs[source].at[take(me, me)], outputs[target].at[put(me, me)], local.at[number]
            ).start()

    for number, flow in enumerate(flows):
        source, target, goes, take, put = flow

        def finish(k, carry, flow=flow, number=number, goes=goes):
            other = (me + k) % count

            @pl.when(goes(me, other))
            def _():
                remote(flow, number, me, other, k).wait_send()

            before = (me + count - k) % count

            @pl.when(goes(before, me))
            def _():
                remote(flow, number, before, me, k).wait_recv()

            return carry

        lax.fori_loop(1, count, finish, 0)

        @pl.when(goes(me, me))
        def _(source=source, target=target, take=take, put=put, number=number):
            pltpu.make_async_copy(
                inputs[source].at[take(me, me)], outputs[target].at[put(me, me)], local.at[number]
            ).wait()


def exchange(net, name, number, flows, sources, shapes):
    moved = sum(math.prod(s.shape) * s.dtype.itemsize for s in shapes)
    return pl.pallas_call(
        functools.partial(exchange_kernel, net, flows, len(sources)),
        out_shape=shapes,
        in_specs=[ANY] * len(sources),
        out_specs=[ANY] * len(shapes),
        scratch_shapes=[
            pltpu.SemaphoreType.DMA((len(flows), net.count)),
            pltpu.SemaphoreType.DMA((len(flows), net.count)),
            pltpu.SemaphoreType.DMA((len(flows),)),
        ],
        compiler_params=pltpu.CompilerParams(collective_id=number, has_side_effects=True),
        cost_estimate=pl.CostEstimate(flops=0, bytes_accessed=8 * moved, transcendentals=0),
        name=name,
    )(*sources)


def gather_kernel(net, x_ref, w_ref, all_ref, wall_ref, send, receive, wsend, wreceive, local):
    count = net.count
    planes = count // GROUP
    me = net.me()
    plane = me // GROUP
    place = me % GROUP
    half = place // 4
    spot = place % 4
    across = me + 4 - 8 * half
    beside = me + 1 - 2 * (spot % 2)
    sibling = me + 2 - 4 * (spot // 2)
    net.meet(me)

    def remote(source, target, index, device):
        return pltpu.make_async_remote_copy(
            source, target, send.at[index], receive.at[index], device_id=net.at(device), device_id_type=MESH
        )

    swap = remote(x_ref.at[1 - half], all_ref.at[plane, half, spot], 0, across)
    swap.start()
    mine = pltpu.make_async_copy(x_ref.at[half], all_ref.at[plane, half, spot], local.at[0])
    mine.start()
    mine.wait()

    def second(step, which):
        target = (me + step * GROUP) % count
        block = all_ref.at[plane, which, spot]
        return remote(block, block, 1 + (step - 1) * 2 + (which + half) % 2, target)

    third_base = 1 + 2 * (planes - 1)

    def third(step, which):
        source_plane = (plane + planes - step) % planes
        block = all_ref.at[source_plane, which, spot]
        return remote(block, block, third_base + step * 2 + which, beside)

    fourth_base = third_base + 2 * planes

    def fourth(step, which):
        source_plane = (plane + planes - step) % planes
        block = all_ref.at[source_plane, which, pl.ds((spot // 2) * 2, 2)]
        return remote(block, block, fourth_base + step * 2 + which, sibling)

    for step in range(1, planes):
        second(step, half).start()

    def weights(combo):
        target = device_of(combo)
        return pltpu.make_async_remote_copy(
            w_ref.at[combo % HEADS],
            wall_ref.at[me],
            wsend.at[combo],
            wreceive.at[me],
            device_id=net.at(target),
            device_id_type=MESH,
        )

    def send_weights(combo, carry):
        @pl.when(device_of(combo) != me)
        def _():
            weights(combo).start()

        return carry

    lax.fori_loop(0, 2 * HEADS, send_weights, 0)

    swap.wait_recv()
    for step in range(1, planes):
        second(step, 1 - half).start()
    for which in range(2):
        third(0, which).start()
    for step in range(planes):
        if step > 0:
            second(step, half).wait_recv()
            second(step, 1 - half).wait_recv()
            for which in range(2):
                third(step, which).start()
        if step > 0:
            for which in range(2):
                third(step - 1, which).wait_recv()
            for which in range(2):
                fourth(step - 1, which).start()
    for which in range(2):
        third(planes - 1, which).wait_recv()
    for which in range(2):
        fourth(planes - 1, which).start()
    for step in range(planes):
        for which in range(2):
            fourth(step, which).wait_recv()

    @pl.when(attends(me))
    def _():
        own = pltpu.make_async_copy(w_ref.at[combo_of(me) % HEADS], wall_ref.at[me], local.at[1])
        own.start()
        own.wait()

        def took(k, carry):
            before = (me + k) % count
            pltpu.make_async_remote_copy(
                w_ref.at[0],
                wall_ref.at[before],
                wsend.at[0],
                wreceive.at[before],
                device_id=net.at(before),
                device_id_type=MESH,
            ).wait_recv()
            return carry

        lax.fori_loop(1, count, took, 0)

    def sent(combo, carry):
        @pl.when(device_of(combo) != me)
        def _():
            weights(combo).wait_send()

        return carry

    lax.fori_loop(0, 2 * HEADS, sent, 0)
    swap.wait_send()
    for step in range(1, planes):
        second(step, half).wait_send()
        second(step, 1 - half).wait_send()
    for step in range(planes):
        for which in range(2):
            third(step, which).wait_send()
            fourth(step, which).wait_send()


def gather_tokens(net, number, normed, columns):
    planes = net.count // GROUP
    copies = 1 + 2 * (planes - 1) + 4 * planes
    shapes = [
        jax.ShapeDtypeStruct((planes, 2, 4) + normed.shape[1:], normed.dtype),
        jax.ShapeDtypeStruct((net.count,) + columns.shape[1:], columns.dtype),
    ]
    return pl.pallas_call(
        functools.partial(gather_kernel, net),
        out_shape=shapes,
        in_specs=[ANY] * 2,
        out_specs=[ANY] * 2,
        scratch_shapes=[
            pltpu.SemaphoreType.DMA((copies,)),
            pltpu.SemaphoreType.DMA((copies,)),
            pltpu.SemaphoreType.DMA((2 * HEADS,)),
            pltpu.SemaphoreType.DMA((net.count,)),
            pltpu.SemaphoreType.DMA((2,)),
        ],
        compiler_params=pltpu.CompilerParams(collective_id=number, has_side_effects=True),
        cost_estimate=pl.CostEstimate(flops=0, bytes_accessed=100 * 2**20, transcendentals=0),
        name="gather_tokens",
    )(normed, columns)


def rope_rows(values, cosine, sine):
    first, second = values[:HALF], values[HALF:]
    return jnp.concatenate([first * cosine - second * sine, second * cosine + first * sine], axis=0)


def rope_rows_back(values, cosine, sine):
    first, second = values[:HALF], values[HALF:]
    return jnp.concatenate([first * cosine + second * sine, second * cosine - first * sine], axis=0)


def columns_of(index):
    return pl.ds(pl.multiple_of(index * BLOCK, BLOCK), BLOCK)


def positions(query_block, key_block):
    shape = (BLOCK, BLOCK)
    key = key_block * BLOCK + lax.broadcasted_iota(jnp.int32, shape, 0)
    query = query_block * BLOCK + lax.broadcasted_iota(jnp.int32, shape, 1)
    return key, query


def fold(rows):
    return jnp.concatenate([rows[:HALF], rows[HALF:]], axis=1)


def unfold(rows):
    return jnp.concatenate([rows[:, :HEAD_DIM], rows[:, HEAD_DIM:]], axis=0)


def attend_kernel(first_ref, x_ref, w_ref, cos_ref, sin_ref, start_ref, qkv_ref, mixed_ref, total_ref, packed_ref, key_rows):
    blocks = qkv_ref.shape[1] // BLOCK
    weights = w_ref[...]

    def project(chunk, carry):
        tokens = x_ref[chunk // 2, chunk % 2].reshape(BLOCK, D)
        here = columns_of(chunk)
        made = nt(weights, tokens)
        cosine, sine = cos_ref[:, here], sin_ref[:, here]
        query = rope_rows(made[:HEAD_DIM], cosine, sine)
        key = rope_rows(made[HEAD_DIM : 2 * HEAD_DIM], cosine, sine)
        qkv_ref[:HEAD_DIM, here] = query.astype(jnp.bfloat16)
        qkv_ref[HEAD_DIM : 2 * HEAD_DIM, here] = key.astype(jnp.bfloat16)
        qkv_ref[2 * HEAD_DIM :, here] = made[2 * HEAD_DIM :].astype(jnp.bfloat16)
        key_rows[here, :] = key.T.astype(jnp.bfloat16)
        return carry

    lax.fori_loop(0, blocks, project, 0)

    def query_step(query_block, carry):
        here = columns_of(query_block)
        query = qkv_ref[:HEAD_DIM, here]
        start = start_ref[:, here]

        def key_step(key_block, held):
            top, total, mixed = held
            there = columns_of(key_block)
            scores = nn(key_rows[there, :], query) * SCALE
            key_at, query_at = positions(query_block, key_block)
            allowed = (key_at <= query_at) & (key_at >= start)
            scores = jnp.where(allowed, scores, NEGATIVE)
            new_top = jnp.maximum(top, jnp.max(scores, axis=0, keepdims=True))
            weights = jnp.where(allowed, jnp.exp(scores - new_top), 0.0)
            factor = jnp.exp(top - new_top)
            total = total * factor + jnp.sum(weights, axis=0, keepdims=True)
            mixed = mixed * factor + nn(qkv_ref[2 * HEAD_DIM :, there], weights.astype(jnp.bfloat16))
            return new_top, total, mixed

        top, total, mixed = lax.fori_loop(
            first_ref[query_block],
            query_block + 1,
            key_step,
            (
                jnp.full((1, BLOCK), NEGATIVE, jnp.float32),
                jnp.zeros((1, BLOCK), jnp.float32),
                jnp.zeros((HEAD_DIM, BLOCK), jnp.float32),
            ),
        )
        mixed = mixed / total
        mixed_ref[:, here] = mixed
        total_ref[:, here] = top + jnp.log(total)
        rows = mixed.T
        for part in range(BLOCK // 64):
            packed_ref[query_block * (BLOCK // 64) + part] = fold(rows[part * 64 : part * 64 + 64]).astype(
                jnp.bfloat16
            )
        return carry

    lax.fori_loop(0, blocks, query_step, 0)


def attend(net, first, tokens, weights, cosine, sine, start):
    length = start.shape[1]
    return pl.pallas_call(
        attend_kernel,
        out_shape=[
            jax.ShapeDtypeStruct((3 * HEAD_DIM, length), jnp.bfloat16),
            jax.ShapeDtypeStruct((HEAD_DIM, length), jnp.float32),
            jax.ShapeDtypeStruct((1, length), jnp.float32),
            jax.ShapeDtypeStruct((net.count, HALF, 128), jnp.bfloat16),
        ],
        in_specs=[SMEM] + [VMEM] * 5,
        out_specs=[VMEM] * 4,
        scratch_shapes=[pltpu.VMEM((length, HEAD_DIM), jnp.bfloat16)],
        cost_estimate=pl.CostEstimate(flops=2 * 10**9, bytes_accessed=8 * 2**20, transcendentals=2 * 10**6),
        name="attend",
    )(first, tokens, weights, cosine, sine, start)


def attend_back_kernel(
    first_ref,
    x_ref,
    qkv_ref,
    mixed_ref,
    total_ref,
    cos_ref,
    sin_ref,
    start_ref,
    grad_ref,
    packed_ref,
    weight_ref,
    query_rows,
    key_rows,
    value_rows,
    grad_rows,
    grad_columns,
    correction,
    key_grad,
    value_grad,
    all_grad,
):
    blocks = qkv_ref.shape[1] // BLOCK
    parts = BLOCK // 64

    def prepare(chunk, carry):
        here = columns_of(chunk)
        turned = qkv_ref[:, here].astype(jnp.float32)
        query_rows[here, :] = turned[:HEAD_DIM].T.astype(jnp.bfloat16)
        key_rows[here, :] = turned[HEAD_DIM : 2 * HEAD_DIM].T.astype(jnp.bfloat16)
        value_rows[here, :] = turned[2 * HEAD_DIM :].T.astype(jnp.bfloat16)
        pieces = [unfold(grad_ref[chunk * parts + part].astype(jnp.float32)) for part in range(parts)]
        rows = jnp.concatenate(pieces, axis=0)
        grad_rows[here, :] = rows.astype(jnp.bfloat16)
        across = rows.T
        grad_columns[:, here] = across.astype(jnp.bfloat16)
        correction[:, here] = jnp.sum(across * mixed_ref[:, here], axis=0, keepdims=True)
        key_grad[here, :] = jnp.zeros((BLOCK, HEAD_DIM), jnp.float32)
        value_grad[here, :] = jnp.zeros((BLOCK, HEAD_DIM), jnp.float32)
        return carry

    lax.fori_loop(0, blocks, prepare, 0)

    def query_step(query_block, carry):
        here = columns_of(query_block)
        query = qkv_ref[:HEAD_DIM, here]
        start = start_ref[:, here]
        total = total_ref[:, here]
        fix = correction[:, here]
        grad = grad_columns[:, here]
        query_in_rows = query_rows[here, :]
        grad_in_rows = grad_rows[here, :]

        def key_step(key_block, query_grad):
            there = columns_of(key_block)
            scores = nn(key_rows[there, :], query) * SCALE
            key_at, query_at = positions(query_block, key_block)
            allowed = (key_at <= query_at) & (key_at >= start)
            weights = jnp.where(allowed, jnp.exp(scores - total), 0.0)
            value_grad[there, :] += nn(weights.astype(jnp.bfloat16), grad_in_rows)
            slope = nn(value_rows[there, :], grad)
            change = (weights * (slope - fix) * SCALE).astype(jnp.bfloat16)
            key_grad[there, :] += nn(change, query_in_rows)
            return query_grad + nn(qkv_ref[HEAD_DIM : 2 * HEAD_DIM, there], change)

        query_grad = lax.fori_loop(
            first_ref[query_block], query_block + 1, key_step, jnp.zeros((HEAD_DIM, BLOCK), jnp.float32)
        )
        query_grad = rope_rows_back(query_grad, cos_ref[:, here], sin_ref[:, here])
        all_grad[:HEAD_DIM, here] = query_grad.astype(jnp.bfloat16)
        rows = query_grad.T.astype(jnp.bfloat16)
        for part in range(parts):
            packed_ref[query_block * parts + part, :64, :HEAD_DIM] = rows[part * 64 : part * 64 + 64]
        return carry

    lax.fori_loop(0, blocks, query_step, 0)
    weight_ref[...] = jnp.zeros(weight_ref.shape, jnp.float32)

    def close(chunk, carry):
        here = columns_of(chunk)
        key = rope_rows_back(key_grad[here, :].T, cos_ref[:, here], sin_ref[:, here])
        value = value_grad[here, :]
        all_grad[HEAD_DIM : 2 * HEAD_DIM, here] = key.astype(jnp.bfloat16)
        all_grad[2 * HEAD_DIM :, here] = value.T.astype(jnp.bfloat16)
        rows = key.T.astype(jnp.bfloat16)
        for part in range(parts):
            token = chunk * parts + part
            packed_ref[token, :64, HEAD_DIM:] = rows[part * 64 : part * 64 + 64]
            packed_ref[token, 64:, :] = fold(value[part * 64 : part * 64 + 64]).astype(jnp.bfloat16)
        tokens = x_ref[chunk // 2, chunk % 2].reshape(BLOCK, D)
        weight_ref[...] += nn(all_grad[:, here], tokens)
        return carry

    lax.fori_loop(0, blocks, close, 0)


def attend_back(net, first, tokens, qkv, mixed, total, cosine, sine, start, grad):
    length = start.shape[1]
    rows = pltpu.VMEM((length, HEAD_DIM), jnp.bfloat16)
    sums = pltpu.VMEM((length, HEAD_DIM), jnp.float32)
    return pl.pallas_call(
        attend_back_kernel,
        out_shape=[
            jax.ShapeDtypeStruct((net.count, 96, 128), jnp.bfloat16),
            jax.ShapeDtypeStruct((3 * HEAD_DIM, D), jnp.float32),
        ],
        in_specs=[SMEM] + [VMEM] * 8,
        out_specs=[VMEM] * 2,
        scratch_shapes=[
            rows,
            rows,
            rows,
            rows,
            pltpu.VMEM((HEAD_DIM, length), jnp.bfloat16),
            pltpu.VMEM((1, length), jnp.float32),
            sums,
            sums,
            pltpu.VMEM((3 * HEAD_DIM, length), jnp.bfloat16),
        ],
        cost_estimate=pl.CostEstimate(flops=4 * 10**9, bytes_accessed=12 * 2**20, transcendentals=2 * 10**6),
        name="attend_back",
    )(first, tokens, qkv, mixed, total, cosine, sine, start, grad)


def layer_norm(values):
    center = values - jnp.mean(values, axis=-1, keepdims=True)
    spread = jnp.mean(center * center, axis=-1, keepdims=True)
    return center * lax.rsqrt(spread + EPSILON)


def norm_back(values, gradient):
    center = values - jnp.mean(values, axis=-1, keepdims=True)
    inverse = lax.rsqrt(jnp.mean(center * center, axis=-1, keepdims=True) + EPSILON)
    normed = center * inverse
    return inverse * (
        gradient
        - jnp.mean(gradient, axis=-1, keepdims=True)
        - normed * jnp.mean(gradient * normed, axis=-1, keepdims=True)
    )


def newton(matrix):
    values = matrix.astype(jnp.float32)
    frobenius = jnp.sqrt(jnp.sum(values * values))
    current = (values / (frobenius + 1e-07)).astype(jnp.bfloat16)
    for _ in range(NS_STEPS):
        gram = nt(current, current).astype(jnp.bfloat16)
        polynomial = (COEFF_B * gram.astype(jnp.float32) + COEFF_C * nn(gram, gram)).astype(jnp.bfloat16)
        current = (COEFF_A * current.astype(jnp.float32) + nn(polynomial, current)).astype(jnp.bfloat16)
    return current


def on_device(net, tokens, doc_ids, cotangent, attn_weight, ffn_weight, attn_moment, ffn_moment):
    micro_count, token_count, width = tokens.shape
    rows = attn_weight.shape[1]
    count = net.count
    length = count * token_count
    me = net.me()
    both = micro_count * token_count

    attn_low = attn_weight.astype(jnp.bfloat16)
    ffn_low = ffn_weight.astype(jnp.bfloat16)
    late_low = jnp.concatenate([ffn_low[0], ffn_low[1], ffn_low[2], attn_low[3]], axis=1)
    late_full = lax.all_gather(late_low, ("blk", "head"), axis=0, tiled=True)
    gate_full, up_full, down_full = (late_full[:, FF * k : FF * (k + 1)] for k in range(3))
    out_full = late_full[:, 3 * FF :]

    hidden = tokens.astype(jnp.float32).reshape(both, width)
    normed = layer_norm(hidden).astype(jnp.bfloat16)
    counts = jnp.sum((doc_ids[:, :, None] == jnp.arange(DOCS)[None, None, :]).astype(jnp.float32), axis=1)
    tail = jnp.pad(counts.reshape(-1).astype(jnp.bfloat16), (0, HEAD_DIM - micro_count * DOCS))
    columns = attn_low[:3].reshape(3, rows, HEADS, HEAD_DIM).transpose(2, 1, 0, 3).reshape(HEADS, rows, 3 * HEAD_DIM)
    columns = jnp.concatenate([columns, jnp.broadcast_to(tail, (HEADS, rows, HEAD_DIM))], axis=2)
    all_tokens, all_columns = gather_tokens(net, 0, normed.reshape(micro_count, token_count, width), columns)

    micro = (me % GROUP) // 4
    head_weights = all_columns[:, :, : 3 * HEAD_DIM].reshape(D, 3 * HEAD_DIM).T
    every_count = jnp.sum(all_columns[:, 0, 3 * HEAD_DIM :].astype(jnp.float32), axis=0)
    own_count = lax.dynamic_slice_in_dim(every_count, micro * DOCS, DOCS, 0)
    starts = jnp.cumsum(own_count) - own_count
    index = jnp.arange(length).astype(jnp.float32)
    start = jnp.max(jnp.where(starts[:, None] <= index[None, :], starts[:, None], 0.0), axis=0)
    inverse = 10000.0 ** (-(jnp.arange(HALF, dtype=jnp.float32) * 2.0) / HEAD_DIM)
    angles = inverse[:, None] * (index - start)[None, :]
    cosine, sine = jnp.cos(angles), jnp.sin(angles)
    start = start.astype(jnp.int32)
    block_index = jnp.arange(length // BLOCK, dtype=jnp.int32)
    first = jnp.clip(start[::BLOCK] // BLOCK, 0, block_index)
    start = start[None, :]

    qkv, mixed, total, packed = attend(net, first, all_tokens, head_weights, cosine, sine, start)
    (mixed_parts,) = exchange(
        net,
        "mixed_exchange",
        1,
        [(0, 0, lambda i, j: attends(i), lambda i, j: j, lambda i, j: combo_of(i))],
        [packed],
        [jax.ShapeDtypeStruct((2 * HEADS, HALF, 128), jnp.bfloat16)],
    )
    mixed_tokens = (
        mixed_parts.reshape(micro_count, HEADS, HALF, 2, HEAD_DIM).transpose(0, 3, 2, 1, 4).reshape(both, width)
    )

    middle = hidden + nn(mixed_tokens, out_full)
    second = layer_norm(middle).astype(jnp.bfloat16)
    gate, up = nn(second, gate_full), nn(second, up_full)
    gate_sigmoid = jax.nn.sigmoid(gate)
    gate_silu = gate * gate_sigmoid
    product = (gate_silu * up).astype(jnp.bfloat16)
    output = (middle + nt(product, down_full)).astype(jnp.bfloat16)
    out_grad = cotangent.reshape(both, width)
    product_grad = nn(out_grad, down_full)
    gate_grad = (product_grad * up * gate_sigmoid * (1.0 + gate * (1.0 - gate_sigmoid))).astype(jnp.bfloat16)
    up_grad = (product_grad * gate_silu).astype(jnp.bfloat16)
    second_grad = nt(gate_grad, gate_full) + nt(up_grad, up_full)
    middle_grad = out_grad.astype(jnp.float32) + norm_back(middle, second_grad)
    middle_low = middle_grad.astype(jnp.bfloat16)
    mixed_grad = nt(middle_low, out_full).astype(jnp.bfloat16)
    folded = (
        mixed_grad.reshape(micro_count, 2, HALF, HEADS, HEAD_DIM).transpose(0, 3, 2, 1, 4).reshape(2 * HEADS, HALF, 128)
    )

    def tn(a, b):
        return lax.dot_general(a, b, (((0,), (0,)), ((), ())), preferred_element_type=jnp.float32)

    late_terms = jnp.concatenate(
        [
            tn(second, gate_grad).astype(jnp.bfloat16),
            tn(second, up_grad).astype(jnp.bfloat16),
            tn(out_grad, product).astype(jnp.bfloat16),
            tn(mixed_tokens, middle_low).astype(jnp.bfloat16),
        ],
        axis=1,
    )
    late_grad = lax.psum_scatter(late_terms, ("blk", "head"), scatter_dimension=0, tiled=True).astype(jnp.float32)

    (grad_parts,) = exchange(
        net,
        "mixed_grad_exchange",
        2,
        [(0, 0, lambda i, j: attends(j), lambda i, j: combo_of(j), lambda i, j: i)],
        [folded],
        [jax.ShapeDtypeStruct((count, HALF, 128), jnp.bfloat16)],
    )
    grad_packed, head_grad = attend_back(
        net, first, all_tokens, qkv, mixed, total, cosine, sine, start, grad_parts
    )
    head_rows = jnp.pad(head_grad.T.astype(jnp.bfloat16).reshape(count, rows, 3 * HEAD_DIM), ((0, 0), (0, 0), (0, 64)))
    row_parts, token_parts = exchange(
        net,
        "grad_exchange",
        3,
        [
            (0, 0, lambda i, j: attends(i), lambda i, j: j, lambda i, j: combo_of(i)),
            (1, 1, lambda i, j: attends(i), lambda i, j: j, lambda i, j: combo_of(i)),
        ],
        [head_rows, grad_packed],
        [
            jax.ShapeDtypeStruct((2 * HEADS, rows, 256), jnp.bfloat16),
            jax.ShapeDtypeStruct((2 * HEADS, 96, 128), jnp.bfloat16),
        ],
    )
    summed = jnp.sum(row_parts.reshape(micro_count, HEADS, rows, 256).astype(jnp.float32), axis=0)
    early_grad = summed[:, :, : 3 * HEAD_DIM].reshape(HEADS, rows, 3, HEAD_DIM).transpose(2, 1, 0, 3).reshape(3, rows, D)

    attn_grad = jnp.concatenate([early_grad, late_grad[None, :, 3 * FF :]], axis=0)
    ffn_grad = late_grad[:, : 3 * FF].reshape(rows, 3, FF).transpose(1, 0, 2)
    attn_moment_new = 0.5 * attn_moment + 0.5 * attn_grad
    ffn_moment_new = 0.5 * ffn_moment + 0.5 * ffn_grad
    attn_update = (0.5 * attn_grad + 0.5 * attn_moment_new).astype(jnp.bfloat16)
    ffn_update = (0.5 * ffn_grad + 0.5 * ffn_moment_new).astype(jnp.bfloat16)

    def to_owner(matrix):
        return lambda i, j: j == OWNERS[matrix]

    def from_owner(matrix):
        return lambda i, j: i == OWNERS[matrix]

    attn_whole, ffn_whole = exchange(
        net,
        "update_exchange",
        4,
        [(0, 0, to_owner(k), lambda i, j, k=k: k, lambda i, j: i) for k in range(4)]
        + [(1, 1, to_owner(4 + k), lambda i, j, k=k: k, lambda i, j: i) for k in range(3)],
        [attn_update, ffn_update],
        [
            jax.ShapeDtypeStruct((count, rows, D), jnp.bfloat16),
            jax.ShapeDtypeStruct((count, rows, FF), jnp.bfloat16),
        ],
    )
    kind = jnp.int32(2)
    for matrix in range(7):
        kind = jnp.where(me == OWNERS[matrix], jnp.int32(matrix // 4), kind)

    def solve_attn(attn, ffn):
        return newton(attn.reshape(D, D)).reshape(attn.shape), ffn

    def solve_ffn(attn, ffn):
        return attn, newton(ffn.reshape(D, FF)).reshape(ffn.shape)

    attn_done, ffn_done = lax.switch(
        kind, [solve_attn, solve_ffn, lambda attn, ffn: (attn, ffn)], attn_whole, ffn_whole
    )
    attn_step, ffn_step = exchange(
        net,
        "step_exchange",
        5,
        [(0, 0, from_owner(k), lambda i, j: j, lambda i, j, k=k: k) for k in range(4)]
        + [(1, 1, from_owner(4 + k), lambda i, j: j, lambda i, j, k=k: k) for k in range(3)],
        [attn_done, ffn_done],
        [
            jax.ShapeDtypeStruct((4, rows, D), jnp.bfloat16),
            jax.ShapeDtypeStruct((3, rows, FF), jnp.bfloat16),
        ],
    )

    attn_full = lax.all_gather(attn_low[:3], ("blk", "head"), axis=1, tiled=True)
    pair = token_parts[:, :64, :].reshape(micro_count, HEADS, token_count, 2, HEAD_DIM)
    query_key = pair.transpose(3, 0, 2, 1, 4).reshape(2, both, width)
    value = (
        token_parts[:, 64:, :].reshape(micro_count, HEADS, HALF, 2, HEAD_DIM).transpose(0, 3, 2, 1, 4).reshape(both, width)
    )
    normed_grad = nt(query_key[0], attn_full[0]) + nt(query_key[1], attn_full[1]) + nt(value, attn_full[2])
    input_grad = middle_grad + norm_back(hidden, normed_grad)

    rates = jnp.asarray(RATES, jnp.float32)[:, None, None]
    attn_master = attn_weight - rates[:4] * attn_step.astype(jnp.float32)
    ffn_master = ffn_weight - rates[4:] * ffn_step.astype(jnp.float32)
    shape = (micro_count, token_count, width)
    return (
        output.reshape(shape),
        input_grad.reshape(shape),
        attn_grad,
        ffn_grad,
        attn_master,
        ffn_master,
        attn_moment_new,
        ffn_moment_new,
        attn_master.astype(jnp.bfloat16),
        ffn_master.astype(jnp.bfloat16),
    )


def solution(mesh):
    wide = P(None, ("blk", "head"), None)
    return jax.shard_map(
        functools.partial(on_device, Net(mesh)),
        mesh=mesh,
        in_specs=(wide, P(None, ("blk", "head")), wide, wide, wide, wide, wide),
        out_specs=(wide,) * 10,
        check_vma=False,
    )
```

```python
import functools
import math

import jax
import jax.numpy as jnp
from jax import lax
from jax.experimental import pallas as pl
from jax.experimental.pallas import tpu as pltpu
from jax.sharding import PartitionSpec as P

D = 768
HEADS = 12
HEAD_DIM = 64
HALF = 32
FF = 2048
DOCS = 4
NS_STEPS = 5
GROUP = 8
SPARE = 2
BLOCK = 256

EPSILON = 1e-05
NEGATIVE = -1e30
RATES = (0.5, 0.5, 0.5, 7.0, 1.0, 1.0, 0.5)
COEFF_A = 3.4445
COEFF_B = -4.775
COEFF_C = 2.0315
OWNERS = (8, 9, 12, 21, 16, 17, 20)
MESH = pl.DeviceIdType.MESH
ANY = pl.BlockSpec(memory_space=pl.ANY)
VMEM = pl.BlockSpec(memory_space=pltpu.VMEM)
SMEM = pl.BlockSpec(memory_space=pltpu.SMEM)
SCALE = HEAD_DIM ** (-0.5)


def nt(a, b):
    return lax.dot_general(a, b, (((1,), (1,)), ((), ())), preferred_element_type=jnp.float32)


def nn(a, b):
    return jnp.dot(a, b, preferred_element_type=jnp.float32)


def attends(device):
    plane = device // GROUP
    return jnp.logical_and(plane < 4, plane != SPARE)


def combo_of(device):
    plane = device // GROUP
    place = device % GROUP
    return (place // 4) * HEADS + 4 * (plane - plane // 3) + place % 4


def device_of(combo):
    group = (combo % HEADS) // 4
    return GROUP * (group + group // 2) + 4 * (combo // HEADS) + combo % 4


class Net:
    def __init__(self, mesh):
        self.inner = mesh.shape["head"]
        self.count = mesh.shape["head"] * mesh.shape["blk"]
        self.planes = self.count // GROUP

    def permute(self, values, pairs):
        outer = self.count // self.inner

        def place(device):
            return (device % self.inner) * outer + device // self.inner

        return lax.ppermute(values, ("head", "blk"), [(place(i), place(j)) for i, j in pairs])

    def me(self):
        return lax.axis_index("blk") * self.inner + lax.axis_index("head")

    def at(self, device):
        return {"blk": device // self.inner, "head": device % self.inner}

    def meet(self, me, size):
        barrier = pltpu.get_barrier_semaphore()

        def greet(k, carry):
            pl.semaphore_signal(barrier, inc=1, device_id=self.at(peer(me, k, size)), device_id_type=MESH)
            return carry

        lax.fori_loop(1, size, greet, 0)
        pl.semaphore_wait(barrier, size - 1)

    def meet_attending(self, me):
        barrier = pltpu.get_barrier_semaphore()

        @pl.when(attends(me))
        def _():
            def greet(k, carry):
                other = peer(me, k, self.count)

                @pl.when(attends(other))
                def _():
                    pl.semaphore_signal(barrier, inc=1, device_id=self.at(other), device_id_type=MESH)

                return carry

            lax.fori_loop(1, self.count, greet, 0)
            pl.semaphore_wait(barrier, 2 * HEADS - 1)

    def shift(self, values, steps):
        far = GROUP * steps
        return self.permute(values, [(i, (i + far) % self.count) for i in range(self.count)])

    def flip(self, values, distance):
        return self.permute(values, [(i, i ^ distance) for i in range(self.count)])


def peer(me, k, size):
    return (me // size) * size + (me % size + k) % size


def flip_x(device):
    return device + 4 - 8 * ((device % GROUP) // 4)


def flip_y(device):
    return device + 1 - 2 * (device % 2)


def flip_core(device):
    return device + 2 - 4 * ((device % 4) // 2)


def spot_of(device):
    return 2 * (device % 4) + (device % GROUP) // 4


class Flow:
    def __init__(self, source, target, take, put, goes=None, size=None):
        self.source, self.target, self.take, self.put = source, target, take, put
        self.goes = goes or (lambda i, j: i >= 0)
        self.size = size

    def scratch(self):
        return []

    def semaphores(self):
        return self.size

    def bind(self, net, inputs, outputs, scratch, send, receive, local):
        self.net = net
        self.input, self.output = inputs[self.source], outputs[self.target]
        self.held = scratch
        self.send, self.receive, self.local = send, receive, local

    def copy(self, source, target, index, device):
        return pltpu.make_async_remote_copy(
            source,
            target,
            self.send.at[index],
            self.receive.at[index],
            device_id=self.net.at(device),
            device_id_type=MESH,
        )

    def remote(self, i, j, k):
        return self.copy(self.input.at[self.take(i, j)], self.output.at[self.put(i, j)], k, j)

    def near(self, i):
        return pltpu.make_async_copy(self.input.at[self.take(i, i)], self.output.at[self.put(i, i)], self.local)

    def start(self, me):
        def one(k, carry):
            other = peer(me, k, self.size)

            @pl.when(self.goes(me, other))
            def _():
                self.remote(me, other, k).start()

            return carry

        lax.fori_loop(1, self.size, one, 0)

        @pl.when(self.goes(me, me))
        def _():
            self.near(me).start()

    def middle(self, me):
        pass

    def finish(self, me):
        def one(k, carry):
            other = peer(me, k, self.size)

            @pl.when(self.goes(me, other))
            def _():
                self.remote(me, other, k).wait_send()

            before = peer(me, self.size - k, self.size)

            @pl.when(self.goes(before, me))
            def _():
                self.remote(before, me, k).wait_recv()

            return carry

        lax.fori_loop(1, self.size, one, 0)

        @pl.when(self.goes(me, me))
        def _():
            self.near(me).wait()


class Across(Flow):
    def semaphores(self):
        return self.net_planes

    def __init__(self, net, source, target, take, put):
        super().__init__(source, target, take, put, None, net.count)
        self.net_planes = net.planes

    def other(self, me, k):
        return (me + k * GROUP) % self.size

    def start(self, me):
        for k in range(1, self.net_planes):
            self.remote(me, self.other(me, k), k).start()
        self.near(me).start()

    def finish(self, me):
        for k in range(1, self.net_planes):
            self.remote(me, self.other(me, k), k).wait_send()
            self.remote(self.other(me, self.net_planes - k), me, k).wait_recv()
        self.near(me).wait()


class FanIn(Flow):
    def __init__(self, source, target, owner, take, put, goes=None, size=None):
        super().__init__(source, target, take, put, goes, size)
        self.owner = owner

    def sends(self, me):
        here = jnp.logical_and(me // self.size == self.owner // self.size, me != self.owner)
        return jnp.logical_and(here, self.goes(me, self.owner))

    def step(self, me):
        return (self.owner - me + self.net.count) % self.size

    def start(self, me):
        @pl.when(self.sends(me))
        def _():
            self.remote(me, self.owner, self.step(me)).start()

        @pl.when(jnp.logical_and(me == self.owner, self.goes(me, me)))
        def _():
            self.near(me).start()

    def finish(self, me):
        @pl.when(self.sends(me))
        def _():
            self.remote(me, self.owner, self.step(me)).wait_send()

        @pl.when(me == self.owner)
        def _():
            def one(k, carry):
                before = peer(me, self.size - k, self.size)

                @pl.when(self.goes(before, me))
                def _():
                    self.remote(before, me, k).wait_recv()

                return carry

            lax.fori_loop(1, self.size, one, 0)

        @pl.when(jnp.logical_and(me == self.owner, self.goes(me, me)))
        def _():
            self.near(me).wait()


class FanOut(Flow):
    def __init__(self, source, target, owner, take, put):
        super().__init__(source, target, take, put)
        self.owner = owner

    def start(self, me):
        @pl.when(me == self.owner)
        def _():
            def one(k, carry):
                self.remote(me, peer(me, k, self.size), k).start()
                return carry

            lax.fori_loop(1, self.size, one, 0)
            self.near(me).start()

    def finish(self, me):
        @pl.when(me == self.owner)
        def _():
            def one(k, carry):
                self.remote(me, peer(me, k, self.size), k).wait_send()
                return carry

            lax.fori_loop(1, self.size, one, 0)
            self.near(me).wait()

        @pl.when(me != self.owner)
        def _():
            self.remote(self.owner, me, (me - self.owner + self.net.count) % self.size).wait_recv()


class PlaneGather(Flow):
    def __init__(self, source, target):
        super().__init__(source, target, None, None)

    def semaphores(self):
        return GROUP

    def partners(self, me):
        return [flip_x(me), flip_y(me), flip_x(flip_y(me))]

    def own(self, me, index, device):
        return self.copy(self.input, self.output.at[spot_of(me)], index, device)

    def passed(self, me, index, partner):
        block = self.output.at[spot_of(partner)]
        return self.copy(block, block, 4 + index, flip_core(me))

    def start(self, me):
        for index, partner in enumerate(self.partners(me)):
            self.own(me, 1 + index, partner).start()
        self.own(me, 0, flip_core(me)).start()
        pltpu.make_async_copy(self.input, self.output.at[spot_of(me)], self.local).start()

    def middle(self, me):
        for index, partner in enumerate(self.partners(me)):
            self.own(me, 1 + index, partner).wait_recv()
            self.passed(me, index, partner).start()

    def finish(self, me):
        for index, partner in enumerate(self.partners(me)):
            self.own(me, 1 + index, partner).wait_send()
            self.passed(me, index, partner).wait()
        self.own(me, 0, flip_core(me)).wait()
        pltpu.make_async_copy(self.input, self.output.at[spot_of(me)], self.local).wait()


class PlaneScatter(Flow):
    def __init__(self, source, target, block, planes=0):
        super().__init__(source, target, None, None)
        self.block, self.planes = block, planes

    def scratch(self):
        shapes = [pltpu.VMEM((4,) + self.block, jnp.bfloat16)] * 2 + [pltpu.VMEM((3,) + self.block, jnp.bfloat16)]
        if self.planes:
            shapes += [
                pltpu.VMEM(self.block, jnp.bfloat16),
                pltpu.VMEM((self.planes,) + self.block[1:], jnp.bfloat16),
            ]
        return shapes

    def semaphores(self):
        return 4 + self.planes

    def partners(self, me):
        return [flip_x(me), flip_y(me), flip_x(flip_y(me))]

    def half(self, core):
        return self.input.at[pl.ds(4 * core, 4)]

    def first(self, me):
        return self.copy(self.half(1 - (me % 4) // 2), self.held[1], 0, flip_core(me))

    def mine(self, me):
        return pltpu.make_async_copy(self.half((me % 4) // 2), self.held[0], self.local)

    def second(self, me, index, partner):
        return self.copy(self.held[0].at[spot_of(partner) % 4], self.held[2].at[index], 1 + index, partner)

    def third(self, me, k):
        plane = me // GROUP
        target = (plane + k) % self.planes
        return self.copy(self.held[3].at[target], self.held[4].at[plane], 4 + k, (me + k * GROUP) % self.net.count)

    def start(self, me):
        self.first(me).start()
        self.mine(me).start()

    def middle(self, me):
        self.mine(me).wait()
        self.first(me).wait_recv()
        low = jnp.bfloat16
        for index, partner in enumerate(self.partners(me)):
            slot = spot_of(partner) % 4
            self.held[0][slot] = (
                self.held[0][slot].astype(jnp.float32) + self.held[1][slot].astype(jnp.float32)
            ).astype(low)
            self.second(me, index, partner).start()

    def finish(self, me):
        slot = spot_of(me) % 4
        total = self.held[0][slot].astype(jnp.float32) + self.held[1][slot].astype(jnp.float32)
        for index, partner in enumerate(self.partners(me)):
            self.second(me, index, partner).wait_recv()
            total = total + self.held[2][index].astype(jnp.float32)
        if self.planes:
            self.held[3][...] = total.astype(jnp.bfloat16)
            for k in range(1, self.planes):
                self.third(me, k).start()
            plane = me // GROUP
            total = self.held[3][plane].astype(jnp.float32)
            for k in range(1, self.planes):
                self.third(me, k).wait_recv()
                total = total + self.held[4][(plane + self.planes - k) % self.planes].astype(jnp.float32)
        self.output[...] = total
        self.first(me).wait_send()
        for index, partner in enumerate(self.partners(me)):
            self.second(me, index, partner).wait_send()
        for k in range(1, self.planes):
            self.third(me, k).wait_send()


def bind_all(net, flows, inputs, outputs, scratch, send, receive, local):
    used = 0
    for number, flow in enumerate(flows):
        need = len(flow.scratch())
        flow.bind(
            net, inputs, outputs, scratch[used : used + need], send.at[number], receive.at[number], local.at[number]
        )
        used += need


def exchange_kernel(net, meet, flows, sources, targets, *refs):
    inputs = refs[:sources]
    outputs = refs[sources : sources + targets]
    me = net.me()
    meet(me)
    bind_all(net, flows, inputs, outputs, refs[sources + targets : -3], *refs[-3:])
    for flow in flows:
        flow.start(me)
    for flow in flows:
        flow.middle(me)
    for flow in flows:
        flow.finish(me)


def flow_scratch(flows):
    most = max(flow.semaphores() for flow in flows)
    return [shape for flow in flows for shape in flow.scratch()] + [
        pltpu.SemaphoreType.DMA((len(flows), most)),
        pltpu.SemaphoreType.DMA((len(flows), most)),
        pltpu.SemaphoreType.DMA((len(flows),)),
    ]


def exchange(net, name, number, flows, sources, shapes, size=None, meet=None):
    size = size or net.count
    for flow in flows:
        flow.size = flow.size or size
    summed = {flow.target for flow in flows if isinstance(flow, PlaneScatter)}
    moved = sum(math.prod(s.shape) * s.dtype.itemsize for s in shapes)
    return pl.pallas_call(
        functools.partial(
            exchange_kernel, net, meet or (lambda me: net.meet(me, size)), flows, len(sources), len(shapes)
        ),
        out_shape=shapes,
        in_specs=[ANY] * len(sources),
        out_specs=[VMEM if k in summed else ANY for k in range(len(shapes))],
        scratch_shapes=flow_scratch(flows),
        compiler_params=pltpu.CompilerParams(collective_id=number, has_side_effects=True),
        cost_estimate=pl.CostEstimate(flops=0, bytes_accessed=8 * moved, transcendentals=0),
        name=name,
    )(*sources)


def gather_kernel(net, flows, x_ref, w_ref, cut_ref, out_ref, all_ref, wall_ref, cut_all, out_all, send, receive, wsend, wreceive, local, *refs):
    count = net.count
    planes = net.planes
    me = net.me()
    plane = me // GROUP
    place = me % GROUP
    half = place // 4
    spot = place % 4
    across = flip_x(me)
    beside = flip_y(me)
    sibling = flip_core(me)
    net.meet(me, count)
    bind_all(net, flows, (cut_ref, out_ref), (cut_all, out_all), (), *refs)

    def remote(source, target, index, device):
        return pltpu.make_async_remote_copy(
            source, target, send.at[index], receive.at[index], device_id=net.at(device), device_id_type=MESH
        )

    swap = remote(x_ref.at[1 - half], all_ref.at[plane, half, spot], 0, across)
    swap.start()

    def second(step, which):
        target = (me + step * GROUP) % count
        block = all_ref.at[plane, which, spot]
        return remote(block, block, 1 + (step - 1) * 2 + (which + half) % 2, target)

    def direct(step):
        target = (me + step * GROUP) % count
        return remote(x_ref.at[half], all_ref.at[plane, half, spot], 1 + (step - 1) * 2, target)

    third_base = 1 + 2 * (planes - 1)

    def third(step, which):
        source_plane = (plane + planes - step) % planes
        block = all_ref.at[source_plane, which, spot]
        return remote(block, block, third_base + step * 2 + which, beside)

    fourth_base = third_base + 2 * planes

    def fourth(step, which):
        source_plane = (plane + planes - step) % planes
        block = all_ref.at[source_plane, which, pl.ds((spot // 2) * 2, 2)]
        return remote(block, block, fourth_base + step * 2 + which, sibling)

    for step in range(1, planes):
        direct(step).start()
    mine = pltpu.make_async_copy(x_ref.at[half], all_ref.at[plane, half, spot], local.at[0])
    mine.start()

    def weights(combo):
        target = device_of(combo)
        return pltpu.make_async_remote_copy(
            w_ref.at[combo % HEADS],
            wall_ref.at[me],
            wsend.at[combo],
            wreceive.at[me],
            device_id=net.at(target),
            device_id_type=MESH,
        )

    def send_weights(combo, carry):
        @pl.when(device_of(combo) != me)
        def _():
            weights(combo).start()

        return carry

    mine.wait()
    swap.wait_recv()
    for step in range(1, planes):
        second(step, 1 - half).start()
    for which in range(2):
        third(0, which).start()
    lax.fori_loop(0, 2 * HEADS, send_weights, 0)
    for flow in flows:
        flow.start(me)
    for step in range(planes):
        if step > 0:
            second(step, half).wait_recv()
            second(step, 1 - half).wait_recv()
            for which in range(2):
                third(step, which).start()
            for which in range(2):
                third(step - 1, which).wait_recv()
            for which in range(2):
                fourth(step - 1, which).start()
    for which in range(2):
        third(planes - 1, which).wait_recv()
    for which in range(2):
        fourth(planes - 1, which).start()
    for step in range(planes):
        for which in range(2):
            fourth(step, which).wait_recv()

    @pl.when(attends(me))
    def _():
        own = pltpu.make_async_copy(w_ref.at[combo_of(me) % HEADS], wall_ref.at[me], local.at[1])
        own.start()
        own.wait()

        def took(k, carry):
            before = (me + k) % count
            pltpu.make_async_remote_copy(
                w_ref.at[0],
                wall_ref.at[before],
                wsend.at[0],
                wreceive.at[before],
                device_id=net.at(before),
                device_id_type=MESH,
            ).wait_recv()
            return carry

        lax.fori_loop(1, count, took, 0)

    def sent(combo, carry):
        @pl.when(device_of(combo) != me)
        def _():
            weights(combo).wait_send()

        return carry

    lax.fori_loop(0, 2 * HEADS, sent, 0)
    swap.wait_send()
    for step in range(1, planes):
        direct(step).wait_send()
        second(step, 1 - half).wait_send()
    for step in range(planes):
        for which in range(2):
            third(step, which).wait_send()
            fourth(step, which).wait_send()
    for flow in flows:
        flow.finish(me)


def gather_tokens(net, number, normed, columns, cut, out):
    planes = net.planes
    copies = 1 + 2 * (planes - 1) + 4 * planes
    flows = [
        Flow(0, 0, lambda i, j: j % GROUP, lambda i, j: i % GROUP, size=GROUP),
        Across(net, 1, 1, lambda i, j: 0, lambda i, j: i // GROUP),
    ]
    shapes = [
        jax.ShapeDtypeStruct((planes, 2, 4) + normed.shape[1:], normed.dtype),
        jax.ShapeDtypeStruct((net.count,) + columns.shape[1:], columns.dtype),
        jax.ShapeDtypeStruct(cut.shape, cut.dtype),
        jax.ShapeDtypeStruct((planes,) + out.shape[1:], out.dtype),
    ]
    return pl.pallas_call(
        functools.partial(gather_kernel, net, flows),
        out_shape=shapes,
        in_specs=[ANY] * 4,
        out_specs=[ANY] * 4,
        scratch_shapes=[
            pltpu.SemaphoreType.DMA((copies,)),
            pltpu.SemaphoreType.DMA((copies,)),
            pltpu.SemaphoreType.DMA((2 * HEADS,)),
            pltpu.SemaphoreType.DMA((net.count,)),
            pltpu.SemaphoreType.DMA((2,)),
        ]
        + flow_scratch(flows),
        compiler_params=pltpu.CompilerParams(collective_id=number, has_side_effects=True),
        cost_estimate=pl.CostEstimate(flops=0, bytes_accessed=100 * 2**20, transcendentals=0),
        name="gather_tokens",
    )(normed, columns, cut, out)


def rope_rows(values, cosine, sine):
    first, second = values[:HALF], values[HALF:]
    return jnp.concatenate([first * cosine - second * sine, second * cosine + first * sine], axis=0)


def rope_rows_back(values, cosine, sine):
    first, second = values[:HALF], values[HALF:]
    return jnp.concatenate([first * cosine + second * sine, second * cosine - first * sine], axis=0)


def columns_of(index):
    return pl.ds(pl.multiple_of(index * BLOCK, BLOCK), BLOCK)


def positions(query_block, key_block):
    shape = (BLOCK, BLOCK)
    key = key_block * BLOCK + lax.broadcasted_iota(jnp.int32, shape, 0)
    query = query_block * BLOCK + lax.broadcasted_iota(jnp.int32, shape, 1)
    return key, query


def fold(rows):
    return jnp.concatenate([rows[:HALF], rows[HALF:]], axis=1)


def unfold(rows):
    return jnp.concatenate([rows[:, :HEAD_DIM], rows[:, HEAD_DIM:]], axis=0)


def attend_kernel(net, *refs):
    @pl.when(attends(net.me()))
    def _():
        attend_body(*refs)


def attend_body(first_ref, x_ref, w_ref, cos_ref, sin_ref, start_ref, qkv_ref, mixed_ref, total_ref, packed_ref, key_rows):
    blocks = qkv_ref.shape[1] // BLOCK
    weights = w_ref[...]

    def project(chunk, carry):
        tokens = x_ref[chunk // 2, chunk % 2].reshape(BLOCK, D)
        here = columns_of(chunk)
        made = nt(weights, tokens)
        cosine, sine = cos_ref[:, here], sin_ref[:, here]
        query = rope_rows(made[:HEAD_DIM], cosine, sine)
        key = rope_rows(made[HEAD_DIM : 2 * HEAD_DIM], cosine, sine)
        qkv_ref[:HEAD_DIM, here] = query.astype(jnp.bfloat16)
        qkv_ref[HEAD_DIM : 2 * HEAD_DIM, here] = key.astype(jnp.bfloat16)
        qkv_ref[2 * HEAD_DIM :, here] = made[2 * HEAD_DIM :].astype(jnp.bfloat16)
        key_rows[here, :] = key.T.astype(jnp.bfloat16)
        return carry

    lax.fori_loop(0, blocks, project, 0)

    def query_step(query_block, carry):
        here = columns_of(query_block)
        query = qkv_ref[:HEAD_DIM, here]
        start = start_ref[:, here]

        def key_step(key_block, held):
            top, total, mixed = held
            there = columns_of(key_block)
            scores = nn(key_rows[there, :], query) * SCALE
            key_at, query_at = positions(query_block, key_block)
            allowed = (key_at <= query_at) & (key_at >= start)
            scores = jnp.where(allowed, scores, NEGATIVE)
            new_top = jnp.maximum(top, jnp.max(scores, axis=0, keepdims=True))
            weights = jnp.where(allowed, jnp.exp(scores - new_top), 0.0)
            factor = jnp.exp(top - new_top)
            total = total * factor + jnp.sum(weights, axis=0, keepdims=True)
            mixed = mixed * factor + nn(qkv_ref[2 * HEAD_DIM :, there], weights.astype(jnp.bfloat16))
            return new_top, total, mixed

        top, total, mixed = lax.fori_loop(
            first_ref[query_block],
            query_block + 1,
            key_step,
            (
                jnp.full((1, BLOCK), NEGATIVE, jnp.float32),
                jnp.zeros((1, BLOCK), jnp.float32),
                jnp.zeros((HEAD_DIM, BLOCK), jnp.float32),
            ),
        )
        mixed = mixed / total
        mixed_ref[:, here] = mixed
        total_ref[:, here] = top + jnp.log(total)
        rows = mixed.T
        for part in range(BLOCK // 64):
            packed_ref[query_block * (BLOCK // 64) + part] = fold(rows[part * 64 : part * 64 + 64]).astype(
                jnp.bfloat16
            )
        return carry

    lax.fori_loop(0, blocks, query_step, 0)


def attend(net, first, tokens, weights, cosine, sine, start):
    length = start.shape[1]
    return pl.pallas_call(
        functools.partial(attend_kernel, net),
        out_shape=[
            jax.ShapeDtypeStruct((3 * HEAD_DIM, length), jnp.bfloat16),
            jax.ShapeDtypeStruct((HEAD_DIM, length), jnp.float32),
            jax.ShapeDtypeStruct((1, length), jnp.float32),
            jax.ShapeDtypeStruct((net.count, HALF, 128), jnp.bfloat16),
        ],
        in_specs=[SMEM] + [VMEM] * 5,
        out_specs=[VMEM] * 4,
        scratch_shapes=[pltpu.VMEM((length, HEAD_DIM), jnp.bfloat16)],
        cost_estimate=pl.CostEstimate(flops=2 * 10**9, bytes_accessed=8 * 2**20, transcendentals=2 * 10**6),
        name="attend",
    )(first, tokens, weights, cosine, sine, start)


def attend_back_kernel(net, *refs):
    @pl.when(attends(net.me()))
    def _():
        attend_back_body(*refs)


def attend_back_body(
    first_ref,
    x_ref,
    qkv_ref,
    mixed_ref,
    total_ref,
    cos_ref,
    sin_ref,
    start_ref,
    grad_ref,
    packed_ref,
    weight_ref,
    query_rows,
    key_rows,
    value_rows,
    grad_rows,
    grad_columns,
    correction,
    key_grad,
    value_grad,
    all_grad,
):
    blocks = qkv_ref.shape[1] // BLOCK
    parts = BLOCK // 64

    def prepare(chunk, carry):
        here = columns_of(chunk)
        turned = qkv_ref[:, here].astype(jnp.float32)
        query_rows[here, :] = turned[:HEAD_DIM].T.astype(jnp.bfloat16)
        key_rows[here, :] = turned[HEAD_DIM : 2 * HEAD_DIM].T.astype(jnp.bfloat16)
        value_rows[here, :] = turned[2 * HEAD_DIM :].T.astype(jnp.bfloat16)
        pieces = [unfold(grad_ref[chunk * parts + part].astype(jnp.float32)) for part in range(parts)]
        rows = jnp.concatenate(pieces, axis=0)
        grad_rows[here, :] = rows.astype(jnp.bfloat16)
        across = rows.T
        grad_columns[:, here] = across.astype(jnp.bfloat16)
        correction[:, here] = jnp.sum(across * mixed_ref[:, here], axis=0, keepdims=True)
        key_grad[here, :] = jnp.zeros((BLOCK, HEAD_DIM), jnp.float32)
        value_grad[here, :] = jnp.zeros((BLOCK, HEAD_DIM), jnp.float32)
        return carry

    lax.fori_loop(0, blocks, prepare, 0)

    def query_step(query_block, carry):
        here = columns_of(query_block)
        query = qkv_ref[:HEAD_DIM, here]
        start = start_ref[:, here]
        total = total_ref[:, here]
        fix = correction[:, here]
        grad = grad_columns[:, here]
        query_in_rows = query_rows[here, :]
        grad_in_rows = grad_rows[here, :]

        def key_step(key_block, query_grad):
            there = columns_of(key_block)
            scores = nn(key_rows[there, :], query) * SCALE
            key_at, query_at = positions(query_block, key_block)
            allowed = (key_at <= query_at) & (key_at >= start)
            weights = jnp.where(allowed, jnp.exp(scores - total), 0.0)
            value_grad[there, :] += nn(weights.astype(jnp.bfloat16), grad_in_rows)
            slope = nn(value_rows[there, :], grad)
            change = (weights * (slope - fix) * SCALE).astype(jnp.bfloat16)
            key_grad[there, :] += nn(change, query_in_rows)
            return query_grad + nn(qkv_ref[HEAD_DIM : 2 * HEAD_DIM, there], change)

        query_grad = lax.fori_loop(
            first_ref[query_block], query_block + 1, key_step, jnp.zeros((HEAD_DIM, BLOCK), jnp.float32)
        )
        query_grad = rope_rows_back(query_grad, cos_ref[:, here], sin_ref[:, here])
        all_grad[:HEAD_DIM, here] = query_grad.astype(jnp.bfloat16)
        rows = query_grad.T.astype(jnp.bfloat16)
        for part in range(parts):
            packed_ref[query_block * parts + part, :64, :HEAD_DIM] = rows[part * 64 : part * 64 + 64]
        return carry

    lax.fori_loop(0, blocks, query_step, 0)
    weight_ref[...] = jnp.zeros(weight_ref.shape, jnp.float32)

    def close(chunk, carry):
        here = columns_of(chunk)
        key = rope_rows_back(key_grad[here, :].T, cos_ref[:, here], sin_ref[:, here])
        value = value_grad[here, :]
        all_grad[HEAD_DIM : 2 * HEAD_DIM, here] = key.astype(jnp.bfloat16)
        all_grad[2 * HEAD_DIM :, here] = value.T.astype(jnp.bfloat16)
        rows = key.T.astype(jnp.bfloat16)
        for part in range(parts):
            token = chunk * parts + part
            packed_ref[token, :64, HEAD_DIM:] = rows[part * 64 : part * 64 + 64]
            packed_ref[token, 64:, :] = fold(value[part * 64 : part * 64 + 64]).astype(jnp.bfloat16)
        tokens = x_ref[chunk // 2, chunk % 2].reshape(BLOCK, D)
        weight_ref[...] += nn(all_grad[:, here], tokens)
        return carry

    lax.fori_loop(0, blocks, close, 0)


def attend_back(net, first, tokens, qkv, mixed, total, cosine, sine, start, grad):
    length = start.shape[1]
    rows = pltpu.VMEM((length, HEAD_DIM), jnp.bfloat16)
    sums = pltpu.VMEM((length, HEAD_DIM), jnp.float32)
    return pl.pallas_call(
        functools.partial(attend_back_kernel, net),
        out_shape=[
            jax.ShapeDtypeStruct((net.count, 96, 128), jnp.bfloat16),
            jax.ShapeDtypeStruct((3 * HEAD_DIM, D), jnp.float32),
        ],
        in_specs=[SMEM] + [VMEM] * 8,
        out_specs=[VMEM] * 2,
        scratch_shapes=[
            rows,
            rows,
            rows,
            rows,
            pltpu.VMEM((HEAD_DIM, length), jnp.bfloat16),
            pltpu.VMEM((1, length), jnp.float32),
            sums,
            sums,
            pltpu.VMEM((3 * HEAD_DIM, length), jnp.bfloat16),
        ],
        cost_estimate=pl.CostEstimate(flops=4 * 10**9, bytes_accessed=12 * 2**20, transcendentals=2 * 10**6),
        name="attend_back",
    )(first, tokens, qkv, mixed, total, cosine, sine, start, grad)


def layer_norm(values):
    center = values - jnp.mean(values, axis=-1, keepdims=True)
    spread = jnp.mean(center * center, axis=-1, keepdims=True)
    return center * lax.rsqrt(spread + EPSILON)


def norm_back(values, gradient):
    center = values - jnp.mean(values, axis=-1, keepdims=True)
    inverse = lax.rsqrt(jnp.mean(center * center, axis=-1, keepdims=True) + EPSILON)
    normed = center * inverse
    return inverse * (
        gradient
        - jnp.mean(gradient, axis=-1, keepdims=True)
        - normed * jnp.mean(gradient * normed, axis=-1, keepdims=True)
    )


def newton_kernel(net, head_ref, moment_ref, out_ref, ffn_ref, attn_out, ffn_out, wide, parts, moment, gram, polynomial, semaphore):
    me = net.me()

    def blocks_of(index):
        return pl.ds(pl.multiple_of(index * BLOCK, BLOCK), BLOCK)

    def move(source, target):
        copy = pltpu.make_async_copy(source, target, semaphore)
        copy.start()
        copy.wait()

    def mirror(target, i, j, block):
        target[i * BLOCK : (i + 1) * BLOCK, j * BLOCK : (j + 1) * BLOCK] = block.astype(jnp.bfloat16)
        if i != j:
            target[j * BLOCK : (j + 1) * BLOCK, i * BLOCK : (i + 1) * BLOCK] = block.T.astype(jnp.bfloat16)

    def solve(span, target):
        chunks = span // BLOCK

        def measure(index, total):
            values = wide[:, blocks_of(index)].astype(jnp.float32)
            return total + jnp.sum(values * values, axis=0, keepdims=True)

        total = lax.fori_loop(0, chunks, measure, jnp.zeros((1, BLOCK), jnp.float32))
        frobenius = jnp.sqrt(jnp.sum(total, axis=1, keepdims=True)) + 1e-07

        def scale(index, carry):
            here = blocks_of(index)
            wide[:, here] = (wide[:, here].astype(jnp.float32) / frobenius).astype(jnp.bfloat16)
            return carry

        lax.fori_loop(0, chunks, scale, 0)

        def step(_, carry):
            for i in range(D // BLOCK):
                for j in range(i + 1):
                    mirror(
                        gram,
                        i,
                        j,
                        nt(
                            wide[i * BLOCK : (i + 1) * BLOCK, :span],
                            wide[j * BLOCK : (j + 1) * BLOCK, :span],
                        ),
                    )
            for i in range(D // BLOCK):
                for j in range(i + 1):
                    square = nn(gram[i * BLOCK : (i + 1) * BLOCK, :], gram[:, j * BLOCK : (j + 1) * BLOCK])
                    linear = gram[i * BLOCK : (i + 1) * BLOCK, j * BLOCK : (j + 1) * BLOCK].astype(jnp.float32)
                    mirror(polynomial, i, j, COEFF_B * linear + COEFF_C * square)

            def advance(index, inner):
                here = blocks_of(index)
                old = wide[:, here]
                wide[:, here] = (COEFF_A * old.astype(jnp.float32) + nn(polynomial[...], old)).astype(jnp.bfloat16)
                return inner

            lax.fori_loop(0, chunks, advance, 0)
            return carry

        lax.fori_loop(0, NS_STEPS, step, 0)
        move(wide.at[:, pl.ds(0, span)], target)

    kind = jnp.int32(3)
    for matrix in range(7):
        kind = jnp.where(me == OWNERS[matrix], jnp.int32(0 if matrix < 3 else 1 if matrix == 3 else 2), kind)

    @pl.when(kind == 0)
    def _():
        move(head_ref, parts)
        move(moment_ref, moment)

        def join(pair, carry):
            first = parts[2 * pair].astype(jnp.float32) + parts[HEADS + 2 * pair].astype(jnp.float32)
            second = parts[2 * pair + 1].astype(jnp.float32) + parts[HEADS + 2 * pair + 1].astype(jnp.float32)
            here = pl.ds(pl.multiple_of(pair * 128, 128), 128)
            gradient = jnp.concatenate([first, second], axis=0).T
            wide[:, here] = (0.75 * gradient + 0.25 * moment[:, here].astype(jnp.float32)).astype(jnp.bfloat16)
            return carry

        lax.fori_loop(0, HEADS // 2, join, 0)
        solve(D, attn_out)

    @pl.when(kind == 1)
    def _():
        move(out_ref, wide.at[:, pl.ds(0, D)])
        solve(D, attn_out)

    @pl.when(kind == 2)
    def _():
        move(ffn_ref, wide)
        solve(FF, ffn_out)


def newton(net, heads, moment, out, ffn):
    return pl.pallas_call(
        functools.partial(newton_kernel, net),
        out_shape=[jax.ShapeDtypeStruct(out.shape, out.dtype), jax.ShapeDtypeStruct(ffn.shape, ffn.dtype)],
        in_specs=[ANY] * 4,
        out_specs=[ANY] * 2,
        scratch_shapes=[
            pltpu.VMEM((D, FF), jnp.bfloat16),
            pltpu.VMEM(heads.shape, jnp.bfloat16),
            pltpu.VMEM((D, D), jnp.bfloat16),
            pltpu.VMEM((D, D), jnp.bfloat16),
            pltpu.VMEM((D, D), jnp.bfloat16),
            pltpu.SemaphoreType.DMA,
        ],
        cost_estimate=pl.CostEstimate(flops=25 * 10**9, bytes_accessed=8 * 2**20, transcendentals=0),
        name="newton",
    )(heads, moment, out, ffn)


def pick(values, index):
    return lax.dynamic_index_in_dim(values, index, 0, keepdims=False)


def tn(a, b):
    return lax.dot_general(a, b, (((0,), (0,)), ((), ())), preferred_element_type=jnp.float32)


def on_device(net, tokens, doc_ids, cotangent, attn_weight, ffn_weight, attn_moment, ffn_moment):
    micro_count, token_count, width = tokens.shape
    rows = attn_weight.shape[1]
    count, planes = net.count, net.planes
    length = count * token_count
    me = net.me()
    plane, place = me // GROUP, me % GROUP
    x_bit = place // 4
    both = micro_count * token_count
    part = FF // GROUP
    low = jnp.bfloat16

    attn_low = attn_weight.astype(low)
    ffn_low = ffn_weight.astype(low)
    cut = ffn_low.reshape(3, rows, GROUP, part).transpose(2, 1, 0, 3).reshape(GROUP, rows, 3 * part)
    out_grad = cotangent.reshape(both, width)
    hidden = tokens.astype(jnp.float32).reshape(both, width)
    normed = layer_norm(hidden).astype(low)
    counts = jnp.sum((doc_ids[:, :, None] == jnp.arange(DOCS)[None, None, :]).astype(jnp.float32), axis=1)
    tail = jnp.pad(counts.reshape(-1).astype(low), (0, HEAD_DIM - micro_count * DOCS))
    columns = attn_low[:3].reshape(3, rows, HEADS, HEAD_DIM).transpose(2, 1, 0, 3).reshape(HEADS, rows, 3 * HEAD_DIM)
    columns = jnp.concatenate([columns, jnp.broadcast_to(tail, (HEADS, rows, HEAD_DIM))], axis=2)
    all_tokens, all_columns, plane_cut, plane_out = gather_tokens(
        net, 0, normed.reshape(micro_count, token_count, width), columns, cut, attn_low[3:]
    )
    late_own = plane_cut.reshape(GROUP * rows, 3 * part)
    late_full = jnp.zeros((planes, GROUP * rows, 3 * part), low)
    late_full = lax.dynamic_update_index_in_dim(late_full, late_own, plane, 0)
    for step in range(1, planes):
        late_full = lax.dynamic_update_index_in_dim(
            late_full, net.shift(late_own, step), (plane + planes - step) % planes, 0
        )
    late_full = late_full.reshape(D, 3 * part)
    gate_full, up_full, down_full = (late_full[:, part * k : part * (k + 1)] for k in range(3))

    head_weights = all_columns[:, :, : 3 * HEAD_DIM].reshape(D, 3 * HEAD_DIM).T
    every_count = jnp.sum(all_columns[:, 0, 3 * HEAD_DIM :].astype(jnp.float32), axis=0)
    own_count = lax.dynamic_slice_in_dim(every_count, x_bit * DOCS, DOCS, 0)
    starts = jnp.cumsum(own_count) - own_count
    index = jnp.arange(length).astype(jnp.float32)
    start = jnp.max(jnp.where(starts[:, None] <= index[None, :], starts[:, None], 0.0), axis=0)
    inverse = 10000.0 ** (-(jnp.arange(HALF, dtype=jnp.float32) * 2.0) / HEAD_DIM)
    angles = inverse[:, None] * (index - start)[None, :]
    cosine, sine = jnp.cos(angles), jnp.sin(angles)
    start = start.astype(jnp.int32)
    block_index = jnp.arange(length // BLOCK, dtype=jnp.int32)
    first = jnp.clip(start[::BLOCK] // BLOCK, 0, block_index)
    start = start[None, :]

    qkv, mixed, total, packed = attend(net, first, all_tokens, head_weights, cosine, sine, start)
    mixed_parts, moment_whole, plane_out_grad, out_full = exchange(
        net,
        "mixed_exchange",
        1,
        [PlaneGather(2, 2), PlaneGather(3, 3)]
        + [Flow(0, 0, lambda i, j: j, lambda i, j: combo_of(i), lambda i, j: attends(i))]
        + [FanIn(1, 1, OWNERS[k], lambda i, j, k=k: k, lambda i, j: i) for k in range(3)],
        [packed, attn_moment.astype(low), out_grad, plane_out],
        [
            jax.ShapeDtypeStruct((2 * HEADS, HALF, 128), low),
            jax.ShapeDtypeStruct((count, rows, D), low),
            jax.ShapeDtypeStruct((GROUP, both, width), low),
            jax.ShapeDtypeStruct((GROUP, planes, rows, D), low),
        ],
    )
    plane_out_grad = plane_out_grad.reshape(GROUP * both, width)
    out_full = out_full.reshape(2, 2, 2, planes, rows, D).transpose(3, 2, 0, 1, 4, 5).reshape(D, D)
    mixed_tokens = (
        mixed_parts.reshape(micro_count, HEADS, HALF, 2, HEAD_DIM).transpose(0, 3, 2, 1, 4).reshape(both, width)
    )

    middle = hidden + nn(mixed_tokens, out_full)
    second = layer_norm(middle).astype(low)
    (plane_second,) = exchange(
        net,
        "second_exchange",
        7,
        [PlaneGather(0, 0)],
        [second],
        [jax.ShapeDtypeStruct((GROUP, both, width), low)],
        GROUP,
    )
    plane_second = plane_second.reshape(GROUP * both, width)
    gate, up = nn(plane_second, gate_full), nn(plane_second, up_full)
    gate_sigmoid = jax.nn.sigmoid(gate)
    gate_silu = gate * gate_sigmoid
    product = (gate_silu * up).astype(low)
    product_grad = nn(plane_out_grad, down_full)
    gate_grad = (product_grad * up * gate_sigmoid * (1.0 + gate * (1.0 - gate_sigmoid))).astype(low)
    up_grad = (product_grad * gate_silu).astype(low)
    second_terms = (nt(gate_grad, gate_full) + nt(up_grad, up_full)).astype(low)
    result_terms = nt(product, down_full).astype(low)
    ffn_terms = jnp.concatenate(
        [
            tn(plane_second, gate_grad).astype(low),
            tn(plane_second, up_grad).astype(low),
            tn(plane_out_grad, product).astype(low),
        ],
        axis=1,
    ).reshape(planes, GROUP * rows, 3 * part)
    (second_grad,) = exchange(
        net,
        "second_grad_exchange",
        8,
        [PlaneScatter(0, 0, (both, width))],
        [second_terms.reshape(GROUP, both, width)],
        [jax.ShapeDtypeStruct((both, width), jnp.float32)],
        GROUP,
    )
    ffn_block = pick(ffn_terms, plane).astype(jnp.float32)
    for step in range(1, planes):
        ffn_block = ffn_block + net.shift(pick(ffn_terms, (plane + step) % planes), step).astype(jnp.float32)
    ffn_block = ffn_block.astype(low)

    middle_grad = out_grad.astype(jnp.float32) + norm_back(middle, second_grad)
    middle_low = middle_grad.astype(low)
    mixed_grad = nt(middle_low, out_full).astype(low)
    folded = (
        mixed_grad.reshape(micro_count, 2, HALF, HEADS, HEAD_DIM).transpose(0, 3, 2, 1, 4).reshape(2 * HEADS, HALF, 128)
    )
    out_terms = tn(mixed_tokens, middle_low).astype(low).reshape(planes, 2, 2, 2, rows, D)
    out_terms = out_terms.transpose(2, 3, 1, 0, 4, 5).reshape(GROUP, planes, rows, D)
    grad_parts, out_row_grad, ffn_parts = exchange(
        net,
        "mixed_grad_exchange",
        2,
        [
            PlaneScatter(1, 1, (planes, rows, D), planes),
            Flow(0, 0, lambda i, j: combo_of(j), lambda i, j: i, lambda i, j: attends(j)),
            Flow(2, 2, lambda i, j: j % GROUP, lambda i, j: i % GROUP, size=GROUP),
        ],
        [folded, out_terms, ffn_block.reshape(GROUP, rows, 3 * part)],
        [
            jax.ShapeDtypeStruct((count, HALF, 128), low),
            jax.ShapeDtypeStruct((rows, D), jnp.float32),
            jax.ShapeDtypeStruct((GROUP, rows, 3 * part), low),
        ],
    )
    ffn_grad = ffn_parts.reshape(GROUP, rows, 3, part).transpose(2, 1, 0, 3).reshape(3, rows, FF).astype(jnp.float32)
    ffn_moment_new = 0.5 * ffn_moment + 0.5 * ffn_grad
    out_moment_new = 0.5 * attn_moment[3] + 0.5 * out_row_grad
    ffn_update = (0.5 * ffn_grad + 0.5 * ffn_moment_new).astype(low)
    out_update = (0.5 * out_row_grad + 0.5 * out_moment_new).astype(low)
    update = jnp.concatenate([ffn_update.transpose(1, 0, 2).reshape(rows, 3 * FF), out_update], axis=1)
    updates = []
    for source in range(planes):
        if source == SPARE:
            updates.append(update)
        else:
            hop = [(GROUP * source + k, GROUP * SPARE + k) for k in range(GROUP)]
            updates.append(net.permute(update, hop))
    updates = jnp.stack(updates)
    ffn_updates = updates[:, :, : 3 * FF].reshape(planes, rows, 3, FF).transpose(2, 0, 1, 3)
    out_updates = updates[None, :, :, 3 * FF :]

    early_low, grad_parts = lax.optimization_barrier((attn_low[:3], grad_parts))
    attn_full = lax.all_gather(early_low, ("blk", "head"), axis=1, tiled=True)
    grad_packed, head_grad = attend_back(
        net, first, all_tokens, qkv, mixed, total, cosine, sine, start, grad_parts
    )
    head_low = head_grad.astype(low)
    grad_packed, head_low, ffn_updates, out_updates = lax.optimization_barrier(
        (grad_packed, head_low, ffn_updates, out_updates)
    )
    everything = (slice(None),)
    ffn_whole, out_whole = exchange(
        net,
        "update_exchange",
        4,
        [
            FanIn(
                0,
                0,
                OWNERS[4 + k],
                lambda i, j, k=k: k,
                lambda i, j: everything + (i % GROUP,),
                size=GROUP,
            )
            for k in range(3)
        ]
        + [FanIn(1, 1, OWNERS[3], lambda i, j: 0, lambda i, j: everything + (i % GROUP,), size=GROUP)],
        [ffn_updates, out_updates],
        [
            jax.ShapeDtypeStruct((planes, GROUP, rows, FF), low),
            jax.ShapeDtypeStruct((planes, GROUP, rows, D), low),
        ],
        GROUP,
    )
    (head_whole,) = exchange(
        net,
        "head_exchange",
        9,
        [
            FanIn(0, 0, OWNERS[k], lambda i, j, k=k: k, lambda i, j: combo_of(i), lambda i, j: attends(i))
            for k in range(3)
        ],
        [head_low.reshape(3, HEAD_DIM, D)],
        [jax.ShapeDtypeStruct((2 * HEADS, HEAD_DIM, D), low)],
        meet=net.meet_attending,
    )

    grad_packed, head_low, head_whole, ffn_whole = lax.optimization_barrier(
        (grad_packed, head_low, head_whole, ffn_whole)
    )
    head_rows = head_low.T.reshape(count, rows, 3 * HEAD_DIM)
    head_rows = jnp.pad(head_rows, ((0, 0), (0, 0), (0, 64))).reshape(planes, GROUP, rows * 2, 128)
    outgoing = jnp.concatenate([grad_packed.reshape(planes, GROUP, 96, 128), head_rows], axis=2)
    arrived = [pick(outgoing, plane)]
    for step in range(1, planes):
        hop = [
            (GROUP * p + k, (GROUP * (p + step) + k) % count) for p in range(4) if p != SPARE for k in range(GROUP)
        ]
        arrived.append(net.permute(pick(outgoing, (plane + step) % planes), hop))

    attn_done, ffn_done = newton(
        net, head_whole, moment_whole.reshape(D, D), out_whole.reshape(D, D), ffn_whole.reshape(D, FF)
    )
    attn_done, ffn_done, *arrived = lax.optimization_barrier((attn_done, ffn_done, *arrived))
    arrived = jnp.stack(arrived)
    arrived = jnp.stack([pick(arrived, (plane + planes - source) % planes) for source in range(4) if source != SPARE])

    attn_step, ffn_step, grads, result = exchange(
        net,
        "step_exchange",
        5,
        [PlaneScatter(3, 3, (both, width))]
        + [FanOut(0, 0, OWNERS[k], lambda i, j: j, lambda i, j, k=k: k) for k in range(4)]
        + [FanOut(1, 1, OWNERS[4 + k], lambda i, j: j, lambda i, j, k=k: k) for k in range(3)]
        + [
            Flow(
                2, 2, lambda i, j: everything + (j % GROUP,), lambda i, j: everything + (i % GROUP,), size=GROUP
            )
        ],
        [
            attn_done.reshape(count, rows, D),
            ffn_done.reshape(count, rows, FF),
            arrived,
            result_terms.reshape(GROUP, both, width),
        ],
        [
            jax.ShapeDtypeStruct((4, rows, D), low),
            jax.ShapeDtypeStruct((3, rows, FF), low),
            jax.ShapeDtypeStruct(arrived.shape, low),
            jax.ShapeDtypeStruct((both, width), jnp.float32),
        ],
    )

    grads = grads.reshape(3, micro_count, 4, 96 + 2 * rows, 128).transpose(1, 0, 2, 3, 4)
    grads = grads.reshape(micro_count, HEADS, 96 + 2 * rows, 128)
    summed = jnp.sum(grads[:, :, 96:].astype(jnp.float32), axis=0).reshape(HEADS, rows, 256)
    early_grad = summed[:, :, : 3 * HEAD_DIM].reshape(HEADS, rows, 3, HEAD_DIM).transpose(2, 1, 0, 3).reshape(3, rows, D)
    attn_grad = jnp.concatenate([early_grad, out_row_grad[None]], axis=0)
    attn_moment_new = 0.5 * attn_moment + 0.5 * attn_grad

    pair = grads[:, :, :64].reshape(micro_count, HEADS, token_count, 2, HEAD_DIM)
    query_key = pair.transpose(3, 0, 2, 1, 4).reshape(2, both, width)
    value = (
        grads[:, :, 64:96].reshape(micro_count, HEADS, HALF, 2, HEAD_DIM).transpose(0, 3, 2, 1, 4).reshape(both, width)
    )
    normed_grad = nt(query_key[0], attn_full[0]) + nt(query_key[1], attn_full[1]) + nt(value, attn_full[2])
    input_grad = middle_grad + norm_back(hidden, normed_grad)

    output = (middle + result).astype(low)

    rates = jnp.asarray(RATES, jnp.float32)[:, None, None]
    attn_master = attn_weight - rates[:4] * attn_step.astype(jnp.float32)
    ffn_master = ffn_weight - rates[4:] * ffn_step.astype(jnp.float32)
    shape = (micro_count, token_count, width)
    return (
        output.reshape(shape),
        input_grad.reshape(shape),
        attn_grad,
        ffn_grad,
        attn_master,
        ffn_master,
        attn_moment_new,
        ffn_moment_new,
        attn_master.astype(low),
        ffn_master.astype(low),
    )


def solution(mesh):
    wide = P(None, ("blk", "head"), None)
    return jax.shard_map(
        functools.partial(on_device, Net(mesh)),
        mesh=mesh,
        in_specs=(wide, P(None, ("blk", "head")), wide, wide, wide, wide, wide),
        out_specs=(wide,) * 10,
        check_vma=False,
    )
```

```python
import functools
import math

import jax
import jax.numpy as jnp
from jax import lax
from jax.experimental import pallas as pl
from jax.experimental.pallas import tpu as pltpu
from jax.sharding import PartitionSpec as P

D = 768
HEADS = 12
HEAD_DIM = 64
HALF = 32
FF = 2048
DOCS = 4
NS_STEPS = 5
GROUP = 8
SPARE = 2
BLOCK = 256
WIDE = 512

EPSILON = 1e-05
NEGATIVE = -1e30
RATES = (0.5, 0.5, 0.5, 7.0, 1.0, 1.0, 0.5)
COEFF_A = 3.4445
COEFF_B = -4.775
COEFF_C = 2.0315
OWNERS = (18, 19, 22, 21, 16, 17, 20)
MESH = pl.DeviceIdType.MESH
ANY = pl.BlockSpec(memory_space=pl.ANY)
VMEM = pl.BlockSpec(memory_space=pltpu.VMEM)
SMEM = pl.BlockSpec(memory_space=pltpu.SMEM)
SCALE = HEAD_DIM ** (-0.5)


def nt(a, b):
    return lax.dot_general(a, b, (((1,), (1,)), ((), ())), preferred_element_type=jnp.float32)


def nn(a, b):
    return jnp.dot(a, b, preferred_element_type=jnp.float32)


def attends(device):
    plane = device // GROUP
    return jnp.logical_and(plane < 4, plane != SPARE)


def combo_of(device):
    plane = device // GROUP
    place = device % GROUP
    return (place // 4) * HEADS + 4 * (plane - plane // 3) + place % 4


def device_of(combo):
    group = (combo % HEADS) // 4
    return GROUP * (group + group // 2) + 4 * (combo // HEADS) + combo % 4


class Net:
    def __init__(self, mesh):
        self.inner = mesh.shape["head"]
        self.count = mesh.shape["head"] * mesh.shape["blk"]
        self.planes = self.count // GROUP

    def permute(self, values, pairs):
        outer = self.count // self.inner

        def place(device):
            return (device % self.inner) * outer + device // self.inner

        return lax.ppermute(values, ("head", "blk"), [(place(i), place(j)) for i, j in pairs])

    def me(self):
        return lax.axis_index("blk") * self.inner + lax.axis_index("head")

    def at(self, device):
        return {"blk": device // self.inner, "head": device % self.inner}

    def meet(self, me, size):
        self.greet(me, size)
        pl.semaphore_wait(pltpu.get_barrier_semaphore(), size - 1)

    def greet(self, me, size):
        barrier = pltpu.get_barrier_semaphore()

        def greet(k, carry):
            pl.semaphore_signal(barrier, inc=1, device_id=self.at(peer(me, k, size)), device_id_type=MESH)
            return carry

        lax.fori_loop(1, size, greet, 0)

    def meet_attending(self, me):
        barrier = pltpu.get_barrier_semaphore()

        @pl.when(attends(me))
        def _():
            def greet(combo, carry):
                other = device_of(combo)

                @pl.when(other != me)
                def _():
                    pl.semaphore_signal(barrier, inc=1, device_id=self.at(other), device_id_type=MESH)

                return carry

            lax.fori_loop(0, 2 * HEADS, greet, 0)
            pl.semaphore_wait(barrier, 2 * HEADS - 1)

    def meet_heads(self, me):
        barrier = pltpu.get_barrier_semaphore()

        @pl.when(attends(me))
        def _():
            for owner in OWNERS[:3]:
                pl.semaphore_signal(barrier, inc=1, device_id=self.at(owner), device_id_type=MESH)
            pl.semaphore_wait(barrier, 3)

        for owner in OWNERS[:3]:

            @pl.when(me == owner)
            def _():
                def greet(combo, carry):
                    pl.semaphore_signal(barrier, inc=1, device_id=self.at(device_of(combo)), device_id_type=MESH)
                    return carry

                lax.fori_loop(0, 2 * HEADS, greet, 0)
                pl.semaphore_wait(barrier, 2 * HEADS)

    def shift(self, values, steps):
        far = GROUP * steps
        return self.permute(values, [(i, (i + far) % self.count) for i in range(self.count)])

    def flip(self, values, distance):
        return self.permute(values, [(i, i ^ distance) for i in range(self.count)])


def peer(me, k, size):
    return (me // size) * size + (me % size + k) % size


def flip_x(device):
    return device + 4 - 8 * ((device % GROUP) // 4)


def flip_y(device):
    return device + 1 - 2 * (device % 2)


def flip_core(device):
    return device + 2 - 4 * ((device % 4) // 2)


class Flow:
    def __init__(self, source, target, take, put, goes=None, size=None):
        self.source, self.target, self.take, self.put = source, target, take, put
        self.goes = goes or (lambda i, j: i >= 0)
        self.size = size

    def scratch(self):
        return []

    def semaphores(self):
        return self.size

    def bind(self, net, inputs, outputs, scratch, send, receive, local):
        self.net = net
        self.input, self.output = inputs[self.source], outputs[self.target]
        self.held = scratch
        self.send, self.receive, self.local = send, receive, local

    def copy(self, source, target, index, device):
        return pltpu.make_async_remote_copy(
            source,
            target,
            self.send.at[index],
            self.receive.at[index],
            device_id=self.net.at(device),
            device_id_type=MESH,
        )

    def remote(self, i, j, k):
        return self.copy(self.input.at[self.take(i, j)], self.output.at[self.put(i, j)], k, j)

    def near(self, i):
        return pltpu.make_async_copy(self.input.at[self.take(i, i)], self.output.at[self.put(i, i)], self.local)

    def start(self, me):
        def one(k, carry):
            other = peer(me, k, self.size)

            @pl.when(self.goes(me, other))
            def _():
                self.remote(me, other, k).start()

            return carry

        lax.fori_loop(1, self.size, one, 0)

        @pl.when(self.goes(me, me))
        def _():
            self.near(me).start()

    def middle(self, me):
        pass

    def finish(self, me):
        def one(k, carry):
            other = peer(me, k, self.size)

            @pl.when(self.goes(me, other))
            def _():
                self.remote(me, other, k).wait_send()

            before = peer(me, self.size - k, self.size)

            @pl.when(self.goes(before, me))
            def _():
                self.remote(before, me, k).wait_recv()

            return carry

        lax.fori_loop(1, self.size, one, 0)

        @pl.when(self.goes(me, me))
        def _():
            self.near(me).wait()


class Across(Flow):
    def __init__(self, net, source, target, take, put, goes=None):
        super().__init__(source, target, take, put, goes, net.count)
        self.planes = net.planes

    def semaphores(self):
        return self.planes

    def other(self, me, k):
        return (me + k * GROUP) % self.size

    def start(self, me):
        for k in range(1, self.planes):
            far = self.other(me, k)

            @pl.when(self.goes(me, far))
            def _(k=k, far=far):
                self.remote(me, far, k).start()

        @pl.when(self.goes(me, me))
        def _():
            self.near(me).start()

    def finish(self, me):
        for k in range(1, self.planes):
            far, before = self.other(me, k), self.other(me, self.planes - k)

            @pl.when(self.goes(me, far))
            def _(k=k, far=far):
                self.remote(me, far, k).wait_send()

            @pl.when(self.goes(before, me))
            def _(k=k, before=before):
                self.remote(before, me, k).wait_recv()

        @pl.when(self.goes(me, me))
        def _():
            self.near(me).wait()


class FanIn(Flow):
    def __init__(self, source, target, owner, take, put, goes=None, size=None):
        super().__init__(source, target, take, put, goes, size)
        self.place = owner

    def owner(self, me):
        return (me // self.size) * self.size + self.place

    def sends(self, me):
        return jnp.logical_and(me % self.size != self.place, self.goes(me, self.owner(me)))

    def step(self, me):
        return (self.place - me % self.size + self.size) % self.size

    def start(self, me):
        @pl.when(self.sends(me))
        def _():
            self.remote(me, self.owner(me), self.step(me)).start()

        @pl.when(jnp.logical_and(me % self.size == self.place, self.goes(me, me)))
        def _():
            self.near(me).start()

    def finish(self, me):
        @pl.when(self.sends(me))
        def _():
            self.remote(me, self.owner(me), self.step(me)).wait_send()

        @pl.when(me % self.size == self.place)
        def _():
            def one(k, carry):
                before = peer(me, self.size - k, self.size)

                @pl.when(self.goes(before, me))
                def _():
                    self.remote(before, me, k).wait_recv()

                return carry

            lax.fori_loop(1, self.size, one, 0)

        @pl.when(jnp.logical_and(me % self.size == self.place, self.goes(me, me)))
        def _():
            self.near(me).wait()


class FanOut(Flow):
    def __init__(self, source, target, owner, take, put):
        super().__init__(source, target, take, put)
        self.owner = owner

    def start(self, me):
        @pl.when(me == self.owner)
        def _():
            def one(k, carry):
                self.remote(me, peer(me, k, self.size), k).start()
                return carry

            lax.fori_loop(1, self.size, one, 0)
            self.near(me).start()

    def finish(self, me):
        @pl.when(me == self.owner)
        def _():
            def one(k, carry):
                self.remote(me, peer(me, k, self.size), k).wait_send()
                return carry

            lax.fori_loop(1, self.size, one, 0)
            self.near(me).wait()

        @pl.when(me != self.owner)
        def _():
            self.remote(self.owner, me, (me - self.owner + self.net.count) % self.size).wait_recv()


class PlaneGather(Flow):
    def __init__(self, source, target, put=lambda i: i % GROUP):
        super().__init__(source, target, None, put)

    def semaphores(self):
        return GROUP

    def partners(self, me):
        return [flip_x(me), flip_y(me), flip_x(flip_y(me))]

    def place(self, device):
        return self.output.at[self.put(device)]

    def own(self, me, index, device):
        return self.copy(self.input, self.place(me), index, device)

    def passed(self, me, index, partner):
        return self.copy(self.place(partner), self.place(partner), 4 + index, flip_core(me))

    def start(self, me):
        for index, partner in enumerate(self.partners(me)):
            self.own(me, 1 + index, partner).start()
        self.own(me, 0, flip_core(me)).start()
        pltpu.make_async_copy(self.input, self.place(me), self.local).start()

    def middle(self, me):
        for index, partner in enumerate(self.partners(me)):
            self.own(me, 1 + index, partner).wait_recv()
            self.passed(me, index, partner).start()

    def finish(self, me):
        for index, partner in enumerate(self.partners(me)):
            self.own(me, 1 + index, partner).wait_send()
            self.passed(me, index, partner).wait()
        self.own(me, 0, flip_core(me)).wait()
        pltpu.make_async_copy(self.input, self.place(me), self.local).wait()


class PlaneScatter(Flow):
    def __init__(self, source, target, block, lead=(), runs=None, gathers=False):
        super().__init__(source, target, None, None)
        self.block, self.lead, self.gathers = block, lead, gathers
        self.runs = runs or (lambda i: i >= 0)
        self.every = (slice(None),) * len(lead)

    def scratch(self):
        pair = pltpu.VMEM(self.lead + (2, 2) + self.block, jnp.bfloat16)
        shapes = [pair, pair, pltpu.VMEM((3,) + self.lead + self.block, jnp.bfloat16)]
        if self.gathers:
            shapes += [
                pltpu.VMEM(self.lead + self.block, jnp.bfloat16),
                pltpu.VMEM(self.lead + self.lead + self.block, jnp.bfloat16),
            ]
        return shapes

    def semaphores(self):
        return 5 + (self.lead[0] if self.gathers else 0)

    def onward(self, me, source):
        spare = GROUP * SPARE + me % GROUP
        return self.copy(self.held[3], self.held[4].at[source], 5 + source, spare)

    def partners(self, me):
        return [flip_x(me), flip_y(me), flip_x(flip_y(me))]

    def half(self, core):
        return self.input.at[self.every + (slice(None), core)]

    def first(self, me):
        return self.copy(self.half(1 - (me % 4) // 2), self.held[1], 0, flip_core(me))

    def mine(self, me):
        return pltpu.make_async_copy(self.half((me % 4) // 2), self.held[0], self.local)

    def spot(self, device):
        return self.every + ((device % GROUP) // 4, device % 2)

    def second(self, me, index, partner):
        return self.copy(self.held[0].at[self.spot(partner)], self.held[2].at[index], 1 + index, partner)

    def start(self, me):
        @pl.when(self.runs(me))
        def _():
            self.first(me).start()
            self.mine(me).start()

    def pair(self, device):
        spot = self.spot(device)
        return self.held[0][spot].astype(jnp.float32) + self.held[1][spot].astype(jnp.float32)

    def middle(self, me):
        @pl.when(self.runs(me))
        def _():
            self.mine(me).wait()
            self.first(me).wait_recv()
            for index, partner in enumerate(self.partners(me)):
                self.held[0][self.spot(partner)] = self.pair(partner).astype(jnp.bfloat16)
                self.second(me, index, partner).start()

    def finish(self, me):
        @pl.when(self.runs(me))
        def _():
            total = self.pair(me)
            for index, partner in enumerate(self.partners(me)):
                self.second(me, index, partner).wait_recv()
                total = total + self.held[2][index].astype(jnp.float32)
            if self.gathers:
                plane = me // GROUP
                self.held[3][...] = total.astype(jnp.bfloat16)

                @pl.when(plane != SPARE)
                def _():
                    self.onward(me, plane).start()

            self.output[...] = total
            self.first(me).wait_send()
            for index, partner in enumerate(self.partners(me)):
                self.second(me, index, partner).wait_send()
            if self.gathers:

                @pl.when(plane != SPARE)
                def _():
                    self.onward(me, plane).wait_send()

                @pl.when(plane == SPARE)
                def _():
                    for source in range(self.lead[0]):
                        if source != SPARE:
                            self.onward(me, source).wait_recv()
                            self.output[...] += self.held[4][source].astype(jnp.float32)


def bind_all(net, flows, inputs, outputs, scratch, send, receive, local):
    used = 0
    for number, flow in enumerate(flows):
        need = len(flow.scratch())
        flow.bind(
            net, inputs, outputs, scratch[used : used + need], send.at[number], receive.at[number], local.at[number]
        )
        used += need


def exchange_kernel(net, meet, flows, sources, targets, *refs):
    inputs = refs[:sources]
    outputs = refs[sources : sources + targets]
    me = net.me()
    meet(me)
    bind_all(net, flows, inputs, outputs, refs[sources + targets : -3], *refs[-3:])
    for flow in flows:
        flow.start(me)
    for flow in flows:
        flow.middle(me)
    for flow in flows:
        flow.finish(me)


def flow_scratch(flows):
    most = max(flow.semaphores() for flow in flows)
    return [shape for flow in flows for shape in flow.scratch()] + [
        pltpu.SemaphoreType.DMA((len(flows), most)),
        pltpu.SemaphoreType.DMA((len(flows), most)),
        pltpu.SemaphoreType.DMA((len(flows),)),
    ]


def exchange(net, name, number, flows, sources, shapes, size=None, meet=None):
    size = size or net.count
    for flow in flows:
        flow.size = flow.size or size
    summed = {flow.target for flow in flows if isinstance(flow, PlaneScatter)}
    moved = sum(math.prod(s.shape) * s.dtype.itemsize for s in shapes)
    return pl.pallas_call(
        functools.partial(
            exchange_kernel, net, meet or (lambda me: net.meet(me, size)), flows, len(sources), len(shapes)
        ),
        out_shape=shapes,
        in_specs=[ANY] * len(sources),
        out_specs=[VMEM if k in summed else ANY for k in range(len(shapes))],
        scratch_shapes=flow_scratch(flows),
        compiler_params=pltpu.CompilerParams(collective_id=number, has_side_effects=True),
        cost_estimate=pl.CostEstimate(flops=0, bytes_accessed=8 * moved, transcendentals=0),
        name=name,
    )(*sources)


def gather_kernel(net, flows, extras, x_ref, w_ref, *refs):
    extra_refs, (all_ref, wall_ref), refs = refs[:extras], refs[extras : extras + 2], refs[extras + 2 :]
    extra_all, (send, receive, wsend, wreceive, local), refs = refs[:extras], refs[extras : extras + 5], refs[extras + 5 :]
    count = net.count
    planes = net.planes
    me = net.me()
    plane = me // GROUP
    place = me % GROUP
    half = place // 4
    spot = place % 4
    across = flip_x(me)
    beside = flip_y(me)
    sibling = flip_core(me)
    net.meet(me, count)
    bind_all(net, flows, extra_refs, extra_all, (), *refs)

    def remote(source, target, index, device):
        return pltpu.make_async_remote_copy(
            source, target, send.at[index], receive.at[index], device_id=net.at(device), device_id_type=MESH
        )

    swap = remote(x_ref.at[1 - half], all_ref.at[plane, half, spot], 0, across)
    swap.start()

    def second(step, which):
        target = (me + step * GROUP) % count
        block = all_ref.at[plane, which, spot]
        return remote(block, block, 1 + (step - 1) * 2 + (which + half) % 2, target)

    def direct(step):
        target = (me + step * GROUP) % count
        return remote(x_ref.at[half], all_ref.at[plane, half, spot], 1 + (step - 1) * 2, target)

    third_base = 1 + 2 * (planes - 1)

    def third(step, which):
        source_plane = (plane + planes - step) % planes
        block = all_ref.at[source_plane, which, spot]
        return remote(block, block, third_base + step * 2 + which, beside)

    fourth_base = third_base + 2 * planes

    def fourth(step, which):
        source_plane = (plane + planes - step) % planes
        block = all_ref.at[source_plane, which, pl.ds((spot // 2) * 2, 2)]
        return remote(block, block, fourth_base + step * 2 + which, sibling)

    for step in range(1, planes):
        direct(step).start()
    mine = pltpu.make_async_copy(x_ref.at[half], all_ref.at[plane, half, spot], local.at[0])
    mine.start()

    def weights(combo):
        target = device_of(combo)
        return pltpu.make_async_remote_copy(
            w_ref.at[combo % HEADS],
            wall_ref.at[me],
            wsend.at[combo],
            wreceive.at[me],
            device_id=net.at(target),
            device_id_type=MESH,
        )

    def send_weights(combo, carry):
        @pl.when(device_of(combo) != me)
        def _():
            weights(combo).start()

        return carry

    mine.wait()
    swap.wait_recv()
    for step in range(1, planes):
        second(step, 1 - half).start()
    for which in range(2):
        third(0, which).start()
    lax.fori_loop(0, 2 * HEADS, send_weights, 0)
    for flow in flows:
        flow.start(me)
    for step in range(planes):
        if step > 0:
            second(step, half).wait_recv()
            second(step, 1 - half).wait_recv()
            for which in range(2):
                third(step, which).start()
            for which in range(2):
                third(step - 1, which).wait_recv()
            for which in range(2):
                fourth(step - 1, which).start()
    for which in range(2):
        third(planes - 1, which).wait_recv()
    for which in range(2):
        fourth(planes - 1, which).start()
    for step in range(planes):
        for which in range(2):
            fourth(step, which).wait_recv()

    @pl.when(attends(me))
    def _():
        own = pltpu.make_async_copy(w_ref.at[combo_of(me) % HEADS], wall_ref.at[me], local.at[1])
        own.start()
        own.wait()

        def took(k, carry):
            before = (me + k) % count
            pltpu.make_async_remote_copy(
                w_ref.at[0],
                wall_ref.at[before],
                wsend.at[0],
                wreceive.at[before],
                device_id=net.at(before),
                device_id_type=MESH,
            ).wait_recv()
            return carry

        lax.fori_loop(1, count, took, 0)

    def sent(combo, carry):
        @pl.when(device_of(combo) != me)
        def _():
            weights(combo).wait_send()

        return carry

    lax.fori_loop(0, 2 * HEADS, sent, 0)
    swap.wait_send()
    for step in range(1, planes):
        direct(step).wait_send()
        second(step, 1 - half).wait_send()
    for step in range(planes):
        for which in range(2):
            third(step, which).wait_send()
            fourth(step, which).wait_send()
    for flow in flows:
        flow.finish(me)


def gather_tokens(net, number, normed, columns, flows, extras, shapes):
    planes = net.planes
    copies = 1 + 2 * (planes - 1) + 4 * planes
    for flow in flows:
        flow.size = flow.size or net.count
    shapes = [
        jax.ShapeDtypeStruct((planes, 2, 4) + normed.shape[1:], normed.dtype),
        jax.ShapeDtypeStruct((net.count,) + columns.shape[1:], columns.dtype),
    ] + shapes
    return pl.pallas_call(
        functools.partial(gather_kernel, net, flows, len(extras)),
        out_shape=shapes,
        in_specs=[ANY] * (2 + len(extras)),
        out_specs=[ANY] * len(shapes),
        scratch_shapes=[
            pltpu.SemaphoreType.DMA((copies,)),
            pltpu.SemaphoreType.DMA((copies,)),
            pltpu.SemaphoreType.DMA((2 * HEADS,)),
            pltpu.SemaphoreType.DMA((net.count,)),
            pltpu.SemaphoreType.DMA((2,)),
        ]
        + flow_scratch(flows),
        compiler_params=pltpu.CompilerParams(collective_id=number, has_side_effects=True),
        cost_estimate=pl.CostEstimate(flops=0, bytes_accessed=100 * 2**20, transcendentals=0),
        name="gather_tokens",
    )(normed, columns, *extras)


def rope_rows(values, cosine, sine):
    first, second = values[:HALF], values[HALF:]
    return jnp.concatenate([first * cosine - second * sine, second * cosine + first * sine], axis=0)


def rope_rows_back(values, cosine, sine):
    first, second = values[:HALF], values[HALF:]
    return jnp.concatenate([first * cosine + second * sine, second * cosine - first * sine], axis=0)


def columns_of(index):
    return pl.ds(pl.multiple_of(index * BLOCK, BLOCK), BLOCK)


def wide_columns(index):
    return pl.ds(pl.multiple_of(index * WIDE, WIDE), WIDE)


def permitted(query_block, key_block, start):
    shape = (BLOCK, WIDE)
    key = key_block * BLOCK + lax.broadcasted_iota(jnp.int32, shape, 0)
    query = query_block * WIDE + lax.broadcasted_iota(jnp.int32, shape, 1)
    return (key <= query) & (key >= start)


def sweep(bounds_ref, query_block, step, carried):
    diagonal = query_block * (WIDE // BLOCK)
    first, whole = bounds_ref[0, query_block], bounds_ref[1, query_block]
    carried = lax.fori_loop(first, whole, functools.partial(step, True), carried)
    carried = lax.fori_loop(whole, diagonal, functools.partial(step, False), carried)
    return lax.fori_loop(diagonal, diagonal + WIDE // BLOCK, functools.partial(step, True), carried)


def fold(rows):
    return jnp.concatenate([rows[:HALF], rows[HALF:]], axis=1)


def unfold(rows):
    return jnp.concatenate([rows[:, :HEAD_DIM], rows[:, HEAD_DIM:]], axis=0)


def attend_kernel(net, *refs):
    @pl.when(attends(net.me()))
    def _():
        attend_body(*refs)


def attend_body(first_ref, x_ref, w_ref, cos_ref, sin_ref, start_ref, qkv_ref, mixed_ref, total_ref, packed_ref, key_rows):
    blocks = qkv_ref.shape[1] // BLOCK
    weights = w_ref[...]

    def project(chunk, carry):
        tokens = x_ref[chunk // 2, chunk % 2].reshape(BLOCK, D)
        here = columns_of(chunk)
        made = nt(weights, tokens)
        cosine, sine = cos_ref[:, here], sin_ref[:, here]
        query = rope_rows(made[:HEAD_DIM], cosine, sine)
        key = rope_rows(made[HEAD_DIM : 2 * HEAD_DIM], cosine, sine)
        qkv_ref[:HEAD_DIM, here] = query.astype(jnp.bfloat16) * SCALE
        qkv_ref[HEAD_DIM : 2 * HEAD_DIM, here] = key.astype(jnp.bfloat16)
        qkv_ref[2 * HEAD_DIM :, here] = made[2 * HEAD_DIM :].astype(jnp.bfloat16)
        key_rows[here, :] = key.T.astype(jnp.bfloat16)
        return carry

    lax.fori_loop(0, blocks, project, 0)

    def query_step(query_block, carry):
        here = wide_columns(query_block)
        query = qkv_ref[:HEAD_DIM, here]
        start = start_ref[:, here]

        def key_step(masked, key_block, held):
            top, total, mixed = held
            there = columns_of(key_block)
            scores = nn(key_rows[there, :], query)
            if masked:
                allowed = permitted(query_block, key_block, start)
                scores = jnp.where(allowed, scores, NEGATIVE)
            new_top = jnp.maximum(top, jnp.max(scores, axis=0, keepdims=True))
            weights = jnp.exp(scores - new_top)
            if masked:
                weights = jnp.where(allowed, weights, 0.0)
            factor = jnp.exp(top - new_top)
            total = total * factor + jnp.sum(weights, axis=0, keepdims=True)
            mixed = mixed * factor + nn(qkv_ref[2 * HEAD_DIM :, there], weights.astype(jnp.bfloat16))
            return new_top, total, mixed

        top, total, mixed = sweep(
            first_ref,
            query_block,
            key_step,
            (
                jnp.full((1, WIDE), NEGATIVE, jnp.float32),
                jnp.zeros((1, WIDE), jnp.float32),
                jnp.zeros((HEAD_DIM, WIDE), jnp.float32),
            ),
        )
        mixed = mixed / total
        mixed_ref[:, here] = mixed
        total_ref[:, here] = top + jnp.log(total)
        rows = mixed.T
        for part in range(WIDE // 64):
            packed_ref[query_block * (WIDE // 64) + part] = fold(rows[part * 64 : part * 64 + 64]).astype(
                jnp.bfloat16
            )
        return carry

    lax.fori_loop(0, qkv_ref.shape[1] // WIDE, query_step, 0)


def attend(net, first, tokens, weights, cosine, sine, start):
    length = start.shape[1]
    return pl.pallas_call(
        functools.partial(attend_kernel, net),
        out_shape=[
            jax.ShapeDtypeStruct((3 * HEAD_DIM, length), jnp.bfloat16),
            jax.ShapeDtypeStruct((HEAD_DIM, length), jnp.float32),
            jax.ShapeDtypeStruct((1, length), jnp.float32),
            jax.ShapeDtypeStruct((net.count, HALF, 128), jnp.bfloat16),
        ],
        in_specs=[SMEM] + [VMEM] * 5,
        out_specs=[VMEM] * 4,
        scratch_shapes=[pltpu.VMEM((length, HEAD_DIM), jnp.bfloat16)],
        cost_estimate=pl.CostEstimate(flops=2 * 10**9, bytes_accessed=8 * 2**20, transcendentals=2 * 10**6),
        name="attend",
    )(first, tokens, weights, cosine, sine, start)


def attend_back_kernel(net, *refs):
    @pl.when(attends(net.me()))
    def _():
        attend_back_body(*refs)


def attend_back_body(
    first_ref,
    x_ref,
    qkv_ref,
    mixed_ref,
    total_ref,
    cos_ref,
    sin_ref,
    start_ref,
    grad_ref,
    packed_ref,
    weight_ref,
    query_rows,
    key_rows,
    value_rows,
    grad_rows,
    grad_columns,
    correction,
    key_grad,
    value_grad,
    all_grad,
):
    blocks = qkv_ref.shape[1] // BLOCK
    parts = BLOCK // 64

    def prepare(chunk, carry):
        here = columns_of(chunk)
        turned = qkv_ref[:, here].astype(jnp.float32)
        query_rows[here, :] = turned[:HEAD_DIM].T.astype(jnp.bfloat16)
        key_rows[here, :] = turned[HEAD_DIM : 2 * HEAD_DIM].T.astype(jnp.bfloat16)
        value_rows[here, :] = turned[2 * HEAD_DIM :].T.astype(jnp.bfloat16)
        pieces = [unfold(grad_ref[chunk * parts + part].astype(jnp.float32)) for part in range(parts)]
        rows = jnp.concatenate(pieces, axis=0)
        grad_rows[here, :] = rows.astype(jnp.bfloat16)
        across = rows.T
        grad_columns[:, here] = across.astype(jnp.bfloat16)
        correction[:, here] = jnp.sum(across * mixed_ref[:, here], axis=0, keepdims=True)
        key_grad[here, :] = jnp.zeros((BLOCK, HEAD_DIM), jnp.float32)
        value_grad[here, :] = jnp.zeros((BLOCK, HEAD_DIM), jnp.float32)
        return carry

    lax.fori_loop(0, blocks, prepare, 0)

    wide_parts = WIDE // 64

    def query_step(query_block, carry):
        here = wide_columns(query_block)
        query = qkv_ref[:HEAD_DIM, here]
        start = start_ref[:, here]
        total = total_ref[:, here]
        fix = correction[:, here]
        grad = grad_columns[:, here]
        query_in_rows = query_rows[here, :]
        grad_in_rows = grad_rows[here, :]

        def key_step(masked, key_block, query_grad):
            there = columns_of(key_block)
            scores = nn(key_rows[there, :], query)
            weights = jnp.exp(scores - total)
            if masked:
                weights = jnp.where(permitted(query_block, key_block, start), weights, 0.0)
            value_grad[there, :] += nn(weights.astype(jnp.bfloat16), grad_in_rows)
            slope = nn(value_rows[there, :], grad)
            change = (weights * (slope - fix)).astype(jnp.bfloat16)
            key_grad[there, :] += nn(change, query_in_rows)
            return query_grad + nn(qkv_ref[HEAD_DIM : 2 * HEAD_DIM, there], change)

        query_grad = sweep(first_ref, query_block, key_step, jnp.zeros((HEAD_DIM, WIDE), jnp.float32))
        query_grad = rope_rows_back(query_grad * SCALE, cos_ref[:, here], sin_ref[:, here])
        all_grad[:HEAD_DIM, here] = query_grad.astype(jnp.bfloat16)
        rows = query_grad.T.astype(jnp.bfloat16)
        for part in range(wide_parts):
            packed_ref[query_block * wide_parts + part, :64, :HEAD_DIM] = rows[part * 64 : part * 64 + 64]
        return carry

    lax.fori_loop(0, qkv_ref.shape[1] // WIDE, query_step, 0)
    weight_ref[...] = jnp.zeros(weight_ref.shape, jnp.float32)

    def close(chunk, carry):
        here = columns_of(chunk)
        key = rope_rows_back(key_grad[here, :].T, cos_ref[:, here], sin_ref[:, here])
        value = value_grad[here, :]
        all_grad[HEAD_DIM : 2 * HEAD_DIM, here] = key.astype(jnp.bfloat16)
        all_grad[2 * HEAD_DIM :, here] = value.T.astype(jnp.bfloat16)
        rows = key.T.astype(jnp.bfloat16)
        for part in range(parts):
            token = chunk * parts + part
            packed_ref[token, :64, HEAD_DIM:] = rows[part * 64 : part * 64 + 64]
            packed_ref[token, 64:, :] = fold(value[part * 64 : part * 64 + 64]).astype(jnp.bfloat16)
        tokens = x_ref[chunk // 2, chunk % 2].reshape(BLOCK, D)
        weight_ref[...] += nn(all_grad[:, here], tokens)
        return carry

    lax.fori_loop(0, blocks, close, 0)


def attend_back(net, first, tokens, qkv, mixed, total, cosine, sine, start, grad):
    length = start.shape[1]
    rows = pltpu.VMEM((length, HEAD_DIM), jnp.bfloat16)
    sums = pltpu.VMEM((length, HEAD_DIM), jnp.float32)
    return pl.pallas_call(
        functools.partial(attend_back_kernel, net),
        out_shape=[
            jax.ShapeDtypeStruct((net.count, 96, 128), jnp.bfloat16),
            jax.ShapeDtypeStruct((3 * HEAD_DIM, D), jnp.float32),
        ],
        in_specs=[SMEM] + [VMEM] * 8,
        out_specs=[VMEM] * 2,
        scratch_shapes=[
            rows,
            rows,
            rows,
            rows,
            pltpu.VMEM((HEAD_DIM, length), jnp.bfloat16),
            pltpu.VMEM((1, length), jnp.float32),
            sums,
            sums,
            pltpu.VMEM((3 * HEAD_DIM, length), jnp.bfloat16),
        ],
        cost_estimate=pl.CostEstimate(flops=4 * 10**9, bytes_accessed=12 * 2**20, transcendentals=2 * 10**6),
        name="attend_back",
    )(first, tokens, qkv, mixed, total, cosine, sine, start, grad)


def tn(a, b):
    return lax.dot_general(a, b, (((0,), (0,)), ((), ())), preferred_element_type=jnp.float32)


def mean_of(values):
    return jnp.mean(values, axis=-1, keepdims=True)


def layer_norm(values):
    center = values - mean_of(values)
    return center * lax.rsqrt(mean_of(center * center) + EPSILON)


def norm_back(values, gradient):
    center = values - mean_of(values)
    inverse = lax.rsqrt(mean_of(center * center) + EPSILON)
    normed = center * inverse
    return inverse * (gradient - mean_of(gradient) - normed * mean_of(gradient * normed))


def after_kernel(parts_ref, tokens_ref, out_ref, mixed_ref, middle_ref, second_ref):
    for micro in range(2):
        here = slice(64 * micro, 64 * micro + 64)
        for pair in range(HEADS // 2):
            two = [unfold(parts_ref[micro * HEADS + 2 * pair + k].astype(jnp.float32)) for k in range(2)]
            mixed_ref[here, 128 * pair : 128 * pair + 128] = jnp.concatenate(two, axis=1).astype(jnp.bfloat16)
    middle = tokens_ref[...].astype(jnp.float32) + nn(mixed_ref[...], out_ref[...])
    middle_ref[...] = middle
    second_ref[...] = layer_norm(middle).astype(jnp.bfloat16)


def after_attention(parts, tokens, out):
    shape = tokens.shape
    return pl.pallas_call(
        after_kernel,
        out_shape=[
            jax.ShapeDtypeStruct(shape, jnp.bfloat16),
            jax.ShapeDtypeStruct(shape, jnp.float32),
            jax.ShapeDtypeStruct(shape, jnp.bfloat16),
        ],
        in_specs=[VMEM] * 3,
        out_specs=[VMEM] * 3,
        cost_estimate=pl.CostEstimate(flops=2 * 10**8, bytes_accessed=3 * 2**20, transcendentals=0),
        name="after_attention",
    )(parts, tokens, out)


def feed_forward_kernel(net, *refs):
    planes = net.planes
    second_ref, cotangent_ref = refs[:2]
    blocks = refs[2 : 2 + planes]
    second_terms, result_terms = refs[2 + planes : 4 + planes]
    terms = refs[4 + planes : 4 + 2 * planes]
    weights, slopes, products, sums = refs[4 + 2 * planes :]
    plane = net.me() // GROUP
    span = D // planes
    part = FF // GROUP
    for step, block in enumerate(blocks):
        source = (plane + planes - step) % planes
        weights[pl.ds(pl.multiple_of(source * span, span), span), :] = block[...]

    def forward(chunk, carry):
        here = columns_of(chunk)
        second, cotangent = second_ref[here, :], cotangent_ref[here, :]
        both = nn(second, weights[:, : 2 * part])
        gate, up = both[:, :part], both[:, part:]
        sigmoid = jax.nn.sigmoid(gate)
        silu = gate * sigmoid
        product = (silu * up).astype(jnp.bfloat16)
        change = nn(cotangent, weights[:, 2 * part :])
        slopes[here, :part] = (change * up * sigmoid * (1.0 + gate * (1.0 - sigmoid))).astype(jnp.bfloat16)
        slopes[here, part:] = (change * silu).astype(jnp.bfloat16)
        products[here, :] = product
        second_terms[here, :] = nt(slopes[here, :], weights[:, : 2 * part]).astype(jnp.bfloat16)
        result_terms[here, :] = nt(product, weights[:, 2 * part :]).astype(jnp.bfloat16)
        return carry

    lax.fori_loop(0, second_ref.shape[0] // BLOCK, forward, 0)
    for begin in range(0, D, BLOCK):
        here = slice(begin, begin + BLOCK)
        sums[here, : 2 * part] = tn(second_ref[:, here], slopes[...]).astype(jnp.bfloat16)
        sums[here, 2 * part :] = tn(cotangent_ref[:, here], products[...]).astype(jnp.bfloat16)
    for step, term in enumerate(terms):
        target = (plane + step) % planes
        term[...] = sums[pl.ds(pl.multiple_of(target * span, span), span), :]


def feed_forward(net, second, cotangent, blocks):
    tokens = second.shape[0]
    part = FF // GROUP
    low = jnp.bfloat16
    return pl.pallas_call(
        functools.partial(feed_forward_kernel, net),
        out_shape=[jax.ShapeDtypeStruct((tokens, D), low)] * 2
        + [jax.ShapeDtypeStruct((D // net.planes, 3 * part), low)] * net.planes,
        in_specs=[VMEM] * (2 + net.planes),
        out_specs=[VMEM] * (2 + net.planes),
        scratch_shapes=[
            pltpu.VMEM((D, 3 * part), low),
            pltpu.VMEM((tokens, 2 * part), low),
            pltpu.VMEM((tokens, part), low),
            pltpu.VMEM((D, 3 * part), low),
        ],
        cost_estimate=pl.CostEstimate(flops=35 * 10**8, bytes_accessed=10 * 2**20, transcendentals=10**6),
        name="feed_forward",
    )(second, cotangent, *blocks)


def before_kernel(second_grad_ref, middle_ref, cotangent_ref, mixed_ref, out_ref, middle_grad_ref, folded_ref, terms_ref):
    middle_grad = cotangent_ref[...].astype(jnp.float32) + norm_back(middle_ref[...], second_grad_ref[...])
    middle_grad_ref[...] = middle_grad
    low = middle_grad.astype(jnp.bfloat16)
    mixed_grad = nt(low, out_ref[...])
    for micro in range(2):
        rows = mixed_grad[64 * micro : 64 * micro + 64]
        for head in range(HEADS):
            folded_ref[micro * HEADS + head] = fold(rows[:, HEAD_DIM * head : HEAD_DIM * head + HEAD_DIM]).astype(
                jnp.bfloat16
            )
    terms_ref[...] = tn(mixed_ref[...], low).astype(jnp.bfloat16)


def before_attention(second_grad, middle, cotangent, mixed, out):
    return pl.pallas_call(
        before_kernel,
        out_shape=[
            jax.ShapeDtypeStruct(middle.shape, jnp.float32),
            jax.ShapeDtypeStruct((2 * HEADS, HALF, 128), jnp.bfloat16),
            jax.ShapeDtypeStruct((D, D), jnp.bfloat16),
        ],
        in_specs=[VMEM] * 5,
        out_specs=[VMEM] * 3,
        cost_estimate=pl.CostEstimate(flops=4 * 10**8, bytes_accessed=5 * 2**20, transcendentals=0),
        name="before_attention",
    )(second_grad, middle, cotangent, mixed, out)


def input_kernel(grads_ref, weights_ref, tokens_ref, middle_grad_ref, input_ref, query, key, value):
    for micro in range(2):
        here = slice(64 * micro, 64 * micro + 64)
        for pair in range(HEADS // 2):
            head = 2 * pair
            two = [grads_ref[HEADS * micro + head + k].astype(jnp.float32) for k in range(2)]
            there = slice(128 * pair, 128 * pair + 128)
            query[here, there] = jnp.concatenate([t[:64, :HEAD_DIM] for t in two], axis=1).astype(jnp.bfloat16)
            key[here, there] = jnp.concatenate([t[:64, HEAD_DIM:] for t in two], axis=1).astype(jnp.bfloat16)
            value[here, there] = jnp.concatenate([unfold(t[64:96]) for t in two], axis=1).astype(jnp.bfloat16)
    gradient = (
        nt(query[...], weights_ref[0]) + nt(key[...], weights_ref[1]) + nt(value[...], weights_ref[2])
    )
    input_ref[...] = middle_grad_ref[...] + norm_back(tokens_ref[...].astype(jnp.float32), gradient)


def input_gradient(grads, weights, tokens, middle_grad):
    rows = pltpu.VMEM(tokens.shape, jnp.bfloat16)
    return pl.pallas_call(
        input_kernel,
        out_shape=jax.ShapeDtypeStruct(tokens.shape, jnp.float32),
        in_specs=[VMEM] * 4,
        out_specs=VMEM,
        scratch_shapes=[rows] * 3,
        cost_estimate=pl.CostEstimate(flops=5 * 10**8, bytes_accessed=6 * 2**20, transcendentals=0),
        name="input_gradient",
    )(grads, weights, tokens, middle_grad)


def solve_heads(me, head_ref, moment_ref, target, scratch):
    wide, semaphore, parts, moment = scratch[0], scratch[3], scratch[4], scratch[5]

    @pl.when(jnp.logical_or(me == OWNERS[0], jnp.logical_or(me == OWNERS[1], me == OWNERS[2])))
    def _():
        move(head_ref, parts, semaphore)
        move(moment_ref, moment, semaphore)

        def join(pair, carry):
            first = parts[2 * pair].astype(jnp.float32) + parts[HEADS + 2 * pair].astype(jnp.float32)
            second = parts[2 * pair + 1].astype(jnp.float32) + parts[HEADS + 2 * pair + 1].astype(jnp.float32)
            here = pl.ds(pl.multiple_of(pair * 128, 128), 128)
            gradient = jnp.concatenate([first, second], axis=0).T
            wide[:, here] = (0.75 * gradient + 0.25 * moment[:, here].astype(jnp.float32)).astype(jnp.bfloat16)
            return carry

        lax.fori_loop(0, HEADS // 2, join, 0)
        solve(D, target, scratch)


def solve_late(me, out_ref, ffn_ref, out_target, ffn_target, scratch):
    wide, semaphore = scratch[0], scratch[3]

    @pl.when(me == OWNERS[3])
    def _():
        move(out_ref, wide.at[:, pl.ds(0, D)], semaphore)
        solve(D, out_target, scratch)

    @pl.when(jnp.logical_or(me == OWNERS[4], jnp.logical_or(me == OWNERS[5], me == OWNERS[6])))
    def _():
        move(ffn_ref, wide, semaphore)
        solve(FF, ffn_target, scratch)


def move(source, target, semaphore):
    copy = pltpu.make_async_copy(source, target, semaphore)
    copy.start()
    copy.wait()


def solve(span, target, scratch):
    wide, gram, polynomial, semaphore = scratch[:4]

    def blocks_of(index):
        return pl.ds(pl.multiple_of(index * BLOCK, BLOCK), BLOCK)

    def mirror(target, i, j, block):
        target[i * BLOCK : (i + 1) * BLOCK, j * BLOCK : (j + 1) * BLOCK] = block.astype(jnp.bfloat16)
        if i != j:
            target[j * BLOCK : (j + 1) * BLOCK, i * BLOCK : (i + 1) * BLOCK] = block.T.astype(jnp.bfloat16)

    chunks = span // BLOCK

    def measure(index, total):
        values = wide[:, blocks_of(index)].astype(jnp.float32)
        return total + jnp.sum(values * values, axis=0, keepdims=True)

    total = lax.fori_loop(0, chunks, measure, jnp.zeros((1, BLOCK), jnp.float32))
    frobenius = jnp.sqrt(jnp.sum(total, axis=1, keepdims=True)) + 1e-07

    def scale(index, carry):
        here = blocks_of(index)
        wide[:, here] = (wide[:, here].astype(jnp.float32) / frobenius).astype(jnp.bfloat16)
        return carry

    lax.fori_loop(0, chunks, scale, 0)

    def step(_, carry):
        for i in range(D // BLOCK):
            for j in range(i + 1):
                mirror(
                    gram,
                    i,
                    j,
                    nt(
                        wide[i * BLOCK : (i + 1) * BLOCK, :span],
                        wide[j * BLOCK : (j + 1) * BLOCK, :span],
                    ),
                )
        for i in range(D // BLOCK):
            for j in range(i + 1):
                square = nn(gram[i * BLOCK : (i + 1) * BLOCK, :], gram[:, j * BLOCK : (j + 1) * BLOCK])
                linear = gram[i * BLOCK : (i + 1) * BLOCK, j * BLOCK : (j + 1) * BLOCK].astype(jnp.float32)
                mirror(polynomial, i, j, COEFF_B * linear + COEFF_C * square)

        def advance(index, inner):
            here = blocks_of(index)
            old = wide[:, here]
            wide[:, here] = (COEFF_A * old.astype(jnp.float32) + nn(polynomial[...], old)).astype(jnp.bfloat16)
            return inner

        lax.fori_loop(0, chunks, advance, 0)
        return carry

    lax.fori_loop(0, NS_STEPS, step, 0)
    move(wide.at[:, pl.ds(0, span)], target, semaphore)


def solve_scratch(span, heads):
    square = pltpu.VMEM((D, D), jnp.bfloat16)
    shapes = [pltpu.VMEM((D, span), jnp.bfloat16), square, square, pltpu.SemaphoreType.DMA]
    if heads:
        shapes += [pltpu.VMEM((2 * HEADS, HEAD_DIM, D), jnp.bfloat16), square]
    return shapes


SQUARE = jax.ShapeDtypeStruct((D, D), jnp.bfloat16)
SOLVE_COST = pl.CostEstimate(flops=25 * 10**9, bytes_accessed=8 * 2**20, transcendentals=0)


def newton_kernel(net, head_ref, moment_ref, out_ref, ffn_ref, attn_target, ffn_target, *scratch):
    me = net.me()
    solve_heads(me, head_ref, moment_ref, attn_target, scratch)
    solve_late(me, out_ref, ffn_ref, attn_target, ffn_target, scratch)


def newton(net, *sources):
    return pl.pallas_call(
        functools.partial(newton_kernel, net),
        out_shape=[SQUARE, jax.ShapeDtypeStruct((D, FF), jnp.bfloat16)],
        in_specs=[ANY] * 4,
        out_specs=[ANY] * 2,
        scratch_shapes=solve_scratch(FF, True),
        cost_estimate=SOLVE_COST,
        name="newton",
    )(*sources)


def on_device(net, tokens, doc_ids, cotangent, attn_weight, ffn_weight, attn_moment, ffn_moment):
    micro_count, token_count, width = tokens.shape
    rows = attn_weight.shape[1]
    count, planes = net.count, net.planes
    length = count * token_count
    me = net.me()
    plane, place = me // GROUP, me % GROUP
    x_bit = place // 4
    both = micro_count * token_count
    part = FF // GROUP
    low = jnp.bfloat16
    everything = (slice(None),)

    attn_low = attn_weight.astype(low)
    ffn_low = ffn_weight.astype(low)

    def cut_up(values):
        return values.reshape(3, rows, GROUP, part).transpose(2, 1, 0, 3).reshape(GROUP, rows, 3 * part)

    cut = cut_up(ffn_low)
    out_grad = cotangent.reshape(both, width)
    hidden = tokens.astype(jnp.float32).reshape(both, width)
    normed = layer_norm(hidden).astype(low)
    counts = jnp.sum((doc_ids[:, :, None] == jnp.arange(DOCS)[None, None, :]).astype(jnp.float32), axis=1)
    tail = jnp.pad(counts.reshape(-1).astype(low), (0, HEAD_DIM - micro_count * DOCS))
    columns = attn_low[:3].reshape(3, rows, HEADS, HEAD_DIM).transpose(2, 1, 0, 3).reshape(HEADS, rows, 3 * HEAD_DIM)
    columns = jnp.concatenate([columns, jnp.broadcast_to(tail, (HEADS, rows, HEAD_DIM))], axis=2)
    moment_low = attn_moment.astype(low)
    all_tokens, all_columns, plane_cut, plane_out, moment_plane, moment_out = gather_tokens(
        net,
        0,
        normed.reshape(micro_count, token_count, width),
        columns,
        [
            Flow(0, 0, lambda i, j: j % GROUP, lambda i, j: i % GROUP, size=GROUP),
            Across(net, 1, 1, lambda i, j: 0, lambda i, j: i // GROUP),
            Across(net, 3, 3, lambda i, j: 0, lambda i, j: i // GROUP, lambda i, j: j // GROUP == SPARE),
        ]
        + [Flow(2, 2, lambda i, j: j % GROUP, lambda i, j: i % GROUP, size=GROUP)],
        [cut, attn_low[3:], cut_up(ffn_moment.astype(low)), moment_low[3:]],
        [
            jax.ShapeDtypeStruct(cut.shape, low),
            jax.ShapeDtypeStruct((planes, rows, D), low),
            jax.ShapeDtypeStruct(cut.shape, low),
            jax.ShapeDtypeStruct((planes, rows, D), low),
        ],
    )
    late_own = plane_cut.reshape(GROUP * rows, 3 * part)
    late_blocks = [late_own] + [net.shift(late_own, step) for step in range(1, planes)]

    head_weights = all_columns[:, :, : 3 * HEAD_DIM].reshape(D, 3 * HEAD_DIM).T
    every_count = jnp.sum(all_columns[:, 0, 3 * HEAD_DIM :].astype(jnp.float32), axis=0)
    own_count = lax.dynamic_slice_in_dim(every_count, x_bit * DOCS, DOCS, 0)
    starts = jnp.cumsum(own_count) - own_count
    index = jnp.arange(length).astype(jnp.float32)
    start = jnp.max(jnp.where(starts[:, None] <= index[None, :], starts[:, None], 0.0), axis=0)
    inverse = 10000.0 ** (-(jnp.arange(HALF, dtype=jnp.float32) * 2.0) / HEAD_DIM)
    angles = inverse[:, None] * (index - start)[None, :]
    cosine, sine = jnp.cos(angles), jnp.sin(angles)
    start = start.astype(jnp.int32)
    diagonal = jnp.arange(length // WIDE, dtype=jnp.int32) * (WIDE // BLOCK)
    first = jnp.clip(start[::WIDE] // BLOCK, 0, diagonal)
    first = jnp.stack([first, jnp.clip((start[WIDE - 1 :: WIDE] + BLOCK - 1) // BLOCK, first, diagonal)])
    start = start[None, :]

    qkv, mixed, total, packed = attend(net, first, all_tokens, head_weights, cosine, sine, start)
    mixed_parts, moment_whole, plane_out_grad, out_full = exchange(
        net,
        "mixed_exchange",
        1,
        [PlaneGather(2, 2), PlaneGather(3, 3, lambda i: everything + (i % GROUP,))]
        + [Flow(0, 0, lambda i, j: j, lambda i, j: combo_of(i), lambda i, j: attends(i))]
        + [FanIn(1, 1, OWNERS[k], lambda i, j, k=k: k, lambda i, j: i) for k in range(3)],
        [packed, moment_low, out_grad, plane_out],
        [
            jax.ShapeDtypeStruct((2 * HEADS, HALF, 128), low),
            jax.ShapeDtypeStruct((count, rows, D), low),
            jax.ShapeDtypeStruct((GROUP, both, width), low),
            jax.ShapeDtypeStruct((planes, GROUP, rows, D), low),
        ],
    )
    plane_out_grad = plane_out_grad.reshape(GROUP * both, width)
    out_full = out_full.reshape(D, D)
    own_tokens = tokens.reshape(both, width)
    mixed_tokens, middle, second = after_attention(mixed_parts, own_tokens, out_full)
    (plane_second,) = exchange(
        net,
        "second_exchange",
        10,
        [PlaneGather(0, 0)],
        [second],
        [jax.ShapeDtypeStruct((GROUP, both, width), low)],
        GROUP,
    )
    plane_second = plane_second.reshape(GROUP * both, width)
    second_terms, result_terms, *ffn_terms = feed_forward(net, plane_second, plane_out_grad, late_blocks)
    sides = (2, 2, 2, both, width)
    (second_grad,) = exchange(
        net,
        "second_grad_exchange",
        8,
        [PlaneScatter(0, 0, (both, width))],
        [second_terms.reshape(sides)],
        [jax.ShapeDtypeStruct((both, width), jnp.float32)],
        GROUP,
    )
    ffn_block = ffn_terms[0].astype(jnp.float32)
    for step in range(1, planes):
        ffn_block = ffn_block + net.shift(ffn_terms[step], step).astype(jnp.float32)
    ffn_update = 0.75 * ffn_block + 0.25 * moment_plane.reshape(GROUP * rows, 3 * part).astype(jnp.float32)
    ffn_update, ffn_block = ffn_update.astype(low), ffn_block.astype(low)
    middle_grad, folded, out_terms = before_attention(second_grad, middle, out_grad, mixed_tokens, out_full)
    grad_parts, out_total, ffn_whole = exchange(
        net,
        "mixed_grad_exchange",
        2,
        [
            PlaneScatter(1, 1, (rows, D), (planes,), gathers=True),
            Flow(0, 0, lambda i, j: combo_of(j), lambda i, j: i, lambda i, j: attends(j)),
        ]
        + [
            FanIn(
                2,
                2,
                OWNERS[4 + k],
                lambda i, j, k=k: (slice(None), pl.ds(part * k, part)),
                lambda i, j: (i // GROUP, slice(None), pl.ds(pl.multiple_of(part * (i % GROUP), part), part)),
            )
            for k in range(3)
        ],
        [folded, out_terms.reshape(planes, 2, 2, 2, rows, D), ffn_update],
        [
            jax.ShapeDtypeStruct((count, HALF, 128), low),
            jax.ShapeDtypeStruct((planes, rows, D), jnp.float32),
            jax.ShapeDtypeStruct((planes, GROUP * rows, FF), low),
        ],
    )
    out_update = (0.75 * out_total + 0.25 * moment_out.astype(jnp.float32)).astype(low)

    early_low, grad_parts = lax.optimization_barrier((attn_low[:3], grad_parts))
    attn_full = lax.all_gather(early_low, ("blk", "head"), axis=1, tiled=True)
    grad_packed, head_grad = attend_back(
        net, first, all_tokens, qkv, mixed, total, cosine, sine, start, grad_parts
    )
    head_low = head_grad.astype(low)
    out_update, grad_packed, head_low = lax.optimization_barrier((out_update, grad_packed, head_low))
    (out_whole,) = exchange(
        net,
        "out_exchange",
        4,
        [
            FanIn(
                0,
                0,
                OWNERS[3] % GROUP,
                lambda i, j: everything,
                lambda i, j: everything + (i % GROUP,),
                lambda i, j: j == OWNERS[3],
            )
        ],
        [out_update],
        [jax.ShapeDtypeStruct((planes, GROUP, rows, D), low)],
        GROUP,
    )
    out_whole, grad_packed, head_low = lax.optimization_barrier((out_whole, grad_packed, head_low))
    (head_whole,) = exchange(
        net,
        "head_exchange",
        9,
        [
            FanIn(0, 0, OWNERS[k], lambda i, j, k=k: k, lambda i, j: combo_of(i), lambda i, j: attends(i))
            for k in range(3)
        ],
        [head_low.reshape(3, HEAD_DIM, D)],
        [jax.ShapeDtypeStruct((2 * HEADS, HEAD_DIM, D), low)],
        meet=net.meet_heads,
    )
    grad_packed, head_low, head_whole = lax.optimization_barrier((grad_packed, head_low, head_whole))
    head_rows = jnp.pad(head_low.T.reshape(count, rows, 3 * HEAD_DIM), ((0, 0), (0, 0), (0, 64)))
    outgoing = jnp.concatenate([grad_packed, head_rows.reshape(count, rows * 2, 128)], axis=1)
    ffn_rows, result_sides = ffn_block.reshape(GROUP, rows, 3 * part), result_terms.reshape(sides)
    last = [
        jax.ShapeDtypeStruct((2 * HEADS, 96 + 2 * rows, 128), low),
        jax.ShapeDtypeStruct((GROUP, rows, 3 * part), low),
        jax.ShapeDtypeStruct((both, width), jnp.float32),
    ]

    def last_flows(base, runs):
        return [
            PlaneScatter(base + 2, base + 2, (both, width), runs=runs),
            Flow(
                base,
                base,
                lambda i, j: j,
                lambda i, j: combo_of(i),
                lambda i, j: jnp.logical_and(attends(i), runs(j)),
            ),
            Flow(
                base + 1,
                base + 1,
                lambda i, j: j % GROUP,
                lambda i, j: i % GROUP,
                lambda i, j: runs(i),
                size=GROUP,
            ),
        ]

    early_last = exchange(
        net,
        "attending_exchange",
        7,
        last_flows(0, attends),
        [outgoing, ffn_rows, result_sides],
        last,
        meet=net.meet_attending,
    )
    attn_done, ffn_done = newton(
        net, head_whole, moment_whole.reshape(D, D), out_whole.reshape(D, D), ffn_whole.reshape(D, FF)
    )
    attn_done, ffn_done, outgoing, *early_last = lax.optimization_barrier(
        (attn_done, ffn_done, outgoing, *early_last)
    )
    attn_step, ffn_step, out_row_grad, *late_last = exchange(
        net,
        "step_exchange",
        5,
        [FanOut(1, 1, OWNERS[4 + k], lambda i, j: j, lambda i, j, k=k: k) for k in range(3)]
        + [FanOut(0, 0, OWNERS[k], lambda i, j: j, lambda i, j, k=k: k) for k in range(4)]
        + [Across(net, 2, 2, lambda i, j: j // GROUP, lambda i, j: 0, lambda i, j: i // GROUP == SPARE)]
        + last_flows(3, lambda i: jnp.logical_not(attends(i))),
        [
            attn_done.reshape(count, rows, D),
            ffn_done.reshape(count, rows, FF),
            out_total.astype(low),
            outgoing,
            ffn_rows,
            result_sides,
        ],
        [
            jax.ShapeDtypeStruct((4, rows, D), low),
            jax.ShapeDtypeStruct((3, rows, FF), low),
            jax.ShapeDtypeStruct((1, rows, D), low),
        ]
        + last,
    )
    grads, ffn_parts, result = (jnp.where(attends(me), a, b) for a, b in zip(early_last, late_last))
    ffn_grad = ffn_parts.reshape(GROUP, rows, 3, part).transpose(2, 1, 0, 3).reshape(3, rows, FF).astype(jnp.float32)
    ffn_moment_new = 0.5 * ffn_moment + 0.5 * ffn_grad

    input_grad = input_gradient(grads, attn_full, own_tokens, middle_grad)
    row_grads = grads[:, 96:].reshape(micro_count, HEADS, rows, 256).astype(jnp.float32)
    summed = jnp.sum(row_grads, axis=0)
    early_grad = summed[:, :, : 3 * HEAD_DIM].reshape(HEADS, rows, 3, HEAD_DIM).transpose(2, 1, 0, 3).reshape(3, rows, D)
    attn_grad = jnp.concatenate([early_grad, out_row_grad.astype(jnp.float32)], axis=0)
    attn_moment_new = 0.5 * attn_moment + 0.5 * attn_grad

    output = (middle + result).astype(low)

    rates = jnp.asarray(RATES, jnp.float32)[:, None, None]
    attn_master = attn_weight - rates[:4] * attn_step.astype(jnp.float32)
    ffn_master = ffn_weight - rates[4:] * ffn_step.astype(jnp.float32)
    shape = (micro_count, token_count, width)
    return (
        output.reshape(shape),
        input_grad.reshape(shape),
        attn_grad,
        ffn_grad,
        attn_master,
        ffn_master,
        attn_moment_new,
        ffn_moment_new,
        attn_master.astype(low),
        ffn_master.astype(low),
    )


def solution(mesh):
    wide = P(None, ("blk", "head"), None)
    return jax.shard_map(
        functools.partial(on_device, Net(mesh)),
        mesh=mesh,
        in_specs=(wide, P(None, ("blk", "head")), wide, wide, wide, wide, wide),
        out_specs=(wide,) * 10,
        check_vma=False,
    )
```

```python
import functools
import math

import jax
import jax.numpy as jnp
from jax import lax
from jax.experimental import pallas as pl
from jax.experimental.pallas import tpu as pltpu
from jax.sharding import PartitionSpec as P

D = 768
HEADS = 12
HEAD_DIM = 64
HALF = 32
FF = 2048
DOCS = 4
NS_STEPS = 5
GROUP = 8
HOST = 1
SPARE = 2
BLOCK = 256
WIDE = 512

EPSILON = 1e-05
NEGATIVE = -1e30
RATES = (0.5, 0.5, 0.5, 7.0, 1.0, 1.0, 0.5)
COEFF_A = 3.4445
COEFF_B = -4.775
COEFF_C = 2.0315
OWNERS = (18, 19, 22, 21, 16, 17, 20)
MESH = pl.DeviceIdType.MESH
ANY = pl.BlockSpec(memory_space=pl.ANY)
VMEM = pl.BlockSpec(memory_space=pltpu.VMEM)
SMEM = pl.BlockSpec(memory_space=pltpu.SMEM)
SCALE = HEAD_DIM ** (-0.5)


def nt(a, b):
    return lax.dot_general(a, b, (((1,), (1,)), ((), ())), preferred_element_type=jnp.float32)


def nn(a, b):
    return jnp.dot(a, b, preferred_element_type=jnp.float32)


def attends(device):
    plane = device // GROUP
    return jnp.logical_and(plane < 4, plane != SPARE)


def combo_of(device):
    plane = device // GROUP
    place = device % GROUP
    return (place // 4) * HEADS + 4 * (plane - plane // 3) + place % 4


def device_of(combo):
    group = (combo % HEADS) // 4
    return GROUP * (group + group // 2) + 4 * (combo // HEADS) + combo % 4


class Net:
    def __init__(self, mesh):
        self.inner = mesh.shape["head"]
        self.count = mesh.shape["head"] * mesh.shape["blk"]
        self.planes = self.count // GROUP

    def permute(self, values, pairs):
        outer = self.count // self.inner

        def place(device):
            return (device % self.inner) * outer + device // self.inner

        return lax.ppermute(values, ("head", "blk"), [(place(i), place(j)) for i, j in pairs])

    def me(self):
        return lax.axis_index("blk") * self.inner + lax.axis_index("head")

    def at(self, device):
        return {"blk": device // self.inner, "head": device % self.inner}

    def meet(self, me, size):
        self.greet(me, size)
        pl.semaphore_wait(pltpu.get_barrier_semaphore(), size - 1)

    def greet(self, me, size):
        barrier = pltpu.get_barrier_semaphore()

        def greet(k, carry):
            pl.semaphore_signal(barrier, inc=1, device_id=self.at(peer(me, k, size)), device_id_type=MESH)
            return carry

        lax.fori_loop(1, size, greet, 0)

    def meet_attending(self, me):
        barrier = pltpu.get_barrier_semaphore()

        @pl.when(attends(me))
        def _():
            def greet(combo, carry):
                other = device_of(combo)

                @pl.when(other != me)
                def _():
                    pl.semaphore_signal(barrier, inc=1, device_id=self.at(other), device_id_type=MESH)

                return carry

            lax.fori_loop(0, 2 * HEADS, greet, 0)
            pl.semaphore_wait(barrier, 2 * HEADS - 1)

    def meet_own_plane(self, me):
        @pl.when(attends(me))
        def _():
            self.meet(me, GROUP)

    def meet_heads(self, me):
        barrier = pltpu.get_barrier_semaphore()

        @pl.when(attends(me))
        def _():
            for owner in OWNERS[:3]:
                pl.semaphore_signal(barrier, inc=1, device_id=self.at(owner), device_id_type=MESH)
            pl.semaphore_wait(barrier, 3)

        for owner in OWNERS[:3]:

            @pl.when(me == owner)
            def _():
                def greet(combo, carry):
                    pl.semaphore_signal(barrier, inc=1, device_id=self.at(device_of(combo)), device_id_type=MESH)
                    return carry

                lax.fori_loop(0, 2 * HEADS, greet, 0)
                pl.semaphore_wait(barrier, 2 * HEADS)

    def shift(self, values, steps):
        far = GROUP * steps
        return self.permute(values, [(i, (i + far) % self.count) for i in range(self.count)])

    def flip(self, values, distance):
        return self.permute(values, [(i, i ^ distance) for i in range(self.count)])


def peer(me, k, size):
    return (me // size) * size + (me % size + k) % size


def flip_x(device):
    return device + 4 - 8 * ((device % GROUP) // 4)


def flip_y(device):
    return device + 1 - 2 * (device % 2)


def flip_core(device):
    return device + 2 - 4 * ((device % 4) // 2)


class Flow:
    def __init__(self, source, target, take, put, goes=None, size=None):
        self.source, self.target, self.take, self.put = source, target, take, put
        self.goes = goes or (lambda i, j: i >= 0)
        self.size = size

    def scratch(self):
        return []

    def semaphores(self):
        return self.size

    def bind(self, net, inputs, outputs, scratch, send, receive, local):
        self.net = net
        self.input, self.output = inputs[self.source], outputs[self.target]
        self.held = scratch
        self.send, self.receive, self.local = send, receive, local

    def copy(self, source, target, index, device):
        return pltpu.make_async_remote_copy(
            source,
            target,
            self.send.at[index],
            self.receive.at[index],
            device_id=self.net.at(device),
            device_id_type=MESH,
        )

    def remote(self, i, j, k):
        return self.copy(self.input.at[self.take(i, j)], self.output.at[self.put(i, j)], k, j)

    def near(self, i):
        return pltpu.make_async_copy(self.input.at[self.take(i, i)], self.output.at[self.put(i, i)], self.local)

    def start(self, me):
        def one(k, carry):
            other = peer(me, k, self.size)

            @pl.when(self.goes(me, other))
            def _():
                self.remote(me, other, k).start()

            return carry

        lax.fori_loop(1, self.size, one, 0)

        @pl.when(self.goes(me, me))
        def _():
            self.near(me).start()

    def middle(self, me):
        pass

    def finish(self, me):
        def one(k, carry):
            other = peer(me, k, self.size)

            @pl.when(self.goes(me, other))
            def _():
                self.remote(me, other, k).wait_send()

            before = peer(me, self.size - k, self.size)

            @pl.when(self.goes(before, me))
            def _():
                self.remote(before, me, k).wait_recv()

            return carry

        lax.fori_loop(1, self.size, one, 0)

        @pl.when(self.goes(me, me))
        def _():
            self.near(me).wait()


class Across(Flow):
    def __init__(self, net, source, target, take, put, goes=None):
        super().__init__(source, target, take, put, goes, net.count)
        self.planes = net.planes

    def semaphores(self):
        return self.planes

    def other(self, me, k):
        return (me + k * GROUP) % self.size

    def start(self, me):
        for k in range(1, self.planes):
            far = self.other(me, k)

            @pl.when(self.goes(me, far))
            def _(k=k, far=far):
                self.remote(me, far, k).start()

        @pl.when(self.goes(me, me))
        def _():
            self.near(me).start()

    def finish(self, me):
        for k in range(1, self.planes):
            far, before = self.other(me, k), self.other(me, self.planes - k)

            @pl.when(self.goes(me, far))
            def _(k=k, far=far):
                self.remote(me, far, k).wait_send()

            @pl.when(self.goes(before, me))
            def _(k=k, before=before):
                self.remote(before, me, k).wait_recv()

        @pl.when(self.goes(me, me))
        def _():
            self.near(me).wait()


class FanAcross(Across):
    def __init__(self, net, source, target, plane, take, put, goes):
        super().__init__(
            net,
            source,
            target,
            take,
            put,
            lambda i, j: jnp.logical_and(goes(i, j), j // GROUP == plane),
        )


class FanIn(Flow):
    def __init__(self, source, target, owner, take, put, goes=None, size=None):
        super().__init__(source, target, take, put, goes, size)
        self.place = owner

    def owner(self, me):
        return (me // self.size) * self.size + self.place

    def sends(self, me):
        return jnp.logical_and(me % self.size != self.place, self.goes(me, self.owner(me)))

    def step(self, me):
        return (self.place - me % self.size + self.size) % self.size

    def start(self, me):
        @pl.when(self.sends(me))
        def _():
            self.remote(me, self.owner(me), self.step(me)).start()

        @pl.when(jnp.logical_and(me % self.size == self.place, self.goes(me, me)))
        def _():
            self.near(me).start()

    def finish(self, me):
        @pl.when(self.sends(me))
        def _():
            self.remote(me, self.owner(me), self.step(me)).wait_send()

        @pl.when(me % self.size == self.place)
        def _():
            def one(k, carry):
                before = peer(me, self.size - k, self.size)

                @pl.when(self.goes(before, me))
                def _():
                    self.remote(before, me, k).wait_recv()

                return carry

            lax.fori_loop(1, self.size, one, 0)

        @pl.when(jnp.logical_and(me % self.size == self.place, self.goes(me, me)))
        def _():
            self.near(me).wait()


class FanOut(Flow):
    def __init__(self, source, target, owner, take, put):
        super().__init__(source, target, take, put)
        self.owner = owner

    def start(self, me):
        @pl.when(me == self.owner)
        def _():
            def one(k, carry):
                self.remote(me, peer(me, k, self.size), k).start()
                return carry

            lax.fori_loop(1, self.size, one, 0)
            self.near(me).start()

    def finish(self, me):
        @pl.when(me == self.owner)
        def _():
            def one(k, carry):
                self.remote(me, peer(me, k, self.size), k).wait_send()
                return carry

            lax.fori_loop(1, self.size, one, 0)
            self.near(me).wait()

        @pl.when(me != self.owner)
        def _():
            self.remote(self.owner, me, (me - self.owner + self.net.count) % self.size).wait_recv()


class PlaneGather(Flow):
    def __init__(self, source, target, put=lambda i: i % GROUP):
        super().__init__(source, target, None, put)

    def semaphores(self):
        return GROUP

    def partners(self, me):
        return [flip_x(me), flip_y(me), flip_x(flip_y(me))]

    def place(self, device):
        return self.output.at[self.put(device)]

    def own(self, me, index, device):
        return self.copy(self.input, self.place(me), index, device)

    def passed(self, me, index, partner):
        return self.copy(self.place(partner), self.place(partner), 4 + index, flip_core(me))

    def start(self, me):
        for index, partner in enumerate(self.partners(me)):
            self.own(me, 1 + index, partner).start()
        self.own(me, 0, flip_core(me)).start()
        pltpu.make_async_copy(self.input, self.place(me), self.local).start()

    def middle(self, me):
        for index, partner in enumerate(self.partners(me)):
            self.own(me, 1 + index, partner).wait_recv()
            self.passed(me, index, partner).start()

    def finish(self, me):
        for index, partner in enumerate(self.partners(me)):
            self.own(me, 1 + index, partner).wait_send()
            self.passed(me, index, partner).wait()
        self.own(me, 0, flip_core(me)).wait()
        pltpu.make_async_copy(self.input, self.place(me), self.local).wait()


class PlaneScatter(Flow):
    def __init__(self, source, target, block, lead=(), runs=None, gathers=False):
        super().__init__(source, target, None, None)
        self.block, self.lead, self.gathers = block, lead, gathers
        self.runs = runs or (lambda i: i >= 0)
        self.every = (slice(None),) * len(lead)

    def scratch(self):
        pair = pltpu.VMEM(self.lead + (2, 2) + self.block, jnp.bfloat16)
        shapes = [pair, pair, pltpu.VMEM((3,) + self.lead + self.block, jnp.bfloat16)]
        if self.gathers:
            shapes += [
                pltpu.VMEM(self.lead + self.block, jnp.bfloat16),
                pltpu.VMEM(self.lead + self.lead + self.block, jnp.bfloat16),
            ]
        return shapes

    def semaphores(self):
        return 5 + (self.lead[0] if self.gathers else 0)

    def onward(self, me, source):
        spare = GROUP * SPARE + me % GROUP
        return self.copy(self.held[3], self.held[4].at[source], 5 + source, spare)

    def partners(self, me):
        return [flip_x(me), flip_y(me), flip_x(flip_y(me))]

    def half(self, core):
        return self.input.at[self.every + (slice(None), core)]

    def first(self, me):
        return self.copy(self.half(1 - (me % 4) // 2), self.held[1], 0, flip_core(me))

    def mine(self, me):
        return pltpu.make_async_copy(self.half((me % 4) // 2), self.held[0], self.local)

    def spot(self, device):
        return self.every + ((device % GROUP) // 4, device % 2)

    def second(self, me, index, partner):
        return self.copy(self.held[0].at[self.spot(partner)], self.held[2].at[index], 1 + index, partner)

    def start(self, me):
        @pl.when(self.runs(me))
        def _():
            self.first(me).start()
            self.mine(me).start()

    def pair(self, device):
        spot = self.spot(device)
        return self.held[0][spot].astype(jnp.float32) + self.held[1][spot].astype(jnp.float32)

    def middle(self, me):
        @pl.when(self.runs(me))
        def _():
            self.mine(me).wait()
            self.first(me).wait_recv()
            for index, partner in enumerate(self.partners(me)):
                self.held[0][self.spot(partner)] = self.pair(partner).astype(jnp.bfloat16)
                self.second(me, index, partner).start()

    def finish(self, me):
        @pl.when(self.runs(me))
        def _():
            total = self.pair(me)
            for index, partner in enumerate(self.partners(me)):
                self.second(me, index, partner).wait_recv()
                total = total + self.held[2][index].astype(jnp.float32)
            if self.gathers:
                plane = me // GROUP
                self.held[3][...] = total.astype(jnp.bfloat16)

                @pl.when(plane != SPARE)
                def _():
                    self.onward(me, plane).start()

            self.output[...] = total
            self.first(me).wait_send()
            for index, partner in enumerate(self.partners(me)):
                self.second(me, index, partner).wait_send()
            if self.gathers:

                @pl.when(plane != SPARE)
                def _():
                    self.onward(me, plane).wait_send()

                @pl.when(plane == SPARE)
                def _():
                    for source in range(self.lead[0]):
                        if source != SPARE:
                            self.onward(me, source).wait_recv()
                            self.output[...] += self.held[4][source].astype(jnp.float32)


def bind_all(net, flows, inputs, outputs, refs):
    for number, flow in enumerate(flows):
        need = len(flow.scratch())
        held, (send, receive), refs = refs[:need], refs[need : need + 2], refs[need + 2 :]
        flow.bind(net, inputs, outputs, held, send, receive, refs[-1].at[number])


def exchange_kernel(net, meet, flows, sources, targets, *refs):
    inputs = refs[:sources]
    outputs = refs[sources : sources + targets]
    me = net.me()
    meet(me)
    bind_all(net, flows, inputs, outputs, refs[sources + targets :])
    for flow in flows:
        flow.start(me)
    for flow in flows:
        flow.middle(me)
    for flow in flows:
        flow.finish(me)


def flow_scratch(flows):
    shapes = []
    for flow in flows:
        shapes += flow.scratch() + [pltpu.SemaphoreType.DMA((flow.semaphores(),))] * 2
    return shapes + [pltpu.SemaphoreType.DMA((len(flows),))]


def exchange(net, name, number, flows, sources, shapes, size=None, meet=None):
    size = size or net.count
    for flow in flows:
        flow.size = flow.size or size
    summed = {flow.target for flow in flows if isinstance(flow, PlaneScatter)}
    moved = sum(math.prod(s.shape) * s.dtype.itemsize for s in shapes)
    return pl.pallas_call(
        functools.partial(
            exchange_kernel, net, meet or (lambda me: net.meet(me, size)), flows, len(sources), len(shapes)
        ),
        out_shape=shapes,
        in_specs=[ANY] * len(sources),
        out_specs=[VMEM if k in summed else ANY for k in range(len(shapes))],
        scratch_shapes=flow_scratch(flows),
        compiler_params=pltpu.CompilerParams(collective_id=number, has_side_effects=True),
        cost_estimate=pl.CostEstimate(flops=0, bytes_accessed=8 * moved, transcendentals=0),
        name=name,
    )(*sources)


def gather_kernel(net, flows, extras, x_ref, w_ref, *refs):
    extra_refs, (all_ref, wall_ref), refs = refs[:extras], refs[extras : extras + 2], refs[extras + 2 :]
    extra_all, (send, receive, wsend, wreceive, local), refs = refs[:extras], refs[extras : extras + 5], refs[extras + 5 :]
    count = net.count
    planes = net.planes
    me = net.me()
    plane = me // GROUP
    place = me % GROUP
    half = place // 4
    spot = place % 4
    across = flip_x(me)
    beside = flip_y(me)
    sibling = flip_core(me)
    net.meet(me, count)
    bind_all(net, flows, extra_refs, extra_all, refs)

    def remote(source, target, index, device):
        return pltpu.make_async_remote_copy(
            source, target, send.at[index], receive.at[index], device_id=net.at(device), device_id_type=MESH
        )

    swap = remote(x_ref.at[1 - half], all_ref.at[plane, half, spot], 0, across)
    swap.start()

    def second(step, which):
        target = (me + step * GROUP) % count
        block = all_ref.at[plane, which, spot]
        return remote(block, block, 1 + (step - 1) * 2 + (which + half) % 2, target)

    def direct(step):
        target = (me + step * GROUP) % count
        return remote(x_ref.at[half], all_ref.at[plane, half, spot], 1 + (step - 1) * 2, target)

    third_base = 1 + 2 * (planes - 1)

    def third(step, which):
        source_plane = (plane + planes - step) % planes
        block = all_ref.at[source_plane, which, spot]
        return remote(block, block, third_base + step * 2 + which, beside)

    fourth_base = third_base + 2 * planes

    def fourth(step, which):
        source_plane = (plane + planes - step) % planes
        block = all_ref.at[source_plane, which, pl.ds((spot // 2) * 2, 2)]
        return remote(block, block, fourth_base + step * 2 + which, sibling)

    for step in range(1, planes):
        direct(step).start()
    mine = pltpu.make_async_copy(x_ref.at[half], all_ref.at[plane, half, spot], local.at[0])
    mine.start()

    def weights(combo):
        target = device_of(combo)
        return pltpu.make_async_remote_copy(
            w_ref.at[combo % HEADS],
            wall_ref.at[me],
            wsend.at[combo],
            wreceive.at[me],
            device_id=net.at(target),
            device_id_type=MESH,
        )

    def send_weights(combo, carry):
        @pl.when(device_of(combo) != me)
        def _():
            weights(combo).start()

        return carry

    mine.wait()
    swap.wait_recv()
    for step in range(1, planes):
        second(step, 1 - half).start()
    for which in range(2):
        third(0, which).start()
    lax.fori_loop(0, 2 * HEADS, send_weights, 0)
    for flow in flows:
        flow.start(me)
    for step in range(planes):
        if step > 0:
            second(step, half).wait_recv()
            second(step, 1 - half).wait_recv()
            for which in range(2):
                third(step, which).start()
            for which in range(2):
                third(step - 1, which).wait_recv()
            for which in range(2):
                fourth(step - 1, which).start()
    for which in range(2):
        third(planes - 1, which).wait_recv()
    for which in range(2):
        fourth(planes - 1, which).start()
    for step in range(planes):
        for which in range(2):
            fourth(step, which).wait_recv()

    @pl.when(attends(me))
    def _():
        own = pltpu.make_async_copy(w_ref.at[combo_of(me) % HEADS], wall_ref.at[me], local.at[1])
        own.start()
        own.wait()

        def took(k, carry):
            before = (me + k) % count
            pltpu.make_async_remote_copy(
                w_ref.at[0],
                wall_ref.at[before],
                wsend.at[0],
                wreceive.at[before],
                device_id=net.at(before),
                device_id_type=MESH,
            ).wait_recv()
            return carry

        lax.fori_loop(1, count, took, 0)

    def sent(combo, carry):
        @pl.when(device_of(combo) != me)
        def _():
            weights(combo).wait_send()

        return carry

    lax.fori_loop(0, 2 * HEADS, sent, 0)
    swap.wait_send()
    for step in range(1, planes):
        direct(step).wait_send()
        second(step, 1 - half).wait_send()
    for step in range(planes):
        for which in range(2):
            third(step, which).wait_send()
            fourth(step, which).wait_send()
    for flow in flows:
        flow.finish(me)


def gather_tokens(net, number, normed, columns, flows, extras, shapes):
    planes = net.planes
    copies = 1 + 2 * (planes - 1) + 4 * planes
    for flow in flows:
        flow.size = flow.size or net.count
    shapes = [
        jax.ShapeDtypeStruct((planes, 2, 4) + normed.shape[1:], normed.dtype),
        jax.ShapeDtypeStruct((net.count,) + columns.shape[1:], columns.dtype),
    ] + shapes
    return pl.pallas_call(
        functools.partial(gather_kernel, net, flows, len(extras)),
        out_shape=shapes,
        in_specs=[ANY] * (2 + len(extras)),
        out_specs=[ANY] * len(shapes),
        scratch_shapes=[
            pltpu.SemaphoreType.DMA((copies,)),
            pltpu.SemaphoreType.DMA((copies,)),
            pltpu.SemaphoreType.DMA((2 * HEADS,)),
            pltpu.SemaphoreType.DMA((net.count,)),
            pltpu.SemaphoreType.DMA((2,)),
        ]
        + flow_scratch(flows),
        compiler_params=pltpu.CompilerParams(collective_id=number, has_side_effects=True),
        cost_estimate=pl.CostEstimate(flops=0, bytes_accessed=100 * 2**20, transcendentals=0),
        name="gather_tokens",
    )(normed, columns, *extras)


def rope_rows(values, cosine, sine):
    first, second = values[:HALF], values[HALF:]
    return jnp.concatenate([first * cosine - second * sine, second * cosine + first * sine], axis=0)


def rope_rows_back(values, cosine, sine):
    first, second = values[:HALF], values[HALF:]
    return jnp.concatenate([first * cosine + second * sine, second * cosine - first * sine], axis=0)


def columns_of(index):
    return pl.ds(pl.multiple_of(index * BLOCK, BLOCK), BLOCK)


def wide_columns(index):
    return pl.ds(pl.multiple_of(index * WIDE, WIDE), WIDE)


def permitted(query_block, key_block, start):
    shape = (BLOCK, WIDE)
    key = key_block * BLOCK + lax.broadcasted_iota(jnp.int32, shape, 0)
    query = query_block * WIDE + lax.broadcasted_iota(jnp.int32, shape, 1)
    return (key <= query) & (key >= start)


def sweep(bounds_ref, query_block, step, carried):
    diagonal = query_block * (WIDE // BLOCK)
    first, whole = bounds_ref[0, query_block], bounds_ref[1, query_block]
    carried = lax.fori_loop(first, whole, functools.partial(step, True), carried)
    carried = lax.fori_loop(whole, diagonal, functools.partial(step, False), carried)
    return lax.fori_loop(diagonal, diagonal + WIDE // BLOCK, functools.partial(step, True), carried)


def fold(rows):
    return jnp.concatenate([rows[:HALF], rows[HALF:]], axis=1)


def unfold(rows):
    return jnp.concatenate([rows[:, :HEAD_DIM], rows[:, HEAD_DIM:]], axis=0)


def attend_kernel(net, *refs):
    @pl.when(attends(net.me()))
    def _():
        attend_body(*refs)


def attend_body(first_ref, x_ref, w_ref, cos_ref, sin_ref, start_ref, qkv_ref, mixed_ref, total_ref, packed_ref, key_rows):
    blocks = qkv_ref.shape[1] // BLOCK
    weights = w_ref[...]

    def project(chunk, carry):
        tokens = x_ref[chunk // 2, chunk % 2].reshape(BLOCK, D)
        here = columns_of(chunk)
        made = nt(weights, tokens)
        cosine, sine = cos_ref[:, here], sin_ref[:, here]
        query = rope_rows(made[:HEAD_DIM], cosine, sine)
        key = rope_rows(made[HEAD_DIM : 2 * HEAD_DIM], cosine, sine)
        qkv_ref[:HEAD_DIM, here] = query.astype(jnp.bfloat16) * SCALE
        qkv_ref[HEAD_DIM : 2 * HEAD_DIM, here] = key.astype(jnp.bfloat16)
        qkv_ref[2 * HEAD_DIM :, here] = made[2 * HEAD_DIM :].astype(jnp.bfloat16)
        key_rows[here, :] = key.T.astype(jnp.bfloat16)
        return carry

    lax.fori_loop(0, blocks, project, 0)

    def query_step(query_block, carry):
        here = wide_columns(query_block)
        query = qkv_ref[:HEAD_DIM, here]
        start = start_ref[:, here]

        def key_step(masked, key_block, held):
            top, total, mixed = held
            there = columns_of(key_block)
            scores = nn(key_rows[there, :], query)
            if masked:
                allowed = permitted(query_block, key_block, start)
                scores = jnp.where(allowed, scores, NEGATIVE)
            new_top = jnp.maximum(top, jnp.max(scores, axis=0, keepdims=True))
            weights = jnp.exp(scores - new_top)
            if masked:
                weights = jnp.where(allowed, weights, 0.0)
            factor = jnp.exp(top - new_top)
            total = total * factor + jnp.sum(weights, axis=0, keepdims=True)
            mixed = mixed * factor + nn(qkv_ref[2 * HEAD_DIM :, there], weights.astype(jnp.bfloat16))
            return new_top, total, mixed

        top, total, mixed = sweep(
            first_ref,
            query_block,
            key_step,
            (
                jnp.full((1, WIDE), NEGATIVE, jnp.float32),
                jnp.zeros((1, WIDE), jnp.float32),
                jnp.zeros((HEAD_DIM, WIDE), jnp.float32),
            ),
        )
        mixed = mixed / total
        mixed_ref[:, here] = mixed
        total_ref[:, here] = top + jnp.log(total)
        rows = mixed.T
        for part in range(WIDE // 64):
            packed_ref[query_block * (WIDE // 64) + part] = fold(rows[part * 64 : part * 64 + 64]).astype(
                jnp.bfloat16
            )
        return carry

    lax.fori_loop(0, qkv_ref.shape[1] // WIDE, query_step, 0)


def attend(net, first, tokens, weights, cosine, sine, start):
    length = start.shape[1]
    return pl.pallas_call(
        functools.partial(attend_kernel, net),
        out_shape=[
            jax.ShapeDtypeStruct((3 * HEAD_DIM, length), jnp.bfloat16),
            jax.ShapeDtypeStruct((HEAD_DIM, length), jnp.float32),
            jax.ShapeDtypeStruct((1, length), jnp.float32),
            jax.ShapeDtypeStruct((net.count, HALF, 128), jnp.bfloat16),
        ],
        in_specs=[SMEM] + [VMEM] * 5,
        out_specs=[VMEM] * 4,
        scratch_shapes=[pltpu.VMEM((length, HEAD_DIM), jnp.bfloat16)],
        cost_estimate=pl.CostEstimate(flops=2 * 10**9, bytes_accessed=8 * 2**20, transcendentals=2 * 10**6),
        name="attend",
    )(first, tokens, weights, cosine, sine, start)


def attend_back_kernel(net, *refs):
    @pl.when(attends(net.me()))
    def _():
        attend_back_body(*refs)


def attend_back_body(
    first_ref,
    x_ref,
    qkv_ref,
    mixed_ref,
    total_ref,
    cos_ref,
    sin_ref,
    start_ref,
    grad_ref,
    packed_ref,
    weight_ref,
    query_rows,
    key_rows,
    value_rows,
    grad_rows,
    grad_columns,
    correction,
    key_grad,
    value_grad,
    all_grad,
):
    blocks = qkv_ref.shape[1] // BLOCK
    parts = BLOCK // 64

    def prepare(chunk, carry):
        here = columns_of(chunk)
        turned = qkv_ref[:, here].astype(jnp.float32)
        query_rows[here, :] = turned[:HEAD_DIM].T.astype(jnp.bfloat16)
        key_rows[here, :] = turned[HEAD_DIM : 2 * HEAD_DIM].T.astype(jnp.bfloat16)
        value_rows[here, :] = turned[2 * HEAD_DIM :].T.astype(jnp.bfloat16)
        pieces = [unfold(grad_ref[chunk * parts + part].astype(jnp.float32)) for part in range(parts)]
        rows = jnp.concatenate(pieces, axis=0)
        grad_rows[here, :] = rows.astype(jnp.bfloat16)
        across = rows.T
        grad_columns[:, here] = across.astype(jnp.bfloat16)
        correction[:, here] = jnp.sum(across * mixed_ref[:, here], axis=0, keepdims=True)
        key_grad[here, :] = jnp.zeros((BLOCK, HEAD_DIM), jnp.float32)
        value_grad[here, :] = jnp.zeros((BLOCK, HEAD_DIM), jnp.float32)
        return carry

    lax.fori_loop(0, blocks, prepare, 0)

    wide_parts = WIDE // 64

    def query_step(query_block, carry):
        here = wide_columns(query_block)
        query = qkv_ref[:HEAD_DIM, here]
        start = start_ref[:, here]
        total = total_ref[:, here]
        fix = correction[:, here]
        grad = grad_columns[:, here]
        query_in_rows = query_rows[here, :]
        grad_in_rows = grad_rows[here, :]

        def key_step(masked, key_block, query_grad):
            there = columns_of(key_block)
            scores = nn(key_rows[there, :], query)
            weights = jnp.exp(scores - total)
            if masked:
                weights = jnp.where(permitted(query_block, key_block, start), weights, 0.0)
            value_grad[there, :] += nn(weights.astype(jnp.bfloat16), grad_in_rows)
            slope = nn(value_rows[there, :], grad)
            change = (weights * (slope - fix)).astype(jnp.bfloat16)
            key_grad[there, :] += nn(change, query_in_rows)
            return query_grad + nn(qkv_ref[HEAD_DIM : 2 * HEAD_DIM, there], change)

        query_grad = sweep(first_ref, query_block, key_step, jnp.zeros((HEAD_DIM, WIDE), jnp.float32))
        query_grad = rope_rows_back(query_grad * SCALE, cos_ref[:, here], sin_ref[:, here])
        all_grad[:HEAD_DIM, here] = query_grad.astype(jnp.bfloat16)
        rows = query_grad.T.astype(jnp.bfloat16)
        for part in range(wide_parts):
            packed_ref[query_block * wide_parts + part, :64, :HEAD_DIM] = rows[part * 64 : part * 64 + 64]
        return carry

    lax.fori_loop(0, qkv_ref.shape[1] // WIDE, query_step, 0)
    weight_ref[...] = jnp.zeros(weight_ref.shape, jnp.float32)

    def close(chunk, carry):
        here = columns_of(chunk)
        key = rope_rows_back(key_grad[here, :].T, cos_ref[:, here], sin_ref[:, here])
        value = value_grad[here, :]
        all_grad[HEAD_DIM : 2 * HEAD_DIM, here] = key.astype(jnp.bfloat16)
        all_grad[2 * HEAD_DIM :, here] = value.T.astype(jnp.bfloat16)
        rows = key.T.astype(jnp.bfloat16)
        for part in range(parts):
            token = chunk * parts + part
            packed_ref[token, :64, HEAD_DIM:] = rows[part * 64 : part * 64 + 64]
            packed_ref[token, 64:, :] = fold(value[part * 64 : part * 64 + 64]).astype(jnp.bfloat16)
        tokens = x_ref[chunk // 2, chunk % 2].reshape(BLOCK, D)
        weight_ref[...] += nn(all_grad[:, here], tokens)
        return carry

    lax.fori_loop(0, blocks, close, 0)


def attend_back(net, first, tokens, qkv, mixed, total, cosine, sine, start, grad):
    length = start.shape[1]
    rows = pltpu.VMEM((length, HEAD_DIM), jnp.bfloat16)
    sums = pltpu.VMEM((length, HEAD_DIM), jnp.float32)
    return pl.pallas_call(
        functools.partial(attend_back_kernel, net),
        out_shape=[
            jax.ShapeDtypeStruct((net.count, 96, 128), jnp.bfloat16),
            jax.ShapeDtypeStruct((3 * HEAD_DIM, D), jnp.float32),
        ],
        in_specs=[SMEM] + [VMEM] * 8,
        out_specs=[VMEM] * 2,
        scratch_shapes=[
            rows,
            rows,
            rows,
            rows,
            pltpu.VMEM((HEAD_DIM, length), jnp.bfloat16),
            pltpu.VMEM((1, length), jnp.float32),
            sums,
            sums,
            pltpu.VMEM((3 * HEAD_DIM, length), jnp.bfloat16),
        ],
        cost_estimate=pl.CostEstimate(flops=4 * 10**9, bytes_accessed=12 * 2**20, transcendentals=2 * 10**6),
        name="attend_back",
    )(first, tokens, qkv, mixed, total, cosine, sine, start, grad)


def tn(a, b):
    return lax.dot_general(a, b, (((0,), (0,)), ((), ())), preferred_element_type=jnp.float32)


def mean_of(values):
    return jnp.mean(values, axis=-1, keepdims=True)


def layer_norm(values):
    center = values - mean_of(values)
    return center * lax.rsqrt(mean_of(center * center) + EPSILON)


def norm_back(values, gradient):
    center = values - mean_of(values)
    inverse = lax.rsqrt(mean_of(center * center) + EPSILON)
    normed = center * inverse
    return inverse * (gradient - mean_of(gradient) - normed * mean_of(gradient * normed))


def after_kernel(parts_ref, tokens_ref, out_ref, mixed_ref, middle_ref, second_ref):
    for micro in range(2):
        here = slice(64 * micro, 64 * micro + 64)
        for pair in range(HEADS // 2):
            two = [unfold(parts_ref[micro * HEADS + 2 * pair + k].astype(jnp.float32)) for k in range(2)]
            mixed_ref[here, 128 * pair : 128 * pair + 128] = jnp.concatenate(two, axis=1).astype(jnp.bfloat16)
    middle = tokens_ref[...].astype(jnp.float32) + nn(mixed_ref[...], out_ref[...])
    middle_ref[...] = middle
    second_ref[...] = layer_norm(middle).astype(jnp.bfloat16)


def after_attention(parts, tokens, out):
    shape = tokens.shape
    return pl.pallas_call(
        after_kernel,
        out_shape=[
            jax.ShapeDtypeStruct(shape, jnp.bfloat16),
            jax.ShapeDtypeStruct(shape, jnp.float32),
            jax.ShapeDtypeStruct(shape, jnp.bfloat16),
        ],
        in_specs=[VMEM] * 3,
        out_specs=[VMEM] * 3,
        cost_estimate=pl.CostEstimate(flops=2 * 10**8, bytes_accessed=3 * 2**20, transcendentals=0),
        name="after_attention",
    )(parts, tokens, out)


def feed_forward_kernel(net, *refs):
    planes = net.planes
    second_ref, cotangent_ref = refs[:2]
    blocks = refs[2 : 2 + planes]
    second_terms, result_terms = refs[2 + planes : 4 + planes]
    terms = refs[4 + planes : 4 + 2 * planes]
    weights, slopes, products, sums = refs[4 + 2 * planes :]
    plane = net.me() // GROUP
    span = D // planes
    part = FF // GROUP
    for step, block in enumerate(blocks):
        source = (plane + planes - step) % planes
        weights[pl.ds(pl.multiple_of(source * span, span), span), :] = block[:, :D]

    def forward(chunk, carry):
        here = columns_of(chunk)
        second, cotangent = second_ref[here, :], cotangent_ref[here, :]
        both = nn(second, weights[:, : 2 * part])
        gate, up = both[:, :part], both[:, part:]
        sigmoid = jax.nn.sigmoid(gate)
        silu = gate * sigmoid
        product = (silu * up).astype(jnp.bfloat16)
        change = nn(cotangent, weights[:, 2 * part :])
        slopes[here, :part] = (change * up * sigmoid * (1.0 + gate * (1.0 - sigmoid))).astype(jnp.bfloat16)
        slopes[here, part:] = (change * silu).astype(jnp.bfloat16)
        products[here, :] = product
        second_terms[here, :] = nt(slopes[here, :], weights[:, : 2 * part]).astype(jnp.bfloat16)
        result_terms[here, :] = nt(product, weights[:, 2 * part :]).astype(jnp.bfloat16)
        return carry

    lax.fori_loop(0, second_ref.shape[0] // BLOCK, forward, 0)
    for begin in range(0, D, BLOCK):
        here = slice(begin, begin + BLOCK)
        sums[here, : 2 * part] = tn(second_ref[:, here], slopes[...]).astype(jnp.bfloat16)
        sums[here, 2 * part :] = tn(cotangent_ref[:, here], products[...]).astype(jnp.bfloat16)
    for step, term in enumerate(terms):
        target = (plane + step) % planes
        term[...] = sums[pl.ds(pl.multiple_of(target * span, span), span), :]


def feed_forward(net, second, cotangent, blocks):
    tokens = second.shape[0]
    part = FF // GROUP
    low = jnp.bfloat16
    return pl.pallas_call(
        functools.partial(feed_forward_kernel, net),
        out_shape=[jax.ShapeDtypeStruct((tokens, D), low)] * 2
        + [jax.ShapeDtypeStruct((D // net.planes, 3 * part), low)] * net.planes,
        in_specs=[VMEM] * (2 + net.planes),
        out_specs=[VMEM] * (2 + net.planes),
        scratch_shapes=[
            pltpu.VMEM((D, 3 * part), low),
            pltpu.VMEM((tokens, 2 * part), low),
            pltpu.VMEM((tokens, part), low),
            pltpu.VMEM((D, 3 * part), low),
        ],
        cost_estimate=pl.CostEstimate(flops=35 * 10**8, bytes_accessed=10 * 2**20, transcendentals=10**6),
        name="feed_forward",
    )(second, cotangent, *blocks)


def before_kernel(second_grad_ref, middle_ref, cotangent_ref, mixed_ref, out_ref, middle_grad_ref, folded_ref, terms_ref):
    middle_grad = cotangent_ref[...].astype(jnp.float32) + norm_back(middle_ref[...], second_grad_ref[...])
    middle_grad_ref[...] = middle_grad
    low = middle_grad.astype(jnp.bfloat16)
    mixed_grad = nt(low, out_ref[...])
    for micro in range(2):
        rows = mixed_grad[64 * micro : 64 * micro + 64]
        for head in range(HEADS):
            folded_ref[micro * HEADS + head] = fold(rows[:, HEAD_DIM * head : HEAD_DIM * head + HEAD_DIM]).astype(
                jnp.bfloat16
            )
    terms_ref[...] = tn(mixed_ref[...], low).astype(jnp.bfloat16)


def before_attention(second_grad, middle, cotangent, mixed, out):
    return pl.pallas_call(
        before_kernel,
        out_shape=[
            jax.ShapeDtypeStruct(middle.shape, jnp.float32),
            jax.ShapeDtypeStruct((2 * HEADS, HALF, 128), jnp.bfloat16),
            jax.ShapeDtypeStruct((D, D), jnp.bfloat16),
        ],
        in_specs=[VMEM] * 5,
        out_specs=[VMEM] * 3,
        cost_estimate=pl.CostEstimate(flops=4 * 10**8, bytes_accessed=5 * 2**20, transcendentals=0),
        name="before_attention",
    )(second_grad, middle, cotangent, mixed, out)


def input_kernel(net, slots, grads_ref, *refs):
    blocks, partial_ref, weights = refs[: net.planes], refs[net.planes], refs[net.planes + 1]
    me = net.me()
    plane = me // GROUP
    span = D // net.planes

    @pl.when(attends(me))
    def _():
        for step, block in enumerate(blocks):
            source = (plane + net.planes - step) % net.planes
            weights[pl.ds(pl.multiple_of(source * span, span), span), :] = block[:, D:]

        def one(slot, carry):
            total = jnp.zeros((GROUP * 64, D), jnp.float32)
            for group in range(3):
                rows = []
                for token in range(GROUP):
                    given = grads_ref[slot, group, token]
                    value = unfold(given[64:].astype(jnp.float32)).astype(jnp.bfloat16)
                    rows.append(jnp.concatenate([given[:64], value], axis=1))
                taken = jnp.concatenate(rows, axis=0)
                total = total + nt(taken, weights[:, 192 * group : 192 * group + 192])
            partial_ref[slot] = total.reshape(GROUP, 64, D).astype(jnp.bfloat16)
            return carry

        lax.fori_loop(0, jnp.where(plane == HOST, slots, 1), one, 0)


def input_partial(net, grads, blocks):
    slots = grads.shape[0]
    return pl.pallas_call(
        functools.partial(input_kernel, net, slots),
        out_shape=jax.ShapeDtypeStruct((slots, GROUP, 64, D), jnp.bfloat16),
        in_specs=[VMEM] * (1 + len(blocks)),
        out_specs=VMEM,
        scratch_shapes=[pltpu.VMEM((D, blocks[0].shape[1] - D), jnp.bfloat16)],
        cost_estimate=pl.CostEstimate(flops=10**9, bytes_accessed=6 * 2**20, transcendentals=0),
        name="input_partial",
    )(grads, *blocks)


def solve_heads(me, head_ref, moment_ref, target, scratch):
    wide, semaphore, parts, moment = scratch[0], scratch[3], scratch[4], scratch[5]

    @pl.when(jnp.logical_or(me == OWNERS[0], jnp.logical_or(me == OWNERS[1], me == OWNERS[2])))
    def _():
        move(head_ref, parts, semaphore)
        move(moment_ref, moment, semaphore)

        def join(pair, carry):
            first = parts[2 * pair].astype(jnp.float32) + parts[HEADS + 2 * pair].astype(jnp.float32)
            second = parts[2 * pair + 1].astype(jnp.float32) + parts[HEADS + 2 * pair + 1].astype(jnp.float32)
            here = pl.ds(pl.multiple_of(pair * 128, 128), 128)
            gradient = jnp.concatenate([first, second], axis=0).T
            wide[:, here] = (0.75 * gradient + 0.25 * moment[:, here].astype(jnp.float32)).astype(jnp.bfloat16)
            return carry

        lax.fori_loop(0, HEADS // 2, join, 0)
        solve(D, target, scratch)


def solve_late(me, out_ref, ffn_ref, out_target, ffn_target, scratch):
    wide, semaphore = scratch[0], scratch[3]

    @pl.when(me == OWNERS[3])
    def _():
        move(out_ref, wide.at[:, pl.ds(0, D)], semaphore)
        solve(D, out_target, scratch)

    @pl.when(jnp.logical_or(me == OWNERS[4], jnp.logical_or(me == OWNERS[5], me == OWNERS[6])))
    def _():
        move(ffn_ref, wide, semaphore)
        solve(FF, ffn_target, scratch)


def move(source, target, semaphore):
    copy = pltpu.make_async_copy(source, target, semaphore)
    copy.start()
    copy.wait()


def solve(span, target, scratch):
    wide, gram, polynomial, semaphore = scratch[:4]

    def blocks_of(index):
        return pl.ds(pl.multiple_of(index * BLOCK, BLOCK), BLOCK)

    def mirror(target, i, j, block):
        target[i * BLOCK : (i + 1) * BLOCK, j * BLOCK : (j + 1) * BLOCK] = block.astype(jnp.bfloat16)
        if i != j:
            target[j * BLOCK : (j + 1) * BLOCK, i * BLOCK : (i + 1) * BLOCK] = block.T.astype(jnp.bfloat16)

    chunks = span // BLOCK

    def measure(index, total):
        values = wide[:, blocks_of(index)].astype(jnp.float32)
        return total + jnp.sum(values * values, axis=0, keepdims=True)

    total = lax.fori_loop(0, chunks, measure, jnp.zeros((1, BLOCK), jnp.float32))
    frobenius = jnp.sqrt(jnp.sum(total, axis=1, keepdims=True)) + 1e-07

    def scale(index, carry):
        here = blocks_of(index)
        wide[:, here] = (wide[:, here].astype(jnp.float32) / frobenius).astype(jnp.bfloat16)
        return carry

    lax.fori_loop(0, chunks, scale, 0)

    def step(_, carry):
        for i in range(D // BLOCK):
            for j in range(i + 1):
                mirror(
                    gram,
                    i,
                    j,
                    nt(
                        wide[i * BLOCK : (i + 1) * BLOCK, :span],
                        wide[j * BLOCK : (j + 1) * BLOCK, :span],
                    ),
                )
        for i in range(D // BLOCK):
            for j in range(i + 1):
                square = nn(gram[i * BLOCK : (i + 1) * BLOCK, :], gram[:, j * BLOCK : (j + 1) * BLOCK])
                linear = gram[i * BLOCK : (i + 1) * BLOCK, j * BLOCK : (j + 1) * BLOCK].astype(jnp.float32)
                mirror(polynomial, i, j, COEFF_B * linear + COEFF_C * square)

        def advance(index, inner):
            here = blocks_of(index)
            old = wide[:, here]
            wide[:, here] = (COEFF_A * old.astype(jnp.float32) + nn(polynomial[...], old)).astype(jnp.bfloat16)
            return inner

        lax.fori_loop(0, chunks, advance, 0)
        return carry

    lax.fori_loop(0, NS_STEPS, step, 0)
    move(wide.at[:, pl.ds(0, span)], target, semaphore)


def solve_scratch(span, heads):
    square = pltpu.VMEM((D, D), jnp.bfloat16)
    shapes = [pltpu.VMEM((D, span), jnp.bfloat16), square, square, pltpu.SemaphoreType.DMA]
    if heads:
        shapes += [pltpu.VMEM((2 * HEADS, HEAD_DIM, D), jnp.bfloat16), square]
    return shapes


SQUARE = jax.ShapeDtypeStruct((D, D), jnp.bfloat16)
SOLVE_COST = pl.CostEstimate(flops=25 * 10**9, bytes_accessed=8 * 2**20, transcendentals=0)


def newton_kernel(net, head_ref, moment_ref, out_ref, ffn_ref, attn_target, ffn_target, *scratch):
    me = net.me()
    solve_heads(me, head_ref, moment_ref, attn_target, scratch)
    solve_late(me, out_ref, ffn_ref, attn_target, ffn_target, scratch)


def newton(net, *sources):
    return pl.pallas_call(
        functools.partial(newton_kernel, net),
        out_shape=[SQUARE, jax.ShapeDtypeStruct((D, FF), jnp.bfloat16)],
        in_specs=[ANY] * 4,
        out_specs=[ANY] * 2,
        scratch_shapes=solve_scratch(FF, True),
        cost_estimate=SOLVE_COST,
        name="newton",
    )(*sources)


def on_device(net, tokens, doc_ids, cotangent, attn_weight, ffn_weight, attn_moment, ffn_moment):
    micro_count, token_count, width = tokens.shape
    rows = attn_weight.shape[1]
    count, planes = net.count, net.planes
    length = count * token_count
    me = net.me()
    plane, place = me // GROUP, me % GROUP
    x_bit = place // 4
    both = micro_count * token_count
    part = FF // GROUP
    low = jnp.bfloat16
    everything = (slice(None),)

    attn_low = attn_weight.astype(low)
    ffn_low = ffn_weight.astype(low)

    def cut_up(values):
        return values.reshape(3, rows, GROUP, part).transpose(2, 1, 0, 3).reshape(GROUP, rows, 3 * part)

    cut = cut_up(ffn_low)
    out_grad = cotangent.reshape(both, width)
    hidden = tokens.astype(jnp.float32).reshape(both, width)
    normed = layer_norm(hidden).astype(low)
    counts = jnp.sum((doc_ids[:, :, None] == jnp.arange(DOCS)[None, None, :]).astype(jnp.float32), axis=1)
    tail = jnp.pad(counts.reshape(-1).astype(low), (0, HEAD_DIM - micro_count * DOCS))
    columns = attn_low[:3].reshape(3, rows, HEADS, HEAD_DIM).transpose(2, 1, 0, 3).reshape(HEADS, rows, 3 * HEAD_DIM)
    shares = columns.reshape(3, 4, rows, 3 * HEAD_DIM).transpose(1, 2, 0, 3).reshape(4, rows, 9 * HEAD_DIM)
    shares = jnp.pad(shares, ((0, 0), (0, 0), (0, HEAD_DIM)))
    columns = jnp.concatenate([columns, jnp.broadcast_to(tail, (HEADS, rows, HEAD_DIM))], axis=2)
    moment_low = attn_moment.astype(low)
    all_tokens, all_columns, plane_cut, plane_out, moment_plane, moment_out, plane_shares = gather_tokens(
        net,
        0,
        normed.reshape(micro_count, token_count, width),
        columns,
        [
            Flow(0, 0, lambda i, j: j % GROUP, lambda i, j: i % GROUP, size=GROUP),
            Across(net, 1, 1, lambda i, j: 0, lambda i, j: i // GROUP),
            Across(net, 3, 3, lambda i, j: 0, lambda i, j: i // GROUP, lambda i, j: j // GROUP == SPARE),
        ]
        + [
            Flow(2, 2, lambda i, j: j % GROUP, lambda i, j: i % GROUP, size=GROUP),
            Flow(4, 4, lambda i, j: j % 4, lambda i, j: i % GROUP, size=GROUP),
        ],
        [cut, attn_low[3:], cut_up(ffn_moment.astype(low)), moment_low[3:], shares],
        [
            jax.ShapeDtypeStruct(cut.shape, low),
            jax.ShapeDtypeStruct((planes, rows, D), low),
            jax.ShapeDtypeStruct(cut.shape, low),
            jax.ShapeDtypeStruct((planes, rows, D), low),
            jax.ShapeDtypeStruct((GROUP,) + shares.shape[1:], low),
        ],
    )
    late_own = jnp.concatenate([plane_cut, plane_shares], axis=2).reshape(GROUP * rows, -1)
    late_blocks = [late_own] + [net.shift(late_own, step) for step in range(1, planes)]

    head_weights = all_columns[:, :, : 3 * HEAD_DIM].reshape(D, 3 * HEAD_DIM).T
    every_count = jnp.sum(all_columns[:, 0, 3 * HEAD_DIM :].astype(jnp.float32), axis=0)
    own_count = lax.dynamic_slice_in_dim(every_count, x_bit * DOCS, DOCS, 0)
    starts = jnp.cumsum(own_count) - own_count
    index = jnp.arange(length).astype(jnp.float32)
    start = jnp.max(jnp.where(starts[:, None] <= index[None, :], starts[:, None], 0.0), axis=0)
    inverse = 10000.0 ** (-(jnp.arange(HALF, dtype=jnp.float32) * 2.0) / HEAD_DIM)
    angles = inverse[:, None] * (index - start)[None, :]
    cosine, sine = jnp.cos(angles), jnp.sin(angles)
    start = start.astype(jnp.int32)
    diagonal = jnp.arange(length // WIDE, dtype=jnp.int32) * (WIDE // BLOCK)
    first = jnp.clip(start[::WIDE] // BLOCK, 0, diagonal)
    first = jnp.stack([first, jnp.clip((start[WIDE - 1 :: WIDE] + BLOCK - 1) // BLOCK, first, diagonal)])
    start = start[None, :]

    qkv, mixed, total, packed = attend(net, first, all_tokens, head_weights, cosine, sine, start)
    mixed_parts, moment_whole, plane_out_grad, out_full = exchange(
        net,
        "mixed_exchange",
        1,
        [PlaneGather(2, 2), PlaneGather(3, 3, lambda i: everything + (i % GROUP,))]
        + [Flow(0, 0, lambda i, j: j, lambda i, j: combo_of(i), lambda i, j: attends(i))]
        + [FanIn(1, 1, OWNERS[k], lambda i, j, k=k: k, lambda i, j: i) for k in range(3)],
        [packed, moment_low, out_grad, plane_out],
        [
            jax.ShapeDtypeStruct((2 * HEADS, HALF, 128), low),
            jax.ShapeDtypeStruct((count, rows, D), low),
            jax.ShapeDtypeStruct((GROUP, both, width), low),
            jax.ShapeDtypeStruct((planes, GROUP, rows, D), low),
        ],
    )
    plane_out_grad = plane_out_grad.reshape(GROUP * both, width)
    out_full = out_full.reshape(D, D)
    own_tokens = tokens.reshape(both, width)
    mixed_tokens, middle, second = after_attention(mixed_parts, own_tokens, out_full)
    (plane_second,) = exchange(
        net,
        "second_exchange",
        10,
        [PlaneGather(0, 0)],
        [second],
        [jax.ShapeDtypeStruct((GROUP, both, width), low)],
        GROUP,
    )
    plane_second = plane_second.reshape(GROUP * both, width)
    second_terms, result_terms, *ffn_terms = feed_forward(net, plane_second, plane_out_grad, late_blocks)
    sides = (2, 2, 2, both, width)
    (second_grad,) = exchange(
        net,
        "second_grad_exchange",
        11,
        [PlaneScatter(0, 0, (both, width))],
        [second_terms.reshape(sides)],
        [jax.ShapeDtypeStruct((both, width), jnp.float32)],
        GROUP,
    )
    ffn_block = ffn_terms[0].astype(jnp.float32)
    for step in range(1, planes):
        ffn_block = ffn_block + net.shift(ffn_terms[step], step).astype(jnp.float32)
    ffn_update = 0.75 * ffn_block + 0.25 * moment_plane.reshape(GROUP * rows, 3 * part).astype(jnp.float32)
    ffn_update, ffn_block = ffn_update.astype(low), ffn_block.astype(low)
    middle_grad, folded, out_terms = before_attention(second_grad, middle, out_grad, mixed_tokens, out_full)
    grad_parts, out_total, ffn_whole = exchange(
        net,
        "mixed_grad_exchange",
        2,
        [
            PlaneScatter(1, 1, (rows, D), (planes,), gathers=True),
            Flow(0, 0, lambda i, j: combo_of(j), lambda i, j: i, lambda i, j: attends(j)),
        ]
        + [
            FanIn(
                2,
                2,
                OWNERS[4 + k],
                lambda i, j, k=k: (slice(None), pl.ds(part * k, part)),
                lambda i, j: (i // GROUP, slice(None), pl.ds(pl.multiple_of(part * (i % GROUP), part), part)),
            )
            for k in range(3)
        ],
        [folded, out_terms.reshape(planes, 2, 2, 2, rows, D), ffn_update],
        [
            jax.ShapeDtypeStruct((count, HALF, 128), low),
            jax.ShapeDtypeStruct((planes, rows, D), jnp.float32),
            jax.ShapeDtypeStruct((planes, GROUP * rows, FF), low),
        ],
    )
    out_update = (0.75 * out_total + 0.25 * moment_out.astype(jnp.float32)).astype(low)

    grad_packed, head_grad = attend_back(
        net, first, all_tokens, qkv, mixed, total, cosine, sine, start, grad_parts
    )
    head_low = head_grad.astype(low)
    out_update, grad_packed, head_low = lax.optimization_barrier((out_update, grad_packed, head_low))
    (out_whole,) = exchange(
        net,
        "out_exchange",
        4,
        [
            FanIn(
                0,
                0,
                OWNERS[3] % GROUP,
                lambda i, j: everything,
                lambda i, j: everything + (i % GROUP,),
                lambda i, j: j == OWNERS[3],
            )
        ],
        [out_update],
        [jax.ShapeDtypeStruct((planes, GROUP, rows, D), low)],
        GROUP,
    )
    out_whole, grad_packed, head_low = lax.optimization_barrier((out_whole, grad_packed, head_low))
    (head_whole,) = exchange(
        net,
        "head_exchange",
        9,
        [
            FanIn(0, 0, OWNERS[k], lambda i, j, k=k: k, lambda i, j: combo_of(i), lambda i, j: attends(i))
            for k in range(3)
        ],
        [head_low.reshape(3, HEAD_DIM, D)],
        [jax.ShapeDtypeStruct((2 * HEADS, HEAD_DIM, D), low)],
        meet=net.meet_heads,
    )
    grad_packed, head_low, head_whole = lax.optimization_barrier((grad_packed, head_low, head_whole))
    guests = [p for p in range(planes) if p >= 4 or p == SPARE]
    slots = 1 + len(guests)
    head_rows = jnp.pad(head_low.T.reshape(count, rows, 3 * HEAD_DIM), ((0, 0), (0, 0), (0, 64)))

    def group_of(device):
        return device // GROUP - (device // GROUP) // 3

    def waits(device):
        return jnp.logical_not(attends(device))

    def head_flow(runs):
        return Flow(
            0, 0, lambda i, j: j, lambda i, j: combo_of(i), lambda i, j: jnp.logical_and(attends(i), runs(j))
        )

    row_shape = jax.ShapeDtypeStruct((2 * HEADS, rows, 256), low)
    early_rows, host_grads = exchange(
        net,
        "attending_exchange",
        7,
        [
            Across(
                net,
                1,
                1,
                lambda i, j: j // GROUP,
                lambda i, j: (0, group_of(i)),
                lambda i, j: jnp.logical_and(attends(i), attends(j)),
            )
        ]
        + [
            FanAcross(
                net, 1, 1, HOST, lambda i, j, p=p: p, lambda i, j, k=k: (1 + k, group_of(i)), lambda i, j: attends(i)
            )
            for k, p in enumerate(guests)
        ]
        + [head_flow(attends)],
        [head_rows, grad_packed.reshape(planes, GROUP, 96, 128)],
        [row_shape, jax.ShapeDtypeStruct((slots, 3, GROUP, 96, 128), low)],
        meet=net.meet_attending,
    )
    partial = input_partial(net, host_grads, late_blocks)
    attn_done, ffn_done = newton(
        net, head_whole, moment_whole.reshape(D, D), out_whole.reshape(D, D), ffn_whole.reshape(D, FF)
    )
    attn_done, ffn_done, partial, early_rows = lax.optimization_barrier((attn_done, ffn_done, partial, early_rows))

    def guest_index(device):
        p = device // GROUP
        return p - SPARE - jnp.minimum(p // 4, 1)

    late_rows, ffn_parts, attn_step, ffn_step, out_row_grad, input_parts, result = exchange(
        net,
        "step_exchange",
        5,
        [PlaneScatter(6, 6, (both, width))]
        + [FanOut(3, 3, OWNERS[4 + k], lambda i, j: j, lambda i, j, k=k: k) for k in range(3)]
        + [FanOut(2, 2, OWNERS[k], lambda i, j: j, lambda i, j, k=k: k) for k in range(4)]
        + [
            Flow(
                5,
                5,
                lambda i, j: (1 + guest_index(j), j % GROUP),
                lambda i, j: i % GROUP,
                lambda i, j: jnp.logical_and(i // GROUP == HOST, waits(j)),
            ),
            Flow(5, 5, lambda i, j: (0, j % GROUP), lambda i, j: i % GROUP, lambda i, j: attends(i), size=GROUP),
            Flow(1, 1, lambda i, j: j % GROUP, lambda i, j: i % GROUP, size=GROUP),
            Across(net, 4, 4, lambda i, j: j // GROUP, lambda i, j: 0, lambda i, j: i // GROUP == SPARE),
            head_flow(waits),
        ],
        [
            head_rows,
            ffn_block.reshape(GROUP, rows, 3 * part),
            attn_done.reshape(count, rows, D),
            ffn_done.reshape(count, rows, FF),
            out_total.astype(low),
            partial,
            result_terms.reshape(sides),
        ],
        [
            row_shape,
            jax.ShapeDtypeStruct((GROUP, rows, 3 * part), low),
            jax.ShapeDtypeStruct((4, rows, D), low),
            jax.ShapeDtypeStruct((3, rows, FF), low),
            jax.ShapeDtypeStruct((1, rows, D), low),
            jax.ShapeDtypeStruct((GROUP, token_count, width), low),
            jax.ShapeDtypeStruct((both, width), jnp.float32),
        ],
    )
    row_parts = jnp.where(attends(me), early_rows, late_rows)
    normed_grad = jnp.sum(input_parts.reshape(2, 4, token_count, width).astype(jnp.float32), axis=1).reshape(both, width)
    input_grad = middle_grad + norm_back(hidden, normed_grad)
    ffn_grad = ffn_parts.reshape(GROUP, rows, 3, part).transpose(2, 1, 0, 3).reshape(3, rows, FF).astype(jnp.float32)
    ffn_moment_new = 0.5 * ffn_moment + 0.5 * ffn_grad

    summed = jnp.sum(row_parts.reshape(micro_count, HEADS, rows, 256).astype(jnp.float32), axis=0)
    early_grad = summed[:, :, : 3 * HEAD_DIM].reshape(HEADS, rows, 3, HEAD_DIM).transpose(2, 1, 0, 3).reshape(3, rows, D)
    attn_grad = jnp.concatenate([early_grad, out_row_grad.astype(jnp.float32)], axis=0)
    attn_moment_new = 0.5 * attn_moment + 0.5 * attn_grad

    output = (middle + result).astype(low)

    rates = jnp.asarray(RATES, jnp.float32)[:, None, None]
    attn_master = attn_weight - rates[:4] * attn_step.astype(jnp.float32)
    ffn_master = ffn_weight - rates[4:] * ffn_step.astype(jnp.float32)
    shape = (micro_count, token_count, width)
    return (
        output.reshape(shape),
        input_grad.reshape(shape),
        attn_grad,
        ffn_grad,
        attn_master,
        ffn_master,
        attn_moment_new,
        ffn_moment_new,
        attn_master.astype(low),
        ffn_master.astype(low),
    )


def solution(mesh):
    wide = P(None, ("blk", "head"), None)
    return jax.shard_map(
        functools.partial(on_device, Net(mesh)),
        mesh=mesh,
        in_specs=(wide, P(None, ("blk", "head")), wide, wide, wide, wide, wide),
        out_specs=(wide,) * 10,
        check_vma=False,
    )
```

```python
import functools
import math

import jax
import jax.numpy as jnp
from jax import lax
from jax.experimental import pallas as pl
from jax.experimental.pallas import tpu as pltpu
from jax.sharding import PartitionSpec as P

D = 768
HEADS = 12
HEAD_DIM = 64
HALF = 32
FF = 2048
DOCS = 4
NS_STEPS = 5
GROUP = 8
HOST = 1
SPARE = 2
KEYS = 512
BLOCK = 256
WIDE = 512

EPSILON = 1e-05
NEGATIVE = -1e30
RATES = (0.5, 0.5, 0.5, 7.0, 1.0, 1.0, 0.5)
COEFF_A = 3.4445
COEFF_B = -4.775
COEFF_C = 2.0315
OWNERS = (18, 19, 22, 21, 16, 17, 20)
MESH = pl.DeviceIdType.MESH
ANY = pl.BlockSpec(memory_space=pl.ANY)
VMEM = pl.BlockSpec(memory_space=pltpu.VMEM)
SMEM = pl.BlockSpec(memory_space=pltpu.SMEM)
SCALE = HEAD_DIM ** (-0.5)


def nt(a, b):
    return lax.dot_general(a, b, (((1,), (1,)), ((), ())), preferred_element_type=jnp.float32)


def nn(a, b):
    return jnp.dot(a, b, preferred_element_type=jnp.float32)


def attends(device):
    plane = device // GROUP
    return jnp.logical_and(plane < 4, plane != SPARE)


def combo_of(device):
    plane = device // GROUP
    place = device % GROUP
    return (place // 4) * HEADS + 4 * (plane - plane // 3) + place % 4


def device_of(combo):
    group = (combo % HEADS) // 4
    return GROUP * (group + group // 2) + 4 * (combo // HEADS) + combo % 4


class Net:
    def __init__(self, mesh):
        self.inner = mesh.shape["head"]
        self.count = mesh.shape["head"] * mesh.shape["blk"]
        self.planes = self.count // GROUP

    def permute(self, values, pairs):
        outer = self.count // self.inner

        def place(device):
            return (device % self.inner) * outer + device // self.inner

        return lax.ppermute(values, ("head", "blk"), [(place(i), place(j)) for i, j in pairs])

    def me(self):
        return lax.axis_index("blk") * self.inner + lax.axis_index("head")

    def at(self, device):
        return {"blk": device // self.inner, "head": device % self.inner}

    def meet(self, me, size):
        self.greet(me, size)
        pl.semaphore_wait(pltpu.get_barrier_semaphore(), size - 1)

    def greet(self, me, size):
        barrier = pltpu.get_barrier_semaphore()

        def greet(k, carry):
            pl.semaphore_signal(barrier, inc=1, device_id=self.at(peer(me, k, size)), device_id_type=MESH)
            return carry

        lax.fori_loop(1, size, greet, 0)

    def meet_attending(self, me):
        barrier = pltpu.get_barrier_semaphore()

        @pl.when(attends(me))
        def _():
            def greet(combo, carry):
                other = device_of(combo)

                @pl.when(other != me)
                def _():
                    pl.semaphore_signal(barrier, inc=1, device_id=self.at(other), device_id_type=MESH)

                return carry

            lax.fori_loop(0, 2 * HEADS, greet, 0)
            pl.semaphore_wait(barrier, 2 * HEADS - 1)

    def meet_heads(self, me):
        barrier = pltpu.get_barrier_semaphore()

        @pl.when(attends(me))
        def _():
            for owner in OWNERS[:3]:
                pl.semaphore_signal(barrier, inc=1, device_id=self.at(owner), device_id_type=MESH)
            pl.semaphore_wait(barrier, 3)

        for owner in OWNERS[:3]:

            @pl.when(me == owner)
            def _():
                def greet(combo, carry):
                    pl.semaphore_signal(barrier, inc=1, device_id=self.at(device_of(combo)), device_id_type=MESH)
                    return carry

                lax.fori_loop(0, 2 * HEADS, greet, 0)
                pl.semaphore_wait(barrier, 2 * HEADS)

    def shift(self, values, steps):
        far = GROUP * steps
        return self.permute(values, [(i, (i + far) % self.count) for i in range(self.count)])

    def flip(self, values, distance):
        return self.permute(values, [(i, i ^ distance) for i in range(self.count)])


def peer(me, k, size):
    return (me // size) * size + (me % size + k) % size


def flip_x(device):
    return device + 4 - 8 * ((device % GROUP) // 4)


def flip_y(device):
    return device + 1 - 2 * (device % 2)


def flip_core(device):
    return device + 2 - 4 * ((device % 4) // 2)


class Flow:
    def __init__(self, source, target, take, put, goes=None, size=None):
        self.source, self.target, self.take, self.put = source, target, take, put
        self.goes = goes or (lambda i, j: i >= 0)
        self.size = size

    def scratch(self):
        return []

    def semaphores(self):
        return self.size

    def bind(self, net, inputs, outputs, scratch, send, receive, local):
        self.net = net
        self.input, self.output = inputs[self.source], outputs[self.target]
        self.held = scratch
        self.send, self.receive, self.local = send, receive, local

    def copy(self, source, target, index, device):
        return pltpu.make_async_remote_copy(
            source,
            target,
            self.send.at[index],
            self.receive.at[index],
            device_id=self.net.at(device),
            device_id_type=MESH,
        )

    def remote(self, i, j, k):
        return self.copy(self.input.at[self.take(i, j)], self.output.at[self.put(i, j)], k, j)

    def near(self, i):
        return pltpu.make_async_copy(self.input.at[self.take(i, i)], self.output.at[self.put(i, i)], self.local)

    def start(self, me):
        def one(k, carry):
            other = peer(me, k, self.size)

            @pl.when(self.goes(me, other))
            def _():
                self.remote(me, other, k).start()

            return carry

        lax.fori_loop(1, self.size, one, 0)

        @pl.when(self.goes(me, me))
        def _():
            self.near(me).start()

    def middle(self, me):
        pass

    def finish(self, me):
        def one(k, carry):
            other = peer(me, k, self.size)

            @pl.when(self.goes(me, other))
            def _():
                self.remote(me, other, k).wait_send()

            before = peer(me, self.size - k, self.size)

            @pl.when(self.goes(before, me))
            def _():
                self.remote(before, me, k).wait_recv()

            return carry

        lax.fori_loop(1, self.size, one, 0)

        @pl.when(self.goes(me, me))
        def _():
            self.near(me).wait()


class Across(Flow):
    def __init__(self, net, source, target, take, put, goes=None):
        super().__init__(source, target, take, put, goes, net.count)
        self.planes = net.planes

    def semaphores(self):
        return self.planes

    def other(self, me, k):
        return (me + k * GROUP) % self.size

    def start(self, me):
        for k in range(1, self.planes):
            far = self.other(me, k)

            @pl.when(self.goes(me, far))
            def _(k=k, far=far):
                self.remote(me, far, k).start()

        @pl.when(self.goes(me, me))
        def _():
            self.near(me).start()

    def finish(self, me):
        for k in range(1, self.planes):
            far, before = self.other(me, k), self.other(me, self.planes - k)

            @pl.when(self.goes(me, far))
            def _(k=k, far=far):
                self.remote(me, far, k).wait_send()

            @pl.when(self.goes(before, me))
            def _(k=k, before=before):
                self.remote(before, me, k).wait_recv()

        @pl.when(self.goes(me, me))
        def _():
            self.near(me).wait()


class FanAcross(Across):
    def __init__(self, net, source, target, plane, take, put, goes):
        super().__init__(
            net,
            source,
            target,
            take,
            put,
            lambda i, j: jnp.logical_and(goes(i, j), j // GROUP == plane),
        )


class FanIn(Flow):
    def __init__(self, source, target, owner, take, put, goes=None, size=None):
        super().__init__(source, target, take, put, goes, size)
        self.place = owner

    def owner(self, me):
        return (me // self.size) * self.size + self.place

    def sends(self, me):
        return jnp.logical_and(me % self.size != self.place, self.goes(me, self.owner(me)))

    def step(self, me):
        return (self.place - me % self.size + self.size) % self.size

    def start(self, me):
        @pl.when(self.sends(me))
        def _():
            self.remote(me, self.owner(me), self.step(me)).start()

        @pl.when(jnp.logical_and(me % self.size == self.place, self.goes(me, me)))
        def _():
            self.near(me).start()

    def finish(self, me):
        @pl.when(self.sends(me))
        def _():
            self.remote(me, self.owner(me), self.step(me)).wait_send()

        @pl.when(me % self.size == self.place)
        def _():
            def one(k, carry):
                before = peer(me, self.size - k, self.size)

                @pl.when(self.goes(before, me))
                def _():
                    self.remote(before, me, k).wait_recv()

                return carry

            lax.fori_loop(1, self.size, one, 0)

        @pl.when(jnp.logical_and(me % self.size == self.place, self.goes(me, me)))
        def _():
            self.near(me).wait()


class FanOut(Flow):
    def __init__(self, source, target, owner, take, put):
        super().__init__(source, target, take, put)
        self.owner = owner

    def start(self, me):
        @pl.when(me == self.owner)
        def _():
            def one(k, carry):
                self.remote(me, peer(me, k, self.size), k).start()
                return carry

            lax.fori_loop(1, self.size, one, 0)
            self.near(me).start()

    def finish(self, me):
        @pl.when(me == self.owner)
        def _():
            def one(k, carry):
                self.remote(me, peer(me, k, self.size), k).wait_send()
                return carry

            lax.fori_loop(1, self.size, one, 0)
            self.near(me).wait()

        @pl.when(me != self.owner)
        def _():
            self.remote(self.owner, me, (me - self.owner + self.net.count) % self.size).wait_recv()


class PlaneGather(Flow):
    def __init__(self, source, target, put=lambda i: i % GROUP):
        super().__init__(source, target, None, put)

    def semaphores(self):
        return GROUP

    def partners(self, me):
        return [flip_x(me), flip_y(me), flip_x(flip_y(me))]

    def place(self, device):
        return self.output.at[self.put(device)]

    def own(self, me, index, device):
        return self.copy(self.input, self.place(me), index, device)

    def passed(self, me, index, partner):
        return self.copy(self.place(partner), self.place(partner), 4 + index, flip_core(me))

    def start(self, me):
        for index, partner in enumerate(self.partners(me)):
            self.own(me, 1 + index, partner).start()
        self.own(me, 0, flip_core(me)).start()
        pltpu.make_async_copy(self.input, self.place(me), self.local).start()

    def middle(self, me):
        for index, partner in enumerate(self.partners(me)):
            self.own(me, 1 + index, partner).wait_recv()
            self.passed(me, index, partner).start()

    def finish(self, me):
        for index, partner in enumerate(self.partners(me)):
            self.own(me, 1 + index, partner).wait_send()
            self.passed(me, index, partner).wait()
        self.own(me, 0, flip_core(me)).wait()
        pltpu.make_async_copy(self.input, self.place(me), self.local).wait()


class PlaneScatter(Flow):
    def __init__(self, source, target, block, lead=(), runs=None, moment=None, whole=None):
        super().__init__(source, target, None, None)
        self.block, self.lead = block, lead
        self.gathers, self.moment_source, self.whole_target = moment is not None, moment, whole
        self.runs = runs or (lambda i: i >= 0)
        self.every = (slice(None),) * len(lead)

    def scratch(self):
        pair = pltpu.VMEM(self.lead + (2, 2) + self.block, jnp.bfloat16)
        shapes = [pair, pair, pltpu.VMEM((3,) + self.lead + self.block, jnp.bfloat16)]
        if self.gathers:
            shapes += [
                pltpu.VMEM(self.lead + self.block, jnp.bfloat16),
                pltpu.VMEM(self.lead + self.lead + self.block, jnp.bfloat16),
                pltpu.VMEM(self.lead + self.block, jnp.bfloat16),
                pltpu.VMEM(self.lead + self.block, jnp.bfloat16),
            ]
        return shapes

    def bind(self, net, inputs, outputs, scratch, send, receive, local):
        super().bind(net, inputs, outputs, scratch, send, receive, local)
        if self.gathers:
            self.moment, self.whole = inputs[self.moment_source], outputs[self.whole_target]

    def momentum(self):
        return pltpu.make_async_copy(self.moment, self.held[5], self.receive.at[5 + SPARE])

    def direction(self, place):
        index = 5 + self.lead[0] + place
        return self.copy(self.held[6], self.whole.at[:, place], index, OWNERS[3])

    def close(self, me):
        place = me % GROUP
        for source in range(self.lead[0]):
            if source != SPARE:
                self.onward(me, source).wait_recv()
                self.output[...] += self.held[4][source].astype(jnp.float32)
        self.momentum().start()
        self.momentum().wait()
        self.held[6][...] = (0.75 * self.output[...] + 0.25 * self.held[5][...].astype(jnp.float32)).astype(jnp.bfloat16)

        @pl.when(me != OWNERS[3])
        def _():
            self.direction(place).start()
            self.direction(place).wait_send()

        @pl.when(me == OWNERS[3])
        def _():
            own = pltpu.make_async_copy(self.held[6], self.whole.at[:, place], self.local)
            own.start()
            own.wait()
            for other in range(GROUP):
                if other != OWNERS[3] % GROUP:
                    self.direction(other).wait_recv()

    def semaphores(self):
        return 5 + (self.lead[0] + GROUP if self.gathers else 0)

    def onward(self, me, source):
        spare = GROUP * SPARE + me % GROUP
        return self.copy(self.held[3], self.held[4].at[source], 5 + source, spare)

    def partners(self, me):
        return [flip_x(me), flip_y(me), flip_x(flip_y(me))]

    def half(self, core):
        return self.input.at[self.every + (slice(None), core)]

    def first(self, me):
        return self.copy(self.half(1 - (me % 4) // 2), self.held[1], 0, flip_core(me))

    def mine(self, me):
        return pltpu.make_async_copy(self.half((me % 4) // 2), self.held[0], self.local)

    def spot(self, device):
        return self.every + ((device % GROUP) // 4, device % 2)

    def second(self, me, index, partner):
        return self.copy(self.held[0].at[self.spot(partner)], self.held[2].at[index], 1 + index, partner)

    def start(self, me):
        @pl.when(self.runs(me))
        def _():
            self.first(me).start()
            self.mine(me).start()

    def pair(self, device):
        spot = self.spot(device)
        return self.held[0][spot].astype(jnp.float32) + self.held[1][spot].astype(jnp.float32)

    def middle(self, me):
        @pl.when(self.runs(me))
        def _():
            self.mine(me).wait()
            self.first(me).wait_recv()
            for index, partner in enumerate(self.partners(me)):
                self.held[0][self.spot(partner)] = self.pair(partner).astype(jnp.bfloat16)
                self.second(me, index, partner).start()

    def finish(self, me):
        @pl.when(self.runs(me))
        def _():
            total = self.pair(me)
            for index, partner in enumerate(self.partners(me)):
                self.second(me, index, partner).wait_recv()
                total = total + self.held[2][index].astype(jnp.float32)
            if self.gathers:
                plane = me // GROUP
                self.held[3][...] = total.astype(jnp.bfloat16)

                @pl.when(plane != SPARE)
                def _():
                    self.onward(me, plane).start()

            self.output[...] = total
            self.first(me).wait_send()
            for index, partner in enumerate(self.partners(me)):
                self.second(me, index, partner).wait_send()
            if self.gathers:

                @pl.when(plane != SPARE)
                def _():
                    self.onward(me, plane).wait_send()

                @pl.when(plane == SPARE)
                def _():
                    self.close(me)


def bind_all(net, flows, inputs, outputs, refs):
    for number, flow in enumerate(flows):
        need = len(flow.scratch())
        held, (send, receive), refs = refs[:need], refs[need : need + 2], refs[need + 2 :]
        flow.bind(net, inputs, outputs, held, send, receive, refs[-1].at[number])


def exchange_kernel(net, meet, flows, sources, targets, *refs):
    inputs = refs[:sources]
    outputs = refs[sources : sources + targets]
    me = net.me()
    meet(me)
    bind_all(net, flows, inputs, outputs, refs[sources + targets :])
    for flow in flows:
        flow.start(me)
    for flow in flows:
        flow.middle(me)
    for flow in flows:
        flow.finish(me)


def flow_scratch(flows):
    shapes = []
    for flow in flows:
        shapes += flow.scratch() + [pltpu.SemaphoreType.DMA((flow.semaphores(),))] * 2
    return shapes + [pltpu.SemaphoreType.DMA((len(flows),))]


def exchange(net, name, number, flows, sources, shapes, size=None, meet=None):
    size = size or net.count
    for flow in flows:
        flow.size = flow.size or size
    summed = {flow.target for flow in flows if isinstance(flow, PlaneScatter)}
    moved = sum(math.prod(s.shape) * s.dtype.itemsize for s in shapes)
    return pl.pallas_call(
        functools.partial(
            exchange_kernel, net, meet or (lambda me: net.meet(me, size)), flows, len(sources), len(shapes)
        ),
        out_shape=shapes,
        in_specs=[ANY] * len(sources),
        out_specs=[VMEM if k in summed else ANY for k in range(len(shapes))],
        scratch_shapes=flow_scratch(flows),
        compiler_params=pltpu.CompilerParams(collective_id=number, has_side_effects=True),
        cost_estimate=pl.CostEstimate(flops=0, bytes_accessed=8 * moved, transcendentals=0),
        name=name,
    )(*sources)


def gather_kernel(net, flows, extras, x_ref, w_ref, *refs):
    extra_refs, (all_ref, wall_ref), refs = refs[:extras], refs[extras : extras + 2], refs[extras + 2 :]
    extra_all, (send, receive, wsend, wreceive, local), refs = refs[:extras], refs[extras : extras + 5], refs[extras + 5 :]
    count = net.count
    planes = net.planes
    me = net.me()
    plane = me // GROUP
    place = me % GROUP
    half = place // 4
    spot = place % 4
    across = flip_x(me)
    beside = flip_y(me)
    sibling = flip_core(me)
    net.meet(me, count)
    bind_all(net, flows, extra_refs, extra_all, refs)

    def remote(source, target, index, device):
        return pltpu.make_async_remote_copy(
            source, target, send.at[index], receive.at[index], device_id=net.at(device), device_id_type=MESH
        )

    swap = remote(x_ref.at[1 - half], all_ref.at[plane, half, spot], 0, across)
    swap.start()

    def second(step, which):
        target = (me + step * GROUP) % count
        block = all_ref.at[plane, which, spot]
        return remote(block, block, 1 + (step - 1) * 2 + (which + half) % 2, target)

    def direct(step):
        target = (me + step * GROUP) % count
        return remote(x_ref.at[half], all_ref.at[plane, half, spot], 1 + (step - 1) * 2, target)

    third_base = 1 + 2 * (planes - 1)

    def third(step, which):
        source_plane = (plane + planes - step) % planes
        block = all_ref.at[source_plane, which, spot]
        return remote(block, block, third_base + step * 2 + which, beside)

    fourth_base = third_base + 2 * planes

    def fourth(step, which):
        source_plane = (plane + planes - step) % planes
        block = all_ref.at[source_plane, which, pl.ds((spot // 2) * 2, 2)]
        return remote(block, block, fourth_base + step * 2 + which, sibling)

    for step in range(1, planes):
        direct(step).start()
    mine = pltpu.make_async_copy(x_ref.at[half], all_ref.at[plane, half, spot], local.at[0])
    mine.start()

    def weights(combo):
        target = device_of(combo)
        return pltpu.make_async_remote_copy(
            w_ref.at[combo % HEADS],
            wall_ref.at[me],
            wsend.at[combo],
            wreceive.at[me],
            device_id=net.at(target),
            device_id_type=MESH,
        )

    def send_weights(combo, carry):
        @pl.when(device_of(combo) != me)
        def _():
            weights(combo).start()

        return carry

    mine.wait()
    swap.wait_recv()
    for step in range(1, planes):
        second(step, 1 - half).start()
    for which in range(2):
        third(0, which).start()
    lax.fori_loop(0, 2 * HEADS, send_weights, 0)
    for flow in flows:
        flow.start(me)
    for step in range(planes):
        if step > 0:
            second(step, half).wait_recv()
            second(step, 1 - half).wait_recv()
            for which in range(2):
                third(step, which).start()
            for which in range(2):
                third(step - 1, which).wait_recv()
            for which in range(2):
                fourth(step - 1, which).start()
    for which in range(2):
        third(planes - 1, which).wait_recv()
    for which in range(2):
        fourth(planes - 1, which).start()
    for step in range(planes):
        for which in range(2):
            fourth(step, which).wait_recv()

    @pl.when(attends(me))
    def _():
        own = pltpu.make_async_copy(w_ref.at[combo_of(me) % HEADS], wall_ref.at[me], local.at[1])
        own.start()
        own.wait()

        def took(k, carry):
            before = (me + k) % count
            pltpu.make_async_remote_copy(
                w_ref.at[0],
                wall_ref.at[before],
                wsend.at[0],
                wreceive.at[before],
                device_id=net.at(before),
                device_id_type=MESH,
            ).wait_recv()
            return carry

        lax.fori_loop(1, count, took, 0)

    def sent(combo, carry):
        @pl.when(device_of(combo) != me)
        def _():
            weights(combo).wait_send()

        return carry

    lax.fori_loop(0, 2 * HEADS, sent, 0)
    swap.wait_send()
    for step in range(1, planes):
        direct(step).wait_send()
        second(step, 1 - half).wait_send()
    for step in range(planes):
        for which in range(2):
            third(step, which).wait_send()
            fourth(step, which).wait_send()
    for flow in flows:
        flow.finish(me)


def gather_tokens(net, number, normed, columns, flows, extras, shapes):
    planes = net.planes
    copies = 1 + 2 * (planes - 1) + 4 * planes
    for flow in flows:
        flow.size = flow.size or net.count
    shapes = [
        jax.ShapeDtypeStruct((planes, 2, 4) + normed.shape[1:], normed.dtype),
        jax.ShapeDtypeStruct((net.count,) + columns.shape[1:], columns.dtype),
    ] + shapes
    return pl.pallas_call(
        functools.partial(gather_kernel, net, flows, len(extras)),
        out_shape=shapes,
        in_specs=[ANY] * (2 + len(extras)),
        out_specs=[ANY] * len(shapes),
        scratch_shapes=[
            pltpu.SemaphoreType.DMA((copies,)),
            pltpu.SemaphoreType.DMA((copies,)),
            pltpu.SemaphoreType.DMA((2 * HEADS,)),
            pltpu.SemaphoreType.DMA((net.count,)),
            pltpu.SemaphoreType.DMA((2,)),
        ]
        + flow_scratch(flows),
        compiler_params=pltpu.CompilerParams(collective_id=number, has_side_effects=True),
        cost_estimate=pl.CostEstimate(flops=0, bytes_accessed=100 * 2**20, transcendentals=0),
        name="gather_tokens",
    )(normed, columns, *extras)


def rope_rows(values, cosine, sine):
    first, second = values[:HALF], values[HALF:]
    return jnp.concatenate([first * cosine - second * sine, second * cosine + first * sine], axis=0)


def rope_rows_back(values, cosine, sine):
    first, second = values[:HALF], values[HALF:]
    return jnp.concatenate([first * cosine + second * sine, second * cosine - first * sine], axis=0)


def columns_of(index):
    return pl.ds(pl.multiple_of(index * BLOCK, BLOCK), BLOCK)


def wide_columns(index):
    return pl.ds(pl.multiple_of(index * WIDE, WIDE), WIDE)


def permitted(query_block, key_block, start):
    shape = (KEYS, WIDE)
    key = key_block * KEYS + lax.broadcasted_iota(jnp.int32, shape, 0)
    query = query_block * WIDE + lax.broadcasted_iota(jnp.int32, shape, 1)
    return (key <= query) & (key >= start)


def sweep(bounds_ref, query_block, step, carried):
    diagonal = query_block * (WIDE // KEYS)
    first, whole = bounds_ref[0, query_block], bounds_ref[1, query_block]
    carried = lax.fori_loop(first, whole, functools.partial(step, True), carried)
    carried = lax.fori_loop(whole, diagonal, functools.partial(step, False), carried)
    return lax.fori_loop(diagonal, diagonal + WIDE // KEYS, functools.partial(step, True), carried)


def fold(rows):
    return jnp.concatenate([rows[:HALF], rows[HALF:]], axis=1)


def unfold(rows):
    return jnp.concatenate([rows[:, :HEAD_DIM], rows[:, HEAD_DIM:]], axis=0)


def attend_kernel(net, *refs):
    @pl.when(attends(net.me()))
    def _():
        attend_body(*refs)


def attend_body(first_ref, x_ref, w_ref, cos_ref, sin_ref, start_ref, qkv_ref, mixed_ref, total_ref, packed_ref, key_rows):
    blocks = qkv_ref.shape[1] // BLOCK
    weights = w_ref[...]

    def project(chunk, carry):
        tokens = x_ref[chunk // 2, chunk % 2].reshape(BLOCK, D)
        here = columns_of(chunk)
        made = nt(weights, tokens)
        cosine, sine = cos_ref[:, here], sin_ref[:, here]
        query = rope_rows(made[:HEAD_DIM], cosine, sine)
        key = rope_rows(made[HEAD_DIM : 2 * HEAD_DIM], cosine, sine)
        qkv_ref[:HEAD_DIM, here] = query.astype(jnp.bfloat16) * SCALE
        qkv_ref[HEAD_DIM : 2 * HEAD_DIM, here] = key.astype(jnp.bfloat16)
        qkv_ref[2 * HEAD_DIM :, here] = made[2 * HEAD_DIM :].astype(jnp.bfloat16)
        key_rows[here, :] = key.T.astype(jnp.bfloat16)
        return carry

    lax.fori_loop(0, blocks, project, 0)

    def query_step(query_block, carry):
        here = wide_columns(query_block)
        query = qkv_ref[:HEAD_DIM, here]
        start = start_ref[:, here]

        def key_step(masked, key_block, held):
            top, total, mixed = held
            there = pl.ds(pl.multiple_of(key_block * KEYS, KEYS), KEYS)
            scores = nn(key_rows[there, :], query)
            if masked:
                allowed = permitted(query_block, key_block, start)
                scores = jnp.where(allowed, scores, NEGATIVE)
            new_top = jnp.maximum(top, jnp.max(scores, axis=0, keepdims=True))
            weights = jnp.exp(scores - new_top)
            if masked:
                weights = jnp.where(allowed, weights, 0.0)
            factor = jnp.exp(top - new_top)
            total = total * factor + jnp.sum(weights, axis=0, keepdims=True)
            mixed = mixed * factor + nn(qkv_ref[2 * HEAD_DIM :, there], weights.astype(jnp.bfloat16))
            return new_top, total, mixed

        top, total, mixed = sweep(
            first_ref,
            query_block,
            key_step,
            (
                jnp.full((1, WIDE), NEGATIVE, jnp.float32),
                jnp.zeros((1, WIDE), jnp.float32),
                jnp.zeros((HEAD_DIM, WIDE), jnp.float32),
            ),
        )
        mixed = mixed / total
        mixed_ref[:, here] = mixed
        total_ref[:, here] = top + jnp.log(total)
        rows = mixed.T
        for part in range(WIDE // 64):
            packed_ref[query_block * (WIDE // 64) + part] = fold(rows[part * 64 : part * 64 + 64]).astype(
                jnp.bfloat16
            )
        return carry

    lax.fori_loop(0, qkv_ref.shape[1] // WIDE, query_step, 0)


def attend(net, first, tokens, weights, cosine, sine, start):
    length = start.shape[1]
    return pl.pallas_call(
        functools.partial(attend_kernel, net),
        out_shape=[
            jax.ShapeDtypeStruct((3 * HEAD_DIM, length), jnp.bfloat16),
            jax.ShapeDtypeStruct((HEAD_DIM, length), jnp.float32),
            jax.ShapeDtypeStruct((1, length), jnp.float32),
            jax.ShapeDtypeStruct((net.count, HALF, 128), jnp.bfloat16),
        ],
        in_specs=[SMEM] + [VMEM] * 5,
        out_specs=[VMEM] * 4,
        scratch_shapes=[pltpu.VMEM((length, HEAD_DIM), jnp.bfloat16)],
        cost_estimate=pl.CostEstimate(flops=2 * 10**9, bytes_accessed=8 * 2**20, transcendentals=2 * 10**6),
        name="attend",
    )(first, tokens, weights, cosine, sine, start)


def attend_back_kernel(net, *refs):
    @pl.when(attends(net.me()))
    def _():
        attend_back_body(*refs)


def attend_back_body(
    first_ref,
    x_ref,
    qkv_ref,
    mixed_ref,
    total_ref,
    cos_ref,
    sin_ref,
    start_ref,
    grad_ref,
    packed_ref,
    weight_ref,
    query_rows,
    key_rows,
    value_rows,
    grad_rows,
    grad_columns,
    correction,
    key_grad,
    value_grad,
    all_grad,
):
    blocks = qkv_ref.shape[1] // BLOCK
    parts = BLOCK // 64

    def prepare(chunk, carry):
        here = columns_of(chunk)
        turned = qkv_ref[:, here].astype(jnp.float32)
        query_rows[here, :] = turned[:HEAD_DIM].T.astype(jnp.bfloat16)
        key_rows[here, :] = turned[HEAD_DIM : 2 * HEAD_DIM].T.astype(jnp.bfloat16)
        value_rows[here, :] = turned[2 * HEAD_DIM :].T.astype(jnp.bfloat16)
        pieces = [unfold(grad_ref[chunk * parts + part].astype(jnp.float32)) for part in range(parts)]
        rows = jnp.concatenate(pieces, axis=0)
        grad_rows[here, :] = rows.astype(jnp.bfloat16)
        across = rows.T
        grad_columns[:, here] = across.astype(jnp.bfloat16)
        correction[:, here] = jnp.sum(across * mixed_ref[:, here], axis=0, keepdims=True)
        key_grad[here, :] = jnp.zeros((BLOCK, HEAD_DIM), jnp.float32)
        value_grad[here, :] = jnp.zeros((BLOCK, HEAD_DIM), jnp.float32)
        return carry

    lax.fori_loop(0, blocks, prepare, 0)

    wide_parts = WIDE // 64

    def query_step(query_block, carry):
        here = wide_columns(query_block)
        query = qkv_ref[:HEAD_DIM, here]
        start = start_ref[:, here]
        total = total_ref[:, here]
        fix = correction[:, here]
        grad = grad_columns[:, here]
        query_in_rows = query_rows[here, :]
        grad_in_rows = grad_rows[here, :]

        def key_step(masked, key_block, query_grad):
            there = pl.ds(pl.multiple_of(key_block * KEYS, KEYS), KEYS)
            scores = nn(key_rows[there, :], query)
            weights = jnp.exp(scores - total)
            if masked:
                weights = jnp.where(permitted(query_block, key_block, start), weights, 0.0)
            value_grad[there, :] += nn(weights.astype(jnp.bfloat16), grad_in_rows)
            slope = nn(value_rows[there, :], grad)
            change = (weights * (slope - fix)).astype(jnp.bfloat16)
            key_grad[there, :] += nn(change, query_in_rows)
            return query_grad + nn(qkv_ref[HEAD_DIM : 2 * HEAD_DIM, there], change)

        query_grad = sweep(first_ref, query_block, key_step, jnp.zeros((HEAD_DIM, WIDE), jnp.float32))
        query_grad = rope_rows_back(query_grad * SCALE, cos_ref[:, here], sin_ref[:, here])
        all_grad[:HEAD_DIM, here] = query_grad.astype(jnp.bfloat16)
        rows = query_grad.T.astype(jnp.bfloat16)
        for part in range(wide_parts):
            packed_ref[query_block * wide_parts + part, :64, :HEAD_DIM] = rows[part * 64 : part * 64 + 64]
        return carry

    lax.fori_loop(0, qkv_ref.shape[1] // WIDE, query_step, 0)
    weight_ref[...] = jnp.zeros(weight_ref.shape, jnp.float32)

    def close(chunk, carry):
        here = columns_of(chunk)
        key = rope_rows_back(key_grad[here, :].T, cos_ref[:, here], sin_ref[:, here])
        value = value_grad[here, :]
        all_grad[HEAD_DIM : 2 * HEAD_DIM, here] = key.astype(jnp.bfloat16)
        all_grad[2 * HEAD_DIM :, here] = value.T.astype(jnp.bfloat16)
        rows = key.T.astype(jnp.bfloat16)
        for part in range(parts):
            token = chunk * parts + part
            packed_ref[token, :64, HEAD_DIM:] = rows[part * 64 : part * 64 + 64]
            packed_ref[token, 64:, :] = fold(value[part * 64 : part * 64 + 64]).astype(jnp.bfloat16)
        tokens = x_ref[chunk // 2, chunk % 2].reshape(BLOCK, D)
        weight_ref[...] += nn(all_grad[:, here], tokens)
        return carry

    lax.fori_loop(0, blocks, close, 0)


def attend_back(net, first, tokens, qkv, mixed, total, cosine, sine, start, grad):
    length = start.shape[1]
    rows = pltpu.VMEM((length, HEAD_DIM), jnp.bfloat16)
    sums = pltpu.VMEM((length, HEAD_DIM), jnp.float32)
    return pl.pallas_call(
        functools.partial(attend_back_kernel, net),
        out_shape=[
            jax.ShapeDtypeStruct((net.count, 96, 128), jnp.bfloat16),
            jax.ShapeDtypeStruct((3 * HEAD_DIM, D), jnp.float32),
        ],
        in_specs=[SMEM] + [VMEM] * 8,
        out_specs=[VMEM] * 2,
        scratch_shapes=[
            rows,
            rows,
            rows,
            rows,
            pltpu.VMEM((HEAD_DIM, length), jnp.bfloat16),
            pltpu.VMEM((1, length), jnp.float32),
            sums,
            sums,
            pltpu.VMEM((3 * HEAD_DIM, length), jnp.bfloat16),
        ],
        cost_estimate=pl.CostEstimate(flops=4 * 10**9, bytes_accessed=12 * 2**20, transcendentals=2 * 10**6),
        name="attend_back",
    )(first, tokens, qkv, mixed, total, cosine, sine, start, grad)


def tn(a, b):
    return lax.dot_general(a, b, (((0,), (0,)), ((), ())), preferred_element_type=jnp.float32)


def mean_of(values):
    return jnp.mean(values, axis=-1, keepdims=True)


def layer_norm(values):
    center = values - mean_of(values)
    return center * lax.rsqrt(mean_of(center * center) + EPSILON)


def norm_back(values, gradient):
    center = values - mean_of(values)
    inverse = lax.rsqrt(mean_of(center * center) + EPSILON)
    normed = center * inverse
    return inverse * (gradient - mean_of(gradient) - normed * mean_of(gradient * normed))


def after_kernel(parts_ref, tokens_ref, out_ref, mixed_ref, middle_ref, second_ref):
    for micro in range(2):
        here = slice(64 * micro, 64 * micro + 64)
        for pair in range(HEADS // 2):
            two = [unfold(parts_ref[micro * HEADS + 2 * pair + k].astype(jnp.float32)) for k in range(2)]
            mixed_ref[here, 128 * pair : 128 * pair + 128] = jnp.concatenate(two, axis=1).astype(jnp.bfloat16)
    middle = tokens_ref[...].astype(jnp.float32) + nn(mixed_ref[...], out_ref[...])
    middle_ref[...] = middle
    second_ref[...] = layer_norm(middle).astype(jnp.bfloat16)


def after_attention(parts, tokens, out):
    shape = tokens.shape
    return pl.pallas_call(
        after_kernel,
        out_shape=[
            jax.ShapeDtypeStruct(shape, jnp.bfloat16),
            jax.ShapeDtypeStruct(shape, jnp.float32),
            jax.ShapeDtypeStruct(shape, jnp.bfloat16),
        ],
        in_specs=[VMEM] * 3,
        out_specs=[VMEM] * 3,
        cost_estimate=pl.CostEstimate(flops=2 * 10**8, bytes_accessed=3 * 2**20, transcendentals=0),
        name="after_attention",
    )(parts, tokens, out)


def feed_forward_kernel(net, *refs):
    planes = net.planes
    second_ref, cotangent_ref = refs[:2]
    blocks = refs[2 : 2 + planes]
    second_terms, result_terms = refs[2 + planes : 4 + planes]
    terms = refs[4 + planes : 4 + 2 * planes]
    weights, slopes, products, sums = refs[4 + 2 * planes :]
    plane = net.me() // GROUP
    span = D // planes
    part = FF // GROUP
    for step, block in enumerate(blocks):
        source = (plane + planes - step) % planes
        weights[pl.ds(pl.multiple_of(source * span, span), span), :] = block[...]

    def forward(chunk, carry):
        here = columns_of(chunk)
        second, cotangent = second_ref[here, :], cotangent_ref[here, :]
        both = nn(second, weights[:, : 2 * part])
        gate, up = both[:, :part], both[:, part:]
        sigmoid = jax.nn.sigmoid(gate)
        silu = gate * sigmoid
        product = (silu * up).astype(jnp.bfloat16)
        change = nn(cotangent, weights[:, 2 * part :])
        slopes[here, :part] = (change * up * sigmoid * (1.0 + gate * (1.0 - sigmoid))).astype(jnp.bfloat16)
        slopes[here, part:] = (change * silu).astype(jnp.bfloat16)
        products[here, :] = product
        second_terms[here, :] = nt(slopes[here, :], weights[:, : 2 * part]).astype(jnp.bfloat16)
        result_terms[here, :] = nt(product, weights[:, 2 * part :]).astype(jnp.bfloat16)
        return carry

    lax.fori_loop(0, second_ref.shape[0] // BLOCK, forward, 0)
    for begin in range(0, D, BLOCK):
        here = slice(begin, begin + BLOCK)
        sums[here, : 2 * part] = tn(second_ref[:, here], slopes[...]).astype(jnp.bfloat16)
        sums[here, 2 * part :] = tn(cotangent_ref[:, here], products[...]).astype(jnp.bfloat16)
    for step, term in enumerate(terms):
        target = (plane + step) % planes
        term[...] = sums[pl.ds(pl.multiple_of(target * span, span), span), :]


def feed_forward(net, second, cotangent, blocks):
    tokens = second.shape[0]
    part = FF // GROUP
    low = jnp.bfloat16
    return pl.pallas_call(
        functools.partial(feed_forward_kernel, net),
        out_shape=[jax.ShapeDtypeStruct((tokens, D), low)] * 2
        + [jax.ShapeDtypeStruct((D // net.planes, 3 * part), low)] * net.planes,
        in_specs=[VMEM] * (2 + net.planes),
        out_specs=[VMEM] * (2 + net.planes),
        scratch_shapes=[
            pltpu.VMEM((D, 3 * part), low),
            pltpu.VMEM((tokens, 2 * part), low),
            pltpu.VMEM((tokens, part), low),
            pltpu.VMEM((D, 3 * part), low),
        ],
        cost_estimate=pl.CostEstimate(flops=35 * 10**8, bytes_accessed=10 * 2**20, transcendentals=10**6),
        name="feed_forward",
    )(second, cotangent, *blocks)


def before_kernel(second_grad_ref, middle_ref, cotangent_ref, mixed_ref, out_ref, middle_grad_ref, folded_ref, terms_ref):
    middle_grad = cotangent_ref[...].astype(jnp.float32) + norm_back(middle_ref[...], second_grad_ref[...])
    middle_grad_ref[...] = middle_grad
    low = middle_grad.astype(jnp.bfloat16)
    mixed_grad = nt(low, out_ref[...])
    for micro in range(2):
        rows = mixed_grad[64 * micro : 64 * micro + 64]
        for head in range(HEADS):
            folded_ref[micro * HEADS + head] = fold(rows[:, HEAD_DIM * head : HEAD_DIM * head + HEAD_DIM]).astype(
                jnp.bfloat16
            )
    terms_ref[...] = tn(mixed_ref[...], low).astype(jnp.bfloat16)


def before_attention(second_grad, middle, cotangent, mixed, out):
    return pl.pallas_call(
        before_kernel,
        out_shape=[
            jax.ShapeDtypeStruct(middle.shape, jnp.float32),
            jax.ShapeDtypeStruct((2 * HEADS, HALF, 128), jnp.bfloat16),
            jax.ShapeDtypeStruct((D, D), jnp.bfloat16),
        ],
        in_specs=[VMEM] * 5,
        out_specs=[VMEM] * 3,
        cost_estimate=pl.CostEstimate(flops=4 * 10**8, bytes_accessed=5 * 2**20, transcendentals=0),
        name="before_attention",
    )(second_grad, middle, cotangent, mixed, out)


def input_kernel(net, slots, grads_ref, *refs):
    blocks, partial_ref, weights = refs[: net.planes], refs[net.planes], refs[net.planes + 1]
    me = net.me()
    plane = me // GROUP
    span = D // net.planes

    @pl.when(attends(me))
    def _():
        for step, block in enumerate(blocks):
            source = (plane + net.planes - step) % net.planes
            weights[pl.ds(pl.multiple_of(source * span, span), span), :] = block[...]

        def one(slot, carry):
            total = jnp.zeros((GROUP * 64, D), jnp.float32)
            for group in range(3):
                rows = []
                for token in range(GROUP):
                    given = grads_ref[slot, group, token]
                    value = unfold(given[64:].astype(jnp.float32)).astype(jnp.bfloat16)
                    rows.append(jnp.concatenate([given[:64], value], axis=1))
                taken = jnp.concatenate(rows, axis=0)
                total = total + nt(taken, weights[:, 192 * group : 192 * group + 192])
            partial_ref[slot] = total.reshape(GROUP, 64, D).astype(jnp.bfloat16)
            return carry

        lax.fori_loop(0, jnp.where(plane == HOST, slots, 1), one, 0)


def input_partial(net, grads, blocks):
    slots = grads.shape[0]
    return pl.pallas_call(
        functools.partial(input_kernel, net, slots),
        out_shape=jax.ShapeDtypeStruct((slots, GROUP, 64, D), jnp.bfloat16),
        in_specs=[VMEM] * (1 + len(blocks)),
        out_specs=VMEM,
        scratch_shapes=[pltpu.VMEM((D, blocks[0].shape[1]), jnp.bfloat16)],
        cost_estimate=pl.CostEstimate(flops=10**9, bytes_accessed=6 * 2**20, transcendentals=0),
        name="input_partial",
    )(grads, *blocks)


def solve_heads(me, head_ref, moment_ref, target, scratch):
    wide, semaphore, parts, moment = scratch[0], scratch[3], scratch[4], scratch[5]

    @pl.when(jnp.logical_or(me == OWNERS[0], jnp.logical_or(me == OWNERS[1], me == OWNERS[2])))
    def _():
        move(head_ref, parts, semaphore)
        move(moment_ref, moment, semaphore)

        def join(pair, carry):
            first = parts[2 * pair].astype(jnp.float32) + parts[HEADS + 2 * pair].astype(jnp.float32)
            second = parts[2 * pair + 1].astype(jnp.float32) + parts[HEADS + 2 * pair + 1].astype(jnp.float32)
            here = pl.ds(pl.multiple_of(pair * 128, 128), 128)
            gradient = jnp.concatenate([first, second], axis=0).T
            wide[:, here] = (0.75 * gradient + 0.25 * moment[:, here].astype(jnp.float32)).astype(jnp.bfloat16)
            return carry

        lax.fori_loop(0, HEADS // 2, join, 0)
        solve(D, target, scratch)


def solve_late(me, out_ref, ffn_ref, out_target, ffn_target, scratch):
    wide, semaphore = scratch[0], scratch[3]

    @pl.when(me == OWNERS[3])
    def _():
        move(out_ref, wide.at[:, pl.ds(0, D)], semaphore)
        solve(D, out_target, scratch)

    @pl.when(jnp.logical_or(me == OWNERS[4], jnp.logical_or(me == OWNERS[5], me == OWNERS[6])))
    def _():
        move(ffn_ref, wide, semaphore)
        solve(FF, ffn_target, scratch)


def move(source, target, semaphore):
    copy = pltpu.make_async_copy(source, target, semaphore)
    copy.start()
    copy.wait()


def solve(span, target, scratch):
    wide, gram, polynomial, semaphore = scratch[:4]

    def blocks_of(index):
        return pl.ds(pl.multiple_of(index * BLOCK, BLOCK), BLOCK)

    def mirror(target, i, j, block):
        target[i * BLOCK : (i + 1) * BLOCK, j * BLOCK : (j + 1) * BLOCK] = block.astype(jnp.bfloat16)
        if i != j:
            target[j * BLOCK : (j + 1) * BLOCK, i * BLOCK : (i + 1) * BLOCK] = block.T.astype(jnp.bfloat16)

    chunks = span // BLOCK

    def measure(index, total):
        values = wide[:, blocks_of(index)].astype(jnp.float32)
        return total + jnp.sum(values * values, axis=0, keepdims=True)

    total = lax.fori_loop(0, chunks, measure, jnp.zeros((1, BLOCK), jnp.float32))
    frobenius = jnp.sqrt(jnp.sum(total, axis=1, keepdims=True)) + 1e-07

    def scale(index, carry):
        here = blocks_of(index)
        wide[:, here] = (wide[:, here].astype(jnp.float32) / frobenius).astype(jnp.bfloat16)
        return carry

    lax.fori_loop(0, chunks, scale, 0)

    def step(_, carry):
        for i in range(D // BLOCK):
            for j in range(i + 1):
                mirror(
                    gram,
                    i,
                    j,
                    nt(
                        wide[i * BLOCK : (i + 1) * BLOCK, :span],
                        wide[j * BLOCK : (j + 1) * BLOCK, :span],
                    ),
                )
        for i in range(D // BLOCK):
            for j in range(i + 1):
                square = nn(gram[i * BLOCK : (i + 1) * BLOCK, :], gram[:, j * BLOCK : (j + 1) * BLOCK])
                linear = gram[i * BLOCK : (i + 1) * BLOCK, j * BLOCK : (j + 1) * BLOCK].astype(jnp.float32)
                mirror(polynomial, i, j, COEFF_B * linear + COEFF_C * square)

        def advance(index, inner):
            here = blocks_of(index)
            old = wide[:, here]
            wide[:, here] = (COEFF_A * old.astype(jnp.float32) + nn(polynomial[...], old)).astype(jnp.bfloat16)
            return inner

        lax.fori_loop(0, chunks, advance, 0)
        return carry

    lax.fori_loop(0, NS_STEPS, step, 0)
    move(wide.at[:, pl.ds(0, span)], target, semaphore)


def solve_scratch(span, heads):
    square = pltpu.VMEM((D, D), jnp.bfloat16)
    shapes = [pltpu.VMEM((D, span), jnp.bfloat16), square, square, pltpu.SemaphoreType.DMA]
    if heads:
        shapes += [pltpu.VMEM((2 * HEADS, HEAD_DIM, D), jnp.bfloat16), square]
    return shapes


SQUARE = jax.ShapeDtypeStruct((D, D), jnp.bfloat16)
SOLVE_COST = pl.CostEstimate(flops=25 * 10**9, bytes_accessed=8 * 2**20, transcendentals=0)


def newton_kernel(net, head_ref, moment_ref, out_ref, ffn_ref, attn_target, ffn_target, *scratch):
    me = net.me()
    solve_heads(me, head_ref, moment_ref, attn_target, scratch)
    solve_late(me, out_ref, ffn_ref, attn_target, ffn_target, scratch)


def newton(net, *sources):
    return pl.pallas_call(
        functools.partial(newton_kernel, net),
        out_shape=[SQUARE, jax.ShapeDtypeStruct((D, FF), jnp.bfloat16)],
        in_specs=[ANY] * 4,
        out_specs=[ANY] * 2,
        scratch_shapes=solve_scratch(FF, True),
        cost_estimate=SOLVE_COST,
        name="newton",
    )(*sources)


def on_device(net, tokens, doc_ids, cotangent, attn_weight, ffn_weight, attn_moment, ffn_moment):
    micro_count, token_count, width = tokens.shape
    rows = attn_weight.shape[1]
    count, planes = net.count, net.planes
    length = count * token_count
    me = net.me()
    plane, place = me // GROUP, me % GROUP
    x_bit = place // 4
    both = micro_count * token_count
    part = FF // GROUP
    low = jnp.bfloat16
    everything = (slice(None),)

    attn_low = attn_weight.astype(low)
    ffn_low = ffn_weight.astype(low)

    def cut_up(values):
        return values.reshape(3, rows, GROUP, part).transpose(2, 1, 0, 3).reshape(GROUP, rows, 3 * part)

    cut = cut_up(ffn_low)
    out_grad = cotangent.reshape(both, width)
    hidden = tokens.astype(jnp.float32).reshape(both, width)
    normed = layer_norm(hidden).astype(low)
    counts = jnp.sum((doc_ids[:, :, None] == jnp.arange(DOCS)[None, None, :]).astype(jnp.float32), axis=1)
    tail = jnp.pad(counts.reshape(-1).astype(low), (0, HEAD_DIM - micro_count * DOCS))
    columns = attn_low[:3].reshape(3, rows, HEADS, HEAD_DIM).transpose(2, 1, 0, 3).reshape(HEADS, rows, 3 * HEAD_DIM)
    shares = columns.reshape(3, 4, rows, 3 * HEAD_DIM).transpose(1, 2, 0, 3).reshape(4, rows, 9 * HEAD_DIM)
    shares = jnp.pad(shares, ((0, 0), (0, 0), (0, HEAD_DIM)))
    columns = jnp.concatenate([columns, jnp.broadcast_to(tail, (HEADS, rows, HEAD_DIM))], axis=2)
    moment_low = attn_moment.astype(low)
    all_tokens, all_columns, plane_cut, plane_out, moment_plane, moment_out, plane_shares = gather_tokens(
        net,
        0,
        normed.reshape(micro_count, token_count, width),
        columns,
        [
            Flow(0, 0, lambda i, j: j % GROUP, lambda i, j: i % GROUP, size=GROUP),
            Across(net, 1, 1, lambda i, j: 0, lambda i, j: i // GROUP),
            Across(net, 3, 3, lambda i, j: 0, lambda i, j: i // GROUP, lambda i, j: j // GROUP == SPARE),
        ]
        + [
            Flow(2, 2, lambda i, j: j % GROUP, lambda i, j: i % GROUP, size=GROUP),
            Flow(4, 4, lambda i, j: j % 4, lambda i, j: i % GROUP, size=GROUP),
        ],
        [cut, attn_low[3:], cut_up(ffn_moment.astype(low)), moment_low[3:], shares],
        [
            jax.ShapeDtypeStruct(cut.shape, low),
            jax.ShapeDtypeStruct((planes, rows, D), low),
            jax.ShapeDtypeStruct(cut.shape, low),
            jax.ShapeDtypeStruct((planes, rows, D), low),
            jax.ShapeDtypeStruct((GROUP,) + shares.shape[1:], low),
        ],
    )
    late_own = plane_cut.reshape(GROUP * rows, 3 * part)
    late_blocks = [late_own] + [net.shift(late_own, step) for step in range(1, planes)]

    head_weights = all_columns[:, :, : 3 * HEAD_DIM].reshape(D, 3 * HEAD_DIM).T
    every_count = jnp.sum(all_columns[:, 0, 3 * HEAD_DIM :].astype(jnp.float32), axis=0)
    own_count = lax.dynamic_slice_in_dim(every_count, x_bit * DOCS, DOCS, 0)
    starts = jnp.cumsum(own_count) - own_count
    index = jnp.arange(length).astype(jnp.float32)
    start = jnp.max(jnp.where(starts[:, None] <= index[None, :], starts[:, None], 0.0), axis=0)
    inverse = 10000.0 ** (-(jnp.arange(HALF, dtype=jnp.float32) * 2.0) / HEAD_DIM)
    angles = inverse[:, None] * (index - start)[None, :]
    cosine, sine = jnp.cos(angles), jnp.sin(angles)
    start = start.astype(jnp.int32)
    diagonal = jnp.arange(length // WIDE, dtype=jnp.int32) * (WIDE // KEYS)
    first = jnp.clip(start[::WIDE] // KEYS, 0, diagonal)
    first = jnp.stack([first, jnp.clip((start[WIDE - 1 :: WIDE] + KEYS - 1) // KEYS, first, diagonal)])
    start = start[None, :]

    qkv, mixed, total, packed = attend(net, first, all_tokens, head_weights, cosine, sine, start)
    mixed_parts, moment_whole, plane_out_grad, out_full = exchange(
        net,
        "mixed_exchange",
        1,
        [PlaneGather(2, 2), PlaneGather(3, 3, lambda i: everything + (i % GROUP,))]
        + [Flow(0, 0, lambda i, j: j, lambda i, j: combo_of(i), lambda i, j: attends(i))]
        + [FanIn(1, 1, OWNERS[k], lambda i, j, k=k: k, lambda i, j: i) for k in range(3)],
        [packed, moment_low, out_grad, plane_out],
        [
            jax.ShapeDtypeStruct((2 * HEADS, HALF, 128), low),
            jax.ShapeDtypeStruct((count, rows, D), low),
            jax.ShapeDtypeStruct((GROUP, both, width), low),
            jax.ShapeDtypeStruct((planes, GROUP, rows, D), low),
        ],
    )
    plane_out_grad = plane_out_grad.reshape(GROUP * both, width)
    out_full = out_full.reshape(D, D)
    own_tokens = tokens.reshape(both, width)
    mixed_tokens, middle, second = after_attention(mixed_parts, own_tokens, out_full)
    (plane_second,) = exchange(
        net,
        "second_exchange",
        10,
        [PlaneGather(0, 0)],
        [second],
        [jax.ShapeDtypeStruct((GROUP, both, width), low)],
        GROUP,
    )
    plane_second = plane_second.reshape(GROUP * both, width)
    second_terms, result_terms, *ffn_terms = feed_forward(net, plane_second, plane_out_grad, late_blocks)
    sides = (2, 2, 2, both, width)
    (second_grad,) = exchange(
        net,
        "second_grad_exchange",
        11,
        [PlaneScatter(0, 0, (both, width))],
        [second_terms.reshape(sides)],
        [jax.ShapeDtypeStruct((both, width), jnp.float32)],
        GROUP,
    )
    ffn_block = ffn_terms[0].astype(jnp.float32)
    for step in range(1, planes):
        ffn_block = ffn_block + net.shift(ffn_terms[step], step).astype(jnp.float32)
    ffn_update = 0.75 * ffn_block + 0.25 * moment_plane.reshape(GROUP * rows, 3 * part).astype(jnp.float32)
    ffn_update, ffn_block = ffn_update.astype(low), ffn_block.astype(low)
    middle_grad, folded, out_terms = before_attention(second_grad, middle, out_grad, mixed_tokens, out_full)
    grad_parts, out_total, ffn_whole, out_whole = exchange(
        net,
        "mixed_grad_exchange",
        2,
        [
            PlaneScatter(1, 1, (rows, D), (planes,), moment=3, whole=3),
            Flow(0, 0, lambda i, j: combo_of(j), lambda i, j: i, lambda i, j: attends(j)),
        ]
        + [
            FanIn(
                2,
                2,
                OWNERS[4 + k],
                lambda i, j, k=k: (slice(None), pl.ds(part * k, part)),
                lambda i, j: (i // GROUP, slice(None), pl.ds(pl.multiple_of(part * (i % GROUP), part), part)),
            )
            for k in range(3)
        ],
        [folded, out_terms.reshape(planes, 2, 2, 2, rows, D), ffn_update, moment_out],
        [
            jax.ShapeDtypeStruct((count, HALF, 128), low),
            jax.ShapeDtypeStruct((planes, rows, D), jnp.float32),
            jax.ShapeDtypeStruct((planes, GROUP * rows, FF), low),
            jax.ShapeDtypeStruct((planes, GROUP, rows, D), low),
        ],
    )
    grad_parts, plane_shares = lax.optimization_barrier((grad_parts, plane_shares))
    share_own = plane_shares.reshape(GROUP * rows, 10 * HEAD_DIM)
    share_blocks = [share_own]
    for step in range(1, planes):
        hop = [(i, (i + GROUP * step) % count) for i in range(count)]
        share_blocks.append(net.permute(share_own, [(i, j) for i, j in hop if j // GROUP < 4 and j // GROUP != SPARE]))
    grad_packed, head_grad = attend_back(
        net, first, all_tokens, qkv, mixed, total, cosine, sine, start, grad_parts
    )
    head_low = head_grad.astype(low)
    (head_whole,) = exchange(
        net,
        "head_exchange",
        9,
        [
            FanIn(0, 0, OWNERS[k], lambda i, j, k=k: k, lambda i, j: combo_of(i), lambda i, j: attends(i))
            for k in range(3)
        ],
        [head_low.reshape(3, HEAD_DIM, D)],
        [jax.ShapeDtypeStruct((2 * HEADS, HEAD_DIM, D), low)],
        meet=net.meet_heads,
    )
    grad_packed, head_low, head_whole = lax.optimization_barrier((grad_packed, head_low, head_whole))
    guests = [p for p in range(planes) if p >= 4 or p == SPARE]
    slots = 1 + len(guests)
    head_rows = jnp.pad(head_low.T.reshape(count, rows, 3 * HEAD_DIM), ((0, 0), (0, 0), (0, 64)))

    def group_of(device):
        return device // GROUP - (device // GROUP) // 3

    def waits(device):
        return jnp.logical_not(attends(device))

    def head_flow(runs):
        return Flow(
            0, 0, lambda i, j: j, lambda i, j: combo_of(i), lambda i, j: jnp.logical_and(attends(i), runs(j))
        )

    row_shape = jax.ShapeDtypeStruct((2 * HEADS, rows, 256), low)
    early_rows, host_grads = exchange(
        net,
        "attending_exchange",
        7,
        [
            Across(
                net,
                1,
                1,
                lambda i, j: j // GROUP,
                lambda i, j: (0, group_of(i)),
                lambda i, j: jnp.logical_and(attends(i), attends(j)),
            )
        ]
        + [
            FanAcross(
                net, 1, 1, HOST, lambda i, j, p=p: p, lambda i, j, k=k: (1 + k, group_of(i)), lambda i, j: attends(i)
            )
            for k, p in enumerate(guests)
        ]
        + [head_flow(attends)],
        [head_rows, grad_packed.reshape(planes, GROUP, 96, 128)],
        [row_shape, jax.ShapeDtypeStruct((slots, 3, GROUP, 96, 128), low)],
        meet=net.meet_attending,
    )
    partial = input_partial(net, host_grads, share_blocks)
    attn_done, ffn_done = newton(
        net, head_whole, moment_whole.reshape(D, D), out_whole.reshape(D, D), ffn_whole.reshape(D, FF)
    )
    attn_done, ffn_done, partial, early_rows = lax.optimization_barrier((attn_done, ffn_done, partial, early_rows))

    def guest_index(device):
        p = device // GROUP
        return p - SPARE - jnp.minimum(p // 4, 1)

    late_rows, ffn_parts, attn_step, ffn_step, out_row_grad, input_parts, result = exchange(
        net,
        "step_exchange",
        5,
        [PlaneScatter(6, 6, (both, width))]
        + [FanOut(3, 3, OWNERS[4 + k], lambda i, j: j, lambda i, j, k=k: k) for k in range(3)]
        + [FanOut(2, 2, OWNERS[k], lambda i, j: j, lambda i, j, k=k: k) for k in range(4)]
        + [
            Flow(
                5,
                5,
                lambda i, j: (1 + guest_index(j), j % GROUP),
                lambda i, j: i % GROUP,
                lambda i, j: jnp.logical_and(i // GROUP == HOST, waits(j)),
            ),
            Flow(5, 5, lambda i, j: (0, j % GROUP), lambda i, j: i % GROUP, lambda i, j: attends(i), size=GROUP),
            Flow(1, 1, lambda i, j: j % GROUP, lambda i, j: i % GROUP, size=GROUP),
            Across(net, 4, 4, lambda i, j: j // GROUP, lambda i, j: 0, lambda i, j: i // GROUP == SPARE),
            head_flow(waits),
        ],
        [
            head_rows,
            ffn_block.reshape(GROUP, rows, 3 * part),
            attn_done.reshape(count, rows, D),
            ffn_done.reshape(count, rows, FF),
            out_total.astype(low),
            partial,
            result_terms.reshape(sides),
        ],
        [
            row_shape,
            jax.ShapeDtypeStruct((GROUP, rows, 3 * part), low),
            jax.ShapeDtypeStruct((4, rows, D), low),
            jax.ShapeDtypeStruct((3, rows, FF), low),
            jax.ShapeDtypeStruct((1, rows, D), low),
            jax.ShapeDtypeStruct((GROUP, token_count, width), low),
            jax.ShapeDtypeStruct((both, width), jnp.float32),
        ],
    )
    row_parts = jnp.where(attends(me), early_rows, late_rows)
    normed_grad = jnp.sum(input_parts.reshape(2, 4, token_count, width).astype(jnp.float32), axis=1).reshape(both, width)
    input_grad = middle_grad + norm_back(hidden, normed_grad)
    ffn_grad = ffn_parts.reshape(GROUP, rows, 3, part).transpose(2, 1, 0, 3).reshape(3, rows, FF).astype(jnp.float32)
    ffn_moment_new = 0.5 * ffn_moment + 0.5 * ffn_grad

    summed = jnp.sum(row_parts.reshape(micro_count, HEADS, rows, 256).astype(jnp.float32), axis=0)
    early_grad = summed[:, :, : 3 * HEAD_DIM].reshape(HEADS, rows, 3, HEAD_DIM).transpose(2, 1, 0, 3).reshape(3, rows, D)
    attn_grad = jnp.concatenate([early_grad, out_row_grad.astype(jnp.float32)], axis=0)
    attn_moment_new = 0.5 * attn_moment + 0.5 * attn_grad

    output = (middle + result).astype(low)

    rates = jnp.asarray(RATES, jnp.float32)[:, None, None]
    attn_master = attn_weight - rates[:4] * attn_step.astype(jnp.float32)
    ffn_master = ffn_weight - rates[4:] * ffn_step.astype(jnp.float32)
    shape = (micro_count, token_count, width)
    return (
        output.reshape(shape),
        input_grad.reshape(shape),
        attn_grad,
        ffn_grad,
        attn_master,
        ffn_master,
        attn_moment_new,
        ffn_moment_new,
        attn_master.astype(low),
        ffn_master.astype(low),
    )


def solution(mesh):
    wide = P(None, ("blk", "head"), None)
    return jax.shard_map(
        functools.partial(on_device, Net(mesh)),
        mesh=mesh,
        in_specs=(wide, P(None, ("blk", "head")), wide, wide, wide, wide, wide),
        out_specs=(wide,) * 10,
        check_vma=False,
    )
```

```python
import functools
import math

import jax
import jax.numpy as jnp
from jax import lax
from jax.experimental import pallas as pl
from jax.experimental.pallas import tpu as pltpu
from jax.sharding import PartitionSpec as P

D = 768
HEADS = 12
HEAD_DIM = 64
HALF = 32
FF = 2048
DOCS = 4
NS_STEPS = 5
GROUP = 8
HOST = 1
SPARE = 2
KEYS = 512
BLOCK = 256
WIDE = 512

EPSILON = 1e-05
NEGATIVE = -1e30
RATES = (0.5, 0.5, 0.5, 7.0, 1.0, 1.0, 0.5)
COEFF_A = 3.4445
COEFF_B = -4.775
COEFF_C = 2.0315
OWNERS = (18, 19, 22, 21, 16, 17, 20)
MESH = pl.DeviceIdType.MESH
ANY = pl.BlockSpec(memory_space=pl.ANY)
VMEM = pl.BlockSpec(memory_space=pltpu.VMEM)
SMEM = pl.BlockSpec(memory_space=pltpu.SMEM)
SCALE = HEAD_DIM ** (-0.5)


def nt(a, b):
    return lax.dot_general(a, b, (((1,), (1,)), ((), ())), preferred_element_type=jnp.float32)


def nn(a, b):
    return jnp.dot(a, b, preferred_element_type=jnp.float32)


def attends(device):
    plane = device // GROUP
    return jnp.logical_and(plane < 4, plane != SPARE)


def combo_of(device):
    plane = device // GROUP
    place = device % GROUP
    return (place // 4) * HEADS + 4 * (plane - plane // 3) + place % 4


def device_of(combo):
    group = (combo % HEADS) // 4
    return GROUP * (group + group // 2) + 4 * (combo // HEADS) + combo % 4


class Net:
    def __init__(self, mesh):
        self.inner = mesh.shape["head"]
        self.count = mesh.shape["head"] * mesh.shape["blk"]
        self.planes = self.count // GROUP

    def permute(self, values, pairs):
        outer = self.count // self.inner

        def place(device):
            return (device % self.inner) * outer + device // self.inner

        return lax.ppermute(values, ("head", "blk"), [(place(i), place(j)) for i, j in pairs])

    def me(self):
        return lax.axis_index("blk") * self.inner + lax.axis_index("head")

    def at(self, device):
        return {"blk": device // self.inner, "head": device % self.inner}

    def meet(self, me, size):
        self.greet(me, size)
        pl.semaphore_wait(pltpu.get_barrier_semaphore(), size - 1)

    def greet(self, me, size):
        barrier = pltpu.get_barrier_semaphore()

        def greet(k, carry):
            pl.semaphore_signal(barrier, inc=1, device_id=self.at(peer(me, k, size)), device_id_type=MESH)
            return carry

        lax.fori_loop(1, size, greet, 0)

    def meet_attending(self, me):
        barrier = pltpu.get_barrier_semaphore()

        @pl.when(attends(me))
        def _():
            def greet(combo, carry):
                other = device_of(combo)

                @pl.when(other != me)
                def _():
                    pl.semaphore_signal(barrier, inc=1, device_id=self.at(other), device_id_type=MESH)

                return carry

            lax.fori_loop(0, 2 * HEADS, greet, 0)
            pl.semaphore_wait(barrier, 2 * HEADS - 1)

    def meet_heads(self, me):
        barrier = pltpu.get_barrier_semaphore()

        @pl.when(attends(me))
        def _():
            for owner in OWNERS[:3]:
                pl.semaphore_signal(barrier, inc=1, device_id=self.at(owner), device_id_type=MESH)
            pl.semaphore_wait(barrier, 3)

        for owner in OWNERS[:3]:

            @pl.when(me == owner)
            def _():
                def greet(combo, carry):
                    pl.semaphore_signal(barrier, inc=1, device_id=self.at(device_of(combo)), device_id_type=MESH)
                    return carry

                lax.fori_loop(0, 2 * HEADS, greet, 0)
                pl.semaphore_wait(barrier, 2 * HEADS)

    def shift(self, values, steps):
        far = GROUP * steps
        return self.permute(values, [(i, (i + far) % self.count) for i in range(self.count)])

    def flip(self, values, distance):
        return self.permute(values, [(i, i ^ distance) for i in range(self.count)])


def peer(me, k, size):
    return (me // size) * size + (me % size + k) % size


def flip_x(device):
    return device + 4 - 8 * ((device % GROUP) // 4)


def flip_y(device):
    return device + 1 - 2 * (device % 2)


def flip_core(device):
    return device + 2 - 4 * ((device % 4) // 2)


class Flow:
    def __init__(self, source, target, take, put, goes=None, size=None):
        self.source, self.target, self.take, self.put = source, target, take, put
        self.goes = goes or (lambda i, j: i >= 0)
        self.size = size

    def scratch(self):
        return []

    def semaphores(self):
        return self.size

    def bind(self, net, inputs, outputs, scratch, send, receive, local):
        self.net = net
        self.input, self.output = inputs[self.source], outputs[self.target]
        self.held = scratch
        self.send, self.receive, self.local = send, receive, local

    def copy(self, source, target, index, device):
        return pltpu.make_async_remote_copy(
            source,
            target,
            self.send.at[index],
            self.receive.at[index],
            device_id=self.net.at(device),
            device_id_type=MESH,
        )

    def remote(self, i, j, k):
        return self.copy(self.input.at[self.take(i, j)], self.output.at[self.put(i, j)], k, j)

    def near(self, i):
        return pltpu.make_async_copy(self.input.at[self.take(i, i)], self.output.at[self.put(i, i)], self.local)

    def start(self, me):
        def one(k, carry):
            other = peer(me, k, self.size)

            @pl.when(self.goes(me, other))
            def _():
                self.remote(me, other, k).start()

            return carry

        lax.fori_loop(1, self.size, one, 0)

        @pl.when(self.goes(me, me))
        def _():
            self.near(me).start()

    def middle(self, me):
        pass

    def finish(self, me):
        def one(k, carry):
            other = peer(me, k, self.size)

            @pl.when(self.goes(me, other))
            def _():
                self.remote(me, other, k).wait_send()

            before = peer(me, self.size - k, self.size)

            @pl.when(self.goes(before, me))
            def _():
                self.remote(before, me, k).wait_recv()

            return carry

        lax.fori_loop(1, self.size, one, 0)

        @pl.when(self.goes(me, me))
        def _():
            self.near(me).wait()


class Across(Flow):
    def __init__(self, net, source, target, take, put, goes=None):
        super().__init__(source, target, take, put, goes, net.count)
        self.planes = net.planes

    def semaphores(self):
        return self.planes

    def other(self, me, k):
        return (me + k * GROUP) % self.size

    def start(self, me):
        for k in range(1, self.planes):
            far = self.other(me, k)

            @pl.when(self.goes(me, far))
            def _(k=k, far=far):
                self.remote(me, far, k).start()

        @pl.when(self.goes(me, me))
        def _():
            self.near(me).start()

    def finish(self, me):
        for k in range(1, self.planes):
            far, before = self.other(me, k), self.other(me, self.planes - k)

            @pl.when(self.goes(me, far))
            def _(k=k, far=far):
                self.remote(me, far, k).wait_send()

            @pl.when(self.goes(before, me))
            def _(k=k, before=before):
                self.remote(before, me, k).wait_recv()

        @pl.when(self.goes(me, me))
        def _():
            self.near(me).wait()


class FanAcross(Across):
    def __init__(self, net, source, target, plane, take, put, goes):
        super().__init__(
            net,
            source,
            target,
            take,
            put,
            lambda i, j: jnp.logical_and(goes(i, j), j // GROUP == plane),
        )


class FanIn(Flow):
    def __init__(self, source, target, owner, take, put, goes=None, size=None):
        super().__init__(source, target, take, put, goes, size)
        self.place = owner

    def owner(self, me):
        return (me // self.size) * self.size + self.place

    def sends(self, me):
        return jnp.logical_and(me % self.size != self.place, self.goes(me, self.owner(me)))

    def step(self, me):
        return (self.place - me % self.size + self.size) % self.size

    def start(self, me):
        @pl.when(self.sends(me))
        def _():
            self.remote(me, self.owner(me), self.step(me)).start()

        @pl.when(jnp.logical_and(me % self.size == self.place, self.goes(me, me)))
        def _():
            self.near(me).start()

    def finish(self, me):
        @pl.when(self.sends(me))
        def _():
            self.remote(me, self.owner(me), self.step(me)).wait_send()

        @pl.when(me % self.size == self.place)
        def _():
            def one(k, carry):
                before = peer(me, self.size - k, self.size)

                @pl.when(self.goes(before, me))
                def _():
                    self.remote(before, me, k).wait_recv()

                return carry

            lax.fori_loop(1, self.size, one, 0)

        @pl.when(jnp.logical_and(me % self.size == self.place, self.goes(me, me)))
        def _():
            self.near(me).wait()


class FanOut(Flow):
    def __init__(self, source, target, owner, take, put):
        super().__init__(source, target, take, put)
        self.owner = owner

    def start(self, me):
        @pl.when(me == self.owner)
        def _():
            def one(k, carry):
                self.remote(me, peer(me, k, self.size), k).start()
                return carry

            lax.fori_loop(1, self.size, one, 0)
            self.near(me).start()

    def finish(self, me):
        @pl.when(me == self.owner)
        def _():
            def one(k, carry):
                self.remote(me, peer(me, k, self.size), k).wait_send()
                return carry

            lax.fori_loop(1, self.size, one, 0)
            self.near(me).wait()

        @pl.when(me != self.owner)
        def _():
            self.remote(self.owner, me, (me - self.owner + self.net.count) % self.size).wait_recv()


class PlaneGather(Flow):
    def __init__(self, source, target, put=lambda i: i % GROUP):
        super().__init__(source, target, None, put)

    def semaphores(self):
        return GROUP

    def partners(self, me):
        return [flip_x(me), flip_y(me), flip_x(flip_y(me))]

    def place(self, device):
        return self.output.at[self.put(device)]

    def own(self, me, index, device):
        return self.copy(self.input, self.place(me), index, device)

    def passed(self, me, index, partner):
        return self.copy(self.place(partner), self.place(partner), 4 + index, flip_core(me))

    def start(self, me):
        for index, partner in enumerate(self.partners(me)):
            self.own(me, 1 + index, partner).start()
        self.own(me, 0, flip_core(me)).start()
        pltpu.make_async_copy(self.input, self.place(me), self.local).start()

    def middle(self, me):
        for index, partner in enumerate(self.partners(me)):
            self.own(me, 1 + index, partner).wait_recv()
            self.passed(me, index, partner).start()

    def finish(self, me):
        for index, partner in enumerate(self.partners(me)):
            self.own(me, 1 + index, partner).wait_send()
            self.passed(me, index, partner).wait()
        self.own(me, 0, flip_core(me)).wait()
        pltpu.make_async_copy(self.input, self.place(me), self.local).wait()


class PlaneScatter(Flow):
    def __init__(self, source, target, block, lead=(), runs=None, moment=None, whole=None):
        super().__init__(source, target, None, None)
        self.block, self.lead = block, lead
        self.gathers, self.moment_source, self.whole_target = moment is not None, moment, whole
        self.runs = runs or (lambda i: i >= 0)
        self.every = (slice(None),) * len(lead)

    def scratch(self):
        pair = pltpu.VMEM(self.lead + (2, 2) + self.block, jnp.bfloat16)
        shapes = [pair, pair, pltpu.VMEM((3,) + self.lead + self.block, jnp.bfloat16)]
        if self.gathers:
            shapes += [
                pltpu.VMEM(self.lead + self.block, jnp.bfloat16),
                pltpu.VMEM(self.lead + self.lead + self.block, jnp.bfloat16),
                pltpu.VMEM(self.lead + self.block, jnp.bfloat16),
                pltpu.VMEM(self.lead + self.block, jnp.bfloat16),
            ]
        return shapes

    def bind(self, net, inputs, outputs, scratch, send, receive, local):
        super().bind(net, inputs, outputs, scratch, send, receive, local)
        if self.gathers:
            self.moment, self.whole = inputs[self.moment_source], outputs[self.whole_target]

    def momentum(self):
        return pltpu.make_async_copy(self.moment, self.held[5], self.receive.at[5 + SPARE])

    def direction(self, place):
        index = 5 + self.lead[0] + place
        return self.copy(self.held[6], self.whole.at[:, place], index, OWNERS[3])

    def close(self, me):
        place = me % GROUP
        for source in range(self.lead[0]):
            if source != SPARE:
                self.onward(me, source).wait_recv()
                self.output[...] += self.held[4][source].astype(jnp.float32)
        self.momentum().start()
        self.momentum().wait()
        self.held[6][...] = (0.75 * self.output[...] + 0.25 * self.held[5][...].astype(jnp.float32)).astype(jnp.bfloat16)

        @pl.when(me != OWNERS[3])
        def _():
            self.direction(place).start()
            self.direction(place).wait_send()

        @pl.when(me == OWNERS[3])
        def _():
            own = pltpu.make_async_copy(self.held[6], self.whole.at[:, place], self.local)
            own.start()
            own.wait()
            for other in range(GROUP):
                if other != OWNERS[3] % GROUP:
                    self.direction(other).wait_recv()

    def semaphores(self):
        return 5 + (self.lead[0] + GROUP if self.gathers else 0)

    def onward(self, me, source):
        spare = GROUP * SPARE + me % GROUP
        return self.copy(self.held[3], self.held[4].at[source], 5 + source, spare)

    def partners(self, me):
        return [flip_x(me), flip_y(me), flip_x(flip_y(me))]

    def half(self, core):
        return self.input.at[self.every + (slice(None), core)]

    def first(self, me):
        return self.copy(self.half(1 - (me % 4) // 2), self.held[1], 0, flip_core(me))

    def mine(self, me):
        return pltpu.make_async_copy(self.half((me % 4) // 2), self.held[0], self.local)

    def spot(self, device):
        return self.every + ((device % GROUP) // 4, device % 2)

    def second(self, me, index, partner):
        return self.copy(self.held[0].at[self.spot(partner)], self.held[2].at[index], 1 + index, partner)

    def start(self, me):
        @pl.when(self.runs(me))
        def _():
            self.first(me).start()
            self.mine(me).start()

    def pair(self, device):
        spot = self.spot(device)
        return self.held[0][spot].astype(jnp.float32) + self.held[1][spot].astype(jnp.float32)

    def middle(self, me):
        @pl.when(self.runs(me))
        def _():
            self.mine(me).wait()
            self.first(me).wait_recv()
            for index, partner in enumerate(self.partners(me)):
                self.held[0][self.spot(partner)] = self.pair(partner).astype(jnp.bfloat16)
                self.second(me, index, partner).start()

    def finish(self, me):
        @pl.when(self.runs(me))
        def _():
            total = self.pair(me)
            for index, partner in enumerate(self.partners(me)):
                self.second(me, index, partner).wait_recv()
                total = total + self.held[2][index].astype(jnp.float32)
            if self.gathers:
                plane = me // GROUP
                self.held[3][...] = total.astype(jnp.bfloat16)

                @pl.when(plane != SPARE)
                def _():
                    self.onward(me, plane).start()

            self.output[...] = total
            self.first(me).wait_send()
            for index, partner in enumerate(self.partners(me)):
                self.second(me, index, partner).wait_send()
            if self.gathers:

                @pl.when(plane != SPARE)
                def _():
                    self.onward(me, plane).wait_send()

                @pl.when(plane == SPARE)
                def _():
                    self.close(me)


def bind_all(net, flows, inputs, outputs, refs):
    for number, flow in enumerate(flows):
        need = len(flow.scratch())
        held, (send, receive), refs = refs[:need], refs[need : need + 2], refs[need + 2 :]
        flow.bind(net, inputs, outputs, held, send, receive, refs[-1].at[number])


def exchange_kernel(net, meet, flows, sources, targets, *refs):
    inputs = refs[:sources]
    outputs = refs[sources : sources + targets]
    me = net.me()
    meet(me)
    bind_all(net, flows, inputs, outputs, refs[sources + targets :])
    for flow in flows:
        flow.start(me)
    for flow in flows:
        flow.middle(me)
    for flow in flows:
        flow.finish(me)


def flow_scratch(flows):
    shapes = []
    for flow in flows:
        shapes += flow.scratch() + [pltpu.SemaphoreType.DMA((flow.semaphores(),))] * 2
    return shapes + [pltpu.SemaphoreType.DMA((len(flows),))]


def exchange(net, name, number, flows, sources, shapes, size=None, meet=None):
    size = size or net.count
    for flow in flows:
        flow.size = flow.size or size
    summed = {flow.target for flow in flows if isinstance(flow, PlaneScatter)}
    moved = sum(math.prod(s.shape) * s.dtype.itemsize for s in shapes)
    return pl.pallas_call(
        functools.partial(
            exchange_kernel, net, meet or (lambda me: net.meet(me, size)), flows, len(sources), len(shapes)
        ),
        out_shape=shapes,
        in_specs=[ANY] * len(sources),
        out_specs=[VMEM if k in summed else ANY for k in range(len(shapes))],
        scratch_shapes=flow_scratch(flows),
        compiler_params=pltpu.CompilerParams(collective_id=number, has_side_effects=True),
        cost_estimate=pl.CostEstimate(flops=0, bytes_accessed=8 * moved, transcendentals=0),
        name=name,
    )(*sources)


def gather_kernel(net, flows, extras, x_ref, w_ref, *refs):
    extra_refs, (all_ref, wall_ref), refs = refs[:extras], refs[extras : extras + 2], refs[extras + 2 :]
    extra_all, (send, receive, wsend, wreceive, local), refs = refs[:extras], refs[extras : extras + 5], refs[extras + 5 :]
    count = net.count
    planes = net.planes
    me = net.me()
    plane = me // GROUP
    place = me % GROUP
    half = place // 4
    spot = place % 4
    across = flip_x(me)
    beside = flip_y(me)
    sibling = flip_core(me)
    net.meet(me, count)
    bind_all(net, flows, extra_refs, extra_all, refs)

    def remote(source, target, index, device):
        return pltpu.make_async_remote_copy(
            source, target, send.at[index], receive.at[index], device_id=net.at(device), device_id_type=MESH
        )

    swap = remote(x_ref.at[1 - half], all_ref.at[plane, half, spot], 0, across)
    swap.start()

    def second(step, which):
        target = (me + step * GROUP) % count
        block = all_ref.at[plane, which, spot]
        return remote(block, block, 1 + (step - 1) * 2 + (which + half) % 2, target)

    def direct(step):
        target = (me + step * GROUP) % count
        return remote(x_ref.at[half], all_ref.at[plane, half, spot], 1 + (step - 1) * 2, target)

    third_base = 1 + 2 * (planes - 1)

    def third(step, which):
        source_plane = (plane + planes - step) % planes
        block = all_ref.at[source_plane, which, spot]
        return remote(block, block, third_base + step * 2 + which, beside)

    fourth_base = third_base + 2 * planes

    def fourth(step, which):
        source_plane = (plane + planes - step) % planes
        block = all_ref.at[source_plane, which, pl.ds((spot // 2) * 2, 2)]
        return remote(block, block, fourth_base + step * 2 + which, sibling)

    for step in range(1, planes):
        direct(step).start()
    mine = pltpu.make_async_copy(x_ref.at[half], all_ref.at[plane, half, spot], local.at[0])
    mine.start()

    def weights(combo):
        target = device_of(combo)
        return pltpu.make_async_remote_copy(
            w_ref.at[combo % HEADS],
            wall_ref.at[me],
            wsend.at[combo],
            wreceive.at[me],
            device_id=net.at(target),
            device_id_type=MESH,
        )

    def send_weights(combo, carry):
        @pl.when(device_of(combo) != me)
        def _():
            weights(combo).start()

        return carry

    mine.wait()
    swap.wait_recv()
    for step in range(1, planes):
        second(step, 1 - half).start()
    for which in range(2):
        third(0, which).start()
    lax.fori_loop(0, 2 * HEADS, send_weights, 0)
    for flow in flows:
        flow.start(me)
    for step in range(planes):
        if step > 0:
            second(step, half).wait_recv()
            second(step, 1 - half).wait_recv()
            for which in range(2):
                third(step, which).start()
            for which in range(2):
                third(step - 1, which).wait_recv()
            for which in range(2):
                fourth(step - 1, which).start()
    for which in range(2):
        third(planes - 1, which).wait_recv()
    for which in range(2):
        fourth(planes - 1, which).start()
    for step in range(planes):
        for which in range(2):
            fourth(step, which).wait_recv()

    @pl.when(attends(me))
    def _():
        own = pltpu.make_async_copy(w_ref.at[combo_of(me) % HEADS], wall_ref.at[me], local.at[1])
        own.start()
        own.wait()

        def took(k, carry):
            before = (me + k) % count
            pltpu.make_async_remote_copy(
                w_ref.at[0],
                wall_ref.at[before],
                wsend.at[0],
                wreceive.at[before],
                device_id=net.at(before),
                device_id_type=MESH,
            ).wait_recv()
            return carry

        lax.fori_loop(1, count, took, 0)

    def sent(combo, carry):
        @pl.when(device_of(combo) != me)
        def _():
            weights(combo).wait_send()

        return carry

    lax.fori_loop(0, 2 * HEADS, sent, 0)
    swap.wait_send()
    for step in range(1, planes):
        direct(step).wait_send()
        second(step, 1 - half).wait_send()
    for step in range(planes):
        for which in range(2):
            third(step, which).wait_send()
            fourth(step, which).wait_send()
    for flow in flows:
        flow.finish(me)


def gather_tokens(net, number, normed, columns, flows, extras, shapes):
    planes = net.planes
    copies = 1 + 2 * (planes - 1) + 4 * planes
    for flow in flows:
        flow.size = flow.size or net.count
    shapes = [
        jax.ShapeDtypeStruct((planes, 2, 4) + normed.shape[1:], normed.dtype),
        jax.ShapeDtypeStruct((net.count,) + columns.shape[1:], columns.dtype),
    ] + shapes
    return pl.pallas_call(
        functools.partial(gather_kernel, net, flows, len(extras)),
        out_shape=shapes,
        in_specs=[ANY] * (2 + len(extras)),
        out_specs=[ANY] * len(shapes),
        scratch_shapes=[
            pltpu.SemaphoreType.DMA((copies,)),
            pltpu.SemaphoreType.DMA((copies,)),
            pltpu.SemaphoreType.DMA((2 * HEADS,)),
            pltpu.SemaphoreType.DMA((net.count,)),
            pltpu.SemaphoreType.DMA((2,)),
        ]
        + flow_scratch(flows),
        compiler_params=pltpu.CompilerParams(collective_id=number, has_side_effects=True),
        cost_estimate=pl.CostEstimate(flops=0, bytes_accessed=100 * 2**20, transcendentals=0),
        name="gather_tokens",
    )(normed, columns, *extras)


def rope_rows(values, cosine, sine):
    first, second = values[:HALF], values[HALF:]
    return jnp.concatenate([first * cosine - second * sine, second * cosine + first * sine], axis=0)


def rope_rows_back(values, cosine, sine):
    first, second = values[:HALF], values[HALF:]
    return jnp.concatenate([first * cosine + second * sine, second * cosine - first * sine], axis=0)


def columns_of(index):
    return pl.ds(pl.multiple_of(index * BLOCK, BLOCK), BLOCK)


def wide_columns(index):
    return pl.ds(pl.multiple_of(index * WIDE, WIDE), WIDE)


def permitted(query_block, key_block, start):
    shape = (KEYS, WIDE)
    key = key_block * KEYS + lax.broadcasted_iota(jnp.int32, shape, 0)
    query = query_block * WIDE + lax.broadcasted_iota(jnp.int32, shape, 1)
    return (key <= query) & (key >= start)


def sweep(bounds_ref, query_block, step, carried):
    diagonal = query_block * (WIDE // KEYS)
    first, whole = bounds_ref[0, query_block], bounds_ref[1, query_block]
    carried = lax.fori_loop(first, whole, functools.partial(step, True), carried)
    carried = lax.fori_loop(whole, diagonal, functools.partial(step, False), carried)
    return lax.fori_loop(diagonal, diagonal + WIDE // KEYS, functools.partial(step, True), carried)


def fold(rows):
    return jnp.concatenate([rows[:HALF], rows[HALF:]], axis=1)


def unfold(rows):
    return jnp.concatenate([rows[:, :HEAD_DIM], rows[:, HEAD_DIM:]], axis=0)


def attend_kernel(net, *refs):
    @pl.when(attends(net.me()))
    def _():
        attend_body(*refs)


def attend_body(first_ref, x_ref, w_ref, cos_ref, sin_ref, start_ref, qkv_ref, mixed_ref, total_ref, packed_ref, key_rows):
    blocks = qkv_ref.shape[1] // BLOCK
    weights = w_ref[...].astype(jnp.float32).T[: 3 * HEAD_DIM].astype(jnp.bfloat16)

    def project(chunk, carry):
        tokens = x_ref[chunk // 2, chunk % 2].reshape(BLOCK, D)
        here = columns_of(chunk)
        made = nt(weights, tokens)
        cosine, sine = cos_ref[:, here], sin_ref[:, here]
        query = rope_rows(made[:HEAD_DIM], cosine, sine)
        key = rope_rows(made[HEAD_DIM : 2 * HEAD_DIM], cosine, sine)
        qkv_ref[:HEAD_DIM, here] = query.astype(jnp.bfloat16) * SCALE
        qkv_ref[HEAD_DIM : 2 * HEAD_DIM, here] = key.astype(jnp.bfloat16)
        qkv_ref[2 * HEAD_DIM :, here] = made[2 * HEAD_DIM :].astype(jnp.bfloat16)
        key_rows[here, :] = key.T.astype(jnp.bfloat16)
        return carry

    lax.fori_loop(0, blocks, project, 0)

    def query_step(query_block, carry):
        here = wide_columns(query_block)
        query = qkv_ref[:HEAD_DIM, here]
        start = start_ref[:, here]

        def key_step(masked, key_block, held):
            top, total, mixed = held
            there = pl.ds(pl.multiple_of(key_block * KEYS, KEYS), KEYS)
            scores = nn(key_rows[there, :], query)
            if masked:
                allowed = permitted(query_block, key_block, start)
                scores = jnp.where(allowed, scores, NEGATIVE)
            new_top = jnp.maximum(top, jnp.max(scores, axis=0, keepdims=True))
            weights = jnp.exp(scores - new_top)
            if masked:
                weights = jnp.where(allowed, weights, 0.0)
            factor = jnp.exp(top - new_top)
            total = total * factor + jnp.sum(weights, axis=0, keepdims=True)
            mixed = mixed * factor + nn(qkv_ref[2 * HEAD_DIM :, there], weights.astype(jnp.bfloat16))
            return new_top, total, mixed

        top, total, mixed = sweep(
            first_ref,
            query_block,
            key_step,
            (
                jnp.full((1, WIDE), NEGATIVE, jnp.float32),
                jnp.zeros((1, WIDE), jnp.float32),
                jnp.zeros((HEAD_DIM, WIDE), jnp.float32),
            ),
        )
        mixed = mixed / total
        mixed_ref[:, here] = mixed
        total_ref[:, here] = top + jnp.log(total)
        rows = mixed.T
        for part in range(WIDE // 64):
            packed_ref[query_block * (WIDE // 64) + part] = fold(rows[part * 64 : part * 64 + 64]).astype(
                jnp.bfloat16
            )
        return carry

    lax.fori_loop(0, qkv_ref.shape[1] // WIDE, query_step, 0)


def attend(net, first, tokens, weights, cosine, sine, start):
    length = start.shape[1]
    return pl.pallas_call(
        functools.partial(attend_kernel, net),
        out_shape=[
            jax.ShapeDtypeStruct((3 * HEAD_DIM, length), jnp.bfloat16),
            jax.ShapeDtypeStruct((HEAD_DIM, length), jnp.float32),
            jax.ShapeDtypeStruct((1, length), jnp.float32),
            jax.ShapeDtypeStruct((net.count, HALF, 128), jnp.bfloat16),
        ],
        in_specs=[SMEM] + [VMEM] * 5,
        out_specs=[VMEM] * 4,
        scratch_shapes=[pltpu.VMEM((length, HEAD_DIM), jnp.bfloat16)],
        cost_estimate=pl.CostEstimate(flops=2 * 10**9, bytes_accessed=8 * 2**20, transcendentals=2 * 10**6),
        name="attend",
    )(first, tokens, weights, cosine, sine, start)


def attend_back_kernel(net, *refs):
    @pl.when(attends(net.me()))
    def _():
        attend_back_body(*refs)


def attend_back_body(
    first_ref,
    x_ref,
    qkv_ref,
    mixed_ref,
    total_ref,
    cos_ref,
    sin_ref,
    start_ref,
    grad_ref,
    packed_ref,
    weight_ref,
    query_rows,
    key_rows,
    value_rows,
    grad_rows,
    grad_columns,
    correction,
    key_grad,
    value_grad,
    all_grad,
):
    blocks = qkv_ref.shape[1] // BLOCK
    parts = BLOCK // 64

    def prepare(chunk, carry):
        here = columns_of(chunk)
        turned = qkv_ref[:, here].astype(jnp.float32)
        query_rows[here, :] = turned[:HEAD_DIM].T.astype(jnp.bfloat16)
        key_rows[here, :] = turned[HEAD_DIM : 2 * HEAD_DIM].T.astype(jnp.bfloat16)
        value_rows[here, :] = turned[2 * HEAD_DIM :].T.astype(jnp.bfloat16)
        pieces = [unfold(grad_ref[chunk * parts + part].astype(jnp.float32)) for part in range(parts)]
        rows = jnp.concatenate(pieces, axis=0)
        grad_rows[here, :] = rows.astype(jnp.bfloat16)
        across = rows.T
        grad_columns[:, here] = across.astype(jnp.bfloat16)
        correction[:, here] = jnp.sum(across * mixed_ref[:, here], axis=0, keepdims=True)
        key_grad[here, :] = jnp.zeros((BLOCK, HEAD_DIM), jnp.float32)
        value_grad[here, :] = jnp.zeros((BLOCK, HEAD_DIM), jnp.float32)
        return carry

    lax.fori_loop(0, blocks, prepare, 0)

    wide_parts = WIDE // 64

    def query_step(query_block, carry):
        here = wide_columns(query_block)
        query = qkv_ref[:HEAD_DIM, here]
        start = start_ref[:, here]
        total = total_ref[:, here]
        fix = correction[:, here]
        grad = grad_columns[:, here]
        query_in_rows = query_rows[here, :]
        grad_in_rows = grad_rows[here, :]

        def key_step(masked, key_block, query_grad):
            there = pl.ds(pl.multiple_of(key_block * KEYS, KEYS), KEYS)
            scores = nn(key_rows[there, :], query)
            weights = jnp.exp(scores - total)
            if masked:
                weights = jnp.where(permitted(query_block, key_block, start), weights, 0.0)
            value_grad[there, :] += nn(weights.astype(jnp.bfloat16), grad_in_rows)
            slope = nn(value_rows[there, :], grad)
            change = (weights * (slope - fix)).astype(jnp.bfloat16)
            key_grad[there, :] += nn(change, query_in_rows)
            return query_grad + nn(qkv_ref[HEAD_DIM : 2 * HEAD_DIM, there], change)

        query_grad = sweep(first_ref, query_block, key_step, jnp.zeros((HEAD_DIM, WIDE), jnp.float32))
        query_grad = rope_rows_back(query_grad * SCALE, cos_ref[:, here], sin_ref[:, here])
        all_grad[:HEAD_DIM, here] = query_grad.astype(jnp.bfloat16)
        rows = query_grad.T.astype(jnp.bfloat16)
        for part in range(wide_parts):
            packed_ref[query_block * wide_parts + part, :64, :HEAD_DIM] = rows[part * 64 : part * 64 + 64]
        return carry

    lax.fori_loop(0, qkv_ref.shape[1] // WIDE, query_step, 0)
    weight_ref[...] = jnp.zeros(weight_ref.shape, jnp.float32)

    def close(chunk, carry):
        here = columns_of(chunk)
        key = rope_rows_back(key_grad[here, :].T, cos_ref[:, here], sin_ref[:, here])
        value = value_grad[here, :]
        all_grad[HEAD_DIM : 2 * HEAD_DIM, here] = key.astype(jnp.bfloat16)
        all_grad[2 * HEAD_DIM :, here] = value.T.astype(jnp.bfloat16)
        rows = key.T.astype(jnp.bfloat16)
        for part in range(parts):
            token = chunk * parts + part
            packed_ref[token, :64, HEAD_DIM:] = rows[part * 64 : part * 64 + 64]
            packed_ref[token, 64:, :] = fold(value[part * 64 : part * 64 + 64]).astype(jnp.bfloat16)
        tokens = x_ref[chunk // 2, chunk % 2].reshape(BLOCK, D)
        weight_ref[...] += nn(all_grad[:, here], tokens)
        return carry

    lax.fori_loop(0, blocks, close, 0)


def attend_back(net, first, tokens, qkv, mixed, total, cosine, sine, start, grad):
    length = start.shape[1]
    rows = pltpu.VMEM((length, HEAD_DIM), jnp.bfloat16)
    sums = pltpu.VMEM((length, HEAD_DIM), jnp.float32)
    return pl.pallas_call(
        functools.partial(attend_back_kernel, net),
        out_shape=[
            jax.ShapeDtypeStruct((net.count, 96, 128), jnp.bfloat16),
            jax.ShapeDtypeStruct((3 * HEAD_DIM, D), jnp.float32),
        ],
        in_specs=[SMEM] + [VMEM] * 8,
        out_specs=[VMEM] * 2,
        scratch_shapes=[
            rows,
            rows,
            rows,
            rows,
            pltpu.VMEM((HEAD_DIM, length), jnp.bfloat16),
            pltpu.VMEM((1, length), jnp.float32),
            sums,
            sums,
            pltpu.VMEM((3 * HEAD_DIM, length), jnp.bfloat16),
        ],
        cost_estimate=pl.CostEstimate(flops=4 * 10**9, bytes_accessed=12 * 2**20, transcendentals=2 * 10**6),
        name="attend_back",
    )(first, tokens, qkv, mixed, total, cosine, sine, start, grad)


def tn(a, b):
    return lax.dot_general(a, b, (((0,), (0,)), ((), ())), preferred_element_type=jnp.float32)


def mean_of(values):
    return jnp.mean(values, axis=-1, keepdims=True)


def layer_norm(values):
    center = values - mean_of(values)
    return center * lax.rsqrt(mean_of(center * center) + EPSILON)


def norm_back(values, gradient):
    center = values - mean_of(values)
    inverse = lax.rsqrt(mean_of(center * center) + EPSILON)
    normed = center * inverse
    return inverse * (gradient - mean_of(gradient) - normed * mean_of(gradient * normed))


def prepare_kernel(
    tokens_ref,
    documents_ref,
    attn_ref,
    ffn_ref,
    attn_moment_ref,
    ffn_moment_ref,
    normed_ref,
    columns_ref,
    shares_ref,
    cut_ref,
    moment_cut_ref,
    out_ref,
    moment_ref,
    out_moment_ref,
):
    low = jnp.bfloat16
    normed_ref[...] = layer_norm(tokens_ref[...].astype(jnp.float32)).astype(low)
    documents = documents_ref[...]
    lane = lax.broadcasted_iota(jnp.int32, (1, HEAD_DIM), 1)
    tail = jnp.zeros((1, HEAD_DIM), jnp.float32)
    for document in range(DOCS):
        counts = jnp.sum((documents == document).astype(jnp.float32), axis=1, keepdims=True)
        for micro in range(documents.shape[0]):
            tail = jnp.where(lane == micro * DOCS + document, counts[micro : micro + 1], tail)
    rows = attn_ref.shape[1]
    tail = jnp.broadcast_to(tail, (rows, HEAD_DIM))
    empty = jnp.zeros((rows, HEAD_DIM), jnp.float32)
    for head in range(HEADS):
        here = slice(HEAD_DIM * head, HEAD_DIM * head + HEAD_DIM)
        three = [attn_ref[matrix, :, here] for matrix in range(3)]
        columns_ref[head] = jnp.concatenate(three + [tail], axis=1).astype(low)
    for share in range(4):
        pieces = []
        for head in range(share, HEADS, 4):
            here = slice(HEAD_DIM * head, HEAD_DIM * head + HEAD_DIM)
            pieces += [attn_ref[matrix, :, here] for matrix in range(3)]
        shares_ref[share] = jnp.concatenate(pieces + [empty], axis=1).astype(low)
    part = FF // GROUP
    for place in range(GROUP):
        here = slice(part * place, part * place + part)
        for matrix in range(3):
            there = slice(part * matrix, part * matrix + part)
            cut_ref[place, :, there] = ffn_ref[matrix, :, here].astype(low)
            moment_cut_ref[place, :, there] = ffn_moment_ref[matrix, :, here].astype(low)
    out_ref[0] = attn_ref[3].astype(low)
    moment_ref[...] = attn_moment_ref[...].astype(low)
    out_moment_ref[0] = attn_moment_ref[3].astype(low)


def prepare(tokens, documents, attn, ffn, attn_moment, ffn_moment):
    rows = attn.shape[1]
    low = jnp.bfloat16
    cut = jax.ShapeDtypeStruct((GROUP, rows, 3 * FF // GROUP), low)
    return pl.pallas_call(
        prepare_kernel,
        out_shape=[
            jax.ShapeDtypeStruct(tokens.shape, low),
            jax.ShapeDtypeStruct((HEADS, rows, 4 * HEAD_DIM), low),
            jax.ShapeDtypeStruct((4, rows, 10 * HEAD_DIM), low),
            cut,
            cut,
            jax.ShapeDtypeStruct((1, rows, D), low),
            jax.ShapeDtypeStruct((4, rows, D), low),
            jax.ShapeDtypeStruct((1, rows, D), low),
        ],
        in_specs=[VMEM] * 6,
        out_specs=[VMEM] * 8,
        cost_estimate=pl.CostEstimate(flops=10**7, bytes_accessed=4 * 2**20, transcendentals=0),
        name="prepare",
    )(tokens, documents, attn, ffn, attn_moment, ffn_moment)


def after_kernel(parts_ref, tokens_ref, out_ref, mixed_ref, middle_ref, second_ref):
    for micro in range(2):
        here = slice(64 * micro, 64 * micro + 64)
        for pair in range(HEADS // 2):
            two = [unfold(parts_ref[micro * HEADS + 2 * pair + k].astype(jnp.float32)) for k in range(2)]
            mixed_ref[here, 128 * pair : 128 * pair + 128] = jnp.concatenate(two, axis=1).astype(jnp.bfloat16)
    middle = tokens_ref[...].astype(jnp.float32) + nn(mixed_ref[...], out_ref[...])
    middle_ref[...] = middle
    second_ref[...] = layer_norm(middle).astype(jnp.bfloat16)


def after_attention(parts, tokens, out):
    shape = tokens.shape
    return pl.pallas_call(
        after_kernel,
        out_shape=[
            jax.ShapeDtypeStruct(shape, jnp.bfloat16),
            jax.ShapeDtypeStruct(shape, jnp.float32),
            jax.ShapeDtypeStruct(shape, jnp.bfloat16),
        ],
        in_specs=[VMEM] * 3,
        out_specs=[VMEM] * 3,
        cost_estimate=pl.CostEstimate(flops=2 * 10**8, bytes_accessed=3 * 2**20, transcendentals=0),
        name="after_attention",
    )(parts, tokens, out)


def feed_forward_kernel(net, *refs):
    planes = net.planes
    second_ref, cotangent_ref = refs[:2]
    blocks = refs[2 : 2 + planes]
    second_terms, result_terms = refs[2 + planes : 4 + planes]
    terms = refs[4 + planes : 4 + 2 * planes]
    weights, slopes, products, sums = refs[4 + 2 * planes :]
    plane = net.me() // GROUP
    span = D // planes
    part = FF // GROUP
    for step, block in enumerate(blocks):
        source = (plane + planes - step) % planes
        weights[pl.ds(pl.multiple_of(source * span, span), span), :] = block[...]

    def forward(chunk, carry):
        here = columns_of(chunk)
        second, cotangent = second_ref[here, :], cotangent_ref[here, :]
        both = nn(second, weights[:, : 2 * part])
        gate, up = both[:, :part], both[:, part:]
        sigmoid = jax.nn.sigmoid(gate)
        silu = gate * sigmoid
        product = (silu * up).astype(jnp.bfloat16)
        change = nn(cotangent, weights[:, 2 * part :])
        slopes[here, :part] = (change * up * sigmoid * (1.0 + gate * (1.0 - sigmoid))).astype(jnp.bfloat16)
        slopes[here, part:] = (change * silu).astype(jnp.bfloat16)
        products[here, :] = product
        second_terms[here, :] = nt(slopes[here, :], weights[:, : 2 * part]).astype(jnp.bfloat16)
        result_terms[here, :] = nt(product, weights[:, 2 * part :]).astype(jnp.bfloat16)
        return carry

    lax.fori_loop(0, second_ref.shape[0] // BLOCK, forward, 0)
    for begin in range(0, D, BLOCK):
        here = slice(begin, begin + BLOCK)
        sums[here, : 2 * part] = tn(second_ref[:, here], slopes[...]).astype(jnp.bfloat16)
        sums[here, 2 * part :] = tn(cotangent_ref[:, here], products[...]).astype(jnp.bfloat16)
    for step, term in enumerate(terms):
        target = (plane + step) % planes
        term[...] = sums[pl.ds(pl.multiple_of(target * span, span), span), :]


def feed_forward(net, second, cotangent, blocks):
    tokens = second.shape[0]
    part = FF // GROUP
    low = jnp.bfloat16
    return pl.pallas_call(
        functools.partial(feed_forward_kernel, net),
        out_shape=[jax.ShapeDtypeStruct((tokens, D), low)] * 2
        + [jax.ShapeDtypeStruct((D // net.planes, 3 * part), low)] * net.planes,
        in_specs=[VMEM] * (2 + net.planes),
        out_specs=[VMEM] * (2 + net.planes),
        scratch_shapes=[
            pltpu.VMEM((D, 3 * part), low),
            pltpu.VMEM((tokens, 2 * part), low),
            pltpu.VMEM((tokens, part), low),
            pltpu.VMEM((D, 3 * part), low),
        ],
        cost_estimate=pl.CostEstimate(flops=35 * 10**8, bytes_accessed=10 * 2**20, transcendentals=10**6),
        name="feed_forward",
    )(second, cotangent, *blocks)


def before_kernel(second_grad_ref, middle_ref, cotangent_ref, mixed_ref, out_ref, middle_grad_ref, folded_ref, terms_ref):
    middle_grad = cotangent_ref[...].astype(jnp.float32) + norm_back(middle_ref[...], second_grad_ref[...])
    middle_grad_ref[...] = middle_grad
    low = middle_grad.astype(jnp.bfloat16)
    mixed_grad = nt(low, out_ref[...])
    for micro in range(2):
        rows = mixed_grad[64 * micro : 64 * micro + 64]
        for head in range(HEADS):
            folded_ref[micro * HEADS + head] = fold(rows[:, HEAD_DIM * head : HEAD_DIM * head + HEAD_DIM]).astype(
                jnp.bfloat16
            )
    terms_ref[...] = tn(mixed_ref[...], low).astype(jnp.bfloat16)


def before_attention(second_grad, middle, cotangent, mixed, out):
    return pl.pallas_call(
        before_kernel,
        out_shape=[
            jax.ShapeDtypeStruct(middle.shape, jnp.float32),
            jax.ShapeDtypeStruct((2 * HEADS, HALF, 128), jnp.bfloat16),
            jax.ShapeDtypeStruct((D, D), jnp.bfloat16),
        ],
        in_specs=[VMEM] * 5,
        out_specs=[VMEM] * 3,
        cost_estimate=pl.CostEstimate(flops=4 * 10**8, bytes_accessed=5 * 2**20, transcendentals=0),
        name="before_attention",
    )(second_grad, middle, cotangent, mixed, out)


def input_kernel(net, slots, grads_ref, *refs):
    blocks, partial_ref, weights = refs[: net.planes], refs[net.planes], refs[net.planes + 1]
    me = net.me()
    plane = me // GROUP
    span = D // net.planes

    @pl.when(attends(me))
    def _():
        for step, block in enumerate(blocks):
            source = (plane + net.planes - step) % net.planes
            weights[pl.ds(pl.multiple_of(source * span, span), span), :] = block[...]

        def one(slot, carry):
            total = jnp.zeros((GROUP * 64, D), jnp.float32)
            for group in range(3):
                rows = []
                for token in range(GROUP):
                    given = grads_ref[slot, group, token]
                    value = unfold(given[64:].astype(jnp.float32)).astype(jnp.bfloat16)
                    rows.append(jnp.concatenate([given[:64], value], axis=1))
                taken = jnp.concatenate(rows, axis=0)
                total = total + nt(taken, weights[:, 192 * group : 192 * group + 192])
            partial_ref[slot] = total.reshape(GROUP, 64, D).astype(jnp.bfloat16)
            return carry

        lax.fori_loop(0, jnp.where(plane == HOST, slots, 1), one, 0)


def input_partial(net, grads, blocks):
    slots = grads.shape[0]
    return pl.pallas_call(
        functools.partial(input_kernel, net, slots),
        out_shape=jax.ShapeDtypeStruct((slots, GROUP, 64, D), jnp.bfloat16),
        in_specs=[VMEM] * (1 + len(blocks)),
        out_specs=VMEM,
        scratch_shapes=[pltpu.VMEM((D, blocks[0].shape[1]), jnp.bfloat16)],
        cost_estimate=pl.CostEstimate(flops=10**9, bytes_accessed=6 * 2**20, transcendentals=0),
        name="input_partial",
    )(grads, *blocks)


def solve_heads(me, head_ref, moment_ref, target, scratch):
    wide, semaphore, parts, moment = scratch[0], scratch[3], scratch[4], scratch[5]

    @pl.when(jnp.logical_or(me == OWNERS[0], jnp.logical_or(me == OWNERS[1], me == OWNERS[2])))
    def _():
        move(head_ref, parts, semaphore)
        move(moment_ref, moment, semaphore)

        def join(pair, carry):
            first = parts[2 * pair].astype(jnp.float32) + parts[HEADS + 2 * pair].astype(jnp.float32)
            second = parts[2 * pair + 1].astype(jnp.float32) + parts[HEADS + 2 * pair + 1].astype(jnp.float32)
            here = pl.ds(pl.multiple_of(pair * 128, 128), 128)
            gradient = jnp.concatenate([first, second], axis=0).T
            wide[:, here] = (0.75 * gradient + 0.25 * moment[:, here].astype(jnp.float32)).astype(jnp.bfloat16)
            return carry

        lax.fori_loop(0, HEADS // 2, join, 0)
        solve(D, target, scratch)


def solve_late(me, out_ref, ffn_ref, out_target, ffn_target, scratch):
    wide, semaphore = scratch[0], scratch[3]

    @pl.when(me == OWNERS[3])
    def _():
        move(out_ref, wide.at[:, pl.ds(0, D)], semaphore)
        solve(D, out_target, scratch)

    @pl.when(jnp.logical_or(me == OWNERS[4], jnp.logical_or(me == OWNERS[5], me == OWNERS[6])))
    def _():
        move(ffn_ref, wide, semaphore)
        solve(FF, ffn_target, scratch)


def move(source, target, semaphore):
    copy = pltpu.make_async_copy(source, target, semaphore)
    copy.start()
    copy.wait()


def solve(span, target, scratch):
    wide, gram, polynomial, semaphore = scratch[:4]

    def blocks_of(index):
        return pl.ds(pl.multiple_of(index * BLOCK, BLOCK), BLOCK)

    def mirror(target, i, j, block):
        target[i * BLOCK : (i + 1) * BLOCK, j * BLOCK : (j + 1) * BLOCK] = block.astype(jnp.bfloat16)
        if i != j:
            target[j * BLOCK : (j + 1) * BLOCK, i * BLOCK : (i + 1) * BLOCK] = block.T.astype(jnp.bfloat16)

    chunks = span // BLOCK

    def measure(index, total):
        values = wide[:, blocks_of(index)].astype(jnp.float32)
        return total + jnp.sum(values * values, axis=0, keepdims=True)

    total = lax.fori_loop(0, chunks, measure, jnp.zeros((1, BLOCK), jnp.float32))
    frobenius = jnp.sqrt(jnp.sum(total, axis=1, keepdims=True)) + 1e-07

    def scale(index, carry):
        here = blocks_of(index)
        wide[:, here] = (wide[:, here].astype(jnp.float32) / frobenius).astype(jnp.bfloat16)
        return carry

    lax.fori_loop(0, chunks, scale, 0)

    def step(_, carry):
        for i in range(D // BLOCK):
            for j in range(i + 1):
                mirror(
                    gram,
                    i,
                    j,
                    nt(
                        wide[i * BLOCK : (i + 1) * BLOCK, :span],
                        wide[j * BLOCK : (j + 1) * BLOCK, :span],
                    ),
                )
        for i in range(D // BLOCK):
            for j in range(i + 1):
                square = nn(gram[i * BLOCK : (i + 1) * BLOCK, :], gram[:, j * BLOCK : (j + 1) * BLOCK])
                linear = gram[i * BLOCK : (i + 1) * BLOCK, j * BLOCK : (j + 1) * BLOCK].astype(jnp.float32)
                mirror(polynomial, i, j, COEFF_B * linear + COEFF_C * square)

        def advance(index, inner):
            here = blocks_of(index)
            old = wide[:, here]
            wide[:, here] = (COEFF_A * old.astype(jnp.float32) + nn(polynomial[...], old)).astype(jnp.bfloat16)
            return inner

        lax.fori_loop(0, chunks, advance, 0)
        return carry

    lax.fori_loop(0, NS_STEPS, step, 0)
    move(wide.at[:, pl.ds(0, span)], target, semaphore)


def solve_scratch(span, heads):
    square = pltpu.VMEM((D, D), jnp.bfloat16)
    shapes = [pltpu.VMEM((D, span), jnp.bfloat16), square, square, pltpu.SemaphoreType.DMA]
    if heads:
        shapes += [pltpu.VMEM((2 * HEADS, HEAD_DIM, D), jnp.bfloat16), square]
    return shapes


SQUARE = jax.ShapeDtypeStruct((D, D), jnp.bfloat16)
SOLVE_COST = pl.CostEstimate(flops=25 * 10**9, bytes_accessed=8 * 2**20, transcendentals=0)


def newton_kernel(net, head_ref, moment_ref, out_ref, ffn_ref, attn_target, ffn_target, *scratch):
    me = net.me()
    solve_heads(me, head_ref, moment_ref, attn_target, scratch)
    solve_late(me, out_ref, ffn_ref, attn_target, ffn_target, scratch)


def newton(net, *sources):
    return pl.pallas_call(
        functools.partial(newton_kernel, net),
        out_shape=[SQUARE, jax.ShapeDtypeStruct((D, FF), jnp.bfloat16)],
        in_specs=[ANY] * 4,
        out_specs=[ANY] * 2,
        scratch_shapes=solve_scratch(FF, True),
        cost_estimate=SOLVE_COST,
        name="newton",
    )(*sources)


def on_device(net, tokens, doc_ids, cotangent, attn_weight, ffn_weight, attn_moment, ffn_moment):
    micro_count, token_count, width = tokens.shape
    rows = attn_weight.shape[1]
    count, planes = net.count, net.planes
    length = count * token_count
    me = net.me()
    plane, place = me // GROUP, me % GROUP
    x_bit = place // 4
    both = micro_count * token_count
    part = FF // GROUP
    low = jnp.bfloat16
    everything = (slice(None),)

    own_tokens = tokens.reshape(both, width)
    out_grad = cotangent.reshape(both, width)
    hidden = own_tokens.astype(jnp.float32)
    normed, columns, shares, cut, moment_cut, out_low, moment_low, out_moment = prepare(
        own_tokens, doc_ids, attn_weight, ffn_weight, attn_moment, ffn_moment
    )
    all_tokens, all_columns, plane_cut, plane_out, moment_plane, moment_out, plane_shares = gather_tokens(
        net,
        0,
        normed.reshape(micro_count, token_count, width),
        columns,
        [
            Flow(0, 0, lambda i, j: j % GROUP, lambda i, j: i % GROUP, size=GROUP),
            Across(net, 1, 1, lambda i, j: 0, lambda i, j: i // GROUP),
            Across(net, 3, 3, lambda i, j: 0, lambda i, j: i // GROUP, lambda i, j: j // GROUP == SPARE),
        ]
        + [
            Flow(2, 2, lambda i, j: j % GROUP, lambda i, j: i % GROUP, size=GROUP),
            Flow(4, 4, lambda i, j: j % 4, lambda i, j: i % GROUP, size=GROUP),
        ],
        [cut, out_low, moment_cut, out_moment, shares],
        [
            jax.ShapeDtypeStruct(cut.shape, low),
            jax.ShapeDtypeStruct((planes, rows, D), low),
            jax.ShapeDtypeStruct(cut.shape, low),
            jax.ShapeDtypeStruct((planes, rows, D), low),
            jax.ShapeDtypeStruct((GROUP,) + shares.shape[1:], low),
        ],
    )
    late_own = plane_cut.reshape(GROUP * rows, 3 * part)
    late_blocks = [late_own] + [net.shift(late_own, step) for step in range(1, planes)]

    head_weights = all_columns.reshape(D, 4 * HEAD_DIM)
    every_count = jnp.sum(all_columns[:, 0, 3 * HEAD_DIM :].astype(jnp.float32), axis=0)
    own_count = lax.dynamic_slice_in_dim(every_count, x_bit * DOCS, DOCS, 0)
    starts = jnp.cumsum(own_count) - own_count
    index = jnp.arange(length).astype(jnp.float32)
    start = jnp.max(jnp.where(starts[:, None] <= index[None, :], starts[:, None], 0.0), axis=0)
    inverse = 10000.0 ** (-(jnp.arange(HALF, dtype=jnp.float32) * 2.0) / HEAD_DIM)
    angles = inverse[:, None] * (index - start)[None, :]
    cosine, sine = jnp.cos(angles), jnp.sin(angles)
    start = start.astype(jnp.int32)
    diagonal = jnp.arange(length // WIDE, dtype=jnp.int32) * (WIDE // KEYS)
    first = jnp.clip(start[::WIDE] // KEYS, 0, diagonal)
    first = jnp.stack([first, jnp.clip((start[WIDE - 1 :: WIDE] + KEYS - 1) // KEYS, first, diagonal)])
    start = start[None, :]

    qkv, mixed, total, packed = attend(net, first, all_tokens, head_weights, cosine, sine, start)
    mixed_parts, moment_whole, plane_out_grad, out_full = exchange(
        net,
        "mixed_exchange",
        1,
        [PlaneGather(2, 2), PlaneGather(3, 3, lambda i: everything + (i % GROUP,))]
        + [Flow(0, 0, lambda i, j: j, lambda i, j: combo_of(i), lambda i, j: attends(i))]
        + [FanIn(1, 1, OWNERS[k], lambda i, j, k=k: k, lambda i, j: i) for k in range(3)],
        [packed, moment_low, out_grad, plane_out],
        [
            jax.ShapeDtypeStruct((2 * HEADS, HALF, 128), low),
            jax.ShapeDtypeStruct((count, rows, D), low),
            jax.ShapeDtypeStruct((GROUP, both, width), low),
            jax.ShapeDtypeStruct((planes, GROUP, rows, D), low),
        ],
    )
    plane_out_grad = plane_out_grad.reshape(GROUP * both, width)
    out_full = out_full.reshape(D, D)
    mixed_tokens, middle, second = after_attention(mixed_parts, own_tokens, out_full)
    (plane_second,) = exchange(
        net,
        "second_exchange",
        10,
        [PlaneGather(0, 0)],
        [second],
        [jax.ShapeDtypeStruct((GROUP, both, width), low)],
        GROUP,
    )
    plane_second = plane_second.reshape(GROUP * both, width)
    second_terms, result_terms, *ffn_terms = feed_forward(net, plane_second, plane_out_grad, late_blocks)
    sides = (2, 2, 2, both, width)
    (second_grad,) = exchange(
        net,
        "second_grad_exchange",
        11,
        [PlaneScatter(0, 0, (both, width))],
        [second_terms.reshape(sides)],
        [jax.ShapeDtypeStruct((both, width), jnp.float32)],
        GROUP,
    )
    ffn_block = ffn_terms[0].astype(jnp.float32)
    for step in range(1, planes):
        ffn_block = ffn_block + net.shift(ffn_terms[step], step).astype(jnp.float32)
    ffn_update = 0.75 * ffn_block + 0.25 * moment_plane.reshape(GROUP * rows, 3 * part).astype(jnp.float32)
    ffn_update, ffn_block = ffn_update.astype(low), ffn_block.astype(low)
    middle_grad, folded, out_terms = before_attention(second_grad, middle, out_grad, mixed_tokens, out_full)
    grad_parts, out_total, ffn_whole, out_whole = exchange(
        net,
        "mixed_grad_exchange",
        2,
        [
            PlaneScatter(1, 1, (rows, D), (planes,), moment=3, whole=3),
            Flow(0, 0, lambda i, j: combo_of(j), lambda i, j: i, lambda i, j: attends(j)),
        ]
        + [
            FanIn(
                2,
                2,
                OWNERS[4 + k],
                lambda i, j, k=k: (slice(None), pl.ds(part * k, part)),
                lambda i, j: (i // GROUP, slice(None), pl.ds(pl.multiple_of(part * (i % GROUP), part), part)),
            )
            for k in range(3)
        ],
        [folded, out_terms.reshape(planes, 2, 2, 2, rows, D), ffn_update, moment_out],
        [
            jax.ShapeDtypeStruct((count, HALF, 128), low),
            jax.ShapeDtypeStruct((planes, rows, D), jnp.float32),
            jax.ShapeDtypeStruct((planes, GROUP * rows, FF), low),
            jax.ShapeDtypeStruct((planes, GROUP, rows, D), low),
        ],
    )
    grad_parts, plane_shares = lax.optimization_barrier((grad_parts, plane_shares))
    share_own = plane_shares.reshape(GROUP * rows, 10 * HEAD_DIM)
    share_blocks = [share_own]
    for step in range(1, planes):
        hop = [(i, (i + GROUP * step) % count) for i in range(count)]
        share_blocks.append(net.permute(share_own, [(i, j) for i, j in hop if j // GROUP < 4 and j // GROUP != SPARE]))
    grad_packed, head_grad = attend_back(
        net, first, all_tokens, qkv, mixed, total, cosine, sine, start, grad_parts
    )
    head_low = head_grad.astype(low)
    (head_whole,) = exchange(
        net,
        "head_exchange",
        9,
        [
            FanIn(0, 0, OWNERS[k], lambda i, j, k=k: k, lambda i, j: combo_of(i), lambda i, j: attends(i))
            for k in range(3)
        ],
        [head_low.reshape(3, HEAD_DIM, D)],
        [jax.ShapeDtypeStruct((2 * HEADS, HEAD_DIM, D), low)],
        meet=net.meet_heads,
    )
    grad_packed, head_low, head_whole = lax.optimization_barrier((grad_packed, head_low, head_whole))
    guests = [p for p in range(planes) if p >= 4 or p == SPARE]
    slots = 1 + len(guests)
    head_rows = jnp.pad(head_low.T.reshape(count, rows, 3 * HEAD_DIM), ((0, 0), (0, 0), (0, 64)))

    def group_of(device):
        return device // GROUP - (device // GROUP) // 3

    def waits(device):
        return jnp.logical_not(attends(device))

    def head_flow(runs):
        return Flow(
            0, 0, lambda i, j: j, lambda i, j: combo_of(i), lambda i, j: jnp.logical_and(attends(i), runs(j))
        )

    row_shape = jax.ShapeDtypeStruct((2 * HEADS, rows, 256), low)
    early_rows, host_grads = exchange(
        net,
        "attending_exchange",
        7,
        [
            Across(
                net,
                1,
                1,
                lambda i, j: j // GROUP,
                lambda i, j: (0, group_of(i)),
                lambda i, j: jnp.logical_and(attends(i), attends(j)),
            )
        ]
        + [
            FanAcross(
                net, 1, 1, HOST, lambda i, j, p=p: p, lambda i, j, k=k: (1 + k, group_of(i)), lambda i, j: attends(i)
            )
            for k, p in enumerate(guests)
        ]
        + [head_flow(attends)],
        [head_rows, grad_packed.reshape(planes, GROUP, 96, 128)],
        [row_shape, jax.ShapeDtypeStruct((slots, 3, GROUP, 96, 128), low)],
        meet=net.meet_attending,
    )
    partial = input_partial(net, host_grads, share_blocks)
    attn_done, ffn_done = newton(
        net, head_whole, moment_whole.reshape(D, D), out_whole.reshape(D, D), ffn_whole.reshape(D, FF)
    )
    attn_done, ffn_done, partial, early_rows = lax.optimization_barrier((attn_done, ffn_done, partial, early_rows))

    def guest_index(device):
        p = device // GROUP
        return p - SPARE - jnp.minimum(p // 4, 1)

    late_rows, ffn_parts, attn_step, ffn_step, out_row_grad, input_parts, result = exchange(
        net,
        "step_exchange",
        5,
        [PlaneScatter(6, 6, (both, width))]
        + [FanOut(3, 3, OWNERS[4 + k], lambda i, j: j, lambda i, j, k=k: k) for k in range(3)]
        + [FanOut(2, 2, OWNERS[k], lambda i, j: j, lambda i, j, k=k: k) for k in range(4)]
        + [
            Flow(
                5,
                5,
                lambda i, j: (1 + guest_index(j), j % GROUP),
                lambda i, j: i % GROUP,
                lambda i, j: jnp.logical_and(i // GROUP == HOST, waits(j)),
            ),
            Flow(5, 5, lambda i, j: (0, j % GROUP), lambda i, j: i % GROUP, lambda i, j: attends(i), size=GROUP),
            Flow(1, 1, lambda i, j: j % GROUP, lambda i, j: i % GROUP, size=GROUP),
            Across(net, 4, 4, lambda i, j: j // GROUP, lambda i, j: 0, lambda i, j: i // GROUP == SPARE),
            head_flow(waits),
        ],
        [
            head_rows,
            ffn_block.reshape(GROUP, rows, 3 * part),
            attn_done.reshape(count, rows, D),
            ffn_done.reshape(count, rows, FF),
            out_total.astype(low),
            partial,
            result_terms.reshape(sides),
        ],
        [
            row_shape,
            jax.ShapeDtypeStruct((GROUP, rows, 3 * part), low),
            jax.ShapeDtypeStruct((4, rows, D), low),
            jax.ShapeDtypeStruct((3, rows, FF), low),
            jax.ShapeDtypeStruct((1, rows, D), low),
            jax.ShapeDtypeStruct((GROUP, token_count, width), low),
            jax.ShapeDtypeStruct((both, width), jnp.float32),
        ],
    )
    row_parts = jnp.where(attends(me), early_rows, late_rows)
    normed_grad = jnp.sum(input_parts.reshape(2, 4, token_count, width).astype(jnp.float32), axis=1).reshape(both, width)
    input_grad = middle_grad + norm_back(hidden, normed_grad)
    ffn_grad = ffn_parts.reshape(GROUP, rows, 3, part).transpose(2, 1, 0, 3).reshape(3, rows, FF).astype(jnp.float32)
    ffn_moment_new = 0.5 * ffn_moment + 0.5 * ffn_grad

    summed = jnp.sum(row_parts.reshape(micro_count, HEADS, rows, 256).astype(jnp.float32), axis=0)
    early_grad = summed[:, :, : 3 * HEAD_DIM].reshape(HEADS, rows, 3, HEAD_DIM).transpose(2, 1, 0, 3).reshape(3, rows, D)
    attn_grad = jnp.concatenate([early_grad, out_row_grad.astype(jnp.float32)], axis=0)
    attn_moment_new = 0.5 * attn_moment + 0.5 * attn_grad

    output = (middle + result).astype(low)

    rates = jnp.asarray(RATES, jnp.float32)[:, None, None]
    attn_master = attn_weight - rates[:4] * attn_step.astype(jnp.float32)
    ffn_master = ffn_weight - rates[4:] * ffn_step.astype(jnp.float32)
    shape = (micro_count, token_count, width)
    return (
        output.reshape(shape),
        input_grad.reshape(shape),
        attn_grad,
        ffn_grad,
        attn_master,
        ffn_master,
        attn_moment_new,
        ffn_moment_new,
        attn_master.astype(low),
        ffn_master.astype(low),
    )


def solution(mesh):
    wide = P(None, ("blk", "head"), None)
    return jax.shard_map(
        functools.partial(on_device, Net(mesh)),
        mesh=mesh,
        in_specs=(wide, P(None, ("blk", "head")), wide, wide, wide, wide, wide),
        out_specs=(wide,) * 10,
        check_vma=False,
    )
```

```python
import functools
import math

import jax
import jax.numpy as jnp
from jax import lax
from jax.experimental import pallas as pl
from jax.experimental.pallas import tpu as pltpu
from jax.sharding import PartitionSpec as P

D = 768
HEADS = 12
HEAD_DIM = 64
HALF = 32
FF = 2048
DOCS = 4
NS_STEPS = 5
GROUP = 8
HOST = 1
SPARE = 2
KEYS = 512
BLOCK = 256
WIDE = 512

EPSILON = 1e-05
NEGATIVE = -1e30
RATES = (0.5, 0.5, 0.5, 7.0, 1.0, 1.0, 0.5)
COEFF_A = 3.4445
COEFF_B = -4.775
COEFF_C = 2.0315
OWNERS = (18, 19, 22, 21, 16, 17, 20)
MESH = pl.DeviceIdType.MESH
ANY = pl.BlockSpec(memory_space=pl.ANY)
VMEM = pl.BlockSpec(memory_space=pltpu.VMEM)
SMEM = pl.BlockSpec(memory_space=pltpu.SMEM)
SCALE = HEAD_DIM ** (-0.5)


def nt(a, b):
    return lax.dot_general(a, b, (((1,), (1,)), ((), ())), preferred_element_type=jnp.float32)


def nn(a, b):
    return jnp.dot(a, b, preferred_element_type=jnp.float32)


def attends(device):
    plane = device // GROUP
    return jnp.logical_and(plane < 4, plane != SPARE)


def combo_of(device):
    plane = device // GROUP
    place = device % GROUP
    return (place // 4) * HEADS + 4 * (plane - plane // 3) + place % 4


def device_of(combo):
    group = (combo % HEADS) // 4
    return GROUP * (group + group // 2) + 4 * (combo // HEADS) + combo % 4


class Net:
    def __init__(self, mesh):
        self.inner = mesh.shape["head"]
        self.count = mesh.shape["head"] * mesh.shape["blk"]
        self.planes = self.count // GROUP

    def permute(self, values, pairs):
        outer = self.count // self.inner

        def place(device):
            return (device % self.inner) * outer + device // self.inner

        return lax.ppermute(values, ("head", "blk"), [(place(i), place(j)) for i, j in pairs])

    def me(self):
        return lax.axis_index("blk") * self.inner + lax.axis_index("head")

    def at(self, device):
        return {"blk": device // self.inner, "head": device % self.inner}

    def meet(self, me, size):
        self.greet(me, size)
        pl.semaphore_wait(pltpu.get_barrier_semaphore(), size - 1)

    def greet(self, me, size):
        barrier = pltpu.get_barrier_semaphore()

        def greet(k, carry):
            pl.semaphore_signal(barrier, inc=1, device_id=self.at(peer(me, k, size)), device_id_type=MESH)
            return carry

        lax.fori_loop(1, size, greet, 0)

    def meet_attending(self, me):
        barrier = pltpu.get_barrier_semaphore()

        @pl.when(attends(me))
        def _():
            def greet(combo, carry):
                other = device_of(combo)

                @pl.when(other != me)
                def _():
                    pl.semaphore_signal(barrier, inc=1, device_id=self.at(other), device_id_type=MESH)

                return carry

            lax.fori_loop(0, 2 * HEADS, greet, 0)
            pl.semaphore_wait(barrier, 2 * HEADS - 1)

    def meet_heads(self, me):
        barrier = pltpu.get_barrier_semaphore()

        @pl.when(attends(me))
        def _():
            for owner in OWNERS[:3]:
                pl.semaphore_signal(barrier, inc=1, device_id=self.at(owner), device_id_type=MESH)
            pl.semaphore_wait(barrier, 3)

        for owner in OWNERS[:3]:

            @pl.when(me == owner)
            def _():
                def greet(combo, carry):
                    pl.semaphore_signal(barrier, inc=1, device_id=self.at(device_of(combo)), device_id_type=MESH)
                    return carry

                lax.fori_loop(0, 2 * HEADS, greet, 0)
                pl.semaphore_wait(barrier, 2 * HEADS)

    def shift(self, values, steps):
        far = GROUP * steps
        return self.permute(values, [(i, (i + far) % self.count) for i in range(self.count)])

    def flip(self, values, distance):
        return self.permute(values, [(i, i ^ distance) for i in range(self.count)])


def peer(me, k, size):
    return (me // size) * size + (me % size + k) % size


def flip_x(device):
    return device + 4 - 8 * ((device % GROUP) // 4)


def flip_y(device):
    return device + 1 - 2 * (device % 2)


def flip_core(device):
    return device + 2 - 4 * ((device % 4) // 2)


class Flow:
    def __init__(self, source, target, take, put, goes=None, size=None):
        self.source, self.target, self.take, self.put = source, target, take, put
        self.goes = goes or (lambda i, j: i >= 0)
        self.size = size

    def scratch(self):
        return []

    def semaphores(self):
        return self.size

    def bind(self, net, inputs, outputs, scratch, send, receive, local):
        self.net = net
        self.input, self.output = inputs[self.source], outputs[self.target]
        self.held = scratch
        self.send, self.receive, self.local = send, receive, local

    def copy(self, source, target, index, device):
        return pltpu.make_async_remote_copy(
            source,
            target,
            self.send.at[index],
            self.receive.at[index],
            device_id=self.net.at(device),
            device_id_type=MESH,
        )

    def remote(self, i, j, k):
        return self.copy(self.input.at[self.take(i, j)], self.output.at[self.put(i, j)], k, j)

    def near(self, i):
        return pltpu.make_async_copy(self.input.at[self.take(i, i)], self.output.at[self.put(i, i)], self.local)

    def start(self, me):
        def one(k, carry):
            other = peer(me, k, self.size)

            @pl.when(self.goes(me, other))
            def _():
                self.remote(me, other, k).start()

            return carry

        lax.fori_loop(1, self.size, one, 0)

        @pl.when(self.goes(me, me))
        def _():
            self.near(me).start()

    def middle(self, me):
        pass

    def finish(self, me):
        def one(k, carry):
            other = peer(me, k, self.size)

            @pl.when(self.goes(me, other))
            def _():
                self.remote(me, other, k).wait_send()

            before = peer(me, self.size - k, self.size)

            @pl.when(self.goes(before, me))
            def _():
                self.remote(before, me, k).wait_recv()

            return carry

        lax.fori_loop(1, self.size, one, 0)

        @pl.when(self.goes(me, me))
        def _():
            self.near(me).wait()


class Across(Flow):
    def __init__(self, net, source, target, take, put, goes=None):
        super().__init__(source, target, take, put, goes, net.count)
        self.planes = net.planes

    def semaphores(self):
        return self.planes

    def other(self, me, k):
        return (me + k * GROUP) % self.size

    def start(self, me):
        for k in range(1, self.planes):
            far = self.other(me, k)

            @pl.when(self.goes(me, far))
            def _(k=k, far=far):
                self.remote(me, far, k).start()

        @pl.when(self.goes(me, me))
        def _():
            self.near(me).start()

    def finish(self, me):
        for k in range(1, self.planes):
            far, before = self.other(me, k), self.other(me, self.planes - k)

            @pl.when(self.goes(me, far))
            def _(k=k, far=far):
                self.remote(me, far, k).wait_send()

            @pl.when(self.goes(before, me))
            def _(k=k, before=before):
                self.remote(before, me, k).wait_recv()

        @pl.when(self.goes(me, me))
        def _():
            self.near(me).wait()


class FanAcross(Across):
    def __init__(self, net, source, target, plane, take, put, goes):
        super().__init__(
            net,
            source,
            target,
            take,
            put,
            lambda i, j: jnp.logical_and(goes(i, j), j // GROUP == plane),
        )


class FanIn(Flow):
    def __init__(self, source, target, owner, take, put, goes=None, size=None):
        super().__init__(source, target, take, put, goes, size)
        self.place = owner

    def owner(self, me):
        return (me // self.size) * self.size + self.place

    def sends(self, me):
        return jnp.logical_and(me % self.size != self.place, self.goes(me, self.owner(me)))

    def step(self, me):
        return (self.place - me % self.size + self.size) % self.size

    def start(self, me):
        @pl.when(self.sends(me))
        def _():
            self.remote(me, self.owner(me), self.step(me)).start()

        @pl.when(jnp.logical_and(me % self.size == self.place, self.goes(me, me)))
        def _():
            self.near(me).start()

    def finish(self, me):
        @pl.when(self.sends(me))
        def _():
            self.remote(me, self.owner(me), self.step(me)).wait_send()

        @pl.when(me % self.size == self.place)
        def _():
            def one(k, carry):
                before = peer(me, self.size - k, self.size)

                @pl.when(self.goes(before, me))
                def _():
                    self.remote(before, me, k).wait_recv()

                return carry

            lax.fori_loop(1, self.size, one, 0)

        @pl.when(jnp.logical_and(me % self.size == self.place, self.goes(me, me)))
        def _():
            self.near(me).wait()


class FanOut(Flow):
    def __init__(self, source, target, owner, take, put):
        super().__init__(source, target, take, put)
        self.owner = owner

    def start(self, me):
        @pl.when(me == self.owner)
        def _():
            def one(k, carry):
                self.remote(me, peer(me, k, self.size), k).start()
                return carry

            lax.fori_loop(1, self.size, one, 0)
            self.near(me).start()

    def finish(self, me):
        @pl.when(me == self.owner)
        def _():
            def one(k, carry):
                self.remote(me, peer(me, k, self.size), k).wait_send()
                return carry

            lax.fori_loop(1, self.size, one, 0)
            self.near(me).wait()

        @pl.when(me != self.owner)
        def _():
            self.remote(self.owner, me, (me - self.owner + self.net.count) % self.size).wait_recv()


class PlaneGather(Flow):
    def __init__(self, source, target, put=lambda i: i % GROUP):
        super().__init__(source, target, None, put)

    def semaphores(self):
        return GROUP

    def partners(self, me):
        return [flip_x(me), flip_y(me), flip_x(flip_y(me))]

    def place(self, device):
        return self.output.at[self.put(device)]

    def own(self, me, index, device):
        return self.copy(self.input, self.place(me), index, device)

    def passed(self, me, index, partner):
        return self.copy(self.place(partner), self.place(partner), 4 + index, flip_core(me))

    def start(self, me):
        for index, partner in enumerate(self.partners(me)):
            self.own(me, 1 + index, partner).start()
        self.own(me, 0, flip_core(me)).start()
        pltpu.make_async_copy(self.input, self.place(me), self.local).start()

    def middle(self, me):
        for index, partner in enumerate(self.partners(me)):
            self.own(me, 1 + index, partner).wait_recv()
            self.passed(me, index, partner).start()

    def finish(self, me):
        for index, partner in enumerate(self.partners(me)):
            self.own(me, 1 + index, partner).wait_send()
            self.passed(me, index, partner).wait()
        self.own(me, 0, flip_core(me)).wait()
        pltpu.make_async_copy(self.input, self.place(me), self.local).wait()


class PlaneScatter(Flow):
    def __init__(self, source, target, block, lead=(), runs=None, moment=None, whole=None):
        super().__init__(source, target, None, None)
        self.block, self.lead = block, lead
        self.gathers, self.moment_source, self.whole_target = moment is not None, moment, whole
        self.runs = runs or (lambda i: i >= 0)
        self.every = (slice(None),) * len(lead)

    def scratch(self):
        pair = pltpu.VMEM(self.lead + (2, 2) + self.block, jnp.bfloat16)
        shapes = [pair, pair, pltpu.VMEM((3,) + self.lead + self.block, jnp.bfloat16)]
        if self.gathers:
            shapes += [
                pltpu.VMEM(self.lead + self.block, jnp.bfloat16),
                pltpu.VMEM(self.lead + self.lead + self.block, jnp.bfloat16),
                pltpu.VMEM(self.lead + self.block, jnp.bfloat16),
                pltpu.VMEM(self.lead + self.block, jnp.bfloat16),
            ]
        return shapes

    def bind(self, net, inputs, outputs, scratch, send, receive, local):
        super().bind(net, inputs, outputs, scratch, send, receive, local)
        if self.gathers:
            self.moment, self.whole = inputs[self.moment_source], outputs[self.whole_target]

    def momentum(self):
        return pltpu.make_async_copy(self.moment, self.held[5], self.receive.at[5 + SPARE])

    def direction(self, place):
        index = 5 + self.lead[0] + place
        return self.copy(self.held[6], self.whole.at[:, place], index, OWNERS[3])

    def close(self, me):
        place = me % GROUP
        for source in range(self.lead[0]):
            if source != SPARE:
                self.onward(me, source).wait_recv()
                self.output[...] += self.held[4][source].astype(jnp.float32)
        self.momentum().start()
        self.momentum().wait()
        self.held[6][...] = (0.75 * self.output[...] + 0.25 * self.held[5][...].astype(jnp.float32)).astype(jnp.bfloat16)

        @pl.when(me != OWNERS[3])
        def _():
            self.direction(place).start()
            self.direction(place).wait_send()

        @pl.when(me == OWNERS[3])
        def _():
            own = pltpu.make_async_copy(self.held[6], self.whole.at[:, place], self.local)
            own.start()
            own.wait()
            for other in range(GROUP):
                if other != OWNERS[3] % GROUP:
                    self.direction(other).wait_recv()

    def semaphores(self):
        return 5 + (self.lead[0] + GROUP if self.gathers else 0)

    def onward(self, me, source):
        spare = GROUP * SPARE + me % GROUP
        return self.copy(self.held[3], self.held[4].at[source], 5 + source, spare)

    def partners(self, me):
        return [flip_x(me), flip_y(me), flip_x(flip_y(me))]

    def half(self, core):
        return self.input.at[self.every + (slice(None), core)]

    def first(self, me):
        return self.copy(self.half(1 - (me % 4) // 2), self.held[1], 0, flip_core(me))

    def mine(self, me):
        return pltpu.make_async_copy(self.half((me % 4) // 2), self.held[0], self.local)

    def spot(self, device):
        return self.every + ((device % GROUP) // 4, device % 2)

    def second(self, me, index, partner):
        return self.copy(self.held[0].at[self.spot(partner)], self.held[2].at[index], 1 + index, partner)

    def start(self, me):
        @pl.when(self.runs(me))
        def _():
            self.first(me).start()
            self.mine(me).start()

    def pair(self, device):
        spot = self.spot(device)
        return self.held[0][spot].astype(jnp.float32) + self.held[1][spot].astype(jnp.float32)

    def middle(self, me):
        @pl.when(self.runs(me))
        def _():
            self.mine(me).wait()
            self.first(me).wait_recv()
            for index, partner in enumerate(self.partners(me)):
                self.held[0][self.spot(partner)] = self.pair(partner).astype(jnp.bfloat16)
                self.second(me, index, partner).start()

    def finish(self, me):
        @pl.when(self.runs(me))
        def _():
            total = self.pair(me)
            for index, partner in enumerate(self.partners(me)):
                self.second(me, index, partner).wait_recv()
                total = total + self.held[2][index].astype(jnp.float32)
            if self.gathers:
                plane = me // GROUP
                self.held[3][...] = total.astype(jnp.bfloat16)

                @pl.when(plane != SPARE)
                def _():
                    self.onward(me, plane).start()

            self.output[...] = total
            self.first(me).wait_send()
            for index, partner in enumerate(self.partners(me)):
                self.second(me, index, partner).wait_send()
            if self.gathers:

                @pl.when(plane != SPARE)
                def _():
                    self.onward(me, plane).wait_send()

                @pl.when(plane == SPARE)
                def _():
                    self.close(me)


def bind_all(net, flows, inputs, outputs, refs):
    for number, flow in enumerate(flows):
        need = len(flow.scratch())
        held, (send, receive), refs = refs[:need], refs[need : need + 2], refs[need + 2 :]
        flow.bind(net, inputs, outputs, held, send, receive, refs[-1].at[number])


def exchange_kernel(net, meet, flows, sources, targets, *refs):
    inputs = refs[:sources]
    outputs = refs[sources : sources + targets]
    me = net.me()
    meet(me)
    bind_all(net, flows, inputs, outputs, refs[sources + targets :])
    for flow in flows:
        flow.start(me)
    for flow in flows:
        flow.middle(me)
    for flow in flows:
        flow.finish(me)


def flow_scratch(flows):
    shapes = []
    for flow in flows:
        shapes += flow.scratch() + [pltpu.SemaphoreType.DMA((flow.semaphores(),))] * 2
    return shapes + [pltpu.SemaphoreType.DMA((len(flows),))]


def exchange(net, name, number, flows, sources, shapes, size=None, meet=None):
    size = size or net.count
    for flow in flows:
        flow.size = flow.size or size
    summed = {flow.target for flow in flows if isinstance(flow, PlaneScatter)}
    moved = sum(math.prod(s.shape) * s.dtype.itemsize for s in shapes)
    return pl.pallas_call(
        functools.partial(
            exchange_kernel, net, meet or (lambda me: net.meet(me, size)), flows, len(sources), len(shapes)
        ),
        out_shape=shapes,
        in_specs=[ANY] * len(sources),
        out_specs=[VMEM if k in summed else ANY for k in range(len(shapes))],
        scratch_shapes=flow_scratch(flows),
        compiler_params=pltpu.CompilerParams(collective_id=number, has_side_effects=True),
        cost_estimate=pl.CostEstimate(flops=0, bytes_accessed=8 * moved, transcendentals=0),
        name=name,
    )(*sources)


def gather_kernel(net, flows, extras, x_ref, w_ref, *refs):
    extra_refs, (all_ref, wall_ref), refs = refs[:extras], refs[extras : extras + 2], refs[extras + 2 :]
    extra_all, (send, receive, wsend, wreceive, local), refs = refs[:extras], refs[extras : extras + 5], refs[extras + 5 :]
    count = net.count
    planes = net.planes
    me = net.me()
    plane = me // GROUP
    place = me % GROUP
    half = place // 4
    spot = place % 4
    across = flip_x(me)
    beside = flip_y(me)
    sibling = flip_core(me)
    net.meet(me, count)
    bind_all(net, flows, extra_refs, extra_all, refs)

    def remote(source, target, index, device):
        return pltpu.make_async_remote_copy(
            source, target, send.at[index], receive.at[index], device_id=net.at(device), device_id_type=MESH
        )

    swap = remote(x_ref.at[1 - half], all_ref.at[plane, half, spot], 0, across)
    swap.start()

    def second(step, which):
        target = (me + step * GROUP) % count
        block = all_ref.at[plane, which, spot]
        return remote(block, block, 1 + (step - 1) * 2 + (which + half) % 2, target)

    def direct(step):
        target = (me + step * GROUP) % count
        return remote(x_ref.at[half], all_ref.at[plane, half, spot], 1 + (step - 1) * 2, target)

    third_base = 1 + 2 * (planes - 1)

    def third(step, which):
        source_plane = (plane + planes - step) % planes
        block = all_ref.at[source_plane, which, spot]
        return remote(block, block, third_base + step * 2 + which, beside)

    fourth_base = third_base + 2 * planes

    def fourth(step, which):
        source_plane = (plane + planes - step) % planes
        block = all_ref.at[source_plane, which, pl.ds((spot // 2) * 2, 2)]
        return remote(block, block, fourth_base + step * 2 + which, sibling)

    for step in range(1, planes):
        direct(step).start()
    mine = pltpu.make_async_copy(x_ref.at[half], all_ref.at[plane, half, spot], local.at[0])
    mine.start()

    def weights(combo):
        target = device_of(combo)
        return pltpu.make_async_remote_copy(
            w_ref.at[combo % HEADS],
            wall_ref.at[me],
            wsend.at[combo],
            wreceive.at[me],
            device_id=net.at(target),
            device_id_type=MESH,
        )

    def send_weights(combo, carry):
        @pl.when(device_of(combo) != me)
        def _():
            weights(combo).start()

        return carry

    mine.wait()
    swap.wait_recv()
    for step in range(1, planes):
        second(step, 1 - half).start()
    for which in range(2):
        third(0, which).start()
    lax.fori_loop(0, 2 * HEADS, send_weights, 0)
    for flow in flows:
        flow.start(me)
    for step in range(planes):
        if step > 0:
            second(step, half).wait_recv()
            second(step, 1 - half).wait_recv()
            for which in range(2):
                third(step, which).start()
            for which in range(2):
                third(step - 1, which).wait_recv()
            for which in range(2):
                fourth(step - 1, which).start()
    for which in range(2):
        third(planes - 1, which).wait_recv()
    for which in range(2):
        fourth(planes - 1, which).start()
    for step in range(planes):
        for which in range(2):
            fourth(step, which).wait_recv()

    @pl.when(attends(me))
    def _():
        own = pltpu.make_async_copy(w_ref.at[combo_of(me) % HEADS], wall_ref.at[me], local.at[1])
        own.start()
        own.wait()

        def took(k, carry):
            before = (me + k) % count
            pltpu.make_async_remote_copy(
                w_ref.at[0],
                wall_ref.at[before],
                wsend.at[0],
                wreceive.at[before],
                device_id=net.at(before),
                device_id_type=MESH,
            ).wait_recv()
            return carry

        lax.fori_loop(1, count, took, 0)

    def sent(combo, carry):
        @pl.when(device_of(combo) != me)
        def _():
            weights(combo).wait_send()

        return carry

    lax.fori_loop(0, 2 * HEADS, sent, 0)
    swap.wait_send()
    for step in range(1, planes):
        direct(step).wait_send()
        second(step, 1 - half).wait_send()
    for step in range(planes):
        for which in range(2):
            third(step, which).wait_send()
            fourth(step, which).wait_send()
    for flow in flows:
        flow.finish(me)


def gather_tokens(net, number, normed, columns, flows, extras, shapes):
    planes = net.planes
    copies = 1 + 2 * (planes - 1) + 4 * planes
    for flow in flows:
        flow.size = flow.size or net.count
    shapes = [
        jax.ShapeDtypeStruct((planes, 2, 4) + normed.shape[1:], normed.dtype),
        jax.ShapeDtypeStruct((net.count,) + columns.shape[1:], columns.dtype),
    ] + shapes
    return pl.pallas_call(
        functools.partial(gather_kernel, net, flows, len(extras)),
        out_shape=shapes,
        in_specs=[ANY] * (2 + len(extras)),
        out_specs=[ANY] * len(shapes),
        scratch_shapes=[
            pltpu.SemaphoreType.DMA((copies,)),
            pltpu.SemaphoreType.DMA((copies,)),
            pltpu.SemaphoreType.DMA((2 * HEADS,)),
            pltpu.SemaphoreType.DMA((net.count,)),
            pltpu.SemaphoreType.DMA((2,)),
        ]
        + flow_scratch(flows),
        compiler_params=pltpu.CompilerParams(collective_id=number, has_side_effects=True),
        cost_estimate=pl.CostEstimate(flops=0, bytes_accessed=100 * 2**20, transcendentals=0),
        name="gather_tokens",
    )(normed, columns, *extras)


def rope_rows(values, cosine, sine):
    first, second = values[:HALF], values[HALF:]
    return jnp.concatenate([first * cosine - second * sine, second * cosine + first * sine], axis=0)


def rope_rows_back(values, cosine, sine):
    first, second = values[:HALF], values[HALF:]
    return jnp.concatenate([first * cosine + second * sine, second * cosine - first * sine], axis=0)


def columns_of(index):
    return pl.ds(pl.multiple_of(index * BLOCK, BLOCK), BLOCK)


def wide_columns(index):
    return pl.ds(pl.multiple_of(index * WIDE, WIDE), WIDE)


def permitted(query_block, key_block, start):
    shape = (KEYS, WIDE)
    key = key_block * KEYS + lax.broadcasted_iota(jnp.int32, shape, 0)
    query = query_block * WIDE + lax.broadcasted_iota(jnp.int32, shape, 1)
    return (key <= query) & (key >= start)


def sweep(bounds_ref, query_block, step, carried):
    diagonal = query_block * (WIDE // KEYS)
    first, whole = bounds_ref[0, query_block], bounds_ref[1, query_block]
    carried = lax.fori_loop(first, whole, functools.partial(step, True), carried)
    carried = lax.fori_loop(whole, diagonal, functools.partial(step, False), carried)
    return lax.fori_loop(diagonal, diagonal + WIDE // KEYS, functools.partial(step, True), carried)


def fold(rows):
    return jnp.concatenate([rows[:HALF], rows[HALF:]], axis=1)


def unfold(rows):
    return jnp.concatenate([rows[:, :HEAD_DIM], rows[:, HEAD_DIM:]], axis=0)


def attend_kernel(net, *refs):
    @pl.when(attends(net.me()))
    def _():
        attend_body(*refs)


def attend_body(first_ref, x_ref, w_ref, cos_ref, sin_ref, start_ref, qkv_ref, mixed_ref, total_ref, packed_ref, key_rows):
    blocks = qkv_ref.shape[1] // BLOCK
    weights = w_ref[...].astype(jnp.float32).T[: 3 * HEAD_DIM].astype(jnp.bfloat16)

    def project(chunk, carry):
        tokens = x_ref[chunk // 2, chunk % 2].reshape(BLOCK, D)
        here = columns_of(chunk)
        made = nt(weights, tokens)
        cosine, sine = cos_ref[:, here], sin_ref[:, here]
        query = rope_rows(made[:HEAD_DIM], cosine, sine)
        key = rope_rows(made[HEAD_DIM : 2 * HEAD_DIM], cosine, sine)
        qkv_ref[:HEAD_DIM, here] = query.astype(jnp.bfloat16) * SCALE
        qkv_ref[HEAD_DIM : 2 * HEAD_DIM, here] = key.astype(jnp.bfloat16)
        qkv_ref[2 * HEAD_DIM :, here] = made[2 * HEAD_DIM :].astype(jnp.bfloat16)
        key_rows[here, :] = key.T.astype(jnp.bfloat16)
        return carry

    lax.fori_loop(0, blocks, project, 0)

    def query_step(query_block, carry):
        here = wide_columns(query_block)
        query = qkv_ref[:HEAD_DIM, here]
        start = start_ref[:, here]

        def key_step(masked, key_block, held):
            top, total, mixed = held
            there = pl.ds(pl.multiple_of(key_block * KEYS, KEYS), KEYS)
            scores = nn(key_rows[there, :], query)
            if masked:
                allowed = permitted(query_block, key_block, start)
                scores = jnp.where(allowed, scores, NEGATIVE)
            new_top = jnp.maximum(top, jnp.max(scores, axis=0, keepdims=True))
            weights = jnp.exp(scores - new_top)
            if masked:
                weights = jnp.where(allowed, weights, 0.0)
            factor = jnp.exp(top - new_top)
            total = total * factor + jnp.sum(weights, axis=0, keepdims=True)
            mixed = mixed * factor + nn(qkv_ref[2 * HEAD_DIM :, there], weights.astype(jnp.bfloat16))
            return new_top, total, mixed

        top, total, mixed = sweep(
            first_ref,
            query_block,
            key_step,
            (
                jnp.full((1, WIDE), NEGATIVE, jnp.float32),
                jnp.zeros((1, WIDE), jnp.float32),
                jnp.zeros((HEAD_DIM, WIDE), jnp.float32),
            ),
        )
        mixed = mixed / total
        mixed_ref[:, here] = mixed
        total_ref[:, here] = top + jnp.log(total)
        rows = mixed.T
        for part in range(WIDE // 64):
            packed_ref[query_block * (WIDE // 64) + part] = fold(rows[part * 64 : part * 64 + 64]).astype(
                jnp.bfloat16
            )
        return carry

    lax.fori_loop(0, qkv_ref.shape[1] // WIDE, query_step, 0)


def attend(net, first, tokens, weights, cosine, sine, start):
    length = start.shape[1]
    return pl.pallas_call(
        functools.partial(attend_kernel, net),
        out_shape=[
            jax.ShapeDtypeStruct((3 * HEAD_DIM, length), jnp.bfloat16),
            jax.ShapeDtypeStruct((HEAD_DIM, length), jnp.float32),
            jax.ShapeDtypeStruct((1, length), jnp.float32),
            jax.ShapeDtypeStruct((net.count, HALF, 128), jnp.bfloat16),
        ],
        in_specs=[SMEM] + [VMEM] * 5,
        out_specs=[VMEM] * 4,
        scratch_shapes=[pltpu.VMEM((length, HEAD_DIM), jnp.bfloat16)],
        cost_estimate=pl.CostEstimate(flops=2 * 10**9, bytes_accessed=8 * 2**20, transcendentals=2 * 10**6),
        name="attend",
    )(first, tokens, weights, cosine, sine, start)


def attend_back_kernel(net, *refs):
    @pl.when(attends(net.me()))
    def _():
        attend_back_body(*refs)


def attend_back_body(
    first_ref,
    x_ref,
    qkv_ref,
    mixed_ref,
    total_ref,
    cos_ref,
    sin_ref,
    start_ref,
    grad_ref,
    packed_ref,
    low_ref,
    turned_ref,
    query_rows,
    key_rows,
    value_rows,
    grad_rows,
    grad_columns,
    correction,
    key_grad,
    value_grad,
    all_grad,
    weight_ref,
):
    blocks = qkv_ref.shape[1] // BLOCK
    parts = BLOCK // 64

    def prepare(chunk, carry):
        here = columns_of(chunk)
        turned = qkv_ref[:, here].astype(jnp.float32)
        query_rows[here, :] = turned[:HEAD_DIM].T.astype(jnp.bfloat16)
        key_rows[here, :] = turned[HEAD_DIM : 2 * HEAD_DIM].T.astype(jnp.bfloat16)
        value_rows[here, :] = turned[2 * HEAD_DIM :].T.astype(jnp.bfloat16)
        pieces = [unfold(grad_ref[chunk * parts + part].astype(jnp.float32)) for part in range(parts)]
        rows = jnp.concatenate(pieces, axis=0)
        grad_rows[here, :] = rows.astype(jnp.bfloat16)
        across = rows.T
        grad_columns[:, here] = across.astype(jnp.bfloat16)
        correction[:, here] = jnp.sum(across * mixed_ref[:, here], axis=0, keepdims=True)
        key_grad[here, :] = jnp.zeros((BLOCK, HEAD_DIM), jnp.float32)
        value_grad[here, :] = jnp.zeros((BLOCK, HEAD_DIM), jnp.float32)
        return carry

    lax.fori_loop(0, blocks, prepare, 0)

    wide_parts = WIDE // 64

    def query_step(query_block, carry):
        here = wide_columns(query_block)
        query = qkv_ref[:HEAD_DIM, here]
        start = start_ref[:, here]
        total = total_ref[:, here]
        fix = correction[:, here]
        grad = grad_columns[:, here]
        query_in_rows = query_rows[here, :]
        grad_in_rows = grad_rows[here, :]

        def key_step(masked, key_block, query_grad):
            there = pl.ds(pl.multiple_of(key_block * KEYS, KEYS), KEYS)
            scores = nn(key_rows[there, :], query)
            weights = jnp.exp(scores - total)
            if masked:
                weights = jnp.where(permitted(query_block, key_block, start), weights, 0.0)
            value_grad[there, :] += nn(weights.astype(jnp.bfloat16), grad_in_rows)
            slope = nn(value_rows[there, :], grad)
            change = (weights * (slope - fix)).astype(jnp.bfloat16)
            key_grad[there, :] += nn(change, query_in_rows)
            return query_grad + nn(qkv_ref[HEAD_DIM : 2 * HEAD_DIM, there], change)

        query_grad = sweep(first_ref, query_block, key_step, jnp.zeros((HEAD_DIM, WIDE), jnp.float32))
        query_grad = rope_rows_back(query_grad * SCALE, cos_ref[:, here], sin_ref[:, here])
        all_grad[:HEAD_DIM, here] = query_grad.astype(jnp.bfloat16)
        rows = query_grad.T.astype(jnp.bfloat16)
        for part in range(wide_parts):
            packed_ref[query_block * wide_parts + part, :64, :HEAD_DIM] = rows[part * 64 : part * 64 + 64]
        return carry

    lax.fori_loop(0, qkv_ref.shape[1] // WIDE, query_step, 0)
    weight_ref[...] = jnp.zeros(weight_ref.shape, jnp.float32)

    def close(chunk, carry):
        here = columns_of(chunk)
        key = rope_rows_back(key_grad[here, :].T, cos_ref[:, here], sin_ref[:, here])
        value = value_grad[here, :]
        all_grad[HEAD_DIM : 2 * HEAD_DIM, here] = key.astype(jnp.bfloat16)
        all_grad[2 * HEAD_DIM :, here] = value.T.astype(jnp.bfloat16)
        rows = key.T.astype(jnp.bfloat16)
        for part in range(parts):
            token = chunk * parts + part
            packed_ref[token, :64, HEAD_DIM:] = rows[part * 64 : part * 64 + 64]
            packed_ref[token, 64:, :] = fold(value[part * 64 : part * 64 + 64]).astype(jnp.bfloat16)
        tokens = x_ref[chunk // 2, chunk % 2].reshape(BLOCK, D)
        weight_ref[...] += nn(all_grad[:, here], tokens)
        return carry

    lax.fori_loop(0, blocks, close, 0)
    low_ref[...] = weight_ref[...].astype(jnp.bfloat16)
    turned_ref[:, : 3 * HEAD_DIM] = weight_ref[...].T.astype(jnp.bfloat16)
    turned_ref[:, 3 * HEAD_DIM :] = jnp.zeros((D, HEAD_DIM), jnp.bfloat16)


def attend_back(net, first, tokens, qkv, mixed, total, cosine, sine, start, grad):
    length = start.shape[1]
    rows = pltpu.VMEM((length, HEAD_DIM), jnp.bfloat16)
    sums = pltpu.VMEM((length, HEAD_DIM), jnp.float32)
    return pl.pallas_call(
        functools.partial(attend_back_kernel, net),
        out_shape=[
            jax.ShapeDtypeStruct((net.count, 96, 128), jnp.bfloat16),
            jax.ShapeDtypeStruct((3 * HEAD_DIM, D), jnp.bfloat16),
            jax.ShapeDtypeStruct((D, 4 * HEAD_DIM), jnp.bfloat16),
        ],
        in_specs=[SMEM] + [VMEM] * 8,
        out_specs=[VMEM] * 3,
        scratch_shapes=[
            rows,
            rows,
            rows,
            rows,
            pltpu.VMEM((HEAD_DIM, length), jnp.bfloat16),
            pltpu.VMEM((1, length), jnp.float32),
            sums,
            sums,
            pltpu.VMEM((3 * HEAD_DIM, length), jnp.bfloat16),
            pltpu.VMEM((3 * HEAD_DIM, D), jnp.float32),
        ],
        cost_estimate=pl.CostEstimate(flops=4 * 10**9, bytes_accessed=12 * 2**20, transcendentals=2 * 10**6),
        name="attend_back",
    )(first, tokens, qkv, mixed, total, cosine, sine, start, grad)


def tn(a, b):
    return lax.dot_general(a, b, (((0,), (0,)), ((), ())), preferred_element_type=jnp.float32)


def mean_of(values):
    return jnp.mean(values, axis=-1, keepdims=True)


def layer_norm(values):
    center = values - mean_of(values)
    return center * lax.rsqrt(mean_of(center * center) + EPSILON)


def norm_back(values, gradient):
    center = values - mean_of(values)
    inverse = lax.rsqrt(mean_of(center * center) + EPSILON)
    normed = center * inverse
    return inverse * (gradient - mean_of(gradient) - normed * mean_of(gradient * normed))


def prepare_kernel(
    tokens_ref,
    documents_ref,
    attn_ref,
    ffn_ref,
    attn_moment_ref,
    ffn_moment_ref,
    normed_ref,
    columns_ref,
    shares_ref,
    cut_ref,
    moment_cut_ref,
    out_ref,
    moment_ref,
    out_moment_ref,
):
    low = jnp.bfloat16
    normed_ref[...] = layer_norm(tokens_ref[...].astype(jnp.float32)).astype(low)
    documents = documents_ref[...]
    lane = lax.broadcasted_iota(jnp.int32, (1, HEAD_DIM), 1)
    tail = jnp.zeros((1, HEAD_DIM), jnp.float32)
    for document in range(DOCS):
        counts = jnp.sum((documents == document).astype(jnp.float32), axis=1, keepdims=True)
        for micro in range(documents.shape[0]):
            tail = jnp.where(lane == micro * DOCS + document, counts[micro : micro + 1], tail)
    rows = attn_ref.shape[1]
    tail = jnp.broadcast_to(tail, (rows, HEAD_DIM))
    empty = jnp.zeros((rows, HEAD_DIM), jnp.float32)
    for head in range(HEADS):
        here = slice(HEAD_DIM * head, HEAD_DIM * head + HEAD_DIM)
        three = [attn_ref[matrix, :, here] for matrix in range(3)]
        columns_ref[head] = jnp.concatenate(three + [tail], axis=1).astype(low)
    for share in range(4):
        pieces = []
        for head in range(share, HEADS, 4):
            here = slice(HEAD_DIM * head, HEAD_DIM * head + HEAD_DIM)
            pieces += [attn_ref[matrix, :, here] for matrix in range(3)]
        shares_ref[share] = jnp.concatenate(pieces + [empty], axis=1).astype(low)
    part = FF // GROUP
    for place in range(GROUP):
        here = slice(part * place, part * place + part)
        for matrix in range(3):
            there = slice(part * matrix, part * matrix + part)
            cut_ref[place, :, there] = ffn_ref[matrix, :, here].astype(low)
            moment_cut_ref[place, :, there] = ffn_moment_ref[matrix, :, here].astype(low)
    out_ref[0] = attn_ref[3].astype(low)
    moment_ref[...] = attn_moment_ref[...].astype(low)
    out_moment_ref[0] = attn_moment_ref[3].astype(low)


def prepare(tokens, documents, attn, ffn, attn_moment, ffn_moment):
    rows = attn.shape[1]
    low = jnp.bfloat16
    cut = jax.ShapeDtypeStruct((GROUP, rows, 3 * FF // GROUP), low)
    return pl.pallas_call(
        prepare_kernel,
        out_shape=[
            jax.ShapeDtypeStruct(tokens.shape, low),
            jax.ShapeDtypeStruct((HEADS, rows, 4 * HEAD_DIM), low),
            jax.ShapeDtypeStruct((4, rows, 10 * HEAD_DIM), low),
            cut,
            cut,
            jax.ShapeDtypeStruct((1, rows, D), low),
            jax.ShapeDtypeStruct((4, rows, D), low),
            jax.ShapeDtypeStruct((1, rows, D), low),
        ],
        in_specs=[VMEM] * 6,
        out_specs=[VMEM] * 8,
        cost_estimate=pl.CostEstimate(flops=10**7, bytes_accessed=4 * 2**20, transcendentals=0),
        name="prepare",
    )(tokens, documents, attn, ffn, attn_moment, ffn_moment)


def after_kernel(parts_ref, tokens_ref, out_ref, mixed_ref, middle_ref, second_ref):
    for micro in range(2):
        here = slice(64 * micro, 64 * micro + 64)
        for pair in range(HEADS // 2):
            two = [unfold(parts_ref[micro * HEADS + 2 * pair + k].astype(jnp.float32)) for k in range(2)]
            mixed_ref[here, 128 * pair : 128 * pair + 128] = jnp.concatenate(two, axis=1).astype(jnp.bfloat16)
    middle = tokens_ref[...].astype(jnp.float32) + nn(mixed_ref[...], out_ref[...])
    middle_ref[...] = middle
    second_ref[...] = layer_norm(middle).astype(jnp.bfloat16)


def after_attention(parts, tokens, out):
    shape = tokens.shape
    return pl.pallas_call(
        after_kernel,
        out_shape=[
            jax.ShapeDtypeStruct(shape, jnp.bfloat16),
            jax.ShapeDtypeStruct(shape, jnp.float32),
            jax.ShapeDtypeStruct(shape, jnp.bfloat16),
        ],
        in_specs=[VMEM] * 3,
        out_specs=[VMEM] * 3,
        cost_estimate=pl.CostEstimate(flops=2 * 10**8, bytes_accessed=3 * 2**20, transcendentals=0),
        name="after_attention",
    )(parts, tokens, out)


def feed_forward_kernel(net, *refs):
    planes = net.planes
    second_ref, cotangent_ref = refs[:2]
    blocks = refs[2 : 2 + planes]
    second_terms, result_terms = refs[2 + planes : 4 + planes]
    terms = refs[4 + planes : 4 + 2 * planes]
    weights, slopes, products, sums = refs[4 + 2 * planes :]
    plane = net.me() // GROUP
    span = D // planes
    part = FF // GROUP
    for step, block in enumerate(blocks):
        source = (plane + planes - step) % planes
        weights[pl.ds(pl.multiple_of(source * span, span), span), :] = block[...]

    def forward(chunk, carry):
        here = columns_of(chunk)
        second, cotangent = second_ref[here, :], cotangent_ref[here, :]
        both = nn(second, weights[:, : 2 * part])
        gate, up = both[:, :part], both[:, part:]
        sigmoid = jax.nn.sigmoid(gate)
        silu = gate * sigmoid
        product = (silu * up).astype(jnp.bfloat16)
        change = nn(cotangent, weights[:, 2 * part :])
        slopes[here, :part] = (change * up * sigmoid * (1.0 + gate * (1.0 - sigmoid))).astype(jnp.bfloat16)
        slopes[here, part:] = (change * silu).astype(jnp.bfloat16)
        products[here, :] = product
        second_terms[here, :] = nt(slopes[here, :], weights[:, : 2 * part]).astype(jnp.bfloat16)
        result_terms[here, :] = nt(product, weights[:, 2 * part :]).astype(jnp.bfloat16)
        return carry

    lax.fori_loop(0, second_ref.shape[0] // BLOCK, forward, 0)
    for begin in range(0, D, BLOCK):
        here = slice(begin, begin + BLOCK)
        sums[here, : 2 * part] = tn(second_ref[:, here], slopes[...]).astype(jnp.bfloat16)
        sums[here, 2 * part :] = tn(cotangent_ref[:, here], products[...]).astype(jnp.bfloat16)
    for step, term in enumerate(terms):
        target = (plane + step) % planes
        term[...] = sums[pl.ds(pl.multiple_of(target * span, span), span), :]


def feed_forward(net, second, cotangent, blocks):
    tokens = second.shape[0]
    part = FF // GROUP
    low = jnp.bfloat16
    return pl.pallas_call(
        functools.partial(feed_forward_kernel, net),
        out_shape=[jax.ShapeDtypeStruct((tokens, D), low)] * 2
        + [jax.ShapeDtypeStruct((D // net.planes, 3 * part), low)] * net.planes,
        in_specs=[VMEM] * (2 + net.planes),
        out_specs=[VMEM] * (2 + net.planes),
        scratch_shapes=[
            pltpu.VMEM((D, 3 * part), low),
            pltpu.VMEM((tokens, 2 * part), low),
            pltpu.VMEM((tokens, part), low),
            pltpu.VMEM((D, 3 * part), low),
        ],
        cost_estimate=pl.CostEstimate(flops=35 * 10**8, bytes_accessed=10 * 2**20, transcendentals=10**6),
        name="feed_forward",
    )(second, cotangent, *blocks)


def before_kernel(second_grad_ref, middle_ref, cotangent_ref, mixed_ref, out_ref, middle_grad_ref, folded_ref, terms_ref):
    middle_grad = cotangent_ref[...].astype(jnp.float32) + norm_back(middle_ref[...], second_grad_ref[...])
    middle_grad_ref[...] = middle_grad
    low = middle_grad.astype(jnp.bfloat16)
    mixed_grad = nt(low, out_ref[...])
    for micro in range(2):
        rows = mixed_grad[64 * micro : 64 * micro + 64]
        for head in range(HEADS):
            folded_ref[micro * HEADS + head] = fold(rows[:, HEAD_DIM * head : HEAD_DIM * head + HEAD_DIM]).astype(
                jnp.bfloat16
            )
    terms_ref[...] = tn(mixed_ref[...], low).astype(jnp.bfloat16)


def before_attention(second_grad, middle, cotangent, mixed, out):
    return pl.pallas_call(
        before_kernel,
        out_shape=[
            jax.ShapeDtypeStruct(middle.shape, jnp.float32),
            jax.ShapeDtypeStruct((2 * HEADS, HALF, 128), jnp.bfloat16),
            jax.ShapeDtypeStruct((D, D), jnp.bfloat16),
        ],
        in_specs=[VMEM] * 5,
        out_specs=[VMEM] * 3,
        cost_estimate=pl.CostEstimate(flops=4 * 10**8, bytes_accessed=5 * 2**20, transcendentals=0),
        name="before_attention",
    )(second_grad, middle, cotangent, mixed, out)


def input_kernel(net, slots, grads_ref, *refs):
    blocks, partial_ref, weights = refs[: net.planes], refs[net.planes], refs[net.planes + 1]
    me = net.me()
    plane = me // GROUP
    span = D // net.planes

    @pl.when(attends(me))
    def _():
        for step, block in enumerate(blocks):
            source = (plane + net.planes - step) % net.planes
            weights[pl.ds(pl.multiple_of(source * span, span), span), :] = block[...]

        def one(slot, carry):
            total = jnp.zeros((GROUP * 64, D), jnp.float32)
            for group in range(3):
                rows = []
                for token in range(GROUP):
                    given = grads_ref[slot, group, token]
                    value = unfold(given[64:].astype(jnp.float32)).astype(jnp.bfloat16)
                    rows.append(jnp.concatenate([given[:64], value], axis=1))
                taken = jnp.concatenate(rows, axis=0)
                total = total + nt(taken, weights[:, 192 * group : 192 * group + 192])
            partial_ref[slot] = total.reshape(GROUP, 64, D).astype(jnp.bfloat16)
            return carry

        lax.fori_loop(0, jnp.where(plane == HOST, slots, 1), one, 0)


def input_partial(net, grads, blocks):
    slots = grads.shape[0]
    return pl.pallas_call(
        functools.partial(input_kernel, net, slots),
        out_shape=jax.ShapeDtypeStruct((slots, GROUP, 64, D), jnp.bfloat16),
        in_specs=[VMEM] * (1 + len(blocks)),
        out_specs=VMEM,
        scratch_shapes=[pltpu.VMEM((D, blocks[0].shape[1]), jnp.bfloat16)],
        cost_estimate=pl.CostEstimate(flops=10**9, bytes_accessed=6 * 2**20, transcendentals=0),
        name="input_partial",
    )(grads, *blocks)


def solve_heads(me, head_ref, moment_ref, target, scratch):
    wide, semaphore, parts, moment = scratch[0], scratch[3], scratch[4], scratch[5]

    @pl.when(jnp.logical_or(me == OWNERS[0], jnp.logical_or(me == OWNERS[1], me == OWNERS[2])))
    def _():
        move(head_ref, parts, semaphore)
        move(moment_ref, moment, semaphore)

        def join(pair, carry):
            first = parts[2 * pair].astype(jnp.float32) + parts[HEADS + 2 * pair].astype(jnp.float32)
            second = parts[2 * pair + 1].astype(jnp.float32) + parts[HEADS + 2 * pair + 1].astype(jnp.float32)
            here = pl.ds(pl.multiple_of(pair * 128, 128), 128)
            gradient = jnp.concatenate([first, second], axis=0).T
            wide[:, here] = (0.75 * gradient + 0.25 * moment[:, here].astype(jnp.float32)).astype(jnp.bfloat16)
            return carry

        lax.fori_loop(0, HEADS // 2, join, 0)
        solve(D, target, scratch)


def solve_late(me, out_ref, ffn_ref, out_target, ffn_target, scratch):
    wide, semaphore = scratch[0], scratch[3]

    @pl.when(me == OWNERS[3])
    def _():
        move(out_ref, wide.at[:, pl.ds(0, D)], semaphore)
        solve(D, out_target, scratch)

    @pl.when(jnp.logical_or(me == OWNERS[4], jnp.logical_or(me == OWNERS[5], me == OWNERS[6])))
    def _():
        move(ffn_ref, wide, semaphore)
        solve(FF, ffn_target, scratch)


def move(source, target, semaphore):
    copy = pltpu.make_async_copy(source, target, semaphore)
    copy.start()
    copy.wait()


def solve(span, target, scratch):
    wide, gram, polynomial, semaphore = scratch[:4]

    def blocks_of(index):
        return pl.ds(pl.multiple_of(index * BLOCK, BLOCK), BLOCK)

    def mirror(target, i, j, block):
        target[i * BLOCK : (i + 1) * BLOCK, j * BLOCK : (j + 1) * BLOCK] = block.astype(jnp.bfloat16)
        if i != j:
            target[j * BLOCK : (j + 1) * BLOCK, i * BLOCK : (i + 1) * BLOCK] = block.T.astype(jnp.bfloat16)

    chunks = span // BLOCK

    def measure(index, total):
        values = wide[:, blocks_of(index)].astype(jnp.float32)
        return total + jnp.sum(values * values, axis=0, keepdims=True)

    total = lax.fori_loop(0, chunks, measure, jnp.zeros((1, BLOCK), jnp.float32))
    frobenius = jnp.sqrt(jnp.sum(total, axis=1, keepdims=True)) + 1e-07

    def scale(index, carry):
        here = blocks_of(index)
        wide[:, here] = (wide[:, here].astype(jnp.float32) / frobenius).astype(jnp.bfloat16)
        return carry

    lax.fori_loop(0, chunks, scale, 0)

    def step(_, carry):
        for i in range(D // BLOCK):
            for j in range(i + 1):
                mirror(
                    gram,
                    i,
                    j,
                    nt(
                        wide[i * BLOCK : (i + 1) * BLOCK, :span],
                        wide[j * BLOCK : (j + 1) * BLOCK, :span],
                    ),
                )
        for i in range(D // BLOCK):
            for j in range(i + 1):
                square = nn(gram[i * BLOCK : (i + 1) * BLOCK, :], gram[:, j * BLOCK : (j + 1) * BLOCK])
                linear = gram[i * BLOCK : (i + 1) * BLOCK, j * BLOCK : (j + 1) * BLOCK].astype(jnp.float32)
                mirror(polynomial, i, j, COEFF_B * linear + COEFF_C * square)

        def advance(index, inner):
            here = blocks_of(index)
            old = wide[:, here]
            wide[:, here] = (COEFF_A * old.astype(jnp.float32) + nn(polynomial[...], old)).astype(jnp.bfloat16)
            return inner

        lax.fori_loop(0, chunks, advance, 0)
        return carry

    lax.fori_loop(0, NS_STEPS, step, 0)
    move(wide.at[:, pl.ds(0, span)], target, semaphore)


def solve_scratch(span, heads):
    square = pltpu.VMEM((D, D), jnp.bfloat16)
    shapes = [pltpu.VMEM((D, span), jnp.bfloat16), square, square, pltpu.SemaphoreType.DMA]
    if heads:
        shapes += [pltpu.VMEM((2 * HEADS, HEAD_DIM, D), jnp.bfloat16), square]
    return shapes


SQUARE = jax.ShapeDtypeStruct((D, D), jnp.bfloat16)
SOLVE_COST = pl.CostEstimate(flops=25 * 10**9, bytes_accessed=8 * 2**20, transcendentals=0)


def newton_kernel(net, head_ref, moment_ref, out_ref, ffn_ref, attn_target, ffn_target, *scratch):
    me = net.me()
    solve_heads(me, head_ref, moment_ref, attn_target, scratch)
    solve_late(me, out_ref, ffn_ref, attn_target, ffn_target, scratch)


def newton(net, *sources):
    return pl.pallas_call(
        functools.partial(newton_kernel, net),
        out_shape=[SQUARE, jax.ShapeDtypeStruct((D, FF), jnp.bfloat16)],
        in_specs=[ANY] * 4,
        out_specs=[ANY] * 2,
        scratch_shapes=solve_scratch(FF, True),
        cost_estimate=SOLVE_COST,
        name="newton",
    )(*sources)


def on_device(net, tokens, doc_ids, cotangent, attn_weight, ffn_weight, attn_moment, ffn_moment):
    micro_count, token_count, width = tokens.shape
    rows = attn_weight.shape[1]
    count, planes = net.count, net.planes
    length = count * token_count
    me = net.me()
    plane, place = me // GROUP, me % GROUP
    x_bit = place // 4
    both = micro_count * token_count
    part = FF // GROUP
    low = jnp.bfloat16
    everything = (slice(None),)

    own_tokens = tokens.reshape(both, width)
    out_grad = cotangent.reshape(both, width)
    hidden = own_tokens.astype(jnp.float32)
    normed, columns, shares, cut, moment_cut, out_low, moment_low, out_moment = prepare(
        own_tokens, doc_ids, attn_weight, ffn_weight, attn_moment, ffn_moment
    )
    all_tokens, all_columns, plane_cut, plane_out, moment_plane, moment_out, plane_shares = gather_tokens(
        net,
        0,
        normed.reshape(micro_count, token_count, width),
        columns,
        [
            Flow(0, 0, lambda i, j: j % GROUP, lambda i, j: i % GROUP, size=GROUP),
            Across(net, 1, 1, lambda i, j: 0, lambda i, j: i // GROUP),
            Across(net, 3, 3, lambda i, j: 0, lambda i, j: i // GROUP, lambda i, j: j // GROUP == SPARE),
        ]
        + [
            Flow(2, 2, lambda i, j: j % GROUP, lambda i, j: i % GROUP, size=GROUP),
            Flow(4, 4, lambda i, j: j % 4, lambda i, j: i % GROUP, size=GROUP),
        ],
        [cut, out_low, moment_cut, out_moment, shares],
        [
            jax.ShapeDtypeStruct(cut.shape, low),
            jax.ShapeDtypeStruct((planes, rows, D), low),
            jax.ShapeDtypeStruct(cut.shape, low),
            jax.ShapeDtypeStruct((planes, rows, D), low),
            jax.ShapeDtypeStruct((GROUP,) + shares.shape[1:], low),
        ],
    )
    late_own = plane_cut.reshape(GROUP * rows, 3 * part)
    late_blocks = [late_own] + [net.shift(late_own, step) for step in range(1, planes)]

    head_weights = all_columns.reshape(D, 4 * HEAD_DIM)
    every_count = jnp.sum(all_columns[:, 0, 3 * HEAD_DIM :].astype(jnp.float32), axis=0)
    own_count = lax.dynamic_slice_in_dim(every_count, x_bit * DOCS, DOCS, 0)
    starts = jnp.cumsum(own_count) - own_count
    index = jnp.arange(length).astype(jnp.float32)
    start = jnp.max(jnp.where(starts[:, None] <= index[None, :], starts[:, None], 0.0), axis=0)
    inverse = 10000.0 ** (-(jnp.arange(HALF, dtype=jnp.float32) * 2.0) / HEAD_DIM)
    angles = inverse[:, None] * (index - start)[None, :]
    cosine, sine = jnp.cos(angles), jnp.sin(angles)
    start = start.astype(jnp.int32)
    diagonal = jnp.arange(length // WIDE, dtype=jnp.int32) * (WIDE // KEYS)
    first = jnp.clip(start[::WIDE] // KEYS, 0, diagonal)
    first = jnp.stack([first, jnp.clip((start[WIDE - 1 :: WIDE] + KEYS - 1) // KEYS, first, diagonal)])
    start = start[None, :]

    qkv, mixed, total, packed = attend(net, first, all_tokens, head_weights, cosine, sine, start)
    mixed_parts, moment_whole, plane_out_grad, out_full = exchange(
        net,
        "mixed_exchange",
        1,
        [PlaneGather(2, 2), PlaneGather(3, 3, lambda i: everything + (i % GROUP,))]
        + [Flow(0, 0, lambda i, j: j, lambda i, j: combo_of(i), lambda i, j: attends(i))]
        + [FanIn(1, 1, OWNERS[k], lambda i, j, k=k: k, lambda i, j: i) for k in range(3)],
        [packed, moment_low, out_grad, plane_out],
        [
            jax.ShapeDtypeStruct((2 * HEADS, HALF, 128), low),
            jax.ShapeDtypeStruct((count, rows, D), low),
            jax.ShapeDtypeStruct((GROUP, both, width), low),
            jax.ShapeDtypeStruct((planes, GROUP, rows, D), low),
        ],
    )
    plane_out_grad = plane_out_grad.reshape(GROUP * both, width)
    out_full = out_full.reshape(D, D)
    mixed_tokens, middle, second = after_attention(mixed_parts, own_tokens, out_full)
    (plane_second,) = exchange(
        net,
        "second_exchange",
        10,
        [PlaneGather(0, 0)],
        [second],
        [jax.ShapeDtypeStruct((GROUP, both, width), low)],
        GROUP,
    )
    plane_second = plane_second.reshape(GROUP * both, width)
    second_terms, result_terms, *ffn_terms = feed_forward(net, plane_second, plane_out_grad, late_blocks)
    sides = (2, 2, 2, both, width)
    (second_grad,) = exchange(
        net,
        "second_grad_exchange",
        11,
        [PlaneScatter(0, 0, (both, width))],
        [second_terms.reshape(sides)],
        [jax.ShapeDtypeStruct((both, width), jnp.float32)],
        GROUP,
    )
    ffn_block = ffn_terms[0].astype(jnp.float32)
    for step in range(1, planes):
        ffn_block = ffn_block + net.shift(ffn_terms[step], step).astype(jnp.float32)
    ffn_update = 0.75 * ffn_block + 0.25 * moment_plane.reshape(GROUP * rows, 3 * part).astype(jnp.float32)
    ffn_update, ffn_block = ffn_update.astype(low), ffn_block.astype(low)
    middle_grad, folded, out_terms = before_attention(second_grad, middle, out_grad, mixed_tokens, out_full)
    grad_parts, out_total, ffn_whole, out_whole = exchange(
        net,
        "mixed_grad_exchange",
        2,
        [
            PlaneScatter(1, 1, (rows, D), (planes,), moment=3, whole=3),
            Flow(0, 0, lambda i, j: combo_of(j), lambda i, j: i, lambda i, j: attends(j)),
        ]
        + [
            FanIn(
                2,
                2,
                OWNERS[4 + k],
                lambda i, j, k=k: (slice(None), pl.ds(part * k, part)),
                lambda i, j: (i // GROUP, slice(None), pl.ds(pl.multiple_of(part * (i % GROUP), part), part)),
            )
            for k in range(3)
        ],
        [folded, out_terms.reshape(planes, 2, 2, 2, rows, D), ffn_update, moment_out],
        [
            jax.ShapeDtypeStruct((count, HALF, 128), low),
            jax.ShapeDtypeStruct((planes, rows, D), jnp.float32),
            jax.ShapeDtypeStruct((planes, GROUP * rows, FF), low),
            jax.ShapeDtypeStruct((planes, GROUP, rows, D), low),
        ],
    )
    grad_parts, plane_shares = lax.optimization_barrier((grad_parts, plane_shares))
    share_own = plane_shares.reshape(GROUP * rows, 10 * HEAD_DIM)
    share_blocks = [share_own]
    for step in range(1, planes):
        hop = [(i, (i + GROUP * step) % count) for i in range(count)]
        share_blocks.append(net.permute(share_own, [(i, j) for i, j in hop if j // GROUP < 4 and j // GROUP != SPARE]))
    grad_packed, head_low, head_rows = attend_back(
        net, first, all_tokens, qkv, mixed, total, cosine, sine, start, grad_parts
    )
    (head_whole,) = exchange(
        net,
        "head_exchange",
        9,
        [
            FanIn(0, 0, OWNERS[k], lambda i, j, k=k: k, lambda i, j: combo_of(i), lambda i, j: attends(i))
            for k in range(3)
        ],
        [head_low.reshape(3, HEAD_DIM, D)],
        [jax.ShapeDtypeStruct((2 * HEADS, HEAD_DIM, D), low)],
        meet=net.meet_heads,
    )
    grad_packed, head_low, head_whole = lax.optimization_barrier((grad_packed, head_low, head_whole))
    guests = [p for p in range(planes) if p >= 4 or p == SPARE]
    slots = 1 + len(guests)
    head_rows = head_rows.reshape(count, rows, 4 * HEAD_DIM)

    def group_of(device):
        return device // GROUP - (device // GROUP) // 3

    def waits(device):
        return jnp.logical_not(attends(device))

    def head_flow(runs):
        return Flow(
            0, 0, lambda i, j: j, lambda i, j: combo_of(i), lambda i, j: jnp.logical_and(attends(i), runs(j))
        )

    row_shape = jax.ShapeDtypeStruct((2 * HEADS, rows, 256), low)
    early_rows, host_grads = exchange(
        net,
        "attending_exchange",
        7,
        [
            Across(
                net,
                1,
                1,
                lambda i, j: j // GROUP,
                lambda i, j: (0, group_of(i)),
                lambda i, j: jnp.logical_and(attends(i), attends(j)),
            )
        ]
        + [
            FanAcross(
                net, 1, 1, HOST, lambda i, j, p=p: p, lambda i, j, k=k: (1 + k, group_of(i)), lambda i, j: attends(i)
            )
            for k, p in enumerate(guests)
        ]
        + [head_flow(attends)],
        [head_rows, grad_packed.reshape(planes, GROUP, 96, 128)],
        [row_shape, jax.ShapeDtypeStruct((slots, 3, GROUP, 96, 128), low)],
        meet=net.meet_attending,
    )
    partial = input_partial(net, host_grads, share_blocks)
    attn_done, ffn_done = newton(
        net, head_whole, moment_whole.reshape(D, D), out_whole.reshape(D, D), ffn_whole.reshape(D, FF)
    )
    attn_done, ffn_done, partial, early_rows = lax.optimization_barrier((attn_done, ffn_done, partial, early_rows))

    def guest_index(device):
        p = device // GROUP
        return p - SPARE - jnp.minimum(p // 4, 1)

    late_rows, ffn_parts, attn_step, ffn_step, out_row_grad, input_parts, result = exchange(
        net,
        "step_exchange",
        5,
        [PlaneScatter(6, 6, (both, width))]
        + [FanOut(3, 3, OWNERS[4 + k], lambda i, j: j, lambda i, j, k=k: k) for k in range(3)]
        + [FanOut(2, 2, OWNERS[k], lambda i, j: j, lambda i, j, k=k: k) for k in range(4)]
        + [
            Flow(
                5,
                5,
                lambda i, j: (1 + guest_index(j), j % GROUP),
                lambda i, j: i % GROUP,
                lambda i, j: jnp.logical_and(i // GROUP == HOST, waits(j)),
            ),
            Flow(5, 5, lambda i, j: (0, j % GROUP), lambda i, j: i % GROUP, lambda i, j: attends(i), size=GROUP),
            Flow(1, 1, lambda i, j: j % GROUP, lambda i, j: i % GROUP, size=GROUP),
            Across(net, 4, 4, lambda i, j: j // GROUP, lambda i, j: 0, lambda i, j: i // GROUP == SPARE),
            head_flow(waits),
        ],
        [
            head_rows,
            ffn_block.reshape(GROUP, rows, 3 * part),
            attn_done.reshape(count, rows, D),
            ffn_done.reshape(count, rows, FF),
            out_total.astype(low),
            partial,
            result_terms.reshape(sides),
        ],
        [
            row_shape,
            jax.ShapeDtypeStruct((GROUP, rows, 3 * part), low),
            jax.ShapeDtypeStruct((4, rows, D), low),
            jax.ShapeDtypeStruct((3, rows, FF), low),
            jax.ShapeDtypeStruct((1, rows, D), low),
            jax.ShapeDtypeStruct((GROUP, token_count, width), low),
            jax.ShapeDtypeStruct((both, width), jnp.float32),
        ],
    )
    row_parts = jnp.where(attends(me), early_rows, late_rows)
    normed_grad = jnp.sum(input_parts.reshape(2, 4, token_count, width).astype(jnp.float32), axis=1).reshape(both, width)
    input_grad = middle_grad + norm_back(hidden, normed_grad)
    ffn_grad = ffn_parts.reshape(GROUP, rows, 3, part).transpose(2, 1, 0, 3).reshape(3, rows, FF).astype(jnp.float32)
    ffn_moment_new = 0.5 * ffn_moment + 0.5 * ffn_grad

    summed = jnp.sum(row_parts.reshape(micro_count, HEADS, rows, 256).astype(jnp.float32), axis=0)
    early_grad = summed[:, :, : 3 * HEAD_DIM].reshape(HEADS, rows, 3, HEAD_DIM).transpose(2, 1, 0, 3).reshape(3, rows, D)
    attn_grad = jnp.concatenate([early_grad, out_row_grad.astype(jnp.float32)], axis=0)
    attn_moment_new = 0.5 * attn_moment + 0.5 * attn_grad

    output = (middle + result).astype(low)

    rates = jnp.asarray(RATES, jnp.float32)[:, None, None]
    attn_master = attn_weight - rates[:4] * attn_step.astype(jnp.float32)
    ffn_master = ffn_weight - rates[4:] * ffn_step.astype(jnp.float32)
    shape = (micro_count, token_count, width)
    return (
        output.reshape(shape),
        input_grad.reshape(shape),
        attn_grad,
        ffn_grad,
        attn_master,
        ffn_master,
        attn_moment_new,
        ffn_moment_new,
        attn_master.astype(low),
        ffn_master.astype(low),
    )


def solution(mesh):
    wide = P(None, ("blk", "head"), None)
    return jax.shard_map(
        functools.partial(on_device, Net(mesh)),
        mesh=mesh,
        in_specs=(wide, P(None, ("blk", "head")), wide, wide, wide, wide, wide),
        out_specs=(wide,) * 10,
        check_vma=False,
    )
```
